32 devices in a mesh: ctx: 8 (over y, x, core), wsh: 4 (over z).
Axes of the slice: x: 2, y: 2, z: 4, core: 2. Of those that a mesh axis runs over, the one named last changes fastest.
Arguments:
- tokens: bfloat16 [4, 2048, 1088], P('wsh', 'ctx'), may hold values from -6 to 6
- seq_lengths: int32 [4, 5], P('wsh'), may hold values from 96 to 1280, as said below
- cotangent: bfloat16 [4, 2048, 1088], P('wsh', 'ctx'), may hold values from -6 to 6
- ln1_gain: bfloat16 [1088], P('wsh'), may hold values from 0.5 to 1.5
- ln1_bias: bfloat16 [1088], P('wsh'), may hold values from -1.25 to 1.25
- w_qkv: bfloat16 [1088, 3264], P('wsh'), may hold values from -0.1875 to 0.1875
- b_query: bfloat16 [1088], P('wsh'), may hold values from -1.75 to 1.75
- b_value: bfloat16 [1088], P('wsh'), may hold values from -0.625 to 0.625
- w_out: bfloat16 [1088, 1088], P('wsh'), may hold values from -0.375 to 0.375
- b_out: bfloat16 [1088], P('wsh'), may hold values from -1.25 to 1.25
- ln2_gain: bfloat16 [1088], P('wsh'), may hold values from 0.5 to 1.5
- ln2_bias: bfloat16 [1088], P('wsh'), may hold values from -1.25 to 1.25
- w_up: bfloat16 [1088, 4352], P('wsh'), may hold values from -0.1875 to 0.1875
- b_up: bfloat16 [4352], P('wsh'), may hold values from -1.75 to 1.75
- w_down: bfloat16 [4352, 1088], P('wsh'), may hold values from -0.09375 to 0.09375
- b_down: bfloat16 [1088], P('wsh'), may hold values from -1.25 to 1.25
Outputs:
- output: bfloat16 [4, 2048, 1088], P('wsh', 'ctx')
- grad_tokens: float32 [4, 2048, 1088], P('wsh', 'ctx')
- grad_ln1_gain: float32 [1088], P('wsh')
- grad_ln1_bias: float32 [1088], P('wsh')
- grad_w_qkv: float32 [1088, 3264], P('wsh')
- grad_b_query: float32 [1088], P('wsh')
- grad_b_value: float32 [1088], P('wsh')
- grad_w_out: float32 [1088, 1088], P('wsh')
- grad_b_out: float32 [1088], P('wsh')
- grad_ln2_gain: float32 [1088], P('wsh')
- grad_ln2_bias: float32 [1088], P('wsh')
- grad_w_up: float32 [1088, 4352], P('wsh')
- grad_b_up: float32 [4352], P('wsh')
- grad_w_down: float32 [4352, 1088], P('wsh')
- grad_b_down: float32 [1088], P('wsh')
The draws below stay inside these ranges and needn't reach their ends.
Inputs may be any that keep to these rules, and one draw needn't show every extreme that they name: seq_lengths[g] holds group g's prompt length first, then the lengths of its 4 continuations, all positive; they sum to 2048 and the prompt is the longest.
All inputs are finite; a program needn't handle non-finite values.
Results may differ from the reference program's by a relative error of at most 0.018.
Values may be sent and summed in bfloat16 or wider, within the bound.
A program may use at most 320 MiB of HBM per device.

```python
import math
import jax
import jax.numpy as jnp
from jax import lax

D = 1088
HEADS = 17
HEAD_DIM = 64
FF = 4352
NCONT = 4
GROUP = 2048
GROUPS = 4
N_WSH = 4


def draw_seq_lengths(key, part):
    prompt_key, cut_key = jax.random.split(key)
    prompts = GROUP // 2 + jax.random.randint(prompt_key, (GROUPS, 1), 0, GROUP // 8 + 1, dtype=jnp.int32)
    prompts = prompts.at[0, 0].set(GROUP // 2 + GROUP // 8)
    remains = GROUP - prompts
    base_len = (GROUP // 2 - GROUP // 8) // NCONT
    cuts = jax.random.randint(cut_key, (GROUPS, NCONT - 1), 0, base_len // 2 + 1, dtype=jnp.int32)
    cuts = cuts.at[0, 0].set(base_len // 2)
    leading = remains // NCONT - cuts
    trailing = remains - jnp.sum(leading, axis=1, keepdims=True)
    return jnp.concatenate([prompts, leading, trailing], axis=1).astype(jnp.int32)


def shard_levels(own_key, shape, pieces, smallest, largest):
    loudness = 1.0
    for position, shards_of in pieces:
        draws = jax.random.uniform(jax.random.fold_in(jax.random.fold_in(own_key, 6), position), (shards_of,), jnp.float32, smallest / len(pieces), largest / len(pieces))
        loudness = loudness * jnp.repeat(jnp.exp(draws), shape[position] // shards_of).reshape((-1,) + (1,) * (len(shape) - 1 - position))
    return loudness


def bell_draw(rng, extent, width, bound, cuts=(), held_as=jnp.bfloat16):
    values = jax.random.normal(rng, extent, jnp.float32) * width
    if len(cuts) > 0:
        values = shard_levels(rng, extent, cuts, -0.22, 0.18) * values
    return jnp.clip(values, min=-bound, max=bound).astype(held_as)


def setup_inputs(seed: int = 0) -> dict:
    key_of = jax.random.split(jax.random.key(seed), 17)
    return {
        "tokens": bell_draw(key_of[0], (GROUPS, GROUP, D), 1.0, 6.0, ((0, 4), (1, 8))),
        "seq_lengths": draw_seq_lengths(jax.random.fold_in(key_of[16], 71), 0),
        "cotangent": bell_draw(key_of[2], (GROUPS, GROUP, D), 1.0, 6.0, ((0, 4), (1, 8))),
        "ln1_gain": jnp.clip(1.0 + 0.1 * jax.random.normal(key_of[3], (D,), jnp.float32), 0.5, 1.5).astype(jnp.bfloat16),
        "ln1_bias": bell_draw(key_of[4], (D,), 0.2, 1.25, ((0, 4),)),
        "w_qkv": bell_draw(key_of[5], (D, 3 * D), D ** -0.5, 0.1875, ((0, 4),)),
        "b_query": bell_draw(key_of[6], (D,), 0.3, 1.75, ((0, 4),)),
        "b_value": bell_draw(key_of[7], (D,), 0.1, 0.625, ((0, 4),)),
        "w_out": bell_draw(key_of[8], (D, D), (D // 4) ** -0.5, 0.375, ((0, 4),)),
        "b_out": bell_draw(key_of[9], (D,), 0.2, 1.25, ((0, 4),)),
        "ln2_gain": jnp.clip(1.0 + 0.1 * jax.random.normal(key_of[10], (D,), jnp.float32), 0.5, 1.5).astype(jnp.bfloat16),
        "ln2_bias": bell_draw(key_of[11], (D,), 0.2, 1.25, ((0, 4),)),
        "w_up": bell_draw(key_of[12], (D, FF), D ** -0.5, 0.1875, ((0, 4),)),
        "b_up": bell_draw(key_of[13], (FF,), 0.3, 1.75, ((0, 4),)),
        "w_down": bell_draw(key_of[14], (FF, D), FF ** -0.5, 0.09375, ((0, 4),)),
        "b_down": bell_draw(key_of[15], (D,), 0.2, 1.25, ((0, 4),)),
    }


@jax.custom_vjp
def low(v):
    return lax.optimization_barrier(v.astype(jnp.bfloat16)).astype(jnp.float32)

@jax.custom_vjp
def low_back(v):
    return v

def low_keep(v):
    return (low(v), None)

def low_pass(kept, grad):
    return (grad,)

def back_keep(v):
    return (v, None)

def back_low(kept, grad):
    return (low(grad),)
low.defvjp(low_keep, low_pass)
low_back.defvjp(back_keep, back_low)
exact_mode = lax.Precision.HIGHEST

def matmul(left, right):
    return jnp.dot(left, right, precision=exact_mode)

def layer_norm(inputs, gain, shift):
    center = inputs - lax.optimization_barrier(jnp.mean(inputs, -1, keepdims=True))
    spread = lax.optimization_barrier(jnp.mean(center * center, -1, keepdims=True))
    return center * lax.rsqrt(spread + 1e-05) * gain + shift

def sequence_ids(lengths, positions):
    bounds = jnp.cumsum(lengths).astype(jnp.int32)
    return lax.optimization_barrier(jnp.sum((positions[:, None] >= bounds[None, :]).astype(jnp.int32), axis=1))

def attend(queries, key_rows, value_rows, lengths):
    positions = jnp.arange(GROUP, dtype=jnp.int32)
    owners = sequence_ids(lengths, positions)
    key_heads = key_rows.reshape(GROUP, HEADS, HEAD_DIM)
    value_heads = value_rows.reshape(GROUP, HEADS, HEAD_DIM)
    block_rows = math.gcd(GROUP, 512)

    def one_block(block_index):
        first_row = block_index * block_rows
        query_heads = lax.dynamic_slice_in_dim(queries, first_row, block_rows, 0).reshape(block_rows, HEADS, HEAD_DIM)
        query_pos = first_row + jnp.arange(block_rows, dtype=jnp.int32)
        query_owner = lax.dynamic_slice_in_dim(owners, first_row, block_rows, 0)
        scores = low_back(jnp.einsum('qhd,khd->hqk', query_heads, key_heads, precision=exact_mode) * HEAD_DIM ** (-0.5))
        allowed = (positions[None, :] <= query_pos[:, None]) & ((owners[None, :] == 0) | (owners[None, :] == query_owner[:, None]))
        scores = jnp.where(allowed[None], scores, -1e+30)
        peak = lax.optimization_barrier(jnp.max(scores, -1, keepdims=True))
        expos = jnp.exp(scores - peak)
        totals = lax.optimization_barrier(jnp.sum(expos, -1))
        mixed = jnp.einsum('hqk,khd->qhd', low(expos), value_heads, precision=exact_mode) / totals.T[:, :, None]
        return mixed.reshape(block_rows, HEADS * HEAD_DIM)
    blocks = lax.map(jax.checkpoint(one_block), jnp.arange(GROUP // block_rows, dtype=jnp.int32))
    return blocks.reshape(GROUP, HEADS * HEAD_DIM)

def forward(tokens_f, seq_lengths, params):
    ln1_gain, ln1_bias, w_qkv, b_query, b_value, w_out, b_out, ln2_gain, ln2_bias, w_up, b_up, w_down, b_down = params
    results = []
    for group_index in range(N_WSH):
        inputs = tokens_f[group_index]
        normed = low(layer_norm(inputs, ln1_gain, ln1_bias))
        joint_proj = matmul(normed, w_qkv)
        queries = low(low_back(joint_proj[:, :D] + b_query))
        key_rows = low(low_back(joint_proj[:, D:2 * D]))
        value_rows = low(low_back(joint_proj[:, 2 * D:] + b_value))
        mixed = low(low_back(attend(queries, key_rows, value_rows, seq_lengths[group_index])))
        middle = inputs + low_back(matmul(mixed, w_out) + b_out)
        normed_two = low(layer_norm(middle, ln2_gain, ln2_bias))
        hidden = low(jax.nn.gelu(low_back(matmul(normed_two, w_up) + b_up), approximate=False))
        results.append(middle + low_back(matmul(hidden, w_down) + b_down))
    return jnp.stack(results)

def reference(tokens, seq_lengths, cotangent, ln1_gain, ln1_bias, w_qkv, b_query, b_value, w_out, b_out, ln2_gain, ln2_bias, w_up, b_up, w_down, b_down):
    params = tuple((weight.astype(jnp.float32) for weight in (ln1_gain, ln1_bias, w_qkv, b_query, b_value, w_out, b_out, ln2_gain, ln2_bias, w_up, b_up, w_down, b_down)))
    tokens_f = tokens.astype(jnp.float32)

    def whole(tokens_in, *weights):
        return forward(tokens_in, seq_lengths, weights)
    result, pullback = jax.vjp(whole, tokens_f, *params)
    grads = pullback(cotangent.astype(jnp.float32))
    return (result.astype(jnp.bfloat16), grads[0], grads[1], grads[2], grads[3], grads[4], grads[5], grads[6], grads[7], grads[8], grads[9], grads[10], grads[11], grads[12], grads[13])
```

```python
import functools
import math

import jax
import jax.numpy as jnp
from jax import lax
from jax.experimental import pallas as pl
from jax.experimental.pallas import tpu as pltpu
from jax.sharding import PartitionSpec as P

D = 1088
HEADS = 17
HEAD_DIM = 64


def normalize(inputs):
    center = inputs - jnp.mean(inputs, -1, keepdims=True)
    inverse = lax.rsqrt(jnp.mean(center * center, -1, keepdims=True) + 1e-05)
    return (center * inverse, inverse)


def norm_back(grad_in, normed, inverse, gain):
    scaled = grad_in * gain
    return inverse * (
        scaled
        - jnp.mean(scaled, -1, keepdims=True)
        - normed * jnp.mean(scaled * normed, -1, keepdims=True)
    )


def rows_product(left, right):
    return lax.dot_general(
        left, right, (((0,), (0,)), ((), ())), preferred_element_type=jnp.float32
    )


def cols_product(left, right):
    return lax.dot_general(
        left, right, (((1,), (1,)), ((), ())), preferred_element_type=jnp.float32
    )


def sequence_ids(lengths, positions):
    bounds = jnp.cumsum(lengths)
    return jnp.sum((positions[:, None] >= bounds[None, :]).astype(jnp.int32), axis=1)


def allowed_pairs(lengths, query_pos, key_pos):
    query_owner = sequence_ids(lengths, query_pos)
    key_owner = sequence_ids(lengths, key_pos)
    return (key_pos[None, :] <= query_pos[:, None]) & (
        (key_owner[None, :] == 0) | (key_owner[None, :] == query_owner[:, None])
    )


def over_blocks(state_in, arrays, step_fn):
    total_rows = arrays[0].shape[0]
    block_rows = math.gcd(total_rows, 512)

    def advance(block_index, state_now):
        offset = block_index * block_rows
        pieces = tuple((lax.dynamic_slice_in_dim(array, offset, block_rows, 0) for array in arrays))
        return step_fn(state_now, pieces, offset)

    return lax.fori_loop(0, total_rows // block_rows, advance, state_in)


def sectioned_sum(partials):
    shares = lax.psum_scatter(partials, "wsh", scatter_dimension=0, tiled=True)
    return lax.psum(shares, "ctx")


def on_device(
    tokens,
    seq_lengths,
    cotangent,
    ln1_gain,
    ln1_bias,
    w_qkv,
    b_query,
    b_value,
    w_out,
    b_out,
    ln2_gain,
    ln2_bias,
    w_up,
    b_up,
    w_down,
    b_down,
):
    token_rows, grad_rows = (tokens[0], cotangent[0])
    shards = (
        w_qkv,
        w_out,
        w_up,
        w_down,
        b_query,
        b_value,
        b_out,
        b_up,
        b_down,
        ln1_gain,
        ln1_bias,
        ln2_gain,
        ln2_bias,
    )
    gathered = (
        lax.all_gather(shards[0], "wsh", axis=0, tiled=True),
        lax.all_gather(shards[1], "wsh", axis=0, tiled=True),
        lax.all_gather(shards[2], "wsh", axis=0, tiled=True),
        lax.all_gather(shards[3], "wsh", axis=0, tiled=True),
        lax.all_gather(shards[4], "wsh", axis=0, tiled=True),
        lax.all_gather(shards[5], "wsh", axis=0, tiled=True),
        lax.all_gather(shards[6], "wsh", axis=0, tiled=True),
        lax.all_gather(shards[7], "wsh", axis=0, tiled=True),
        lax.all_gather(shards[8], "wsh", axis=0, tiled=True),
        lax.all_gather(shards[9], "wsh", axis=0, tiled=True),
        lax.all_gather(shards[10], "wsh", axis=0, tiled=True),
        lax.all_gather(shards[11], "wsh", axis=0, tiled=True),
        lax.all_gather(shards[12], "wsh", axis=0, tiled=True),
    )
    qkv_full, out_full, up_full, down_full = (gathered[0], gathered[1], gathered[2], gathered[3])
    query_bias, value_bias, out_bias, up_bias, down_bias = [
        piece.astype(jnp.float32) for piece in gathered[4:9]
    ]
    gain_one, shift_one, gain_two, shift_two = [
        piece.astype(jnp.float32) for piece in gathered[9:13]
    ]
    lengths = seq_lengths[0]
    tok_rows = token_rows.shape[0]
    my_pos = lax.axis_index("ctx") * tok_rows + jnp.arange(tok_rows, dtype=jnp.int32)
    scale_qk = HEAD_DIM ** (-0.5)
    inputs = token_rows.astype(jnp.float32)
    normed_one, inverse_one = normalize(inputs)
    hidden_one = (normed_one * gain_one + shift_one).astype(jnp.bfloat16)
    joint_proj = jnp.dot(hidden_one, qkv_full, preferred_element_type=jnp.float32)
    queries = (joint_proj[:, :D] + query_bias).astype(jnp.bfloat16)
    key_rows = joint_proj[:, D : 2 * D].astype(jnp.bfloat16)
    value_rows = (joint_proj[:, 2 * D :] + value_bias).astype(jnp.bfloat16)
    query_heads = queries.reshape(tok_rows, HEADS, HEAD_DIM)
    my_key_heads = key_rows.reshape(tok_rows, HEADS, HEAD_DIM)
    my_value_heads = value_rows.reshape(tok_rows, HEADS, HEAD_DIM)

    def forward_step(state_now, pieces, first_row):
        key_heads = pieces[0].reshape(-1, HEADS, HEAD_DIM)
        value_heads = pieces[1].reshape(-1, HEADS, HEAD_DIM)
        key_pos = first_row + jnp.arange(key_heads.shape[0], dtype=jnp.int32)
        allowed = allowed_pairs(lengths, my_pos, key_pos)

        def forward_compute(inner):
            peak_old, total_old, accum_old = inner
            scores = (
                jnp.einsum(
                    "qhd,khd->hqk", query_heads, key_heads, preferred_element_type=jnp.float32
                )
                * scale_qk
            )
            scores = jnp.where(allowed[None], scores, -1e30)
            peak_new = jnp.maximum(peak_old, jnp.max(scores, -1))
            factor = jnp.exp(peak_old - peak_new)
            expos = jnp.where(allowed[None], jnp.exp(scores - peak_new[:, :, None]), 0.0)
            total_new = total_old * factor + jnp.sum(expos, -1)
            accum_new = accum_old * factor.T[:, :, None] + jnp.einsum(
                "hqk,khd->qhd",
                expos.astype(jnp.bfloat16),
                value_heads,
                preferred_element_type=jnp.float32,
            )
            return (peak_new, total_new, accum_new)

        return lax.cond(jnp.any(allowed), forward_compute, lambda inner: inner, state_now)

    start_state = (
        jnp.full((HEADS, tok_rows), -1e30, jnp.float32),
        jnp.zeros((HEADS, tok_rows), jnp.float32),
        jnp.zeros((tok_rows, HEADS, HEAD_DIM), jnp.float32),
    )
    peak, total, accum = over_blocks(
        start_state,
        (
            lax.all_gather(key_rows, "ctx", axis=0, tiled=True),
            lax.all_gather(value_rows, "ctx", axis=0, tiled=True),
        ),
        forward_step,
    )
    mixed = accum / total.T[:, :, None]
    log_sum = (peak + jnp.log(total)).T
    mixed_low = mixed.reshape(tok_rows, D).astype(jnp.bfloat16)
    middle = inputs + jnp.dot(mixed_low, out_full, preferred_element_type=jnp.float32) + out_bias
    normed_two, inverse_two = normalize(middle)
    hidden_two = (normed_two * gain_two + shift_two).astype(jnp.bfloat16)
    pre_act = jnp.dot(hidden_two, up_full, preferred_element_type=jnp.float32) + up_bias
    activ_low = jax.nn.gelu(pre_act, approximate=False).astype(jnp.bfloat16)
    result = middle + jnp.dot(activ_low, down_full, preferred_element_type=jnp.float32) + down_bias
    output_rows = result.astype(jnp.bfloat16)
    grad_top_f = grad_rows.astype(jnp.float32)
    grad_down = rows_product(activ_low, grad_rows)
    grad_down_bias = jnp.sum(grad_top_f, 0)
    grad_act = cols_product(grad_rows, down_full)
    cdf_part = 0.5 * (1.0 + lax.erf(pre_act * math.sqrt(0.5)))
    pdf_part = jnp.exp(-0.5 * pre_act * pre_act) / math.sqrt(2.0 * math.pi)
    grad_pre = (grad_act * (cdf_part + pre_act * pdf_part)).astype(jnp.bfloat16)
    grad_up = rows_product(hidden_two, grad_pre)
    grad_up_bias = jnp.sum(grad_pre.astype(jnp.float32), 0)
    grad_h2 = cols_product(grad_pre, up_full)
    grad_gain_two = jnp.sum(grad_h2 * normed_two, 0)
    grad_shift_two = jnp.sum(grad_h2, 0)
    grad_mid = grad_top_f + norm_back(grad_h2, normed_two, inverse_two, gain_two)
    grad_mid_low = grad_mid.astype(jnp.bfloat16)
    grad_out_w = rows_product(mixed_low, grad_mid_low)
    grad_out_bias = jnp.sum(grad_mid_low.astype(jnp.float32), 0)
    grad_mixed = cols_product(grad_mid_low, out_full).astype(jnp.bfloat16)
    grad_heads = grad_mixed.reshape(tok_rows, HEADS, HEAD_DIM)
    delta = jnp.sum(grad_heads.astype(jnp.float32) * mixed, -1)
    lse_all, delta_all = (
        lax.all_gather(log_sum, "ctx", axis=0, tiled=True),
        lax.all_gather(delta, "ctx", axis=0, tiled=True),
    )

    def query_step(state_now, pieces, first_row):
        key_heads = pieces[0].reshape(-1, HEADS, HEAD_DIM)
        value_heads = pieces[1].reshape(-1, HEADS, HEAD_DIM)
        key_pos = first_row + jnp.arange(key_heads.shape[0], dtype=jnp.int32)
        allowed = allowed_pairs(lengths, my_pos, key_pos)

        def query_compute(accum_old):
            scores = (
                jnp.einsum(
                    "qhd,khd->hqk", query_heads, key_heads, preferred_element_type=jnp.float32
                )
                * scale_qk
            )
            probs = jnp.where(allowed[None], jnp.exp(scores - log_sum.T[:, :, None]), 0.0)
            grad_probs = jnp.einsum(
                "qhd,khd->hqk", grad_heads, value_heads, preferred_element_type=jnp.float32
            )
            grad_scores = (probs * (grad_probs - delta.T[:, :, None])).astype(jnp.bfloat16)
            return accum_old + jnp.einsum(
                "hqk,khd->qhd", grad_scores, key_heads, preferred_element_type=jnp.float32
            )

        return lax.cond(jnp.any(allowed), query_compute, lambda inner: inner, state_now)

    zero_heads = jnp.zeros((tok_rows, HEADS, HEAD_DIM), jnp.float32)
    grad_query = over_blocks(
        zero_heads,
        (
            lax.all_gather(key_rows, "ctx", axis=0, tiled=True),
            lax.all_gather(value_rows, "ctx", axis=0, tiled=True),
        ),
        query_step,
    )

    def key_step(state_now, pieces, first_row):
        other_queries = pieces[0].reshape(-1, HEADS, HEAD_DIM)
        other_grads = pieces[1].reshape(-1, HEADS, HEAD_DIM)
        other_count = other_queries.shape[0]
        other_pos = first_row + jnp.arange(other_count, dtype=jnp.int32)
        other_lse = lax.dynamic_slice_in_dim(lse_all, first_row, other_count, 0)
        other_delta = lax.dynamic_slice_in_dim(delta_all, first_row, other_count, 0)
        allowed = allowed_pairs(lengths, other_pos, my_pos)

        def key_compute(inner):
            grad_key_old, grad_value_old = inner
            scores = (
                jnp.einsum(
                    "qhd,khd->hqk", other_queries, my_key_heads, preferred_element_type=jnp.float32
                )
                * scale_qk
            )
            probs = jnp.where(allowed[None], jnp.exp(scores - other_lse.T[:, :, None]), 0.0)
            grad_value_new = grad_value_old + jnp.einsum(
                "hqk,qhd->khd",
                probs.astype(jnp.bfloat16),
                other_grads,
                preferred_element_type=jnp.float32,
            )
            grad_probs = jnp.einsum(
                "qhd,khd->hqk", other_grads, my_value_heads, preferred_element_type=jnp.float32
            )
            grad_scores = (probs * (grad_probs - other_delta.T[:, :, None])).astype(jnp.bfloat16)
            grad_key_new = grad_key_old + jnp.einsum(
                "hqk,qhd->khd", grad_scores, other_queries, preferred_element_type=jnp.float32
            )
            return (grad_key_new, grad_value_new)

        return lax.cond(jnp.any(allowed), key_compute, lambda inner: inner, state_now)

    grad_key, grad_value = over_blocks(
        (zero_heads, zero_heads),
        (
            lax.all_gather(queries, "ctx", axis=0, tiled=True),
            lax.all_gather(grad_mixed, "ctx", axis=0, tiled=True),
        ),
        key_step,
    )
    grad_joint = jnp.concatenate(
        [
            (grad_query * scale_qk).reshape(tok_rows, D),
            (grad_key * scale_qk).reshape(tok_rows, D),
            grad_value.reshape(tok_rows, D),
        ],
        axis=1,
    ).astype(jnp.bfloat16)
    grad_qkv_w = rows_product(hidden_one, grad_joint)
    grad_joint_f = grad_joint.astype(jnp.float32)
    grad_query_bias = jnp.sum(grad_joint_f[:, :D], 0)
    grad_value_bias = jnp.sum(grad_joint_f[:, 2 * D :], 0)
    grad_h1 = cols_product(grad_joint, qkv_full)
    grad_gain_one = jnp.sum(grad_h1 * normed_one, 0)
    grad_shift_one = jnp.sum(grad_h1, 0)
    grad_input = grad_mid + norm_back(grad_h1, normed_one, inverse_one, gain_one)
    matrices = (grad_qkv_w, grad_out_w, grad_up, grad_down)
    vectors = (
        grad_query_bias,
        grad_value_bias,
        grad_out_bias,
        grad_up_bias,
        grad_down_bias,
        grad_gain_one,
        grad_shift_one,
        grad_gain_two,
        grad_shift_two,
    )
    totals = sectioned_sum(matrices + vectors)
    return (
        output_rows[None],
        grad_input[None],
        totals[9],
        totals[10],
        totals[0],
        totals[4],
        totals[5],
        totals[1],
        totals[6],
        totals[11],
        totals[12],
        totals[2],
        totals[7],
        totals[3],
        totals[8],
    )


SLOTS = 5
WIDE = 384
ROWS = 256
CHIPS = 4
MESH_ID = pl.DeviceIdType.MESH
F32, BF16 = (jnp.float32, jnp.bfloat16)
NEG = -1e30
HEAD_TABLE = ((0, 5, 9, 13, -40), (1, 6, 10, 14, -40), (2, 7, 11, 15, -40), (3, 4, 8, 12, 16))


def nn(left, right):
    return jnp.dot(left, right, preferred_element_type=F32)


def position():
    c, z = (lax.axis_index("ctx"), lax.axis_index("wsh"))
    return c // 2, c % 2, z


def greet(t, p, z):
    barrier = pltpu.get_barrier_semaphore()
    for k in range(1, CHIPS):
        pl.semaphore_signal(
            barrier, inc=1, device_id=((t + k) % CHIPS * 2 + p, z), device_id_type=MESH_ID
        )
    pl.semaphore_signal(barrier, inc=1, device_id=(t * 2 + 1 - p, z), device_id_type=MESH_ID)
    pl.semaphore_wait(barrier, CHIPS)


def to_chip(src, dst, send, recv, t, p, z, k):
    return pltpu.make_async_remote_copy(
        src_ref=src,
        dst_ref=dst,
        send_sem=send,
        recv_sem=recv,
        device_id=((t + k) % CHIPS * 2 + p, z),
        device_id_type=MESH_ID,
    )


def to_twin(src, dst, send, recv, t, p, z):
    return pltpu.make_async_remote_copy(
        src_ref=src,
        dst_ref=dst,
        send_sem=send,
        recv_sem=recv,
        device_id=(t * 2 + 1 - p, z),
        device_id_type=MESH_ID,
    )


def rows16(start, size):
    return pl.ds(pl.multiple_of(start, 16), size)


def weight_copies(half, whole, block, keep, step, local, send, recv, t, p, z, base=0):
    copies = []
    for i in range(4):
        copies.append(
            pltpu.make_async_copy(
                half.at[i, rows16(base, keep)],
                whole.at[rows16(i * block + p * step, keep)],
                local.at[i],
            )
        )
        copies.append(
            to_twin(
                half.at[i, rows16(base + p * (keep - step), step)],
                whole.at[rows16(i * block + p * keep, step)],
                send.at[i],
                recv.at[i],
                t,
                p,
                z,
            )
        )
    return copies


def params(number, mib=56):
    return pltpu.CompilerParams(
        collective_id=number, has_side_effects=True, vmem_limit_bytes=mib * 2**20
    )


def vmem(count):
    return [pl.BlockSpec(memory_space=pltpu.VMEM)] * count


def project_kernel(
    x, half, gain, shift, bias_q, bias_v,
    q_out, k_out, v_out, h_out, whole,
    send, recv, w_local, w_send, w_recv, kv_send, kv_recv,
):
    t, p, z = position()
    greet(t, p, z)
    weights = weight_copies(half, whole, 272, 144, 128, w_local, w_send, w_recv, t, p, z)
    for copy in weights:
        copy.start()
    normed, _ = normalize(x[...].astype(F32))
    h_out[t] = (normed * gain[...] + shift[...]).astype(BF16)
    sends = [
        to_chip(h_out.at[t], h_out.at[t], send.at[k], recv.at[k], t, p, z, k)
        for k in range(1, CHIPS)
    ]
    for copy in sends:
        copy.start()
    for copy in weights:
        copy.wait()

    def block(k, carry):
        src = (t + CHIPS - k) % CHIPS

        @pl.when(k > 0)
        def _():
            to_chip(h_out.at[src], h_out.at[src], send.at[k], recv.at[k], t, p, z, 0 * k + 1).wait_recv()

        h = h_out[src]
        q_out[src] = ((nn(h, whole[:, :WIDE]) + bias_q[...]).astype(BF16) * 0.125).astype(BF16)
        mine = src * 2 + p
        k_out[mine] = nn(h, whole[:, WIDE : 2 * WIDE]).astype(BF16)
        to_twin(k_out.at[mine], k_out.at[mine], kv_send.at[k], kv_recv.at[k], t, p, z).start()
        v_out[mine] = (nn(h, whole[:, 2 * WIDE :]) + bias_v[...]).astype(BF16)
        to_twin(
            v_out.at[mine], v_out.at[mine], kv_send.at[k + CHIPS], kv_recv.at[k + CHIPS], t, p, z
        ).start()
        return carry

    lax.fori_loop(0, CHIPS, block, 0)
    for copy in sends:
        copy.wait_send()
    for k in range(CHIPS):
        other = (t + CHIPS - k) % CHIPS * 2 + 1 - p
        mine = (t + CHIPS - k) % CHIPS * 2 + p
        for ref, j in ((k_out, k), (v_out, k + CHIPS)):
            to_twin(ref.at[mine], ref.at[mine], kv_send.at[j], kv_recv.at[j], t, p, z).wait_send()
            to_twin(ref.at[other], ref.at[other], kv_send.at[j], kv_recv.at[j], t, p, z).wait_recv()


def project(x, half, gain, shift, bias_q, bias_v):
    blocks = jax.ShapeDtypeStruct((CHIPS, ROWS, WIDE), BF16)
    keys = jax.ShapeDtypeStruct((2 * CHIPS, ROWS, WIDE), BF16)
    dma = pltpu.SemaphoreType.DMA
    return pl.pallas_call(
        project_kernel,
        out_shape=(
            blocks, keys, keys,
            jax.ShapeDtypeStruct((CHIPS, ROWS, D), BF16),
            jax.ShapeDtypeStruct((D, 3 * WIDE), BF16),
        ),
        in_specs=vmem(6),
        out_specs=tuple(vmem(5)),
        scratch_shapes=[
            dma((CHIPS,)), dma((CHIPS,)), dma((4,)), dma((4,)), dma((4,)),
            dma((2 * CHIPS,)), dma((2 * CHIPS,)),
        ],
        compiler_params=params(1),
        name="project",
    )(x, half, gain, shift, bias_q, bias_v)


def tile_bounds(lengths, block):
    ends = [lengths[0]]
    for i in range(1, 4):
        ends.append(ends[-1] + lengths[i])
    first = block * ROWS
    start_first = 0 * first
    for end in ends:
        start_first = jnp.where(first >= end, end, start_first)
    free = jnp.minimum(block, ends[0] // ROWS)
    resume = jnp.maximum(free + 1, start_first // ROWS)
    masked = jnp.where(free < block, 1 + jnp.maximum(block - resume, 0), 0)
    query_pos = first + lax.broadcasted_iota(jnp.int32, (1, ROWS), 1)
    start = jnp.zeros((1, ROWS), jnp.int32)
    for end in ends:
        start = jnp.where(query_pos >= end, end, start)
    return ends[0], query_pos, start, free, resume, masked


def visible(key_block, prompt, query_pos, start):
    key_pos = key_block * ROWS + lax.broadcasted_iota(jnp.int32, (ROWS, ROWS), 0)
    return (key_pos <= query_pos) & ((key_pos < prompt) | (key_pos >= start))


def half_of(rows, h):
    lane = lax.broadcasted_iota(jnp.int32, rows.shape, 1)
    return jnp.where((lane >= h * HEAD_DIM) & (lane < (h + 1) * HEAD_DIM), rows, jnp.zeros_like(rows))


def attend_kernel(lengths, parity, q, k, v, mixed, lse, turned):
    slab = pl.program_id(0)
    for j in range(2 * CHIPS):
        turned[j] = v[j].astype(F32).T.astype(BF16)

    def run(heads):
        def one(i, carry):
            block = 2 * i + parity[0]
            prompt, query_pos, start, free, resume, masked = tile_bounds(lengths, block)
            queries = [half_of(q[i], h) for h in heads]

            def tile(j, state, mask):
                keys = k[j]
                values = turned[j]
                new = []
                for h, (peak, total, accum) in zip(heads, state):
                    scores = cols_product(keys, queries[h])
                    if mask is not None:
                        scores = jnp.where(mask, scores, NEG)
                    peak_new = jnp.maximum(peak, jnp.max(scores, 0, keepdims=True))
                    factor = jnp.exp(peak - peak_new)
                    expos = jnp.exp(scores - peak_new)
                    total_new = total * factor + jnp.sum(expos, 0, keepdims=True)
                    part = values[h * HEAD_DIM : (h + 1) * HEAD_DIM]
                    accum_new = accum * factor + nn(part, expos.astype(BF16))
                    new.append((peak_new, total_new, accum_new))
                return tuple(new)

            state = tuple(
                (
                    jnp.full((1, ROWS), NEG, F32),
                    jnp.zeros((1, ROWS), F32),
                    jnp.zeros((HEAD_DIM, ROWS), F32),
                )
                for _ in heads
            )
            state = tile(block, state, visible(block, prompt, query_pos, start))
            state = lax.fori_loop(0, free, lambda j, s: tile(j, s, None), state)

            def other(m, s):
                j = jnp.where(m == 0, free, resume + m - 1)
                return tile(j, s, visible(j, prompt, query_pos, start))

            state = lax.fori_loop(0, masked, other, state)
            outs = []
            for h, (peak, total, accum) in zip(heads, state):
                outs.append(accum / total)
                lse[0, pl.ds(h * CHIPS + i, 1), :] = peak + jnp.log(total)
            if len(heads) == 1:
                outs.append(jnp.zeros((HEAD_DIM, ROWS), F32))
            mixed[i] = jnp.concatenate(outs, 0).T.astype(BF16)
            return carry

        lax.fori_loop(0, CHIPS, one, 0)

    @pl.when(slab < SLOTS // 2)
    def _():
        run((0, 1))

    @pl.when(slab >= SLOTS // 2)
    def _():
        lse[...] = jnp.zeros_like(lse)
        run((0,))


def slab_spec(count):
    return pl.BlockSpec((count, ROWS, 128), lambda s, *_: (0, 0, s))


def attend(lengths, parity, q, k, v):
    return pl.pallas_call(
        attend_kernel,
        out_shape=(
            jax.ShapeDtypeStruct((CHIPS, ROWS, WIDE), BF16),
            jax.ShapeDtypeStruct((3, 2 * CHIPS, ROWS), F32),
        ),
        grid_spec=pltpu.PrefetchScalarGridSpec(
            num_scalar_prefetch=2,
            grid=(3,),
            in_specs=[slab_spec(CHIPS), slab_spec(2 * CHIPS), slab_spec(2 * CHIPS)],
            out_specs=(
                slab_spec(CHIPS),
                pl.BlockSpec((1, 2 * CHIPS, ROWS), lambda s, *_: (s, 0, 0)),
            ),
            scratch_shapes=[pltpu.VMEM((2 * CHIPS, 128, ROWS), BF16)],
        ),
        compiler_params=pltpu.CompilerParams(vmem_limit_bytes=48 * 2**20),
        cost_estimate=pl.CostEstimate(flops=4 * 10**9, bytes_accessed=5 * 10**6, transcendentals=6 * 10**6),
        name="attend",
    )(lengths, parity, q, k, v)


def attend_back_kernel(
    lengths, parity, q, k, v, mixed, grad, lse, dq, dk, dv, turned, acc_k, acc_v
):
    slab = pl.program_id(0)
    for j in range(2 * CHIPS):
        turned[j] = k[j].astype(F32).T.astype(BF16)
    acc_k[...] = jnp.zeros_like(acc_k)
    acc_v[...] = jnp.zeros_like(acc_v)

    def run(heads):
        def one(i, carry):
            block = 2 * i + parity[0]
            prompt, query_pos, start, free, resume, masked = tile_bounds(lengths, block)
            queries = [half_of(q[i], h) for h in heads]
            grads = [half_of(grad[i], h) for h in heads]
            product = (grad[i].astype(F32) * mixed[i].astype(F32)).T
            deltas = [
                jnp.sum(product[h * HEAD_DIM : (h + 1) * HEAD_DIM], 0, keepdims=True) for h in heads
            ]
            sums = [lse[0, pl.ds(h * CHIPS + i, 1), :] for h in heads]

            def tile(j, state, mask):
                keys, values, keys_t = (k[j], v[j], turned[j])
                new = []
                add_k, add_v = (None, None)
                for h, accum in zip(heads, state):
                    scores = cols_product(keys, queries[h]) - sums[h]
                    if mask is not None:
                        scores = jnp.where(mask, scores, NEG)
                    probs = jnp.exp(scores)
                    grad_probs = cols_product(values, grads[h])
                    ds = (probs * (grad_probs - deltas[h])).astype(BF16)
                    part_v = nn(probs.astype(BF16), grads[h])
                    part_k = nn(ds, queries[h])
                    add_v = part_v if add_v is None else add_v + part_v
                    add_k = part_k if add_k is None else add_k + part_k
                    new.append(accum + nn(keys_t[h * HEAD_DIM : (h + 1) * HEAD_DIM], ds))
                acc_v[j] += add_v
                acc_k[j] += add_k
                return tuple(new)

            state = tuple(jnp.zeros((HEAD_DIM, ROWS), F32) for _ in heads)
            state = tile(block, state, visible(block, prompt, query_pos, start))
            state = lax.fori_loop(0, free, lambda j, s: tile(j, s, None), state)

            def other(m, s):
                j = jnp.where(m == 0, free, resume + m - 1)
                return tile(j, s, visible(j, prompt, query_pos, start))

            state = list(lax.fori_loop(0, masked, other, state))
            if len(heads) == 1:
                state.append(jnp.zeros((HEAD_DIM, ROWS), F32))
            dq[i] = (jnp.concatenate(state, 0) * 0.125).T.astype(BF16)
            return carry

        lax.fori_loop(0, CHIPS, one, 0)

    @pl.when(slab < SLOTS // 2)
    def _():
        run((0, 1))

    @pl.when(slab >= SLOTS // 2)
    def _():
        run((0,))

    dk[...] = acc_k[...].astype(BF16)
    dv[...] = acc_v[...].astype(BF16)


def attend_back(lengths, parity, q, k, v, mixed, grad, lse):
    few, many = (slab_spec(CHIPS), slab_spec(2 * CHIPS))
    return pl.pallas_call(
        attend_back_kernel,
        out_shape=(
            jax.ShapeDtypeStruct((CHIPS, ROWS, WIDE), BF16),
            jax.ShapeDtypeStruct((2 * CHIPS, ROWS, WIDE), BF16),
            jax.ShapeDtypeStruct((2 * CHIPS, ROWS, WIDE), BF16),
        ),
        grid_spec=pltpu.PrefetchScalarGridSpec(
            num_scalar_prefetch=2,
            grid=(3,),
            in_specs=[
                few, many, many, few, few,
                pl.BlockSpec((1, 2 * CHIPS, ROWS), lambda s, *_: (s, 0, 0)),
            ],
            out_specs=(few, many, many),
            scratch_shapes=[
                pltpu.VMEM((2 * CHIPS, 128, ROWS), BF16),
                pltpu.VMEM((2 * CHIPS, ROWS, 128), F32),
                pltpu.VMEM((2 * CHIPS, ROWS, 128), F32),
            ],
        ),
        compiler_params=pltpu.CompilerParams(vmem_limit_bytes=48 * 2**20),
        cost_estimate=pl.CostEstimate(flops=10 * 10**9, bytes_accessed=9 * 10**6, transcendentals=6 * 10**6),
        name="attend_back",
    )(lengths, parity, q, k, v, mixed, grad, lse)


def out_kernel(
    x, mixed, half, bias, middle, whole, raw, parts, landed, send, recv, w_local, w_send, w_recv
):
    t, p, z = position()
    greet(t, p, z)
    weights = weight_copies(half, raw, 80, 48, 32, w_local, w_send, w_recv, t, p, z)
    for copy in weights:
        copy.start()
    for copy in weights:
        copy.wait()

    @pl.when(t == CHIPS - 1)
    def _():
        whole[: SLOTS * HEAD_DIM] = raw[...]

    @pl.when(t < CHIPS - 1)
    def _():
        for i in range(4):
            whole[i * HEAD_DIM : (i + 1) * HEAD_DIM] = raw[i * 80 : i * 80 + HEAD_DIM]
        whole[4 * HEAD_DIM : 5 * HEAD_DIM] = jnp.zeros((HEAD_DIM, D), BF16)

    whole[SLOTS * HEAD_DIM :] = jnp.zeros((WIDE - SLOTS * HEAD_DIM, D), BF16)

    def part(k, carry):
        parts[k] = nn(mixed[(t + k) % CHIPS], whole[...]).astype(BF16)
        to_chip(parts.at[k], landed.at[k], send.at[k], recv.at[k], t, p, z, k).start()
        return carry

    lax.fori_loop(1, CHIPS, part, 0)
    total = x[...].astype(F32) + bias[...] + nn(mixed[t], whole[...])
    for k in range(1, CHIPS):
        to_chip(parts.at[k], landed.at[k], send.at[k], recv.at[k], t, p, z, k).wait()
        total = total + landed[k].astype(F32)
    middle[...] = total


def out_project(x, mixed, half, bias):
    dma = pltpu.SemaphoreType.DMA
    return pl.pallas_call(
        out_kernel,
        out_shape=(
            jax.ShapeDtypeStruct((ROWS, D), F32),
            jax.ShapeDtypeStruct((WIDE, D), BF16),
        ),
        in_specs=vmem(4),
        out_specs=tuple(vmem(2)),
        scratch_shapes=[
            pltpu.VMEM((SLOTS * HEAD_DIM, D), BF16),
            pltpu.VMEM((CHIPS, ROWS, D), BF16),
            pltpu.VMEM((CHIPS, ROWS, D), BF16),
            dma((CHIPS,)), dma((CHIPS,)), dma((4,)), dma((4,)), dma((4,)),
        ],
        compiler_params=params(2),
        name="out_project",
    )(x, mixed, half, bias)


def feed_kernel(
    middle, cot, halves, up_bias, gain, shift, down_bias, out_w, mixed,
    output, grad_mid, gh_heads, g_out, g_feed, sums, up_sum,
    up, down, hid, cots, act, gpre, part_o, part_h, land_o, land_h, gmid, full_up, full_down, land_up, land_down, raw, land_out,
    send, recv, w_local, w_send, w_recv, g_send, g_recv,
):
    t, p, z = position()
    greet(t, p, z)
    weights = weight_copies(
        halves, up, 272, 144, 128, w_local.at[0], w_send.at[0], w_recv.at[0], t, p, z
    ) + weight_copies(
        halves, down, 272, 144, 128, w_local.at[1], w_send.at[1], w_recv.at[1], t, p, z, 144
    )
    normed, inverse = normalize(middle[...])
    hid[t] = (normed * gain[...] + shift[...]).astype(BF16)
    cots[t] = cot[...]
    for k in range(1, CHIPS):
        to_chip(hid.at[t], hid.at[t], send.at[0, k], recv.at[0, k], t, p, z, k).start()
    for copy in weights:
        copy.start()
    for k in range(1, CHIPS):
        to_chip(cots.at[t], cots.at[t], send.at[1, k], recv.at[1, k], t, p, z, k).start()
    for copy in weights:
        copy.wait()
    up_sum[...] = jnp.zeros_like(up_sum)

    def block(k, carry):
        src = (t + CHIPS - k) % CHIPS

        @pl.when(k > 0)
        def _():
            to_chip(hid.at[src], hid.at[src], send.at[0, k], recv.at[0, k], t, p, z, 1).wait_recv()

        pre = nn(hid[src], up[...]) + up_bias[...]
        cdf = 0.5 * (1.0 + lax.erf(pre * math.sqrt(0.5)))
        slope = cdf + pre * (jnp.exp(-0.5 * pre * pre) * (1.0 / math.sqrt(2.0 * math.pi)))
        act[src] = (pre * cdf).astype(BF16)

        @pl.when(k > 0)
        def _():
            to_chip(cots.at[src], cots.at[src], send.at[1, k], recv.at[1, k], t, p, z, 1).wait_recv()

        grad = cols_product(cots[src], down[...]) * slope
        low = grad.astype(BF16)
        gpre[src] = low
        up_sum[...] += jnp.sum(low.astype(F32), 0, keepdims=True)
        part_h[src] = cols_product(low, up[...]).astype(BF16)

        @pl.when(k > 0)
        def _():
            to_chip(part_h.at[src], land_h.at[t], send.at[2, k], recv.at[2, k], t, p, z, CHIPS - k).start()

        part_o[src] = nn(act[src], down[...]).astype(BF16)
        return carry

    lax.fori_loop(0, CHIPS, block, 0)

    for k in range(1, CHIPS):
        src = (t + CHIPS - k) % CHIPS
        to_chip(part_o.at[src], land_o.at[t], send.at[3, k], recv.at[3, k], t, p, z, CHIPS - k).start()

    def stack(ref):
        return ref[...].reshape(CHIPS * ROWS, ref.shape[-1])

    full_up[...] = rows_product(stack(hid), stack(gpre)).astype(BF16)
    full_down[...] = rows_product(stack(act), stack(cots)).astype(BF16)
    swaps = []
    for i in range(4):
        for j, (full, land) in enumerate(((full_up, land_up), (full_down, land_down))):
            swaps.append(
                to_twin(
                    full.at[rows16(i * 272 + (1 - p) * 128, 144)],
                    land.at[i],
                    g_send.at[j, i],
                    g_recv.at[j, i],
                    t,
                    p,
                    z,
                )
            )
    for copy in swaps:
        copy.start()

    total = part_h[t].astype(F32)
    for k in range(1, CHIPS):
        to_chip(part_h.at[t], land_h.at[t], send.at[2, k], recv.at[2, k], t, p, z, k).wait()
        total = total + land_h[(t + k) % CHIPS].astype(F32)
    top = cot[...].astype(F32)
    grad_middle = top + norm_back(total, normed, inverse, gain[...])
    grad_mid[...] = grad_middle
    low = grad_middle.astype(BF16)
    gmid[t] = low
    for k in range(1, CHIPS):
        to_chip(gmid.at[t], gmid.at[t], send.at[4, k], recv.at[4, k], t, p, z, k).start()
    sums[0:1] = jnp.sum(low.astype(F32), 0, keepdims=True)
    sums[1:2] = jnp.sum(top, 0, keepdims=True)
    sums[2:3] = jnp.sum(total * normed, 0, keepdims=True)
    sums[3:4] = jnp.sum(total, 0, keepdims=True)
    sums[4:8] = jnp.zeros((4, D), F32)

    for copy in swaps:
        copy.wait()
    for i in range(4):
        for j, (full, land) in enumerate(((full_up, land_up), (full_down, land_down))):
            own = full[rows16(i * 272 + p * 128, 144)].astype(F32)
            g_feed[i, j * 144 : (j + 1) * 144] = (own + land[i].astype(F32)).astype(BF16)

    def heads(k, carry):
        src = (t + CHIPS - k) % CHIPS

        @pl.when(k > 0)
        def _():
            to_chip(gmid.at[src], gmid.at[src], send.at[4, k], recv.at[4, k], t, p, z, 1).wait_recv()

        gh_heads[src] = cols_product(gmid[src], out_w[...]).astype(BF16)
        return carry

    lax.fori_loop(0, CHIPS, heads, 0)
    grad_out = rows_product(stack(mixed), stack(gmid)).astype(BF16)

    @pl.when(t == CHIPS - 1)
    def _():
        raw[...] = grad_out[: SLOTS * HEAD_DIM]

    @pl.when(t < CHIPS - 1)
    def _():
        for i in range(4):
            raw[i * 80 : i * 80 + HEAD_DIM] = grad_out[i * HEAD_DIM : (i + 1) * HEAD_DIM]
            raw[i * 80 + HEAD_DIM : (i + 1) * 80] = jnp.zeros((16, D), BF16)

    swaps = [
        to_twin(
            raw.at[rows16(i * 80 + (1 - p) * 32, 48)],
            land_out.at[i],
            g_send.at[2, i],
            g_recv.at[2, i],
            t,
            p,
            z,
        )
        for i in range(4)
    ]
    for copy in swaps:
        copy.start()
    for copy in swaps:
        copy.wait()
    for i in range(4):
        own = raw[rows16(i * 80 + p * 32, 48)].astype(F32)
        g_out[i] = (own + land_out[i].astype(F32)).astype(BF16)

    result = middle[...] + down_bias[...] + part_o[t].astype(F32)
    for k in range(1, CHIPS):
        to_chip(part_o.at[t], land_o.at[t], send.at[3, k], recv.at[3, k], t, p, z, k).wait()
        result = result + land_o[(t + k) % CHIPS].astype(F32)
    output[...] = result.astype(BF16)
    for k in range(1, CHIPS):
        to_chip(hid.at[t], hid.at[t], send.at[0, k], recv.at[0, k], t, p, z, k).wait_send()
        to_chip(cots.at[t], cots.at[t], send.at[1, k], recv.at[1, k], t, p, z, k).wait_send()
        to_chip(gmid.at[t], gmid.at[t], send.at[4, k], recv.at[4, k], t, p, z, k).wait_send()


def feed(middle, cot, halves, up_bias, gain, shift, down_bias, out_w, mixed):
    dma = pltpu.SemaphoreType.DMA
    blocks = pltpu.VMEM((CHIPS, ROWS, D), BF16)
    matrix = pltpu.VMEM((D, D), BF16)
    piece = pltpu.VMEM((4, 144, D), BF16)
    return pl.pallas_call(
        feed_kernel,
        out_shape=(
            jax.ShapeDtypeStruct((ROWS, D), BF16),
            jax.ShapeDtypeStruct((ROWS, D), F32),
            jax.ShapeDtypeStruct((CHIPS, ROWS, WIDE), BF16),
            jax.ShapeDtypeStruct((4, 48, D), BF16),
            jax.ShapeDtypeStruct((4, 288, D), BF16),
            jax.ShapeDtypeStruct((8, D), F32),
            jax.ShapeDtypeStruct((1, D), F32),
        ),
        in_specs=vmem(9),
        out_specs=tuple(vmem(7)),
        scratch_shapes=[matrix, matrix]
        + [blocks] * 9
        + [matrix, matrix, piece, piece]
        + [
            pltpu.VMEM((SLOTS * HEAD_DIM, D), BF16),
            pltpu.VMEM((4, 48, D), BF16),
            dma((5, CHIPS)), dma((5, CHIPS)), dma((2, 4)), dma((2, 4)), dma((2, 4)),
            dma((3, 4)), dma((3, 4)),
        ],
        compiler_params=params(3, 63),
        name="feed",
    )(middle, cot, halves, up_bias, gain, shift, down_bias, out_w, mixed)


def back_kernel(
    x, grad_mid, dq, dk, dv, hid, whole, gain,
    grad_x, g_qkv, sums, head_sums,
    joint, full, land, land_k, land_v, part, land_h,
    send, recv, kv_send, kv_recv, g_send, g_recv,
):
    t, p, z = position()
    greet(t, p, z)
    swaps = []
    for k in range(CHIPS):
        other = (t + CHIPS - k) % CHIPS * 2 + 1 - p
        mine = (t + CHIPS - k) % CHIPS
        for j, (ref, dst) in enumerate(((dk, land_k), (dv, land_v))):
            swaps.append(
                to_twin(ref.at[other], dst.at[mine], kv_send.at[j, k], kv_recv.at[j, k], t, p, z)
            )
    for copy in swaps:
        copy.start()
    normed, inverse = normalize(x[...].astype(F32))
    for copy in swaps:
        copy.wait()
    head_sums[...] = jnp.zeros_like(head_sums)

    def block(k, carry):
        dst = (t + k) % CHIPS
        mine = dst * 2 + p
        joint[dst, :, :WIDE] = dq[dst]
        joint[dst, :, WIDE : 2 * WIDE] = (dk[mine].astype(F32) + land_k[dst].astype(F32)).astype(BF16)
        low_v = (dv[mine].astype(F32) + land_v[dst].astype(F32)).astype(BF16)
        joint[dst, :, 2 * WIDE :] = low_v
        head_sums[0:1] += jnp.sum(dq[dst].astype(F32), 0, keepdims=True)
        head_sums[1:2] += jnp.sum(low_v.astype(F32), 0, keepdims=True)
        part[dst] = cols_product(joint[dst], whole[...]).astype(BF16)

        to_chip(part.at[dst], land_h.at[t], send.at[k], recv.at[k], t, p, z, k).start()
        return carry

    lax.fori_loop(1, CHIPS, block, 0)
    joint[t, :, :WIDE] = dq[t]
    joint[t, :, WIDE : 2 * WIDE] = (dk[t * 2 + p].astype(F32) + land_k[t].astype(F32)).astype(BF16)
    low_v = (dv[t * 2 + p].astype(F32) + land_v[t].astype(F32)).astype(BF16)
    joint[t, :, 2 * WIDE :] = low_v
    head_sums[0:1] += jnp.sum(dq[t].astype(F32), 0, keepdims=True)
    head_sums[1:2] += jnp.sum(low_v.astype(F32), 0, keepdims=True)
    total = cols_product(joint[t], whole[...])

    def stack(ref):
        return ref[...].reshape(CHIPS * ROWS, ref.shape[-1])

    full[...] = rows_product(stack(hid), stack(joint)).astype(BF16)
    swaps = [
        to_twin(
            full.at[rows16(i * 272 + (1 - p) * 128, 144)],
            land.at[i],
            g_send.at[i],
            g_recv.at[i],
            t,
            p,
            z,
        )
        for i in range(4)
    ]
    for copy in swaps:
        copy.start()
    for copy in swaps:
        copy.wait()
    for i in range(4):
        own = full[rows16(i * 272 + p * 128, 144)].astype(F32)
        g_qkv[i] = (own + land[i].astype(F32)).astype(BF16)
    for k in range(1, CHIPS):
        dst = (t + k) % CHIPS
        to_chip(part.at[dst], land_h.at[t], send.at[k], recv.at[k], t, p, z, k).wait()
        total = total + land_h[(t + CHIPS - k) % CHIPS].astype(F32)
    grad_x[...] = grad_mid[...] + norm_back(total, normed, inverse, gain[...])
    sums[0:1] = jnp.sum(total * normed, 0, keepdims=True)
    sums[1:2] = jnp.sum(total, 0, keepdims=True)
    sums[2:8] = jnp.zeros((6, D), F32)


def back(x, grad_mid, dq, dk, dv, hid, whole, gain):
    dma = pltpu.SemaphoreType.DMA
    heads = pltpu.VMEM((CHIPS, ROWS, WIDE), BF16)
    blocks = pltpu.VMEM((CHIPS, ROWS, D), BF16)
    return pl.pallas_call(
        back_kernel,
        out_shape=(
            jax.ShapeDtypeStruct((ROWS, D), F32),
            jax.ShapeDtypeStruct((4, 144, 3 * WIDE), BF16),
            jax.ShapeDtypeStruct((8, D), F32),
            jax.ShapeDtypeStruct((8, WIDE), F32),
        ),
        in_specs=vmem(8),
        out_specs=tuple(vmem(4)),
        scratch_shapes=[
            pltpu.VMEM((CHIPS, ROWS, 3 * WIDE), BF16),
            pltpu.VMEM((D, 3 * WIDE), BF16),
            pltpu.VMEM((4, 144, 3 * WIDE), BF16),
            heads, heads, blocks, blocks,
            dma((CHIPS,)), dma((CHIPS,)), dma((2, CHIPS)), dma((2, CHIPS)), dma((4,)), dma((4,)),
        ],
        compiler_params=params(4),
        name="back",
    )(x, grad_mid, dq, dk, dv, hid, whole, gain)


def shares(array):
    return lax.psum_scatter(array.reshape((-1, array.shape[-1])), "wsh", scatter_dimension=0, tiled=True)


def joined(pieces, keep):
    pairs = pieces.reshape(CHIPS, 2, keep, pieces.shape[-1])
    return jnp.concatenate([pairs[:, 0], pairs[:, 1, 16:]], axis=1)


def plane_device(
    tokens, seq_lengths, cotangent, ln1_gain, ln1_bias, w_qkv, b_query, b_value, w_out, b_out,
    ln2_gain, ln2_bias, w_up, b_up, w_down, b_down,
):
    c = lax.axis_index("ctx")
    z = lax.axis_index("wsh")
    t, p = (c // 2, c % 2)
    x, cot, lengths = (tokens[0], cotangent[0], seq_lengths[0])
    parity = p[None].astype(jnp.int32)
    shard = D // 4
    integers = functools.partial(jnp.arange, dtype=jnp.int32)

    def columns_of(heads):
        heads = jnp.concatenate([heads, jnp.full((1,), -40, jnp.int32)])
        columns = jnp.repeat(heads, HEAD_DIM) * HEAD_DIM + integers(WIDE) % HEAD_DIM
        return (integers(D)[:, None] == columns[None, :]).astype(BF16)

    table = jnp.asarray(HEAD_TABLE, jnp.int32)
    select = columns_of(lax.dynamic_index_in_dim(table, t, 0, keepdims=False))

    vectors = jnp.stack(
        [
            b_query, b_value, b_out, b_down, ln1_gain, ln1_bias, ln2_gain, ln2_bias,
            lax.dynamic_slice_in_dim(b_up, t * shard, shard),
        ]
    )
    vectors = lax.all_gather(vectors, "wsh", axis=1, tiled=True)
    head_bias = jnp.dot(vectors[:2], select, preferred_element_type=F32)
    vectors = vectors.astype(F32)
    bias_q, bias_v = (head_bias[0:1], head_bias[1:2])
    bias_o, bias_d, gain_1, shift_1, gain_2, shift_2, bias_u = [
        vectors[i : i + 1] for i in range(2, 9)
    ]

    qkv_rows = lax.dynamic_slice_in_dim(w_qkv, p * 128, 144, 0)
    qkv_half = jnp.concatenate(
        [
            jnp.dot(qkv_rows[:, i * D : (i + 1) * D], select, preferred_element_type=F32)
            for i in range(3)
        ],
        axis=1,
    ).astype(BF16)
    qkv_half = lax.all_gather(qkv_half, "wsh", axis=0)

    ahead = jnp.asarray((0, 48, 32, 16), jnp.int32)[z]
    i = p * 32 + integers(48)
    early = jnp.where(i < HEAD_DIM, ahead + HEAD_DIM * t + i, -1)
    late = jnp.where(i < ahead, i, 192 + i)
    taken = jnp.where(t < CHIPS - 1, early, late)
    pick = (taken[:, None] == integers(shard)[None, :]).astype(BF16)
    out_half = jnp.dot(pick, w_out, preferred_element_type=F32).astype(BF16)
    out_half = lax.all_gather(out_half, "wsh", axis=0)

    up_rows = lax.dynamic_slice_in_dim(w_up, p * 128, 144, 0)
    up_half = jnp.concatenate(
        [lax.dynamic_slice_in_dim(up_rows, i * D + t * shard, shard, 1) for i in range(4)], axis=1
    )
    down_half = lax.dynamic_slice_in_dim(w_down, t * shard + p * 128, 144, 0)
    halves = lax.all_gather(jnp.concatenate([up_half, down_half]), "wsh", axis=0)

    q, k, v, hid, whole = project(x, qkv_half, gain_1, shift_1, bias_q, bias_v)
    mixed, lse = attend(lengths, parity, q, k, v)
    middle, out_w = out_project(x, mixed, out_half, bias_o)
    output, grad_mid, grad_heads, g_out, g_feed, sums, up_sum = feed(
        middle, cot, halves, bias_u, gain_2, shift_2, bias_d, out_w, mixed
    )
    feed_all = lax.all_gather(shares(g_feed), "ctx", axis=0)
    out_all = lax.all_gather(shares(g_out), "ctx", axis=0)
    dq, dk, dv = attend_back(lengths, parity, q, k, v, mixed, grad_heads, lse)
    grad_x, g_qkv, sums_1, head_sums = back(x, grad_mid, dq, dk, dv, hid, whole, gain_1)
    qkv_all = lax.all_gather(shares(g_qkv), "ctx", axis=0)

    up_all = joined(feed_all[:, :144], 144)
    grad_up = jnp.transpose(up_all.reshape(CHIPS, shard, 4, shard), (1, 2, 0, 3))
    grad_up = grad_up.reshape(shard, 4 * D).astype(F32)
    grad_down = joined(feed_all[:, 144:], 144).reshape(D, D).astype(F32)
    row = integers(shard)
    inner = row - ahead
    source = jnp.where(
        row < ahead,
        240 + row,
        jnp.where(inner < 192, inner // HEAD_DIM * 80 + inner % HEAD_DIM, 48 + row),
    )
    place = (source[:, None] == integers(320)[None, :]).astype(BF16)
    grad_out = jnp.dot(place, joined(out_all, 48).reshape(320, D), preferred_element_type=F32)
    selects = jnp.stack([columns_of(table[i]) for i in range(CHIPS)])
    grad_qkv = jnp.concatenate(
        [
            lax.dot_general(
                part, selects, (((0, 2), (0, 2)), ((), ())), preferred_element_type=F32
            )
            for part in jnp.split(joined(qkv_all, 144), 3, axis=2)
        ],
        axis=1,
    )

    head_vectors = lax.dot_general(
        head_sums[:2],
        select.astype(F32),
        (((1,), (1,)), ((), ())),
        precision=lax.Precision.HIGHEST,
        preferred_element_type=F32,
    )
    ups = lax.dynamic_update_slice(
        jnp.zeros((4, D), F32), up_sum.reshape(4, shard), (jnp.int32(0), t * shard)
    )
    totals = jnp.concatenate([sums[:4], sums_1[:2], head_vectors, ups])
    totals = lax.psum(totals, ("ctx", "wsh"))
    mine = lax.dynamic_slice_in_dim(totals, z * shard, shard, 1)
    grad_b_up = lax.dynamic_index_in_dim(totals, 8 + z, 0, keepdims=False)
    return (
        output[None], grad_x[None],
        mine[4], mine[5], grad_qkv, mine[6], mine[7], grad_out, mine[0],
        mine[2], mine[3], grad_up, grad_b_up, grad_down, mine[1],
    )


def solution(mesh):
    in_specs = (
        P("wsh", "ctx", None),
        P("wsh", None),
        P("wsh", "ctx", None),
        P("wsh"),
        P("wsh"),
        P("wsh", None),
        P("wsh"),
        P("wsh"),
        P("wsh", None),
        P("wsh"),
        P("wsh"),
        P("wsh"),
        P("wsh", None),
        P("wsh"),
        P("wsh", None),
        P("wsh"),
    )
    out_specs = (
        P("wsh", "ctx", None),
        P("wsh", "ctx", None),
        P("wsh"),
        P("wsh"),
        P("wsh", None),
        P("wsh"),
        P("wsh"),
        P("wsh", None),
        P("wsh"),
        P("wsh"),
        P("wsh"),
        P("wsh", None),
        P("wsh"),
        P("wsh", None),
        P("wsh"),
    )
    sizes = (mesh.shape["ctx"], mesh.shape["wsh"])
    body = plane_device if sizes == (2 * CHIPS, 4) else on_device
    return jax.shard_map(
        body, mesh=mesh, in_specs=in_specs, out_specs=out_specs, check_vma=False
    )
```

```python
import functools
import math

import jax
import jax.numpy as jnp
from jax import lax
from jax.experimental import pallas as pl
from jax.experimental.pallas import tpu as pltpu
from jax.sharding import PartitionSpec as P

D = 1088
HEADS = 17
HEAD_DIM = 64


def normalize(inputs):
    center = inputs - jnp.mean(inputs, -1, keepdims=True)
    inverse = lax.rsqrt(jnp.mean(center * center, -1, keepdims=True) + 1e-05)
    return (center * inverse, inverse)


def norm_back(grad_in, normed, inverse, gain):
    scaled = grad_in * gain
    return inverse * (
        scaled
        - jnp.mean(scaled, -1, keepdims=True)
        - normed * jnp.mean(scaled * normed, -1, keepdims=True)
    )


def rows_product(left, right):
    return lax.dot_general(
        left, right, (((0,), (0,)), ((), ())), preferred_element_type=jnp.float32
    )


def cols_product(left, right):
    return lax.dot_general(
        left, right, (((1,), (1,)), ((), ())), preferred_element_type=jnp.float32
    )


def sequence_ids(lengths, positions):
    bounds = jnp.cumsum(lengths)
    return jnp.sum((positions[:, None] >= bounds[None, :]).astype(jnp.int32), axis=1)


def allowed_pairs(lengths, query_pos, key_pos):
    query_owner = sequence_ids(lengths, query_pos)
    key_owner = sequence_ids(lengths, key_pos)
    return (key_pos[None, :] <= query_pos[:, None]) & (
        (key_owner[None, :] == 0) | (key_owner[None, :] == query_owner[:, None])
    )


def over_blocks(state_in, arrays, step_fn):
    total_rows = arrays[0].shape[0]
    block_rows = math.gcd(total_rows, 512)

    def advance(block_index, state_now):
        offset = block_index * block_rows
        pieces = tuple((lax.dynamic_slice_in_dim(array, offset, block_rows, 0) for array in arrays))
        return step_fn(state_now, pieces, offset)

    return lax.fori_loop(0, total_rows // block_rows, advance, state_in)


def sectioned_sum(partials):
    shares = lax.psum_scatter(partials, "wsh", scatter_dimension=0, tiled=True)
    return lax.psum(shares, "ctx")


def on_device(
    tokens,
    seq_lengths,
    cotangent,
    ln1_gain,
    ln1_bias,
    w_qkv,
    b_query,
    b_value,
    w_out,
    b_out,
    ln2_gain,
    ln2_bias,
    w_up,
    b_up,
    w_down,
    b_down,
):
    token_rows, grad_rows = (tokens[0], cotangent[0])
    shards = (
        w_qkv,
        w_out,
        w_up,
        w_down,
        b_query,
        b_value,
        b_out,
        b_up,
        b_down,
        ln1_gain,
        ln1_bias,
        ln2_gain,
        ln2_bias,
    )
    gathered = (
        lax.all_gather(shards[0], "wsh", axis=0, tiled=True),
        lax.all_gather(shards[1], "wsh", axis=0, tiled=True),
        lax.all_gather(shards[2], "wsh", axis=0, tiled=True),
        lax.all_gather(shards[3], "wsh", axis=0, tiled=True),
        lax.all_gather(shards[4], "wsh", axis=0, tiled=True),
        lax.all_gather(shards[5], "wsh", axis=0, tiled=True),
        lax.all_gather(shards[6], "wsh", axis=0, tiled=True),
        lax.all_gather(shards[7], "wsh", axis=0, tiled=True),
        lax.all_gather(shards[8], "wsh", axis=0, tiled=True),
        lax.all_gather(shards[9], "wsh", axis=0, tiled=True),
        lax.all_gather(shards[10], "wsh", axis=0, tiled=True),
        lax.all_gather(shards[11], "wsh", axis=0, tiled=True),
        lax.all_gather(shards[12], "wsh", axis=0, tiled=True),
    )
    qkv_full, out_full, up_full, down_full = (gathered[0], gathered[1], gathered[2], gathered[3])
    query_bias, value_bias, out_bias, up_bias, down_bias = [
        piece.astype(jnp.float32) for piece in gathered[4:9]
    ]
    gain_one, shift_one, gain_two, shift_two = [
        piece.astype(jnp.float32) for piece in gathered[9:13]
    ]
    lengths = seq_lengths[0]
    tok_rows = token_rows.shape[0]
    my_pos = lax.axis_index("ctx") * tok_rows + jnp.arange(tok_rows, dtype=jnp.int32)
    scale_qk = HEAD_DIM ** (-0.5)
    inputs = token_rows.astype(jnp.float32)
    normed_one, inverse_one = normalize(inputs)
    hidden_one = (normed_one * gain_one + shift_one).astype(jnp.bfloat16)
    joint_proj = jnp.dot(hidden_one, qkv_full, preferred_element_type=jnp.float32)
    queries = (joint_proj[:, :D] + query_bias).astype(jnp.bfloat16)
    key_rows = joint_proj[:, D : 2 * D].astype(jnp.bfloat16)
    value_rows = (joint_proj[:, 2 * D :] + value_bias).astype(jnp.bfloat16)
    query_heads = queries.reshape(tok_rows, HEADS, HEAD_DIM)
    my_key_heads = key_rows.reshape(tok_rows, HEADS, HEAD_DIM)
    my_value_heads = value_rows.reshape(tok_rows, HEADS, HEAD_DIM)

    def forward_step(state_now, pieces, first_row):
        key_heads = pieces[0].reshape(-1, HEADS, HEAD_DIM)
        value_heads = pieces[1].reshape(-1, HEADS, HEAD_DIM)
        key_pos = first_row + jnp.arange(key_heads.shape[0], dtype=jnp.int32)
        allowed = allowed_pairs(lengths, my_pos, key_pos)

        def forward_compute(inner):
            peak_old, total_old, accum_old = inner
            scores = (
                jnp.einsum(
                    "qhd,khd->hqk", query_heads, key_heads, preferred_element_type=jnp.float32
                )
                * scale_qk
            )
            scores = jnp.where(allowed[None], scores, -1e30)
            peak_new = jnp.maximum(peak_old, jnp.max(scores, -1))
            factor = jnp.exp(peak_old - peak_new)
            expos = jnp.where(allowed[None], jnp.exp(scores - peak_new[:, :, None]), 0.0)
            total_new = total_old * factor + jnp.sum(expos, -1)
            accum_new = accum_old * factor.T[:, :, None] + jnp.einsum(
                "hqk,khd->qhd",
                expos.astype(jnp.bfloat16),
                value_heads,
                preferred_element_type=jnp.float32,
            )
            return (peak_new, total_new, accum_new)

        return lax.cond(jnp.any(allowed), forward_compute, lambda inner: inner, state_now)

    start_state = (
        jnp.full((HEADS, tok_rows), -1e30, jnp.float32),
        jnp.zeros((HEADS, tok_rows), jnp.float32),
        jnp.zeros((tok_rows, HEADS, HEAD_DIM), jnp.float32),
    )
    peak, total, accum = over_blocks(
        start_state,
        (
            lax.all_gather(key_rows, "ctx", axis=0, tiled=True),
            lax.all_gather(value_rows, "ctx", axis=0, tiled=True),
        ),
        forward_step,
    )
    mixed = accum / total.T[:, :, None]
    log_sum = (peak + jnp.log(total)).T
    mixed_low = mixed.reshape(tok_rows, D).astype(jnp.bfloat16)
    middle = inputs + jnp.dot(mixed_low, out_full, preferred_element_type=jnp.float32) + out_bias
    normed_two, inverse_two = normalize(middle)
    hidden_two = (normed_two * gain_two + shift_two).astype(jnp.bfloat16)
    pre_act = jnp.dot(hidden_two, up_full, preferred_element_type=jnp.float32) + up_bias
    activ_low = jax.nn.gelu(pre_act, approximate=False).astype(jnp.bfloat16)
    result = middle + jnp.dot(activ_low, down_full, preferred_element_type=jnp.float32) + down_bias
    output_rows = result.astype(jnp.bfloat16)
    grad_top_f = grad_rows.astype(jnp.float32)
    grad_down = rows_product(activ_low, grad_rows)
    grad_down_bias = jnp.sum(grad_top_f, 0)
    grad_act = cols_product(grad_rows, down_full)
    cdf_part = 0.5 * (1.0 + lax.erf(pre_act * math.sqrt(0.5)))
    pdf_part = jnp.exp(-0.5 * pre_act * pre_act) / math.sqrt(2.0 * math.pi)
    grad_pre = (grad_act * (cdf_part + pre_act * pdf_part)).astype(jnp.bfloat16)
    grad_up = rows_product(hidden_two, grad_pre)
    grad_up_bias = jnp.sum(grad_pre.astype(jnp.float32), 0)
    grad_h2 = cols_product(grad_pre, up_full)
    grad_gain_two = jnp.sum(grad_h2 * normed_two, 0)
    grad_shift_two = jnp.sum(grad_h2, 0)
    grad_mid = grad_top_f + norm_back(grad_h2, normed_two, inverse_two, gain_two)
    grad_mid_low = grad_mid.astype(jnp.bfloat16)
    grad_out_w = rows_product(mixed_low, grad_mid_low)
    grad_out_bias = jnp.sum(grad_mid_low.astype(jnp.float32), 0)
    grad_mixed = cols_product(grad_mid_low, out_full).astype(jnp.bfloat16)
    grad_heads = grad_mixed.reshape(tok_rows, HEADS, HEAD_DIM)
    delta = jnp.sum(grad_heads.astype(jnp.float32) * mixed, -1)
    lse_all, delta_all = (
        lax.all_gather(log_sum, "ctx", axis=0, tiled=True),
        lax.all_gather(delta, "ctx", axis=0, tiled=True),
    )

    def query_step(state_now, pieces, first_row):
        key_heads = pieces[0].reshape(-1, HEADS, HEAD_DIM)
        value_heads = pieces[1].reshape(-1, HEADS, HEAD_DIM)
        key_pos = first_row + jnp.arange(key_heads.shape[0], dtype=jnp.int32)
        allowed = allowed_pairs(lengths, my_pos, key_pos)

        def query_compute(accum_old):
            scores = (
                jnp.einsum(
                    "qhd,khd->hqk", query_heads, key_heads, preferred_element_type=jnp.float32
                )
                * scale_qk
            )
            probs = jnp.where(allowed[None], jnp.exp(scores - log_sum.T[:, :, None]), 0.0)
            grad_probs = jnp.einsum(
                "qhd,khd->hqk", grad_heads, value_heads, preferred_element_type=jnp.float32
            )
            grad_scores = (probs * (grad_probs - delta.T[:, :, None])).astype(jnp.bfloat16)
            return accum_old + jnp.einsum(
                "hqk,khd->qhd", grad_scores, key_heads, preferred_element_type=jnp.float32
            )

        return lax.cond(jnp.any(allowed), query_compute, lambda inner: inner, state_now)

    zero_heads = jnp.zeros((tok_rows, HEADS, HEAD_DIM), jnp.float32)
    grad_query = over_blocks(
        zero_heads,
        (
            lax.all_gather(key_rows, "ctx", axis=0, tiled=True),
            lax.all_gather(value_rows, "ctx", axis=0, tiled=True),
        ),
        query_step,
    )

    def key_step(state_now, pieces, first_row):
        other_queries = pieces[0].reshape(-1, HEADS, HEAD_DIM)
        other_grads = pieces[1].reshape(-1, HEADS, HEAD_DIM)
        other_count = other_queries.shape[0]
        other_pos = first_row + jnp.arange(other_count, dtype=jnp.int32)
        other_lse = lax.dynamic_slice_in_dim(lse_all, first_row, other_count, 0)
        other_delta = lax.dynamic_slice_in_dim(delta_all, first_row, other_count, 0)
        allowed = allowed_pairs(lengths, other_pos, my_pos)

        def key_compute(inner):
            grad_key_old, grad_value_old = inner
            scores = (
                jnp.einsum(
                    "qhd,khd->hqk", other_queries, my_key_heads, preferred_element_type=jnp.float32
                )
                * scale_qk
            )
            probs = jnp.where(allowed[None], jnp.exp(scores - other_lse.T[:, :, None]), 0.0)
            grad_value_new = grad_value_old + jnp.einsum(
                "hqk,qhd->khd",
                probs.astype(jnp.bfloat16),
                other_grads,
                preferred_element_type=jnp.float32,
            )
            grad_probs = jnp.einsum(
                "qhd,khd->hqk", other_grads, my_value_heads, preferred_element_type=jnp.float32
            )
            grad_scores = (probs * (grad_probs - other_delta.T[:, :, None])).astype(jnp.bfloat16)
            grad_key_new = grad_key_old + jnp.einsum(
                "hqk,qhd->khd", grad_scores, other_queries, preferred_element_type=jnp.float32
            )
            return (grad_key_new, grad_value_new)

        return lax.cond(jnp.any(allowed), key_compute, lambda inner: inner, state_now)

    grad_key, grad_value = over_blocks(
        (zero_heads, zero_heads),
        (
            lax.all_gather(queries, "ctx", axis=0, tiled=True),
            lax.all_gather(grad_mixed, "ctx", axis=0, tiled=True),
        ),
        key_step,
    )
    grad_joint = jnp.concatenate(
        [
            (grad_query * scale_qk).reshape(tok_rows, D),
            (grad_key * scale_qk).reshape(tok_rows, D),
            grad_value.reshape(tok_rows, D),
        ],
        axis=1,
    ).astype(jnp.bfloat16)
    grad_qkv_w = rows_product(hidden_one, grad_joint)
    grad_joint_f = grad_joint.astype(jnp.float32)
    grad_query_bias = jnp.sum(grad_joint_f[:, :D], 0)
    grad_value_bias = jnp.sum(grad_joint_f[:, 2 * D :], 0)
    grad_h1 = cols_product(grad_joint, qkv_full)
    grad_gain_one = jnp.sum(grad_h1 * normed_one, 0)
    grad_shift_one = jnp.sum(grad_h1, 0)
    grad_input = grad_mid + norm_back(grad_h1, normed_one, inverse_one, gain_one)
    matrices = (grad_qkv_w, grad_out_w, grad_up, grad_down)
    vectors = (
        grad_query_bias,
        grad_value_bias,
        grad_out_bias,
        grad_up_bias,
        grad_down_bias,
        grad_gain_one,
        grad_shift_one,
        grad_gain_two,
        grad_shift_two,
    )
    totals = sectioned_sum(matrices + vectors)
    return (
        output_rows[None],
        grad_input[None],
        totals[9],
        totals[10],
        totals[0],
        totals[4],
        totals[5],
        totals[1],
        totals[6],
        totals[11],
        totals[12],
        totals[2],
        totals[7],
        totals[3],
        totals[8],
    )


SLOTS = 5
WIDE = 384
ROWS = 256
HALF = ROWS // 2
CHIPS = 4
TILE = 128
FEED_ROWS = 304
MESH_ID = pl.DeviceIdType.MESH
F32, BF16 = (jnp.float32, jnp.bfloat16)
NEG = -1e30
HEAD_TABLE = ((0, 5, 9, 13, -40), (1, 6, 10, 14, -40), (2, 7, 11, 15, -40), (3, 4, 8, 12, 16))
B_QUERY, B_VALUE, B_OUT, B_DOWN, GAIN_1, SHIFT_1, GAIN_2, SHIFT_2, B_UP = range(9)


def nn(left, right):
    return jnp.dot(left, right, preferred_element_type=F32)


def remote(src, dst, send, recv, where):
    return pltpu.make_async_remote_copy(
        src_ref=src, dst_ref=dst, send_sem=send, recv_sem=recv, device_id=where, device_id_type=MESH_ID
    )


def rows16(start, size):
    return pl.ds(pl.multiple_of(start, 16), size)


class Place:
    def __init__(self):
        self.c, self.z = (lax.axis_index("ctx"), lax.axis_index("wsh"))
        self.t, self.p = (self.c // 2, self.c % 2)
        self.tx, self.ty, self.td = (self.flip(1, 0), self.flip(0, 1), self.flip(1, 1))

    def flip(self, dx, dy):
        return (self.t // 2 + dy) % 2 * 2 + (self.t % 2 + dx) % 2

    def chip(self, chip):
        return (chip * 2 + self.p, self.z)

    def twin(self):
        return (self.t * 2 + 1 - self.p, self.z)

    def plane(self, step):
        return (self.c, (self.z + step) % 4)

    def greet(self, planes=True):
        barrier = pltpu.get_barrier_semaphore()
        others = [self.chip(self.tx), self.chip(self.ty), self.twin()]
        if planes:
            others += [self.plane(1), self.plane(2), self.plane(3)]
        for where in others:
            pl.semaphore_signal(barrier, inc=1, device_id=where, device_id_type=MESH_ID)
        pl.semaphore_wait(barrier, len(others))


class Gather:
    def __init__(self, e, own, view, rows, cut, send, recv):
        self.e, self.own, self.view, self.send, self.recv = (e, own, view, send, recv)
        self.parts = (pl.ds(0, cut), pl.ds(cut, rows - cut))

    def copy(self, i):
        e = self.e
        chip = (e.t, e.t, e.t, e.t, e.tx, e.ty)[i]
        part = self.parts[(0, 1, 1, 0, 0, 1)[i]]
        src = self.own if i < 4 else self.view(chip)
        where = e.chip((e.tx, e.tx, e.ty, e.ty, e.ty, e.tx)[i])
        return remote(src.at[part], self.view(chip).at[part], self.send.at[i], self.recv.at[i], where)

    def start(self):
        for i in (0, 2, 1, 3):
            self.copy(i).start()

    def forward(self):
        self.copy(0).wait_recv()
        self.copy(4).start()
        self.copy(2).wait_recv()
        self.copy(5).start()

    def have_x(self):
        self.copy(1).wait_recv()

    def have_y(self):
        self.copy(3).wait_recv()

    def have_far(self):
        self.copy(4).wait_recv()
        self.copy(5).wait_recv()

    def sent(self):
        for i in range(6):
            self.copy(i).wait_send()


class Scatter:
    def __init__(self, e, part, land, send, recv):
        self.e, self.part, self.land, self.send, self.recv = (e, part, land, send, recv)

    def copy(self, i):
        e = self.e
        chip = (e.td, e.td, e.tx, e.tx, e.ty, e.ty)[i]
        part = pl.ds((0, HALF, 0, HALF, HALF, 0)[i], HALF)
        where = e.chip((e.tx, e.ty, e.tx, e.tx, e.ty, e.ty)[i])
        return remote(
            self.part.at[chip, part], self.land.at[i], self.send.at[i], self.recv.at[i], where
        )

    def far_ready(self):
        self.copy(0).start()
        self.copy(1).start()

    def x_ready(self):
        self.copy(2).start()

    def y_ready(self):
        self.copy(4).start()

    def relay(self):
        self.copy(1).wait_recv()
        chip = self.e.tx
        self.part[chip, HALF:] = (self.part[chip, HALF:].astype(F32) + self.land[1].astype(F32)).astype(BF16)
        self.copy(3).start()
        self.copy(0).wait_recv()
        chip = self.e.ty
        self.part[chip, :HALF] = (self.part[chip, :HALF].astype(F32) + self.land[0].astype(F32)).astype(BF16)
        self.copy(5).start()

    def total(self):
        for i in (2, 4, 3, 5):
            self.copy(i).wait_recv()
        first = self.land[2].astype(F32) + self.land[5].astype(F32)
        second = self.land[4].astype(F32) + self.land[3].astype(F32)
        return jnp.concatenate([first, second], 0)

    def sent(self):
        for i in range(6):
            self.copy(i).wait_send()


class ZGather:
    def __init__(self, e, own, held, send, recv, put):
        self.e, self.own, self.held, self.send, self.recv, self.put = (e, own, held, send, recv, put)

    def copy(self, way, j):
        e = self.e
        shard = e.z - j if way == 0 else e.z + j
        src = self.own if j == 0 else self.held.at[shard]
        return remote(
            src, self.held.at[shard], self.send.at[way, j], self.recv.at[way, j], e.plane(1 if way == 0 else 3)
        )

    def sends(self, way, j):
        z = self.e.z
        return (z < 3) & (z >= j) if way == 0 else (z > 0) & (z <= 3 - j)

    def step(self, j):
        z = self.e.z
        for way in range(2):
            if j > 0:
                @pl.when(z >= j if way == 0 else z <= 3 - j)
                def _():
                    self.copy(way, j - 1).wait_recv()
            if j < 3:
                @pl.when(self.sends(way, j))
                def _():
                    self.copy(way, j).start()
            if j > 0:
                @pl.when(z >= j if way == 0 else z <= 3 - j)
                def _():
                    self.put(z - j if way == 0 else z + j)

    def sent(self):
        for way in range(2):
            for j in range(3):
                @pl.when(self.sends(way, j))
                def _():
                    self.copy(way, j).wait_send()


class ZScatter:
    def __init__(self, e, own, staged, right, left, send, recv):
        self.e, self.own, self.staged, self.land = (e, own, staged, (right, left))
        self.send, self.recv = (send, recv)

    def copy(self, way, j, src):
        return remote(
            src, self.land[way].at[j], self.send.at[way, j], self.recv.at[way, j],
            self.e.plane(1 if way == 0 else 3),
        )

    def begin(self):
        for plane, way in ((0, 0), (3, 1)):
            @pl.when(self.e.z == plane)
            def _():
                for j in range(3):
                    self.copy(way, j, self.own.at[3 - j if way == 0 else j]).start()

    def relay(self, way, j):
        dest = 3 - j if way == 0 else j
        self.copy(way, j, self.staged.at[dest]).wait_recv()
        self.staged[dest] = (self.own[dest].astype(F32) + self.land[way][j].astype(F32)).astype(BF16)
        self.copy(way, j, self.staged.at[dest]).start()

    def first(self):
        for plane, way in ((1, 0), (2, 1)):
            @pl.when(self.e.z == plane)
            def _():
                self.relay(way, 0)

    def second(self):
        for plane, way in ((1, 0), (2, 1)):
            @pl.when(self.e.z == plane)
            def _():
                self.relay(1 - way, 0)
                self.relay(way, 1)

    def last(self, out):
        right, left = self.land
        for z in range(4):
            @pl.when(self.e.z == z)
            def _():
                total = self.own[z].astype(F32)
                if z > 0:
                    self.copy(0, 3 - z, self.own.at[z]).wait_recv()
                    total = total + right[3 - z].astype(F32)
                if z < 3:
                    self.copy(1, z, self.own.at[z]).wait_recv()
                    total = total + left[z].astype(F32)
                out[...] = total.astype(BF16)
                for way in range(2):
                    for j in range((3 - z) if way == 0 else z):
                        self.copy(way, j, self.own.at[z]).wait_send()


def dma(*shape):
    return pltpu.SemaphoreType.DMA(shape)


def params(number, mib=56):
    return pltpu.CompilerParams(
        collective_id=number, has_side_effects=True, vmem_limit_bytes=mib * 2**20
    )


def vmem(count):
    return [pl.BlockSpec(memory_space=pltpu.VMEM)] * count


class Halves:
    def __init__(self, e, whole, block, keep, step, local, send, recv):
        self.e, self.whole, self.block, self.keep, self.step = (e, whole, block, keep, step)
        self.local, self.send, self.recv = (local, send, recv)

    def copies(self, src, shard):
        e = self.e
        return (
            pltpu.make_async_copy(
                src, self.whole.at[rows16(shard * self.block + e.p * self.step, self.keep)], self.local.at[shard]
            ),
            remote(
                src.at[rows16(e.p * (self.keep - self.step), self.step)],
                self.whole.at[rows16(shard * self.block + e.p * self.keep, self.step)],
                self.send.at[shard], self.recv.at[shard], e.twin(),
            ),
        )

    def put(self, src, shard):
        for copy in self.copies(src, shard):
            copy.start()

    def wait(self, src):
        for shard in range(4):
            for copy in self.copies(src, shard):
                copy.wait()


def project_kernel(
    x, cot, half, half_o, vec_in, select,
    q_out, k_out, v_out, h_out, cots, whole, out_w, vecs,
    held, held_o, raw, vec_land,
    v_send, v_recv, z_send, z_recv, a_send, a_recv, w_local, w_send, w_recv, kv_send, kv_recv,
):
    e = Place()
    t, p, z = (e.t, e.p, e.z)
    e.greet()
    vectors = [
        remote(vec_in, vec_land.at[k], v_send.at[k], v_recv.at[k], e.plane(k)) for k in range(1, 4)
    ]
    for copy in vectors:
        copy.start()
    into = Halves(e, whole, 272, 144, 128, w_local.at[0], w_send.at[0], w_recv.at[0])
    into_o = Halves(e, raw, 80, 48, 32, w_local.at[1], w_send.at[1], w_recv.at[1])
    chain = ZGather(
        e, half, held, z_send.at[0], z_recv.at[0], lambda shard: into.put(held.at[shard], shard)
    )
    chain_o = ZGather(
        e, half_o, held_o, z_send.at[1], z_recv.at[1], lambda shard: into_o.put(held_o.at[shard], shard)
    )
    chain.step(0)
    into.put(half, z)
    normed, _ = normalize(x[...].astype(F32))
    total = vec_in[...].astype(F32)
    for k in range(1, 4):
        vectors[k - 1].wait_recv()
        total = total + vec_land[k].astype(F32)
    vecs[...] = total
    h_out[t] = (normed * vecs[GAIN_1 : GAIN_1 + 1] + vecs[SHIFT_1 : SHIFT_1 + 1]).astype(BF16)
    hidden = Gather(e, h_out.at[t], lambda chip: h_out.at[chip], ROWS, HALF, a_send.at[0], a_recv.at[0])
    hidden.start()
    bias = nn(total.astype(BF16), select[...])
    bias_q, bias_v = (bias[B_QUERY : B_QUERY + 1], bias[B_VALUE : B_VALUE + 1])
    cots[t] = cot[...]
    chain.step(1)
    hidden.forward()
    tops = Gather(e, cot, lambda chip: cots.at[chip], ROWS, HALF, a_send.at[1], a_recv.at[1])
    tops.start()
    chain.step(2)
    chain_o.step(0)
    into_o.put(half_o, z)
    chain.step(3)
    into.wait(half)

    def block(k, carry):
        src = e.flip((k + 1) // 2 % 2, k // 2)

        @pl.when(k == 1)
        def _():
            hidden.have_x()

        @pl.when(k == 2)
        def _():
            hidden.have_far()

        @pl.when(k == 3)
        def _():
            hidden.have_y()

        h = h_out[src]
        q_out[src] = ((nn(h, whole[:, :WIDE]) + bias_q).astype(BF16) * 0.125).astype(BF16)
        mine = src * 2 + p
        k_out[mine] = nn(h, whole[:, WIDE : 2 * WIDE]).astype(BF16)
        remote(k_out.at[mine], k_out.at[mine], kv_send.at[k], kv_recv.at[k], e.twin()).start()
        v_out[mine] = (nn(h, whole[:, 2 * WIDE :]) + bias_v).astype(BF16)
        remote(
            v_out.at[mine], v_out.at[mine], kv_send.at[k + CHIPS], kv_recv.at[k + CHIPS], e.twin()
        ).start()
        return carry

    lax.fori_loop(0, CHIPS, block, 0)
    chain_o.step(1)
    tops.forward()
    chain_o.step(2)
    chain_o.step(3)
    into_o.wait(half_o)

    @pl.when(t == CHIPS - 1)
    def _():
        out_w[: SLOTS * HEAD_DIM] = raw[...]

    @pl.when(t < CHIPS - 1)
    def _():
        for i in range(4):
            out_w[i * HEAD_DIM : (i + 1) * HEAD_DIM] = raw[i * 80 : i * 80 + HEAD_DIM]
        out_w[4 * HEAD_DIM : 5 * HEAD_DIM] = jnp.zeros((HEAD_DIM, D), BF16)

    out_w[SLOTS * HEAD_DIM :] = jnp.zeros((WIDE - SLOTS * HEAD_DIM, D), BF16)
    for k in range(CHIPS):
        src = e.flip((k + 1) // 2 % 2, k // 2)
        other = src * 2 + 1 - p
        mine = src * 2 + p
        for ref, j in ((k_out, k), (v_out, k + CHIPS)):
            remote(ref.at[mine], ref.at[mine], kv_send.at[j], kv_recv.at[j], e.twin()).wait_send()
            remote(ref.at[other], ref.at[other], kv_send.at[j], kv_recv.at[j], e.twin()).wait_recv()
    tops.have_x()
    tops.have_y()
    tops.have_far()
    for user in (hidden, tops, chain, chain_o):
        user.sent()
    for copy in vectors:
        copy.wait_send()


def project(x, cot, half, half_o, vec_in, select):
    blocks = jax.ShapeDtypeStruct((CHIPS, ROWS, WIDE), BF16)
    keys = jax.ShapeDtypeStruct((2 * CHIPS, ROWS, WIDE), BF16)
    rows = jax.ShapeDtypeStruct((CHIPS, ROWS, D), BF16)
    return pl.pallas_call(
        project_kernel,
        out_shape=(
            blocks, keys, keys, rows, rows,
            jax.ShapeDtypeStruct((D, 3 * WIDE), BF16),
            jax.ShapeDtypeStruct((WIDE, D), BF16),
            jax.ShapeDtypeStruct((16, D), F32),
        ),
        in_specs=vmem(6),
        out_specs=tuple(vmem(8)),
        scratch_shapes=[
            pltpu.VMEM((4, 144, 3 * WIDE), BF16),
            pltpu.VMEM((4, 48, D), BF16),
            pltpu.VMEM((SLOTS * HEAD_DIM, D), BF16),
            pltpu.VMEM((4, 16, D), BF16),
            dma(4), dma(4), dma(2, 2, 3), dma(2, 2, 3), dma(2, 6), dma(2, 6),
            dma(2, 4), dma(2, 4), dma(2, 4), dma(2 * CHIPS), dma(2 * CHIPS),
        ],
        compiler_params=params(1),
        name="project",
    )(x, cot, half, half_o, vec_in, select)


def tile_bounds(lengths, block):
    ends = [lengths[0]]
    for i in range(1, 4):
        ends.append(ends[-1] + lengths[i])
    first = block * ROWS
    start_first = 0 * first
    for end in ends:
        start_first = jnp.where(first >= end, end, start_first)
    free = jnp.minimum(block, ends[0] // ROWS)
    resume = jnp.maximum(free + 1, start_first // ROWS)
    masked = jnp.where(free < block, 1 + jnp.maximum(block - resume, 0), 0)
    query_pos = first + lax.broadcasted_iota(jnp.int32, (1, ROWS), 1)
    start = jnp.zeros((1, ROWS), jnp.int32)
    for end in ends:
        start = jnp.where(query_pos >= end, end, start)
    return ends[0], query_pos, start, free, resume, masked


def visible(key_block, prompt, query_pos, start):
    key_pos = key_block * ROWS + lax.broadcasted_iota(jnp.int32, (ROWS, ROWS), 0)
    return (key_pos <= query_pos) & ((key_pos < prompt) | (key_pos >= start))


def half_of(rows, h):
    lane = lax.broadcasted_iota(jnp.int32, rows.shape, 1)
    return jnp.where((lane >= h * HEAD_DIM) & (lane < (h + 1) * HEAD_DIM), rows, jnp.zeros_like(rows))


def attend_kernel(lengths, parity, q, k, v, mixed, lse, turned):
    slab = pl.program_id(0)
    for j in range(2 * CHIPS):
        turned[j] = v[j].astype(F32).T.astype(BF16)

    def run(heads):
        def one(i, carry):
            block = 2 * i + parity[0]
            prompt, query_pos, start, free, resume, masked = tile_bounds(lengths, block)
            queries = [half_of(q[i], h) for h in heads]

            def tile(j, state, mask):
                keys = k[j]
                values = turned[j]
                new = []
                for h, (peak, total, accum) in zip(heads, state):
                    scores = cols_product(keys, queries[h])
                    if mask is not None:
                        scores = jnp.where(mask, scores, NEG)
                    peak_new = jnp.maximum(peak, jnp.max(scores, 0, keepdims=True))
                    factor = jnp.exp(peak - peak_new)
                    expos = jnp.exp(scores - peak_new)
                    total_new = total * factor + jnp.sum(expos, 0, keepdims=True)
                    part = values[h * HEAD_DIM : (h + 1) * HEAD_DIM]
                    accum_new = accum * factor + nn(part, expos.astype(BF16))
                    new.append((peak_new, total_new, accum_new))
                return tuple(new)

            state = tuple(
                (
                    jnp.full((1, ROWS), NEG, F32),
                    jnp.zeros((1, ROWS), F32),
                    jnp.zeros((HEAD_DIM, ROWS), F32),
                )
                for _ in heads
            )
            state = tile(block, state, visible(block, prompt, query_pos, start))
            state = lax.fori_loop(0, free, lambda j, s: tile(j, s, None), state)

            def other(m, s):
                j = jnp.where(m == 0, free, resume + m - 1)
                return tile(j, s, visible(j, prompt, query_pos, start))

            state = lax.fori_loop(0, masked, other, state)
            outs = []
            for h, (peak, total, accum) in zip(heads, state):
                outs.append(accum / total)
                lse[0, pl.ds(h * CHIPS + i, 1), :] = peak + jnp.log(total)
            if len(heads) == 1:
                outs.append(jnp.zeros((HEAD_DIM, ROWS), F32))
            mixed[i] = jnp.concatenate(outs, 0).T.astype(BF16)
            return carry

        lax.fori_loop(0, CHIPS, one, 0)

    @pl.when(slab < SLOTS // 2)
    def _():
        run((0, 1))

    @pl.when(slab >= SLOTS // 2)
    def _():
        lse[...] = jnp.zeros_like(lse)
        run((0,))


def slab_spec(count):
    return pl.BlockSpec((count, ROWS, 128), lambda s, *_: (0, 0, s))


def attend(lengths, parity, q, k, v):
    return pl.pallas_call(
        attend_kernel,
        out_shape=(
            jax.ShapeDtypeStruct((CHIPS, ROWS, WIDE), BF16),
            jax.ShapeDtypeStruct((3, 2 * CHIPS, ROWS), F32),
        ),
        grid_spec=pltpu.PrefetchScalarGridSpec(
            num_scalar_prefetch=2,
            grid=(3,),
            in_specs=[slab_spec(CHIPS), slab_spec(2 * CHIPS), slab_spec(2 * CHIPS)],
            out_specs=(
                slab_spec(CHIPS),
                pl.BlockSpec((1, 2 * CHIPS, ROWS), lambda s, *_: (s, 0, 0)),
            ),
            scratch_shapes=[pltpu.VMEM((2 * CHIPS, 128, ROWS), BF16)],
        ),
        compiler_params=pltpu.CompilerParams(vmem_limit_bytes=48 * 2**20),
        cost_estimate=pl.CostEstimate(flops=4 * 10**9, bytes_accessed=5 * 10**6, transcendentals=6 * 10**6),
        name="attend",
    )(lengths, parity, q, k, v)


def attend_back_kernel(
    lengths, parity, q, k, v, mixed, grad, lse, dq, dk, dv, turned, acc_k, acc_v
):
    slab = pl.program_id(0)
    for j in range(2 * CHIPS):
        turned[j] = k[j].astype(F32).T.astype(BF16)
    acc_k[...] = jnp.zeros_like(acc_k)
    acc_v[...] = jnp.zeros_like(acc_v)

    def run(heads):
        def one(i, carry):
            block = 2 * i + parity[0]
            prompt, query_pos, start, free, resume, masked = tile_bounds(lengths, block)
            queries = [half_of(q[i], h) for h in heads]
            grads = [half_of(grad[i], h) for h in heads]
            product = (grad[i].astype(F32) * mixed[i].astype(F32)).T
            deltas = [
                jnp.sum(product[h * HEAD_DIM : (h + 1) * HEAD_DIM], 0, keepdims=True) for h in heads
            ]
            sums = [lse[0, pl.ds(h * CHIPS + i, 1), :] for h in heads]

            def tile(j, state, mask):
                keys, values, keys_t = (k[j], v[j], turned[j])
                new = []
                add_k, add_v = (None, None)
                for h, accum in zip(heads, state):
                    scores = cols_product(keys, queries[h]) - sums[h]
                    if mask is not None:
                        scores = jnp.where(mask, scores, NEG)
                    probs = jnp.exp(scores)
                    grad_probs = cols_product(values, grads[h])
                    ds = (probs * (grad_probs - deltas[h])).astype(BF16)
                    part_v = nn(probs.astype(BF16), grads[h])
                    part_k = nn(ds, queries[h])
                    add_v = part_v if add_v is None else add_v + part_v
                    add_k = part_k if add_k is None else add_k + part_k
                    new.append(accum + nn(keys_t[h * HEAD_DIM : (h + 1) * HEAD_DIM], ds))
                acc_v[j] += add_v
                acc_k[j] += add_k
                return tuple(new)

            state = tuple(jnp.zeros((HEAD_DIM, ROWS), F32) for _ in heads)
            state = tile(block, state, visible(block, prompt, query_pos, start))
            state = lax.fori_loop(0, free, lambda j, s: tile(j, s, None), state)

            def other(m, s):
                j = jnp.where(m == 0, free, resume + m - 1)
                return tile(j, s, visible(j, prompt, query_pos, start))

            state = list(lax.fori_loop(0, masked, other, state))
            if len(heads) == 1:
                state.append(jnp.zeros((HEAD_DIM, ROWS), F32))
            dq[i] = (jnp.concatenate(state, 0) * 0.125).T.astype(BF16)
            return carry

        lax.fori_loop(0, CHIPS, one, 0)

    @pl.when(slab < SLOTS // 2)
    def _():
        run((0, 1))

    @pl.when(slab >= SLOTS // 2)
    def _():
        run((0,))

    dk[...] = acc_k[...].astype(BF16)
    dv[...] = acc_v[...].astype(BF16)


def attend_back(lengths, parity, q, k, v, mixed, grad, lse):
    few, many = (slab_spec(CHIPS), slab_spec(2 * CHIPS))
    return pl.pallas_call(
        attend_back_kernel,
        out_shape=(
            jax.ShapeDtypeStruct((CHIPS, ROWS, WIDE), BF16),
            jax.ShapeDtypeStruct((2 * CHIPS, ROWS, WIDE), BF16),
            jax.ShapeDtypeStruct((2 * CHIPS, ROWS, WIDE), BF16),
        ),
        grid_spec=pltpu.PrefetchScalarGridSpec(
            num_scalar_prefetch=2,
            grid=(3,),
            in_specs=[
                few, many, many, few, few,
                pl.BlockSpec((1, 2 * CHIPS, ROWS), lambda s, *_: (s, 0, 0)),
            ],
            out_specs=(few, many, many),
            scratch_shapes=[
                pltpu.VMEM((2 * CHIPS, 128, ROWS), BF16),
                pltpu.VMEM((2 * CHIPS, ROWS, 128), F32),
                pltpu.VMEM((2 * CHIPS, ROWS, 128), F32),
            ],
        ),
        compiler_params=pltpu.CompilerParams(vmem_limit_bytes=48 * 2**20),
        cost_estimate=pl.CostEstimate(flops=10 * 10**9, bytes_accessed=9 * 10**6, transcendentals=6 * 10**6),
        name="attend_back",
    )(lengths, parity, q, k, v, mixed, grad, lse)


def out_kernel(x, mixed, whole, vecs, middle, part, land, send, recv):
    e = Place()
    e.greet(planes=False)
    sums = Scatter(e, part, land, send, recv)

    def block(k, carry):
        dest = e.flip(1 - k // 2, 1 - k % 2)
        part[dest] = nn(mixed[dest], whole[...]).astype(BF16)

        @pl.when(k == 0)
        def _():
            sums.far_ready()

        @pl.when(k == 1)
        def _():
            sums.x_ready()

        @pl.when(k == 2)
        def _():
            sums.y_ready()

        return carry

    lax.fori_loop(0, CHIPS - 1, block, 0)
    total = x[...].astype(F32) + vecs[B_OUT : B_OUT + 1] + nn(mixed[e.t], whole[...])
    sums.relay()
    middle[...] = total + sums.total()
    sums.sent()


def out_project(x, mixed, whole, vecs):
    return pl.pallas_call(
        out_kernel,
        out_shape=jax.ShapeDtypeStruct((ROWS, D), F32),
        in_specs=vmem(4),
        out_specs=vmem(1)[0],
        scratch_shapes=[
            pltpu.VMEM((CHIPS, ROWS, D), BF16),
            pltpu.VMEM((6, HALF, D), BF16),
            dma(6), dma(6),
        ],
        compiler_params=params(2),
        name="out_project",
    )(x, mixed, whole, vecs)


def feed_kernel(
    middle, cots, halves, vecs, out_w, mixed,
    output, grad_mid, gh_heads, g_out, share, sums, up_sum,
    up, down, hid, act, gpre, part_o, part_h, gmid, sum_o_land, sum_h_land,
    full_up, full_down, land_up, land_down, land_more, g_feed, staged, z_right, z_left, raw, land_out,
    a_send, a_recv, s_send, s_recv, w_local, w_send, w_recv, d_local, d_send, d_recv, g_send, g_recv, z_send, z_recv,
):
    e = Place()
    t, p = (e.t, e.p)
    e.greet()
    into = Halves(e, up, 272, 144, 128, w_local, w_send, w_recv)
    weights = []
    for i in range(4):
        weights.extend(into.copies(halves.at[i, pl.ds(0, 144)], i))
    for i in range(5):
        src = halves.at[i, pl.ds(144, TILE)] if i < 4 else halves.at[t, pl.ds(272, 32)]
        dst = down.at[rows16(256 * i + p * TILE, TILE) if i < 4 else rows16(1024 + p * 32, 32)]
        weights.append(pltpu.make_async_copy(src, dst, d_local.at[i]))
        weights.append(remote(src, dst, d_send.at[i], d_recv.at[i], e.twin()))
    for copy in weights:
        copy.start()
    normed, inverse = normalize(middle[...])
    hid[t] = (normed * vecs[GAIN_2 : GAIN_2 + 1] + vecs[SHIFT_2 : SHIFT_2 + 1]).astype(BF16)
    hidden = Gather(e, hid.at[t], lambda chip: hid.at[chip], ROWS, HALF, a_send.at[0], a_recv.at[0])
    hidden.start()
    sum_h = Scatter(e, part_h, sum_h_land, s_send.at[0], s_recv.at[0])
    sum_o = Scatter(e, part_o, sum_o_land, s_send.at[1], s_recv.at[1])
    for copy in weights:
        copy.wait()
    up_sum[...] = jnp.zeros_like(up_sum)

    def block(k, carry):
        src = e.flip((k + 1) // 2 % 2, k // 2)

        @pl.when(k == 1)
        def _():
            hidden.forward()
            hidden.have_x()

        @pl.when(k == 2)
        def _():
            hidden.have_far()

        @pl.when(k == 3)
        def _():
            hidden.have_y()

        pre = nn(hid[src], up[...]) + vecs[B_UP : B_UP + 1]
        cdf = 0.5 * (1.0 + lax.erf(pre * math.sqrt(0.5)))
        slope = cdf + pre * (jnp.exp(-0.5 * pre * pre) * (1.0 / math.sqrt(2.0 * math.pi)))
        act[src] = (pre * cdf).astype(BF16)
        grad = cols_product(cots[src], down[...]) * slope
        low = grad.astype(BF16)
        gpre[src] = low
        up_sum[...] += jnp.sum(low.astype(F32), 0, keepdims=True)
        part_h[src] = cols_product(low, up[...]).astype(BF16)

        @pl.when(k == 1)
        def _():
            sum_h.x_ready()

        @pl.when(k == 2)
        def _():
            sum_h.far_ready()

        @pl.when(k == 3)
        def _():
            sum_h.y_ready()

        part_o[src] = nn(act[src], down[...]).astype(BF16)
        return carry

    lax.fori_loop(0, CHIPS, block, 0)
    sum_h.relay()

    def stack(ref):
        return ref[...].reshape(CHIPS * ROWS, ref.shape[-1])

    full_up[...] = rows_product(stack(hid), stack(gpre)).astype(BF16)
    full_down[...] = rows_product(stack(act), stack(cots)).astype(BF16)
    swaps = []
    for i in range(4):
        swaps.append(
            remote(
                full_up.at[rows16(i * 272 + (1 - p) * TILE, 144)], land_up.at[i],
                g_send.at[0, i], g_recv.at[0, i], e.twin(),
            )
        )
        swaps.append(
            remote(
                full_down.at[rows16(256 * i + (1 - p) * TILE, TILE)], land_down.at[i],
                g_send.at[1, i], g_recv.at[1, i], e.twin(),
            )
        )
    swaps.append(
        remote(
            full_down.at[rows16(1024 + (1 - p) * 32, 32)], land_more, g_send.at[2, 0], g_recv.at[2, 0], e.twin()
        )
    )
    for copy in swaps:
        copy.start()

    total = part_h[t].astype(F32) + sum_h.total()
    top = cots[t].astype(F32)
    grad_middle = top + norm_back(total, normed, inverse, vecs[GAIN_2 : GAIN_2 + 1])
    grad_mid[...] = grad_middle
    low = grad_middle.astype(BF16)
    gmid[t] = low
    spread = Gather(e, gmid.at[t], lambda chip: gmid.at[chip], ROWS, HALF, a_send.at[1], a_recv.at[1])
    spread.start()
    sums[0:1] = jnp.sum(low.astype(F32), 0, keepdims=True)
    sums[1:2] = jnp.sum(top, 0, keepdims=True)
    sums[2:3] = jnp.sum(total * normed, 0, keepdims=True)
    sums[3:4] = jnp.sum(total, 0, keepdims=True)
    sums[4:8] = jnp.zeros((4, D), F32)

    for copy in swaps:
        copy.wait()
    more = (full_down[rows16(1024 + p * 32, 32)].astype(F32) + land_more[...].astype(F32)).astype(BF16)
    for i in range(4):
        own = full_up[rows16(i * 272 + p * TILE, 144)].astype(F32)
        g_feed[i, :144] = (own + land_up[i].astype(F32)).astype(BF16)
        own = full_down[rows16(256 * i + p * TILE, TILE)].astype(F32)
        g_feed[i, 144:272] = (own + land_down[i].astype(F32)).astype(BF16)
        g_feed[i, 272:] = more
    planes = ZScatter(e, g_feed, staged, z_right, z_left, z_send, z_recv)
    planes.begin()
    spread.forward()
    sum_o.far_ready()
    sum_o.x_ready()
    sum_o.y_ready()

    def heads(k, carry):
        src = e.flip((k + 1) // 2 % 2, k // 2)

        @pl.when(k == 1)
        def _():
            spread.have_x()

        @pl.when(k == 2)
        def _():
            spread.have_far()

        @pl.when(k == 3)
        def _():
            spread.have_y()

        gh_heads[src] = cols_product(gmid[src], out_w[...]).astype(BF16)
        return carry

    lax.fori_loop(0, CHIPS, heads, 0)
    planes.first()
    grad_out = rows_product(stack(mixed), stack(gmid)).astype(BF16)

    @pl.when(t == CHIPS - 1)
    def _():
        raw[...] = grad_out[: SLOTS * HEAD_DIM]

    @pl.when(t < CHIPS - 1)
    def _():
        for i in range(4):
            raw[i * 80 : i * 80 + HEAD_DIM] = grad_out[i * HEAD_DIM : (i + 1) * HEAD_DIM]
            raw[i * 80 + HEAD_DIM : (i + 1) * 80] = jnp.zeros((16, D), BF16)

    swaps = [
        remote(
            raw.at[rows16(i * 80 + (1 - p) * 32, 48)], land_out.at[i], g_send.at[3, i], g_recv.at[3, i], e.twin()
        )
        for i in range(4)
    ]
    for copy in swaps:
        copy.start()
    sum_o.relay()
    for copy in swaps:
        copy.wait()
    for i in range(4):
        own = raw[rows16(i * 80 + p * 32, 48)].astype(F32)
        g_out[i] = (own + land_out[i].astype(F32)).astype(BF16)
    planes.second()
    result = middle[...] + vecs[B_DOWN : B_DOWN + 1] + part_o[t].astype(F32)
    output[...] = (result + sum_o.total()).astype(BF16)
    planes.last(share)
    for user in (hidden, spread, sum_h, sum_o):
        user.sent()


def feed(middle, cots, halves, vecs, out_w, mixed):
    blocks = pltpu.VMEM((CHIPS, ROWS, D), BF16)
    lands = pltpu.VMEM((6, HALF, D), BF16)
    matrix = pltpu.VMEM((D, D), BF16)
    return pl.pallas_call(
        feed_kernel,
        out_shape=(
            jax.ShapeDtypeStruct((ROWS, D), BF16),
            jax.ShapeDtypeStruct((ROWS, D), F32),
            jax.ShapeDtypeStruct((CHIPS, ROWS, WIDE), BF16),
            jax.ShapeDtypeStruct((4, 48, D), BF16),
            jax.ShapeDtypeStruct((FEED_ROWS, D), BF16),
            jax.ShapeDtypeStruct((8, D), F32),
            jax.ShapeDtypeStruct((1, D), F32),
        ),
        in_specs=vmem(6),
        out_specs=tuple(vmem(7)),
        scratch_shapes=[matrix, matrix]
        + [blocks] * 6
        + [lands, lands, matrix, matrix]
        + [
            pltpu.VMEM((4, 144, D), BF16),
            pltpu.VMEM((4, TILE, D), BF16),
            pltpu.VMEM((32, D), BF16),
            pltpu.VMEM((4, FEED_ROWS, D), BF16),
            pltpu.VMEM((4, FEED_ROWS, D), BF16),
            pltpu.VMEM((3, FEED_ROWS, D), BF16),
            pltpu.VMEM((3, FEED_ROWS, D), BF16),
            pltpu.VMEM((SLOTS * HEAD_DIM, D), BF16),
            pltpu.VMEM((4, 48, D), BF16),
            dma(2, 6), dma(2, 6), dma(2, 6), dma(2, 6), dma(4), dma(4), dma(4),
            dma(5), dma(5), dma(5), dma(4, 4), dma(4, 4), dma(2, 3), dma(2, 3),
        ],
        compiler_params=params(3, 63),
        name="feed",
    )(middle, cots, halves, vecs, out_w, mixed)


def back_kernel(
    x, grad_mid, dq, dk, dv, hid, whole, vecs, share, g_out, sums, up_sum,
    grad_x, up_out, down_out, qkv_out, o_out, totals,
    joint, full, land, land_k, land_v, part, sum_land, g_qkv, z_right, z_left, s_qkv,
    s_out, zo_right, zo_left, own_qkv, own_out, all_feed, all_qkv, all_out, local, vec_land,
    kv_send, kv_recv, g_send, g_recv, s_send, s_recv, a_send, a_recv, z_send, z_recv, t_send, t_recv, v_send, v_recv,
):
    e = Place()
    t, p, z = (e.t, e.p, e.z)
    e.greet()
    swaps = []
    for k in range(CHIPS):
        chip = e.flip(1 - k // 2, 1 - k % 2)
        for j, (ref, dst) in enumerate(((dk, land_k), (dv, land_v))):
            swaps.append(
                remote(ref.at[chip * 2 + 1 - p], dst.at[chip], kv_send.at[j, k], kv_recv.at[j, k], e.twin())
            )
    for copy in swaps:
        copy.start()

    def spread(number, own, everything, rows, cut):
        return Gather(
            e, own, lambda chip: everything.at[p, chip], rows, cut, a_send.at[number], a_recv.at[number]
        )

    def hand(number, own, everything, k):
        chip = e.flip(k % 2, k // 2)
        src = own if k == 0 else everything.at[p, chip]
        return remote(
            src, everything.at[p, chip], t_send.at[number, k], t_recv.at[number, k], e.twin()
        )

    def handed(number, own, everything):
        for k in range(CHIPS):
            chip = e.flip(k % 2, k // 2)
            copy = remote(
                own, everything.at[1 - p, chip], t_send.at[number, k], t_recv.at[number, k], e.twin()
            )
            copy.wait_recv()
            copy.wait_send()

    feeds = spread(0, share, all_feed, FEED_ROWS, 144)
    feeds.start()
    outs = ZScatter(e, g_out, s_out, zo_right, zo_left, z_send.at[0], z_recv.at[0])
    outs.begin()
    normed, inverse = normalize(x[...].astype(F32))
    local[...] = jnp.zeros_like(local)
    head_q, head_v = (jnp.zeros((1, WIDE), F32), jnp.zeros((1, WIDE), F32))
    for copy in swaps:
        copy.wait()
    hand(0, share, all_feed, 0).start()
    all_feed[p, t] = share[...]
    for k in range(CHIPS):
        mine = k * 2 + p
        joint[k, :, :WIDE] = dq[k]
        joint[k, :, WIDE : 2 * WIDE] = (dk[mine].astype(F32) + land_k[k].astype(F32)).astype(BF16)
        low_v = (dv[mine].astype(F32) + land_v[k].astype(F32)).astype(BF16)
        joint[k, :, 2 * WIDE :] = low_v
        head_q = head_q + jnp.sum(dq[k].astype(F32), 0, keepdims=True)
        head_v = head_v + jnp.sum(low_v.astype(F32), 0, keepdims=True)
    outs.first()

    def stack(ref):
        return ref[...].reshape(CHIPS * ROWS, ref.shape[-1])

    full[...] = rows_product(stack(hid), stack(joint)).astype(BF16)
    swaps = [
        remote(
            full.at[rows16(i * 272 + (1 - p) * TILE, 144)], land.at[i], g_send.at[i], g_recv.at[i], e.twin()
        )
        for i in range(4)
    ]
    for copy in swaps:
        copy.start()
    feeds.forward()
    outs.second()
    summed = Scatter(e, part, sum_land, s_send, s_recv)

    def block(k, carry):
        dest = e.flip(1 - k // 2, 1 - k % 2)
        part[dest] = cols_product(joint[dest], whole[...]).astype(BF16)

        @pl.when(k == 0)
        def _():
            summed.far_ready()

        @pl.when(k == 1)
        def _():
            summed.x_ready()

        @pl.when(k == 2)
        def _():
            summed.y_ready()

        return carry

    lax.fori_loop(0, 1, block, 0)
    for copy in swaps:
        copy.wait()
    for i in range(4):
        own = full[rows16(i * 272 + p * TILE, 144)].astype(F32)
        g_qkv[i] = (own + land[i].astype(F32)).astype(BF16)
    weights = ZScatter(e, g_qkv, s_qkv, z_right, z_left, z_send.at[1], z_recv.at[1])
    weights.begin()
    lax.fori_loop(1, CHIPS - 1, block, 0)
    outs.last(own_out)
    rows = cols_product(joint[t], whole[...])
    weights.first()
    feeds.have_x()
    feeds.have_y()
    hand(0, share, all_feed, 1).start()
    hand(0, share, all_feed, 2).start()
    feeds.have_far()
    hand(0, share, all_feed, 3).start()
    others = spread(1, own_out, all_out, 48, 32)
    others.start()
    all_out[p, t] = own_out[...]
    hand(1, own_out, all_out, 0).start()
    summed.relay()
    weights.second()
    total = rows + summed.total()
    grad_x[...] = grad_mid[...] + norm_back(total, normed, inverse, vecs[GAIN_1 : GAIN_1 + 1])
    local[:4] = sums[:4]
    local[4:5] = jnp.sum(total * normed, 0, keepdims=True)
    local[5:6] = jnp.sum(total, 0, keepdims=True)
    local[pl.ds(8 + t, 1), :] = up_sum[...]
    local[pl.ds(12 + t, 1), :WIDE] = head_q
    local[pl.ds(12 + t, 1), WIDE : 2 * WIDE] = head_v
    twin = remote(local, vec_land.at[0], v_send.at[0], v_recv.at[0], e.twin())
    twin.start()
    others.forward()
    others.have_x()
    others.have_y()
    hand(1, own_out, all_out, 1).start()
    hand(1, own_out, all_out, 2).start()
    others.have_far()
    hand(1, own_out, all_out, 3).start()
    twin.wait()
    totals[...] = local[...] + vec_land[0]
    planes = [
        remote(totals, vec_land.at[k], v_send.at[k], v_recv.at[k], e.plane(k)) for k in range(1, 4)
    ]
    for copy in planes:
        copy.start()
    weights.last(own_qkv)
    qkvs = spread(2, own_qkv, all_qkv, 144, 80)
    qkvs.start()
    hand(2, own_qkv, all_qkv, 0).start()
    all_qkv[p, t] = own_qkv[...]
    for copy in planes:
        copy.wait()
    local[...] = totals[...] + vec_land[1] + vec_land[2] + vec_land[3]
    chips = [
        remote(local, vec_land.at[3 + k], v_send.at[3 + k], v_recv.at[3 + k], e.chip(chip))
        for k, chip in ((1, e.tx), (2, e.ty), (3, e.td))
    ]
    for copy in chips:
        copy.start()

    handed(0, share, all_feed)
    for s in range(CHIPS):
        for q in range(2):
            rows = slice(q * TILE, q * TILE + 144)
            for i in range(4):
                column = D * i + HEAD_DIM * (i % 2) + 256 * s
                up_out[rows, column : column + 256] = all_feed[q, s, :144, 256 * i : 256 * (i + 1)].astype(F32)
            down_out[rows16(z % 2 * 64 + 256 * s + TILE * q, TILE)] = all_feed[q, s, 144:272].astype(F32)
    for q in range(2):
        rows = slice(q * TILE, q * TILE + 144)
        for s in range(0, CHIPS, 2):
            pair = [all_feed[q, s + i, :144, 1024:].astype(F32) for i in range(2)]
            column = D * s + 1024
            up_out[rows, column : column + TILE] = jnp.concatenate(pair, 1)
        down_out[rows16((1 - z % 2) * 1024 + 32 * q, 32)] = all_feed[q, z, 272:].astype(F32)

    handed(1, own_out, all_out)
    ahead = (CHIPS - z) % CHIPS * 16
    for s in range(CHIPS - 1):
        o_out[rows16(ahead + HEAD_DIM * s, 48)] = all_out[0, s].astype(F32)
        o_out[rows16(ahead + HEAD_DIM * s + 32, 32)] = all_out[1, s, :32].astype(F32)
    for u in range(SLOTS):
        q, first = ((0, 16 * u) if u < 3 else (1, 16 * u - 32))
        strip = all_out[q, CHIPS - 1, first : first + 16].astype(F32)

        @pl.when(16 * u < ahead)
        def _():
            o_out[16 * u : 16 * u + 16] = strip

        @pl.when(16 * u >= ahead)
        def _():
            o_out[192 + 16 * u : 208 + 16 * u] = strip

    qkvs.forward()
    qkvs.have_x()
    qkvs.have_y()
    hand(2, own_qkv, all_qkv, 1).start()
    hand(2, own_qkv, all_qkv, 2).start()
    qkvs.have_far()
    hand(2, own_qkv, all_qkv, 3).start()
    for copy in chips:
        copy.wait()
    totals[...] = local[...] + vec_land[4] + vec_land[5] + vec_land[6]
    handed(2, own_qkv, all_qkv)
    source = {}
    for s, heads in enumerate(HEAD_TABLE):
        for slot, head in enumerate(heads):
            if head >= 0:
                for a in range(3):
                    source[a * HEADS + head] = (s, a * WIDE + slot * HEAD_DIM)
    for q in range(2):
        rows = slice(q * TILE, q * TILE + 144)

        def piece(g, side):
            s, column = source[g]
            tile = all_qkv[q, s, :, column // TILE * TILE : column // TILE * TILE + TILE].astype(F32)
            return tile if column % TILE // HEAD_DIM == side else pltpu.roll(tile, HEAD_DIM, 1)

        left = lax.broadcasted_iota(jnp.int32, (144, TILE), 1) < HEAD_DIM
        for g in range(0, 3 * HEADS - 1, 2):
            column = g * HEAD_DIM
            qkv_out[rows, column : column + TILE] = jnp.where(left, piece(g, 0), piece(g + 1, 1))
        column = (3 * HEADS - 1) * HEAD_DIM
        qkv_out[rows, column : column + HEAD_DIM] = piece(3 * HEADS - 1, 0)[:, :HEAD_DIM]
    for user in (feeds, others, qkvs, summed):
        user.sent()


def back(x, grad_mid, dq, dk, dv, hid, whole, vecs, share, g_out, sums, up_sum):
    heads = pltpu.VMEM((CHIPS, ROWS, WIDE), BF16)
    qkv, out = ((144, 3 * WIDE), (48, D))

    def many(count, shape):
        return pltpu.VMEM((count, *shape), BF16)

    return pl.pallas_call(
        back_kernel,
        out_shape=(
            jax.ShapeDtypeStruct((ROWS, D), F32),
            jax.ShapeDtypeStruct((D // 4, 4 * D), F32),
            jax.ShapeDtypeStruct((D, D), F32),
            jax.ShapeDtypeStruct((D // 4, 3 * D), F32),
            jax.ShapeDtypeStruct((D // 4, D), F32),
            jax.ShapeDtypeStruct((16, D), F32),
        ),
        in_specs=vmem(12),
        out_specs=tuple(vmem(6)),
        scratch_shapes=[
            pltpu.VMEM((CHIPS, ROWS, 3 * WIDE), BF16),
            pltpu.VMEM((D, 3 * WIDE), BF16),
            many(4, qkv),
            heads, heads,
            pltpu.VMEM((CHIPS, ROWS, D), BF16),
            pltpu.VMEM((6, HALF, D), BF16),
            many(4, qkv), many(3, qkv), many(3, qkv), many(4, qkv),
            many(4, out), many(3, out), many(3, out),
            pltpu.VMEM(qkv, BF16), pltpu.VMEM(out, BF16),
            pltpu.VMEM((2, CHIPS, FEED_ROWS, D), BF16),
            pltpu.VMEM((2, CHIPS, *qkv), BF16),
            pltpu.VMEM((2, CHIPS, *out), BF16),
            pltpu.VMEM((16, D), F32),
            pltpu.VMEM((7, 16, D), F32),
            dma(2, CHIPS), dma(2, CHIPS), dma(4), dma(4), dma(6), dma(6), dma(3, 6), dma(3, 6),
            dma(2, 2, 3), dma(2, 2, 3), dma(3, 4), dma(3, 4), dma(7), dma(7),
        ],
        compiler_params=params(4, 63),
        name="back",
    )(x, grad_mid, dq, dk, dv, hid, whole, vecs, share, g_out, sums, up_sum)


def plane_device(
    tokens, seq_lengths, cotangent, ln1_gain, ln1_bias, w_qkv, b_query, b_value, w_out, b_out,
    ln2_gain, ln2_bias, w_up, b_up, w_down, b_down,
):
    c = lax.axis_index("ctx")
    z = lax.axis_index("wsh")
    t, p = (c // 2, c % 2)
    x, cot, lengths = (tokens[0], cotangent[0], seq_lengths[0])
    parity = p[None].astype(jnp.int32)
    shard = D // 4
    integers = functools.partial(jnp.arange, dtype=jnp.int32)

    def columns_of(heads):
        heads = jnp.concatenate([heads, jnp.full((1,), -40, jnp.int32)])
        columns = jnp.repeat(heads, HEAD_DIM) * HEAD_DIM + integers(WIDE) % HEAD_DIM
        return (integers(D)[:, None] == columns[None, :]).astype(BF16)

    table = jnp.asarray(HEAD_TABLE, jnp.int32)
    select = columns_of(lax.dynamic_index_in_dim(table, t, 0, keepdims=False))

    more = 1024 * (1 - z % 2)
    biases = jnp.stack([b_query, b_value, b_out, b_down, ln1_gain, ln1_bias, ln2_gain, ln2_bias])
    vec_in = lax.dynamic_update_slice(jnp.zeros((16, D), BF16), biases, (jnp.int32(0), z * shard))
    first = lax.dynamic_slice_in_dim(b_up, 64 * (z % 2) + 256 * t, 256)
    vec_in = lax.dynamic_update_slice(vec_in, first[None], (jnp.int32(B_UP), 256 * z))
    last = jnp.where(z == t, lax.dynamic_slice_in_dim(b_up, more, 64), jnp.zeros((64,), BF16))
    vec_in = lax.dynamic_update_slice(vec_in, last[None], (jnp.int32(B_UP), jnp.int32(1024)))

    qkv_rows = lax.dynamic_slice_in_dim(w_qkv, p * 128, 144, 0)
    qkv_half = jnp.concatenate(
        [
            jnp.dot(qkv_rows[:, i * D : (i + 1) * D], select, preferred_element_type=F32)
            for i in range(3)
        ],
        axis=1,
    ).astype(BF16)

    ahead = (CHIPS - z) % CHIPS * 16
    i = p * 32 + integers(48)
    early = jnp.where(i < HEAD_DIM, ahead + HEAD_DIM * t + i, -1)
    late = jnp.where(i < ahead, i, 192 + i)
    taken = jnp.where(t < CHIPS - 1, early, late)
    pick = (taken[:, None] == integers(shard)[None, :]).astype(BF16)
    out_half = jnp.dot(pick, w_out, preferred_element_type=F32).astype(BF16)

    q, k, v, hid, cots, whole, out_w, vecs = project(x, cot, qkv_half, out_half, vec_in, select)

    up_rows = lax.dynamic_slice_in_dim(w_up, p * 128, 144, 0)
    up_half = jnp.concatenate(
        [
            lax.dynamic_slice_in_dim(up_rows, i * D + 64 * (i % 2) + t * 256, 256, 1)
            for i in range(4)
        ]
        + [lax.dynamic_slice_in_dim(up_rows, D * t + 1024 * (1 - t % 2), 64, 1)],
        axis=1,
    )
    down_half = lax.dynamic_slice_in_dim(w_down, 64 * (z % 2) + 256 * t + p * 128, 128, 0)
    down_more = lax.dynamic_slice_in_dim(w_down, more + p * 32, 32, 0)
    halves = jnp.concatenate([up_half, down_half, down_more])
    halves, q = lax.optimization_barrier((halves, q))
    halves = lax.all_gather(halves, "wsh", axis=0)

    mixed, lse = attend(lengths, parity, q, k, v)
    middle = out_project(x, mixed, out_w, vecs)
    output, grad_mid, grad_heads, g_out, share, sums, up_sum = feed(
        middle, cots, halves, vecs, out_w, mixed
    )
    dq, dk, dv = attend_back(lengths, parity, q, k, v, mixed, grad_heads, lse)
    grad_x, grad_up, grad_down, grad_qkv, grad_out, totals = back(
        x, grad_mid, dq, dk, dv, hid, whole, vecs, share, g_out, sums, up_sum
    )

    place = {}
    for s, heads in enumerate(HEAD_TABLE):
        for slot, head in enumerate(heads):
            place[head] = (12 + s, slot * HEAD_DIM)

    def head_vector(first):
        pieces = []
        for head in range(HEADS):
            row, column = place[head]
            pieces.append(totals[row, first + column : first + column + HEAD_DIM])
        return jnp.concatenate(pieces)

    vectors = jnp.stack([*(totals[i] for i in range(6)), head_vector(0), head_vector(WIDE)])
    mine = lax.dynamic_slice_in_dim(vectors, z * shard, shard, 1)
    ups = lax.dynamic_slice_in_dim(totals[8:12], z * 256, 256, 1).reshape(D - 64)
    extra = lax.dynamic_index_in_dim(totals[8:12, 1024:], z, 0, keepdims=False)
    grad_b_up = jnp.where(
        z % 2 == 0, jnp.concatenate([ups, extra]), jnp.concatenate([extra, ups])
    )
    return (
        output[None], grad_x[None],
        mine[4], mine[5], grad_qkv, mine[6], mine[7], grad_out, mine[0],
        mine[2], mine[3], grad_up, grad_b_up, grad_down, mine[1],
    )


def solution(mesh):
    in_specs = (
        P("wsh", "ctx", None),
        P("wsh", None),
        P("wsh", "ctx", None),
        P("wsh"),
        P("wsh"),
        P("wsh", None),
        P("wsh"),
        P("wsh"),
        P("wsh", None),
        P("wsh"),
        P("wsh"),
        P("wsh"),
        P("wsh", None),
        P("wsh"),
        P("wsh", None),
        P("wsh"),
    )
    out_specs = (
        P("wsh", "ctx", None),
        P("wsh", "ctx", None),
        P("wsh"),
        P("wsh"),
        P("wsh", None),
        P("wsh"),
        P("wsh"),
        P("wsh", None),
        P("wsh"),
        P("wsh"),
        P("wsh"),
        P("wsh", None),
        P("wsh"),
        P("wsh", None),
        P("wsh"),
    )
    sizes = (mesh.shape["ctx"], mesh.shape["wsh"])
    body = plane_device if sizes == (2 * CHIPS, 4) else on_device
    return jax.shard_map(
        body, mesh=mesh, in_specs=in_specs, out_specs=out_specs, check_vma=False
    )
```

```python
import functools
import math

import jax
import jax.numpy as jnp
from jax import lax
from jax.experimental import pallas as pl
from jax.experimental.pallas import tpu as pltpu
from jax.sharding import PartitionSpec as P

D = 1088
HEADS = 17
HEAD_DIM = 64


def normalize(inputs):
    center = inputs - jnp.mean(inputs, -1, keepdims=True)
    inverse = lax.rsqrt(jnp.mean(center * center, -1, keepdims=True) + 1e-05)
    return (center * inverse, inverse)


def norm_back(grad_in, normed, inverse, gain):
    scaled = grad_in * gain
    return inverse * (
        scaled
        - jnp.mean(scaled, -1, keepdims=True)
        - normed * jnp.mean(scaled * normed, -1, keepdims=True)
    )


def rows_product(left, right):
    return lax.dot_general(
        left, right, (((0,), (0,)), ((), ())), preferred_element_type=jnp.float32
    )


def cols_product(left, right):
    return lax.dot_general(
        left, right, (((1,), (1,)), ((), ())), preferred_element_type=jnp.float32
    )


def sequence_ids(lengths, positions):
    bounds = jnp.cumsum(lengths)
    return jnp.sum((positions[:, None] >= bounds[None, :]).astype(jnp.int32), axis=1)


def allowed_pairs(lengths, query_pos, key_pos):
    query_owner = sequence_ids(lengths, query_pos)
    key_owner = sequence_ids(lengths, key_pos)
    return (key_pos[None, :] <= query_pos[:, None]) & (
        (key_owner[None, :] == 0) | (key_owner[None, :] == query_owner[:, None])
    )


def over_blocks(state_in, arrays, step_fn):
    total_rows = arrays[0].shape[0]
    block_rows = math.gcd(total_rows, 512)

    def advance(block_index, state_now):
        offset = block_index * block_rows
        pieces = tuple((lax.dynamic_slice_in_dim(array, offset, block_rows, 0) for array in arrays))
        return step_fn(state_now, pieces, offset)

    return lax.fori_loop(0, total_rows // block_rows, advance, state_in)


def sectioned_sum(partials):
    shares = lax.psum_scatter(partials, "wsh", scatter_dimension=0, tiled=True)
    return lax.psum(shares, "ctx")


def on_device(
    tokens,
    seq_lengths,
    cotangent,
    ln1_gain,
    ln1_bias,
    w_qkv,
    b_query,
    b_value,
    w_out,
    b_out,
    ln2_gain,
    ln2_bias,
    w_up,
    b_up,
    w_down,
    b_down,
):
    token_rows, grad_rows = (tokens[0], cotangent[0])
    shards = (
        w_qkv,
        w_out,
        w_up,
        w_down,
        b_query,
        b_value,
        b_out,
        b_up,
        b_down,
        ln1_gain,
        ln1_bias,
        ln2_gain,
        ln2_bias,
    )
    gathered = (
        lax.all_gather(shards[0], "wsh", axis=0, tiled=True),
        lax.all_gather(shards[1], "wsh", axis=0, tiled=True),
        lax.all_gather(shards[2], "wsh", axis=0, tiled=True),
        lax.all_gather(shards[3], "wsh", axis=0, tiled=True),
        lax.all_gather(shards[4], "wsh", axis=0, tiled=True),
        lax.all_gather(shards[5], "wsh", axis=0, tiled=True),
        lax.all_gather(shards[6], "wsh", axis=0, tiled=True),
        lax.all_gather(shards[7], "wsh", axis=0, tiled=True),
        lax.all_gather(shards[8], "wsh", axis=0, tiled=True),
        lax.all_gather(shards[9], "wsh", axis=0, tiled=True),
        lax.all_gather(shards[10], "wsh", axis=0, tiled=True),
        lax.all_gather(shards[11], "wsh", axis=0, tiled=True),
        lax.all_gather(shards[12], "wsh", axis=0, tiled=True),
    )
    qkv_full, out_full, up_full, down_full = (gathered[0], gathered[1], gathered[2], gathered[3])
    query_bias, value_bias, out_bias, up_bias, down_bias = [
        piece.astype(jnp.float32) for piece in gathered[4:9]
    ]
    gain_one, shift_one, gain_two, shift_two = [
        piece.astype(jnp.float32) for piece in gathered[9:13]
    ]
    lengths = seq_lengths[0]
    tok_rows = token_rows.shape[0]
    my_pos = lax.axis_index("ctx") * tok_rows + jnp.arange(tok_rows, dtype=jnp.int32)
    scale_qk = HEAD_DIM ** (-0.5)
    inputs = token_rows.astype(jnp.float32)
    normed_one, inverse_one = normalize(inputs)
    hidden_one = (normed_one * gain_one + shift_one).astype(jnp.bfloat16)
    joint_proj = jnp.dot(hidden_one, qkv_full, preferred_element_type=jnp.float32)
    queries = (joint_proj[:, :D] + query_bias).astype(jnp.bfloat16)
    key_rows = joint_proj[:, D : 2 * D].astype(jnp.bfloat16)
    value_rows = (joint_proj[:, 2 * D :] + value_bias).astype(jnp.bfloat16)
    query_heads = queries.reshape(tok_rows, HEADS, HEAD_DIM)
    my_key_heads = key_rows.reshape(tok_rows, HEADS, HEAD_DIM)
    my_value_heads = value_rows.reshape(tok_rows, HEADS, HEAD_DIM)

    def forward_step(state_now, pieces, first_row):
        key_heads = pieces[0].reshape(-1, HEADS, HEAD_DIM)
        value_heads = pieces[1].reshape(-1, HEADS, HEAD_DIM)
        key_pos = first_row + jnp.arange(key_heads.shape[0], dtype=jnp.int32)
        allowed = allowed_pairs(lengths, my_pos, key_pos)

        def forward_compute(inner):
            peak_old, total_old, accum_old = inner
            scores = (
                jnp.einsum(
                    "qhd,khd->hqk", query_heads, key_heads, preferred_element_type=jnp.float32
                )
                * scale_qk
            )
            scores = jnp.where(allowed[None], scores, -1e30)
            peak_new = jnp.maximum(peak_old, jnp.max(scores, -1))
            factor = jnp.exp(peak_old - peak_new)
            expos = jnp.where(allowed[None], jnp.exp(scores - peak_new[:, :, None]), 0.0)
            total_new = total_old * factor + jnp.sum(expos, -1)
            accum_new = accum_old * factor.T[:, :, None] + jnp.einsum(
                "hqk,khd->qhd",
                expos.astype(jnp.bfloat16),
                value_heads,
                preferred_element_type=jnp.float32,
            )
            return (peak_new, total_new, accum_new)

        return lax.cond(jnp.any(allowed), forward_compute, lambda inner: inner, state_now)

    start_state = (
        jnp.full((HEADS, tok_rows), -1e30, jnp.float32),
        jnp.zeros((HEADS, tok_rows), jnp.float32),
        jnp.zeros((tok_rows, HEADS, HEAD_DIM), jnp.float32),
    )
    peak, total, accum = over_blocks(
        start_state,
        (
            lax.all_gather(key_rows, "ctx", axis=0, tiled=True),
            lax.all_gather(value_rows, "ctx", axis=0, tiled=True),
        ),
        forward_step,
    )
    mixed = accum / total.T[:, :, None]
    log_sum = (peak + jnp.log(total)).T
    mixed_low = mixed.reshape(tok_rows, D).astype(jnp.bfloat16)
    middle = inputs + jnp.dot(mixed_low, out_full, preferred_element_type=jnp.float32) + out_bias
    normed_two, inverse_two = normalize(middle)
    hidden_two = (normed_two * gain_two + shift_two).astype(jnp.bfloat16)
    pre_act = jnp.dot(hidden_two, up_full, preferred_element_type=jnp.float32) + up_bias
    activ_low = jax.nn.gelu(pre_act, approximate=False).astype(jnp.bfloat16)
    result = middle + jnp.dot(activ_low, down_full, preferred_element_type=jnp.float32) + down_bias
    output_rows = result.astype(jnp.bfloat16)
    grad_top_f = grad_rows.astype(jnp.float32)
    grad_down = rows_product(activ_low, grad_rows)
    grad_down_bias = jnp.sum(grad_top_f, 0)
    grad_act = cols_product(grad_rows, down_full)
    cdf_part = 0.5 * (1.0 + lax.erf(pre_act * math.sqrt(0.5)))
    pdf_part = jnp.exp(-0.5 * pre_act * pre_act) / math.sqrt(2.0 * math.pi)
    grad_pre = (grad_act * (cdf_part + pre_act * pdf_part)).astype(jnp.bfloat16)
    grad_up = rows_product(hidden_two, grad_pre)
    grad_up_bias = jnp.sum(grad_pre.astype(jnp.float32), 0)
    grad_h2 = cols_product(grad_pre, up_full)
    grad_gain_two = jnp.sum(grad_h2 * normed_two, 0)
    grad_shift_two = jnp.sum(grad_h2, 0)
    grad_mid = grad_top_f + norm_back(grad_h2, normed_two, inverse_two, gain_two)
    grad_mid_low = grad_mid.astype(jnp.bfloat16)
    grad_out_w = rows_product(mixed_low, grad_mid_low)
    grad_out_bias = jnp.sum(grad_mid_low.astype(jnp.float32), 0)
    grad_mixed = cols_product(grad_mid_low, out_full).astype(jnp.bfloat16)
    grad_heads = grad_mixed.reshape(tok_rows, HEADS, HEAD_DIM)
    delta = jnp.sum(grad_heads.astype(jnp.float32) * mixed, -1)
    lse_all, delta_all = (
        lax.all_gather(log_sum, "ctx", axis=0, tiled=True),
        lax.all_gather(delta, "ctx", axis=0, tiled=True),
    )

    def query_step(state_now, pieces, first_row):
        key_heads = pieces[0].reshape(-1, HEADS, HEAD_DIM)
        value_heads = pieces[1].reshape(-1, HEADS, HEAD_DIM)
        key_pos = first_row + jnp.arange(key_heads.shape[0], dtype=jnp.int32)
        allowed = allowed_pairs(lengths, my_pos, key_pos)

        def query_compute(accum_old):
            scores = (
                jnp.einsum(
                    "qhd,khd->hqk", query_heads, key_heads, preferred_element_type=jnp.float32
                )
                * scale_qk
            )
            probs = jnp.where(allowed[None], jnp.exp(scores - log_sum.T[:, :, None]), 0.0)
            grad_probs = jnp.einsum(
                "qhd,khd->hqk", grad_heads, value_heads, preferred_element_type=jnp.float32
            )
            grad_scores = (probs * (grad_probs - delta.T[:, :, None])).astype(jnp.bfloat16)
            return accum_old + jnp.einsum(
                "hqk,khd->qhd", grad_scores, key_heads, preferred_element_type=jnp.float32
            )

        return lax.cond(jnp.any(allowed), query_compute, lambda inner: inner, state_now)

    zero_heads = jnp.zeros((tok_rows, HEADS, HEAD_DIM), jnp.float32)
    grad_query = over_blocks(
        zero_heads,
        (
            lax.all_gather(key_rows, "ctx", axis=0, tiled=True),
            lax.all_gather(value_rows, "ctx", axis=0, tiled=True),
        ),
        query_step,
    )

    def key_step(state_now, pieces, first_row):
        other_queries = pieces[0].reshape(-1, HEADS, HEAD_DIM)
        other_grads = pieces[1].reshape(-1, HEADS, HEAD_DIM)
        other_count = other_queries.shape[0]
        other_pos = first_row + jnp.arange(other_count, dtype=jnp.int32)
        other_lse = lax.dynamic_slice_in_dim(lse_all, first_row, other_count, 0)
        other_delta = lax.dynamic_slice_in_dim(delta_all, first_row, other_count, 0)
        allowed = allowed_pairs(lengths, other_pos, my_pos)

        def key_compute(inner):
            grad_key_old, grad_value_old = inner
            scores = (
                jnp.einsum(
                    "qhd,khd->hqk", other_queries, my_key_heads, preferred_element_type=jnp.float32
                )
                * scale_qk
            )
            probs = jnp.where(allowed[None], jnp.exp(scores - other_lse.T[:, :, None]), 0.0)
            grad_value_new = grad_value_old + jnp.einsum(
                "hqk,qhd->khd",
                probs.astype(jnp.bfloat16),
                other_grads,
                preferred_element_type=jnp.float32,
            )
            grad_probs = jnp.einsum(
                "qhd,khd->hqk", other_grads, my_value_heads, preferred_element_type=jnp.float32
            )
            grad_scores = (probs * (grad_probs - other_delta.T[:, :, None])).astype(jnp.bfloat16)
            grad_key_new = grad_key_old + jnp.einsum(
                "hqk,qhd->khd", grad_scores, other_queries, preferred_element_type=jnp.float32
            )
            return (grad_key_new, grad_value_new)

        return lax.cond(jnp.any(allowed), key_compute, lambda inner: inner, state_now)

    grad_key, grad_value = over_blocks(
        (zero_heads, zero_heads),
        (
            lax.all_gather(queries, "ctx", axis=0, tiled=True),
            lax.all_gather(grad_mixed, "ctx", axis=0, tiled=True),
        ),
        key_step,
    )
    grad_joint = jnp.concatenate(
        [
            (grad_query * scale_qk).reshape(tok_rows, D),
            (grad_key * scale_qk).reshape(tok_rows, D),
            grad_value.reshape(tok_rows, D),
        ],
        axis=1,
    ).astype(jnp.bfloat16)
    grad_qkv_w = rows_product(hidden_one, grad_joint)
    grad_joint_f = grad_joint.astype(jnp.float32)
    grad_query_bias = jnp.sum(grad_joint_f[:, :D], 0)
    grad_value_bias = jnp.sum(grad_joint_f[:, 2 * D :], 0)
    grad_h1 = cols_product(grad_joint, qkv_full)
    grad_gain_one = jnp.sum(grad_h1 * normed_one, 0)
    grad_shift_one = jnp.sum(grad_h1, 0)
    grad_input = grad_mid + norm_back(grad_h1, normed_one, inverse_one, gain_one)
    matrices = (grad_qkv_w, grad_out_w, grad_up, grad_down)
    vectors = (
        grad_query_bias,
        grad_value_bias,
        grad_out_bias,
        grad_up_bias,
        grad_down_bias,
        grad_gain_one,
        grad_shift_one,
        grad_gain_two,
        grad_shift_two,
    )
    totals = sectioned_sum(matrices + vectors)
    return (
        output_rows[None],
        grad_input[None],
        totals[9],
        totals[10],
        totals[0],
        totals[4],
        totals[5],
        totals[1],
        totals[6],
        totals[11],
        totals[12],
        totals[2],
        totals[7],
        totals[3],
        totals[8],
    )


SLOTS = 5
WIDE = 384
ROWS = 256
HALF = ROWS // 2
CHIPS = 4
TILE = 128
UP_ROWS, DOWN_ROWS = (144, 160)
MESH_ID = pl.DeviceIdType.MESH
F32, BF16 = (jnp.float32, jnp.bfloat16)
NEG = -1e30
HEAD_TABLE = ((0, 5, 9, 13, -40), (1, 6, 10, 14, -40), (2, 7, 11, 15, -40), (3, 4, 8, 12, 16))
B_QUERY, B_VALUE, B_OUT, B_DOWN, GAIN_1, SHIFT_1, GAIN_2, SHIFT_2, B_UP = range(9)


def nn(left, right):
    return jnp.dot(left, right, preferred_element_type=F32)


def remote(src, dst, send, recv, where):
    return pltpu.make_async_remote_copy(
        src_ref=src, dst_ref=dst, send_sem=send, recv_sem=recv, device_id=where, device_id_type=MESH_ID
    )


def rows16(start, size):
    return pl.ds(pl.multiple_of(start, 16), size)


class Place:
    def __init__(self):
        self.c, self.z = (lax.axis_index("ctx"), lax.axis_index("wsh"))
        self.t, self.p = (self.c // 2, self.c % 2)
        self.tx, self.ty, self.td = (self.flip(1, 0), self.flip(0, 1), self.flip(1, 1))

    def flip(self, dx, dy):
        return (self.t // 2 + dy) % 2 * 2 + (self.t % 2 + dx) % 2

    def chip(self, chip):
        return (chip * 2 + self.p, self.z)

    def twin(self):
        return (self.t * 2 + 1 - self.p, self.z)

    def plane(self, step):
        return (self.c, (self.z + step) % 4)

    def greet(self, planes=True):
        barrier = pltpu.get_barrier_semaphore()
        others = [self.chip(self.tx), self.chip(self.ty), self.twin()]
        if planes:
            others += [self.plane(1), self.plane(2), self.plane(3)]
        for where in others:
            pl.semaphore_signal(barrier, inc=1, device_id=where, device_id_type=MESH_ID)
        pl.semaphore_wait(barrier, len(others))


class Gather:
    def __init__(self, e, own, view, rows, cut, send, recv):
        self.e, self.own, self.view, self.send, self.recv = (e, own, view, send, recv)
        self.parts = (pl.ds(0, cut), pl.ds(cut, rows - cut))

    def copy(self, i):
        e = self.e
        chip = (e.t, e.t, e.t, e.t, e.tx, e.ty)[i]
        part = self.parts[(0, 1, 1, 0, 0, 1)[i]]
        src = self.own if i < 4 else self.view(chip)
        where = e.chip((e.tx, e.tx, e.ty, e.ty, e.ty, e.tx)[i])
        return remote(src.at[part], self.view(chip).at[part], self.send.at[i], self.recv.at[i], where)

    def start(self):
        for i in (0, 2, 1, 3):
            self.copy(i).start()

    def forward(self):
        self.copy(0).wait_recv()
        self.copy(4).start()
        self.copy(2).wait_recv()
        self.copy(5).start()

    def have_x(self):
        self.copy(1).wait_recv()

    def have_y(self):
        self.copy(3).wait_recv()

    def have_far(self):
        self.copy(4).wait_recv()
        self.copy(5).wait_recv()

    def sent(self):
        for i in range(6):
            self.copy(i).wait_send()


class Scatter:
    def __init__(self, e, part, land, send, recv):
        self.e, self.part, self.land, self.send, self.recv = (e, part, land, send, recv)

    def copy(self, i):
        e = self.e
        chip = (e.td, e.td, e.tx, e.tx, e.ty, e.ty)[i]
        part = pl.ds((0, HALF, 0, HALF, HALF, 0)[i], HALF)
        where = e.chip((e.tx, e.ty, e.tx, e.tx, e.ty, e.ty)[i])
        return remote(
            self.part.at[chip, part], self.land.at[i], self.send.at[i], self.recv.at[i], where
        )

    def far_ready(self):
        self.copy(0).start()
        self.copy(1).start()

    def x_ready(self):
        self.copy(2).start()

    def y_ready(self):
        self.copy(4).start()

    def relay(self):
        self.copy(1).wait_recv()
        chip = self.e.tx
        self.part[chip, HALF:] = (self.part[chip, HALF:].astype(F32) + self.land[1].astype(F32)).astype(BF16)
        self.copy(3).start()
        self.copy(0).wait_recv()
        chip = self.e.ty
        self.part[chip, :HALF] = (self.part[chip, :HALF].astype(F32) + self.land[0].astype(F32)).astype(BF16)
        self.copy(5).start()

    def total(self):
        for i in (2, 4, 3, 5):
            self.copy(i).wait_recv()
        first = self.land[2].astype(F32) + self.land[5].astype(F32)
        second = self.land[4].astype(F32) + self.land[3].astype(F32)
        return jnp.concatenate([first, second], 0)

    def sent(self):
        for i in range(6):
            self.copy(i).wait_send()


class ZGather:
    def __init__(self, e, own, held, send, recv, put):
        self.e, self.own, self.held, self.send, self.recv, self.put = (e, own, held, send, recv, put)

    def copy(self, way, j):
        e = self.e
        shard = e.z - j if way == 0 else e.z + j
        src = self.own if j == 0 else self.held.at[shard]
        return remote(
            src, self.held.at[shard], self.send.at[way, j], self.recv.at[way, j], e.plane(1 if way == 0 else 3)
        )

    def sends(self, way, j):
        z = self.e.z
        return (z < 3) & (z >= j) if way == 0 else (z > 0) & (z <= 3 - j)

    def step(self, j):
        z = self.e.z
        for way in range(2):
            if j > 0:
                @pl.when(z >= j if way == 0 else z <= 3 - j)
                def _():
                    self.copy(way, j - 1).wait_recv()
            if j < 3:
                @pl.when(self.sends(way, j))
                def _():
                    self.copy(way, j).start()
            if j > 0:
                @pl.when(z >= j if way == 0 else z <= 3 - j)
                def _():
                    self.put(z - j if way == 0 else z + j)

    def sent(self):
        for way in range(2):
            for j in range(3):
                @pl.when(self.sends(way, j))
                def _():
                    self.copy(way, j).wait_send()


class ZScatter:
    def __init__(self, e, own, staged, right, left, send, recv):
        self.e, self.own, self.staged, self.land = (e, own, staged, (right, left))
        self.send, self.recv = (send, recv)

    def copy(self, way, j, src):
        return remote(
            src, self.land[way].at[j], self.send.at[way, j], self.recv.at[way, j],
            self.e.plane(1 if way == 0 else 3),
        )

    def begin(self):
        for plane, way in ((0, 0), (3, 1)):
            @pl.when(self.e.z == plane)
            def _():
                for j in range(3):
                    self.copy(way, j, self.own.at[3 - j if way == 0 else j]).start()

    def relay(self, way, j):
        dest = 3 - j if way == 0 else j
        self.copy(way, j, self.staged.at[dest]).wait_recv()
        self.staged[dest] = (self.own[dest].astype(F32) + self.land[way][j].astype(F32)).astype(BF16)
        self.copy(way, j, self.staged.at[dest]).start()

    def first(self):
        for plane, way in ((1, 0), (2, 1)):
            @pl.when(self.e.z == plane)
            def _():
                self.relay(way, 0)

    def second(self):
        for plane, way in ((1, 0), (2, 1)):
            @pl.when(self.e.z == plane)
            def _():
                self.relay(1 - way, 0)
                self.relay(way, 1)

    def last(self, out):
        right, left = self.land
        for z in range(4):
            @pl.when(self.e.z == z)
            def _():
                total = self.own[z].astype(F32)
                if z > 0:
                    self.copy(0, 3 - z, self.own.at[z]).wait_recv()
                    total = total + right[3 - z].astype(F32)
                if z < 3:
                    self.copy(1, z, self.own.at[z]).wait_recv()
                    total = total + left[z].astype(F32)
                out[...] = total.astype(BF16)
                for way in range(2):
                    for j in range((3 - z) if way == 0 else z):
                        self.copy(way, j, self.own.at[z]).wait_send()


def dma(*shape):
    return pltpu.SemaphoreType.DMA(shape)


def params(number, mib=56):
    return pltpu.CompilerParams(
        collective_id=number, has_side_effects=True, vmem_limit_bytes=mib * 2**20
    )


def vmem(count):
    return [pl.BlockSpec(memory_space=pltpu.VMEM)] * count


class Halves:
    def __init__(self, e, whole, block, keep, step, local, send, recv):
        self.e, self.whole, self.block, self.keep, self.step = (e, whole, block, keep, step)
        self.local, self.send, self.recv = (local, send, recv)

    def copies(self, src, shard):
        e = self.e
        return (
            pltpu.make_async_copy(
                src, self.whole.at[rows16(shard * self.block + e.p * self.step, self.keep)], self.local.at[shard]
            ),
            remote(
                src.at[rows16(e.p * (self.keep - self.step), self.step)],
                self.whole.at[rows16(shard * self.block + e.p * self.keep, self.step)],
                self.send.at[shard], self.recv.at[shard], e.twin(),
            ),
        )

    def put(self, src, shard):
        for copy in self.copies(src, shard):
            copy.start()

    def wait(self, src):
        for shard in range(4):
            for copy in self.copies(src, shard):
                copy.wait()


def half_tiles(source, columns):
    def piece(column, side):
        if column is None:
            return jnp.zeros((source.shape[0], TILE), F32)
        start = column // TILE * TILE
        if start + TILE > source.shape[-1]:
            part = source[:, start : start + HEAD_DIM].astype(F32)
            tile = jnp.concatenate([part, jnp.zeros_like(part)], 1)
        else:
            tile = source[:, start : start + TILE].astype(F32)
        return tile if column % TILE // HEAD_DIM == side else pltpu.roll(tile, HEAD_DIM, 1)

    tiles = []
    for i in range(0, len(columns), 2):
        first, second = (piece(columns[i], 0), piece(columns[i + 1], 1))
        lane = lax.broadcasted_iota(jnp.int32, first.shape, 1)
        tiles.append(jnp.where(lane < HEAD_DIM, first, second))
    return tiles


def head_columns(heads, first):
    return [first + head * HEAD_DIM if head >= 0 else None for head in heads] + [None]


def project_kernel(
    x, cot, bias_0, bias_1, bias_2, bias_3, bias_4, bias_5, bias_6, bias_7, b_up, w_qkv, w_out, w_up, w_down,
    q_out, k_out, v_out, h_out, whole, out_w, vecs, halves, cot_out,
    qkv_rows, half, half_o, edge, held, held_o, raw, vec_in, vec_land, bias,
    v_send, v_recv, z_send, z_recv, a_send, a_recv, w_local, w_send, w_recv, kv_send, kv_recv, r_local,
):
    e = Place()
    t, p, z = (e.t, e.p, e.z)
    rows = pltpu.make_async_copy(w_qkv.at[rows16(p * TILE, 144)], qkv_rows, r_local.at[0])
    rows.start()
    loads = []
    for i in range(4):
        column = pl.multiple_of(D * i + HEAD_DIM * (i % 2) + 256 * t, TILE)
        loads.append((w_up.at[rows16(p * TILE, 144), pl.ds(column, 256)], halves.at[pl.ds(0, 144), pl.ds(256 * i, 256)]))
    column = pl.multiple_of(1024 + 2 * D * (t // 2), TILE)
    loads.append((w_up.at[rows16(p * TILE, 144), pl.ds(column, TILE)], edge))
    loads.append((w_down.at[rows16(HEAD_DIM * (z % 2) + 256 * t + TILE * p, TILE)], halves.at[pl.ds(144, TILE)]))
    loads.append((w_down.at[rows16(1024 * (1 - z % 2) + 32 * p, 32)], halves.at[pl.ds(272, 32)]))
    loads = [pltpu.make_async_copy(src, dst, r_local.at[1 + i]) for i, (src, dst) in enumerate(loads)]
    for copy in loads:
        copy.start()
    spot = lax.broadcasted_iota(jnp.int32, (D // 4, D), 1) - D // 4 * z
    match = (spot == lax.broadcasted_iota(jnp.int32, (D // 4, D), 0)).astype(F32).astype(BF16)
    biases = (bias_0, bias_1, bias_2, bias_3, bias_4, bias_5, bias_6, bias_7)
    biases = jnp.concatenate([ref[...].astype(F32).reshape(1, D // 4) for ref in biases], 0)
    vec_in[0] = nn(biases.astype(BF16), match)
    e.greet()

    def exchange(i):
        return [
            remote(vec_in.at[i], vec_land.at[k, i], v_send.at[i, k], v_recv.at[i, k], e.plane(k))
            for k in range(1, 4)
        ]

    vectors = exchange(0)
    for copy in vectors:
        copy.start()
    into = Halves(e, whole, 272, 144, 128, w_local.at[0], w_send.at[0], w_recv.at[0])
    into_o = Halves(e, raw, 80, 48, 32, w_local.at[1], w_send.at[1], w_recv.at[1])
    chain = ZGather(
        e, half, held, z_send.at[0], z_recv.at[0], lambda shard: into.put(held.at[shard], shard)
    )
    chain_o = ZGather(
        e, half_o, held_o, z_send.at[1], z_recv.at[1], lambda shard: into_o.put(held_o.at[shard], shard)
    )
    rows.wait()
    for chip in range(CHIPS):
        @pl.when(t == chip)
        def _():
            for a in range(3):
                tiles = half_tiles(qkv_rows, head_columns(HEAD_TABLE[chip], a * D))
                for i in range(3):
                    half[:, a * WIDE + i * TILE : a * WIDE + (i + 1) * TILE] = tiles[i].astype(BF16)

    chain.step(0)
    into.put(half, z)
    normed, _ = normalize(x[...].astype(F32))
    total = vec_in[0]
    for k in range(1, 4):
        vectors[k - 1].wait_recv()
        total = total + vec_land[k, 0]
    vecs[:8] = total
    h_out[t] = (normed * vecs[GAIN_1 : GAIN_1 + 1] + vecs[SHIFT_1 : SHIFT_1 + 1]).astype(BF16)
    hidden = Gather(e, h_out.at[t], lambda chip: h_out.at[chip], ROWS, HALF, a_send, a_recv)
    hidden.start()
    ahead = (CHIPS - z) % CHIPS * 16
    for m in range(3):
        unit = 16 * (2 * p + m)
        late = jnp.where(unit < ahead, unit, 192 + unit)
        first = jnp.where(t < CHIPS - 1, ahead + HEAD_DIM * t + unit, late)
        half_o[16 * m : 16 * m + 16] = w_out[rows16(first, 16)]
    for chip in range(CHIPS):
        @pl.when(t == chip)
        def _():
            tiles = half_tiles(vecs, head_columns(HEAD_TABLE[chip], 0))
            for i in range(3):
                bias[:, i * TILE : (i + 1) * TILE] = tiles[i]

    spot = lax.broadcasted_iota(jnp.int32, (D, 320), 1)
    at = jnp.where(spot < 256, HEAD_DIM * (z % 2) + 256 * t + spot, 1024 * (1 - z % 2) + spot - 256)
    match = (lax.broadcasted_iota(jnp.int32, (D, 320), 0) == at).astype(F32).astype(BF16)
    ups = nn(b_up[...], match)
    vec_in[1] = jnp.zeros((8, D), F32)
    for i in range(4):
        @pl.when(z == i)
        def _():
            vec_in[1, 0:1, 256 * i : 256 * i + 256] = ups[0:1, :256]

    @pl.when(z == t)
    def _():
        vec_in[1, 0:1, 1024:] = ups[0:1, 256:]

    vectors = vectors + exchange(1)
    for copy in vectors[3:]:
        copy.start()
    cot_out[:ROWS] = cot[...]
    cot_out[ROWS:] = jnp.zeros((8, D), BF16)
    for copy in loads:
        copy.wait()
    column = edge[...].astype(F32)
    column = jnp.where(t % 2 == 1, pltpu.roll(column, HEAD_DIM, 1), column)
    halves[:144, 1024:] = column[:, :HEAD_DIM].astype(BF16)
    chain.step(1)
    hidden.forward()
    chain.step(2)
    chain_o.step(0)
    into_o.put(half_o, z)
    total = vec_in[1]
    for k in range(1, 4):
        vectors[2 + k].wait_recv()
        total = total + vec_land[k, 1]
    vecs[8:] = total
    chain.step(3)
    into.wait(half)

    def block(k, carry):
        src = e.flip((k + 1) // 2 % 2, k // 2)

        @pl.when(k == 1)
        def _():
            hidden.have_x()

        @pl.when(k == 2)
        def _():
            hidden.have_far()

        @pl.when(k == 3)
        def _():
            hidden.have_y()

        h = h_out[src]
        bias_q, bias_v = (bias[B_QUERY : B_QUERY + 1], bias[B_VALUE : B_VALUE + 1])
        q_out[src] = ((nn(h, whole[:, :WIDE]) + bias_q).astype(BF16) * 0.125).astype(BF16)
        mine = src * 2 + p
        k_out[mine] = nn(h, whole[:, WIDE : 2 * WIDE]).astype(BF16)
        remote(k_out.at[mine], k_out.at[mine], kv_send.at[k], kv_recv.at[k], e.twin()).start()
        v_out[mine] = (nn(h, whole[:, 2 * WIDE :]) + bias_v).astype(BF16)
        remote(
            v_out.at[mine], v_out.at[mine], kv_send.at[k + CHIPS], kv_recv.at[k + CHIPS], e.twin()
        ).start()
        return carry

    lax.fori_loop(0, CHIPS, block, 0)
    chain_o.step(1)
    chain_o.step(2)
    chain_o.step(3)
    into_o.wait(half_o)

    @pl.when(t == CHIPS - 1)
    def _():
        out_w[: SLOTS * HEAD_DIM] = raw[...]

    @pl.when(t < CHIPS - 1)
    def _():
        for i in range(4):
            out_w[i * HEAD_DIM : (i + 1) * HEAD_DIM] = raw[i * 80 : i * 80 + HEAD_DIM]
        out_w[4 * HEAD_DIM : 5 * HEAD_DIM] = jnp.zeros((HEAD_DIM, D), BF16)

    out_w[SLOTS * HEAD_DIM :] = jnp.zeros((WIDE - SLOTS * HEAD_DIM, D), BF16)
    for k in range(CHIPS):
        src = e.flip((k + 1) // 2 % 2, k // 2)
        other = src * 2 + 1 - p
        mine = src * 2 + p
        for ref, j in ((k_out, k), (v_out, k + CHIPS)):
            remote(ref.at[mine], ref.at[mine], kv_send.at[j], kv_recv.at[j], e.twin()).wait_send()
            remote(ref.at[other], ref.at[other], kv_send.at[j], kv_recv.at[j], e.twin()).wait_recv()
    for user in (hidden, chain, chain_o):
        user.sent()
    for copy in vectors:
        copy.wait_send()


def project(x, cot, biases, b_up, w_qkv, w_out, w_up, w_down):
    blocks = jax.ShapeDtypeStruct((CHIPS, ROWS, WIDE), BF16)
    keys = jax.ShapeDtypeStruct((2 * CHIPS, ROWS, WIDE), BF16)
    near, far = (vmem(1), [pl.BlockSpec(memory_space=pl.ANY)])
    return pl.pallas_call(
        project_kernel,
        out_shape=(
            blocks, keys, keys,
            jax.ShapeDtypeStruct((CHIPS, ROWS, D), BF16),
            jax.ShapeDtypeStruct((D, 3 * WIDE), BF16),
            jax.ShapeDtypeStruct((WIDE, D), BF16),
            jax.ShapeDtypeStruct((16, D), F32),
            jax.ShapeDtypeStruct((UP_ROWS + DOWN_ROWS, D), BF16),
            jax.ShapeDtypeStruct((ROWS + 8, D), BF16),
        ),
        in_specs=near * 11 + far + near + far * 2,
        out_specs=tuple(near * 9),
        scratch_shapes=[
            pltpu.VMEM((144, 3 * D), BF16),
            pltpu.VMEM((144, 3 * WIDE), BF16),
            pltpu.VMEM((48, D), BF16),
            pltpu.VMEM((144, TILE), BF16),
            pltpu.VMEM((4, 144, 3 * WIDE), BF16),
            pltpu.VMEM((4, 48, D), BF16),
            pltpu.VMEM((SLOTS * HEAD_DIM, D), BF16),
            pltpu.VMEM((2, 8, D), F32),
            pltpu.VMEM((4, 2, 8, D), F32),
            pltpu.VMEM((16, WIDE), F32),
            dma(2, 4), dma(2, 4), dma(2, 2, 3), dma(2, 2, 3), dma(6), dma(6),
            dma(2, 4), dma(2, 4), dma(2, 4), dma(2 * CHIPS), dma(2 * CHIPS), dma(8),
        ],
        compiler_params=params(1),
        name="project",
    )(x, cot, *biases, b_up, w_qkv, w_out, w_up, w_down)


def tile_bounds(lengths, block):
    ends = [lengths[0]]
    for i in range(1, 4):
        ends.append(ends[-1] + lengths[i])
    first = block * ROWS
    start_first = 0 * first
    for end in ends:
        start_first = jnp.where(first >= end, end, start_first)
    free = jnp.minimum(block, ends[0] // ROWS)
    resume = jnp.maximum(free + 1, start_first // ROWS)
    masked = jnp.where(free < block, 1 + jnp.maximum(block - resume, 0), 0)
    query_pos = first + lax.broadcasted_iota(jnp.int32, (1, ROWS), 1)
    start = jnp.zeros((1, ROWS), jnp.int32)
    for end in ends:
        start = jnp.where(query_pos >= end, end, start)
    return ends[0], query_pos, start, free, resume, masked


def visible(key_block, prompt, query_pos, start):
    key_pos = key_block * ROWS + lax.broadcasted_iota(jnp.int32, (ROWS, ROWS), 0)
    return (key_pos <= query_pos) & ((key_pos < prompt) | (key_pos >= start))


def half_of(rows, h):
    lane = lax.broadcasted_iota(jnp.int32, rows.shape, 1)
    return jnp.where((lane >= h * HEAD_DIM) & (lane < (h + 1) * HEAD_DIM), rows, jnp.zeros_like(rows))


def attend_kernel(lengths, parity, q, k, v, mixed, lse, turned):
    slab = pl.program_id(0)
    for j in range(2 * CHIPS):
        turned[j] = v[j].astype(F32).T.astype(BF16)

    def run(heads):
        def one(i, carry):
            block = 2 * i + parity[0]
            prompt, query_pos, start, free, resume, masked = tile_bounds(lengths, block)
            queries = [half_of(q[i], h) for h in heads]

            def tile(j, state, mask):
                keys = k[j]
                values = turned[j]
                new = []
                for h, (peak, total, accum) in zip(heads, state):
                    scores = cols_product(keys, queries[h])
                    if mask is not None:
                        scores = jnp.where(mask, scores, NEG)
                    peak_new = jnp.maximum(peak, jnp.max(scores, 0, keepdims=True))
                    factor = jnp.exp(peak - peak_new)
                    expos = jnp.exp(scores - peak_new)
                    total_new = total * factor + jnp.sum(expos, 0, keepdims=True)
                    part = values[h * HEAD_DIM : (h + 1) * HEAD_DIM]
                    accum_new = accum * factor + nn(part, expos.astype(BF16))
                    new.append((peak_new, total_new, accum_new))
                return tuple(new)

            state = tuple(
                (
                    jnp.full((1, ROWS), NEG, F32),
                    jnp.zeros((1, ROWS), F32),
                    jnp.zeros((HEAD_DIM, ROWS), F32),
                )
                for _ in heads
            )
            state = tile(block, state, visible(block, prompt, query_pos, start))
            state = lax.fori_loop(0, free, lambda j, s: tile(j, s, None), state)

            def other(m, s):
                j = jnp.where(m == 0, free, resume + m - 1)
                return tile(j, s, visible(j, prompt, query_pos, start))

            state = lax.fori_loop(0, masked, other, state)
            outs = []
            for h, (peak, total, accum) in zip(heads, state):
                outs.append(accum / total)
                lse[0, pl.ds(h * CHIPS + i, 1), :] = peak + jnp.log(total)
            if len(heads) == 1:
                outs.append(jnp.zeros((HEAD_DIM, ROWS), F32))
            mixed[i] = jnp.concatenate(outs, 0).T.astype(BF16)
            return carry

        lax.fori_loop(0, CHIPS, one, 0)

    @pl.when(slab < SLOTS // 2)
    def _():
        run((0, 1))

    @pl.when(slab >= SLOTS // 2)
    def _():
        lse[...] = jnp.zeros_like(lse)
        run((0,))


def slab_spec(count):
    return pl.BlockSpec((count, ROWS, 128), lambda s, *_: (0, 0, s))


def attend(lengths, parity, q, k, v):
    return pl.pallas_call(
        attend_kernel,
        out_shape=(
            jax.ShapeDtypeStruct((CHIPS, ROWS, WIDE), BF16),
            jax.ShapeDtypeStruct((3, 2 * CHIPS, ROWS), F32),
        ),
        grid_spec=pltpu.PrefetchScalarGridSpec(
            num_scalar_prefetch=2,
            grid=(3,),
            in_specs=[slab_spec(CHIPS), slab_spec(2 * CHIPS), slab_spec(2 * CHIPS)],
            out_specs=(
                slab_spec(CHIPS),
                pl.BlockSpec((1, 2 * CHIPS, ROWS), lambda s, *_: (s, 0, 0)),
            ),
            scratch_shapes=[pltpu.VMEM((2 * CHIPS, 128, ROWS), BF16)],
        ),
        compiler_params=pltpu.CompilerParams(vmem_limit_bytes=63 * 2**20),
        cost_estimate=pl.CostEstimate(flops=4 * 10**9, bytes_accessed=5 * 10**6, transcendentals=6 * 10**6),
        name="attend",
    )(lengths, parity, q, k, v)


def attend_back_kernel(
    lengths, parity, q, k, v, mixed, grad, lse, dq, dk, dv, turned, acc_k, acc_v
):
    slab = pl.program_id(0)
    for j in range(2 * CHIPS):
        turned[j] = k[j].astype(F32).T.astype(BF16)
    acc_k[...] = jnp.zeros_like(acc_k)
    acc_v[...] = jnp.zeros_like(acc_v)

    def run(heads):
        def one(i, carry):
            block = 2 * i + parity[0]
            prompt, query_pos, start, free, resume, masked = tile_bounds(lengths, block)
            queries = [half_of(q[i], h) for h in heads]
            grads = [half_of(grad[i], h) for h in heads]
            product = (grad[i].astype(F32) * mixed[i].astype(F32)).T
            deltas = [
                jnp.sum(product[h * HEAD_DIM : (h + 1) * HEAD_DIM], 0, keepdims=True) for h in heads
            ]
            sums = [lse[0, pl.ds(h * CHIPS + i, 1), :] for h in heads]

            def tile(j, state, mask):
                keys, values, keys_t = (k[j], v[j], turned[j])
                new = []
                add_k, add_v = (None, None)
                for h, accum in zip(heads, state):
                    scores = cols_product(keys, queries[h]) - sums[h]
                    if mask is not None:
                        scores = jnp.where(mask, scores, NEG)
                    probs = jnp.exp(scores)
                    grad_probs = cols_product(values, grads[h])
                    ds = (probs * (grad_probs - deltas[h])).astype(BF16)
                    part_v = nn(probs.astype(BF16), grads[h])
                    part_k = nn(ds, queries[h])
                    add_v = part_v if add_v is None else add_v + part_v
                    add_k = part_k if add_k is None else add_k + part_k
                    new.append(accum + nn(keys_t[h * HEAD_DIM : (h + 1) * HEAD_DIM], ds))
                acc_v[j] += add_v
                acc_k[j] += add_k
                return tuple(new)

            state = tuple(jnp.zeros((HEAD_DIM, ROWS), F32) for _ in heads)
            state = tile(block, state, visible(block, prompt, query_pos, start))
            state = lax.fori_loop(0, free, lambda j, s: tile(j, s, None), state)

            def other(m, s):
                j = jnp.where(m == 0, free, resume + m - 1)
                return tile(j, s, visible(j, prompt, query_pos, start))

            state = list(lax.fori_loop(0, masked, other, state))
            if len(heads) == 1:
                state.append(jnp.zeros((HEAD_DIM, ROWS), F32))
            dq[i] = (jnp.concatenate(state, 0) * 0.125).T.astype(BF16)
            return carry

        lax.fori_loop(0, CHIPS, one, 0)

    @pl.when(slab < SLOTS // 2)
    def _():
        run((0, 1))

    @pl.when(slab >= SLOTS // 2)
    def _():
        run((0,))

    dk[...] = acc_k[...].astype(BF16)
    dv[...] = acc_v[...].astype(BF16)


def attend_back(lengths, parity, q, k, v, mixed, grad, lse):
    few, many = (slab_spec(CHIPS), slab_spec(2 * CHIPS))
    return pl.pallas_call(
        attend_back_kernel,
        out_shape=(
            jax.ShapeDtypeStruct((CHIPS, ROWS, WIDE), BF16),
            jax.ShapeDtypeStruct((2 * CHIPS, ROWS, WIDE), BF16),
            jax.ShapeDtypeStruct((2 * CHIPS, ROWS, WIDE), BF16),
        ),
        grid_spec=pltpu.PrefetchScalarGridSpec(
            num_scalar_prefetch=2,
            grid=(3,),
            in_specs=[
                few, many, many, few, few,
                pl.BlockSpec((1, 2 * CHIPS, ROWS), lambda s, *_: (s, 0, 0)),
            ],
            out_specs=(few, many, many),
            scratch_shapes=[
                pltpu.VMEM((2 * CHIPS, 128, ROWS), BF16),
                pltpu.VMEM((2 * CHIPS, ROWS, 128), F32),
                pltpu.VMEM((2 * CHIPS, ROWS, 128), F32),
            ],
        ),
        compiler_params=pltpu.CompilerParams(vmem_limit_bytes=63 * 2**20),
        cost_estimate=pl.CostEstimate(flops=10 * 10**9, bytes_accessed=9 * 10**6, transcendentals=6 * 10**6),
        name="attend_back",
    )(lengths, parity, q, k, v, mixed, grad, lse)


def out_kernel(x, mixed, whole, vecs, middle, part, land, send, recv):
    e = Place()
    e.greet(planes=False)
    sums = Scatter(e, part, land, send, recv)

    def block(k, carry):
        dest = e.flip(1 - k // 2, 1 - k % 2)
        part[dest] = nn(mixed[dest], whole[...]).astype(BF16)

        @pl.when(k == 0)
        def _():
            sums.far_ready()

        @pl.when(k == 1)
        def _():
            sums.x_ready()

        @pl.when(k == 2)
        def _():
            sums.y_ready()

        return carry

    lax.fori_loop(0, CHIPS - 1, block, 0)
    total = x[...].astype(F32) + vecs[B_OUT : B_OUT + 1] + nn(mixed[e.t], whole[...])
    sums.relay()
    middle[...] = total + sums.total()
    sums.sent()


def out_project(x, mixed, whole, vecs):
    return pl.pallas_call(
        out_kernel,
        out_shape=jax.ShapeDtypeStruct((ROWS, D), F32),
        in_specs=vmem(4),
        out_specs=vmem(1)[0],
        scratch_shapes=[
            pltpu.VMEM((CHIPS, ROWS, D), BF16),
            pltpu.VMEM((6, HALF, D), BF16),
            dma(6), dma(6),
        ],
        compiler_params=params(2),
        name="out_project",
    )(x, mixed, whole, vecs)


def feed_kernel(
    middle, cot, cot_x, cot_y, cot_far, halves, vecs, out_w, mixed,
    to_x, to_y, to_far, out_own, grad_mid, gh_heads, g_out, g_down, share, sums, up_sum,
    up, down, cots, hid, act, gpre, part_h, gmid, sum_h_land,
    full_up, full_down, land_up, land_down, land_more, g_up, staged, z_right, z_left, raw, land_out,
    a_send, a_recv, s_send, s_recv, w_local, w_send, w_recv, d_local, d_send, d_recv, g_send, g_recv, z_send, z_recv, c_local,
):
    e = Place()
    t, p = (e.t, e.p)
    e.greet()
    into = Halves(e, up, 272, 144, 128, w_local, w_send, w_recv)
    weights = []
    for i in range(4):
        weights.extend(into.copies(halves.at[i, pl.ds(0, 144)], i))
    for i in range(5):
        src = halves.at[i, pl.ds(144, TILE)] if i < 4 else halves.at[t, pl.ds(272, 32)]
        dst = down.at[rows16(256 * i + p * TILE, TILE) if i < 4 else rows16(1024 + p * 32, 32)]
        weights.append(pltpu.make_async_copy(src, dst, d_local.at[i]))
        weights.append(remote(src, dst, d_send.at[i], d_recv.at[i], e.twin()))
    for k, (ref, chip) in enumerate(((cot, t), (cot_x, e.tx), (cot_y, e.ty), (cot_far, e.td))):
        weights.append(pltpu.make_async_copy(ref.at[pl.ds(0, ROWS)], cots.at[chip], c_local.at[k]))
    for copy in weights:
        copy.start()
    normed, inverse = normalize(middle[...])
    hid[t] = (normed * vecs[GAIN_2 : GAIN_2 + 1] + vecs[SHIFT_2 : SHIFT_2 + 1]).astype(BF16)
    hidden = Gather(e, hid.at[t], lambda chip: hid.at[chip], ROWS, HALF, a_send.at[0], a_recv.at[0])
    hidden.start()
    sum_h = Scatter(e, part_h, sum_h_land, s_send, s_recv)
    for copy in weights:
        copy.wait()
    up_sum[...] = jnp.zeros_like(up_sum)

    def block(k, carry):
        src = e.flip((k + 1) // 2 % 2, k // 2)

        @pl.when(k == 1)
        def _():
            hidden.forward()
            hidden.have_x()

        @pl.when(k == 2)
        def _():
            hidden.have_far()

        @pl.when(k == 3)
        def _():
            hidden.have_y()

        pre = nn(hid[src], up[...]) + vecs[B_UP : B_UP + 1]
        cdf = 0.5 * (1.0 + lax.erf(pre * math.sqrt(0.5)))
        slope = cdf + pre * (jnp.exp(-0.5 * pre * pre) * (1.0 / math.sqrt(2.0 * math.pi)))
        act[src] = (pre * cdf).astype(BF16)
        grad = cols_product(cots[src], down[...]) * slope
        low = grad.astype(BF16)
        gpre[src] = low
        up_sum[...] += jnp.sum(low.astype(F32), 0, keepdims=True)
        part_h[src] = cols_product(low, up[...]).astype(BF16)

        @pl.when(k == 1)
        def _():
            sum_h.x_ready()

        @pl.when(k == 2)
        def _():
            sum_h.far_ready()

        @pl.when(k == 3)
        def _():
            sum_h.y_ready()

        return carry

    lax.fori_loop(0, CHIPS, block, 0)
    sum_h.relay()

    def stack(ref):
        return ref[...].reshape(CHIPS * ROWS, ref.shape[-1])

    full_up[...] = rows_product(stack(hid), stack(gpre)).astype(BF16)
    ups = [
        remote(
            full_up.at[rows16(i * 272 + (1 - p) * TILE, UP_ROWS)], land_up.at[i],
            g_send.at[0, i], g_recv.at[0, i], e.twin(),
        )
        for i in range(4)
    ]
    for copy in ups:
        copy.start()
    full_down[...] = rows_product(stack(act), stack(cots)).astype(BF16)
    swaps = [
        remote(
            full_down.at[rows16(256 * i + (1 - p) * TILE, TILE)], land_down.at[i],
            g_send.at[1, i], g_recv.at[1, i], e.twin(),
        )
        for i in range(4)
    ]
    swaps.append(
        remote(
            full_down.at[rows16(1024 + (1 - p) * 32, 32)], land_more, g_send.at[2, 0], g_recv.at[2, 0], e.twin()
        )
    )
    for copy in swaps:
        copy.start()
    for copy in ups:
        copy.wait()
    for i in range(4):
        own = full_up[rows16(i * 272 + p * TILE, UP_ROWS)].astype(F32)
        g_up[i] = (own + land_up[i].astype(F32)).astype(BF16)
    planes = ZScatter(e, g_up, staged, z_right, z_left, z_send, z_recv)
    planes.begin()
    for ref, chip in ((to_x, e.tx), (to_y, e.ty), (to_far, e.td)):
        ref[:ROWS] = nn(act[chip], down[...]).astype(BF16)
    out_own[...] = middle[...] + vecs[B_DOWN : B_DOWN + 1] + nn(act[t], down[...])

    total = part_h[t].astype(F32) + sum_h.total()
    top = cot[:ROWS].astype(F32)
    grad_middle = top + norm_back(total, normed, inverse, vecs[GAIN_2 : GAIN_2 + 1])
    grad_mid[...] = grad_middle
    low = grad_middle.astype(BF16)
    gmid[t] = low
    spread = Gather(e, gmid.at[t], lambda chip: gmid.at[chip], ROWS, HALF, a_send.at[1], a_recv.at[1])
    spread.start()
    sums[0:1] = jnp.sum(low.astype(F32), 0, keepdims=True)
    sums[1:2] = jnp.sum(top, 0, keepdims=True)
    sums[2:3] = jnp.sum(total * normed, 0, keepdims=True)
    sums[3:4] = jnp.sum(total, 0, keepdims=True)
    sums[4:8] = jnp.zeros((4, D), F32)

    planes.first()
    for copy in swaps:
        copy.wait()
    more = (full_down[rows16(1024 + p * 32, 32)].astype(F32) + land_more[...].astype(F32)).astype(BF16)
    for i in range(4):
        own = full_down[rows16(256 * i + p * TILE, TILE)].astype(F32)
        g_down[i, :TILE] = (own + land_down[i].astype(F32)).astype(BF16)
        g_down[i, TILE:] = more
    spread.forward()
    planes.second()

    def heads(k, carry):
        src = e.flip((k + 1) // 2 % 2, k // 2)

        @pl.when(k == 1)
        def _():
            spread.have_x()

        @pl.when(k == 2)
        def _():
            spread.have_far()

        @pl.when(k == 3)
        def _():
            spread.have_y()

        gh_heads[src] = cols_product(gmid[src], out_w[...]).astype(BF16)
        return carry

    lax.fori_loop(0, CHIPS, heads, 0)
    grad_out = rows_product(stack(mixed), stack(gmid)).astype(BF16)

    @pl.when(t == CHIPS - 1)
    def _():
        raw[...] = grad_out[: SLOTS * HEAD_DIM]

    @pl.when(t < CHIPS - 1)
    def _():
        for i in range(4):
            raw[i * 80 : i * 80 + HEAD_DIM] = grad_out[i * HEAD_DIM : (i + 1) * HEAD_DIM]
            raw[i * 80 + HEAD_DIM : (i + 1) * 80] = jnp.zeros((16, D), BF16)

    swaps = [
        remote(
            raw.at[rows16(i * 80 + (1 - p) * 32, 48)], land_out.at[i], g_send.at[3, i], g_recv.at[3, i], e.twin()
        )
        for i in range(4)
    ]
    for copy in swaps:
        copy.start()
    for copy in swaps:
        copy.wait()
    for i in range(4):
        own = raw[rows16(i * 80 + p * 32, 48)].astype(F32)
        g_out[i] = (own + land_out[i].astype(F32)).astype(BF16)
    planes.last(share)
    for ref in (to_x, to_y, to_far):
        ref[ROWS:] = share[...]
    for user in (hidden, spread, sum_h):
        user.sent()


def feed(middle, cot, others, halves, vecs, out_w, mixed):
    blocks = pltpu.VMEM((CHIPS, ROWS, D), BF16)
    lands = pltpu.VMEM((6, HALF, D), BF16)
    matrix = pltpu.VMEM((D, D), BF16)
    mixture = jax.ShapeDtypeStruct((ROWS + UP_ROWS, D), BF16)
    return pl.pallas_call(
        feed_kernel,
        out_shape=(
            mixture, mixture, mixture,
            jax.ShapeDtypeStruct((ROWS, D), F32),
            jax.ShapeDtypeStruct((ROWS, D), F32),
            jax.ShapeDtypeStruct((CHIPS, ROWS, WIDE), BF16),
            jax.ShapeDtypeStruct((4, 48, D), BF16),
            jax.ShapeDtypeStruct((4, DOWN_ROWS, D), BF16),
            jax.ShapeDtypeStruct((UP_ROWS, D), BF16),
            jax.ShapeDtypeStruct((8, D), F32),
            jax.ShapeDtypeStruct((1, D), F32),
        ),
        in_specs=vmem(9),
        out_specs=tuple(vmem(11)),
        scratch_shapes=[matrix, matrix]
        + [blocks] * 6
        + [lands, matrix, matrix]
        + [
            pltpu.VMEM((4, UP_ROWS, D), BF16),
            pltpu.VMEM((4, TILE, D), BF16),
            pltpu.VMEM((32, D), BF16),
            pltpu.VMEM((4, UP_ROWS, D), BF16),
            pltpu.VMEM((4, UP_ROWS, D), BF16),
            pltpu.VMEM((3, UP_ROWS, D), BF16),
            pltpu.VMEM((3, UP_ROWS, D), BF16),
            pltpu.VMEM((SLOTS * HEAD_DIM, D), BF16),
            pltpu.VMEM((4, 48, D), BF16),
            dma(2, 6), dma(2, 6), dma(6), dma(6), dma(4), dma(4), dma(4),
            dma(5), dma(5), dma(5), dma(4, 4), dma(4, 4), dma(2, 3), dma(2, 3), dma(4),
        ],
        compiler_params=params(3, 63),
        name="feed",
    )(middle, cot, *others, halves, vecs, out_w, mixed)


def back_kernel(
    x, grad_mid, dq, dk, dv, hid, whole, vecs, share, from_x, from_y, from_far, share_down, out_own, g_out, sums, up_sum,
    output, grad_x, up_out, down_out, qkv_out, o_out, vec_out, b_up_out,
    joint, full, land, land_k, land_v, part, sum_land, g_qkv, z_right, z_left, s_qkv,
    s_out, zo_right, zo_left, own_qkv, own_out, all_up, all_down, all_qkv, all_out, local, vec_land, totals, wide,
    kv_send, kv_recv, g_send, g_recv, s_send, s_recv, a_send, a_recv, z_send, z_recv, t_send, t_recv, v_send, v_recv, c_local,
):
    e = Place()
    t, p, z = (e.t, e.p, e.z)
    e.greet()
    swaps = []
    for k in range(CHIPS):
        chip = e.flip(1 - k // 2, 1 - k % 2)
        for j, (ref, dst) in enumerate(((dk, land_k), (dv, land_v))):
            swaps.append(
                remote(ref.at[chip * 2 + 1 - p], dst.at[chip], kv_send.at[j, k], kv_recv.at[j, k], e.twin())
            )
    for copy in swaps:
        copy.start()

    def spread(number, own, everything, rows, cut):
        return Gather(
            e, own, lambda chip: everything.at[p, chip], rows, cut, a_send.at[number], a_recv.at[number]
        )

    def hand(number, own, everything, k):
        chip = e.flip(k % 2, k // 2)
        src = own if k == 0 else everything.at[p, chip]
        return remote(
            src, everything.at[p, chip], t_send.at[number, k], t_recv.at[number, k], e.twin()
        )

    def handed(number, own, everything):
        for k in range(CHIPS):
            chip = e.flip(k % 2, k // 2)
            copy = remote(
                own, everything.at[1 - p, chip], t_send.at[number, k], t_recv.at[number, k], e.twin()
            )
            copy.wait_recv()
            copy.wait_send()

    feeds = [share] + [ref.at[pl.ds(ROWS, UP_ROWS)] for ref in (from_x, from_y, from_far)]
    keeps = []
    for k in range(CHIPS):
        slot = all_up.at[p, e.flip(k % 2, k // 2)]
        keeps.append(pltpu.make_async_copy(feeds[k], slot, c_local.at[k]))
    downs = spread(2, share_down, all_down, DOWN_ROWS, 80)
    downs.start()
    outs = ZScatter(e, g_out, s_out, zo_right, zo_left, z_send.at[0], z_recv.at[0])
    outs.begin()
    result = out_own[...]
    for ref in (from_x, from_y, from_far):
        result = result + ref[:ROWS].astype(F32)
    output[...] = result.T.astype(BF16)
    normed, inverse = normalize(x[...].astype(F32))
    local[...] = jnp.zeros_like(local)
    head_q, head_v = (jnp.zeros((1, WIDE), F32), jnp.zeros((1, WIDE), F32))
    for copy in swaps:
        copy.wait()
    for k in range(CHIPS):
        keeps[k].start()
        slot = all_up.at[p, e.flip(k % 2, k // 2)]
        remote(feeds[k], slot, t_send.at[0, k], t_recv.at[0, k], e.twin()).start()
    hand(3, share_down, all_down, 0).start()
    all_down[p, t] = share_down[...]
    for k in range(CHIPS):
        mine = k * 2 + p
        joint[k, :, :WIDE] = dq[k]
        joint[k, :, WIDE : 2 * WIDE] = (dk[mine].astype(F32) + land_k[k].astype(F32)).astype(BF16)
        low_v = (dv[mine].astype(F32) + land_v[k].astype(F32)).astype(BF16)
        joint[k, :, 2 * WIDE :] = low_v
        head_q = head_q + jnp.sum(dq[k].astype(F32), 0, keepdims=True)
        head_v = head_v + jnp.sum(low_v.astype(F32), 0, keepdims=True)
    outs.first()

    def stack(ref):
        return ref[...].reshape(CHIPS * ROWS, ref.shape[-1])

    full[...] = rows_product(stack(hid), stack(joint)).astype(BF16)
    swaps = [
        remote(
            full.at[rows16(i * 272 + (1 - p) * TILE, 144)], land.at[i], g_send.at[i], g_recv.at[i], e.twin()
        )
        for i in range(4)
    ]
    for copy in swaps:
        copy.start()
    downs.forward()
    outs.second()
    summed = Scatter(e, part, sum_land, s_send, s_recv)

    def block(k, carry):
        dest = e.flip(1 - k // 2, 1 - k % 2)
        part[dest] = cols_product(joint[dest], whole[...]).astype(BF16)

        @pl.when(k == 0)
        def _():
            summed.far_ready()

        @pl.when(k == 1)
        def _():
            summed.x_ready()

        @pl.when(k == 2)
        def _():
            summed.y_ready()

        return carry

    lax.fori_loop(0, 1, block, 0)
    for copy in swaps:
        copy.wait()
    for i in range(4):
        own = full[rows16(i * 272 + p * TILE, 144)].astype(F32)
        g_qkv[i] = (own + land[i].astype(F32)).astype(BF16)
    weights = ZScatter(e, g_qkv, s_qkv, z_right, z_left, z_send.at[1], z_recv.at[1])
    weights.begin()
    lax.fori_loop(1, CHIPS - 1, block, 0)
    outs.last(own_out)
    rows = cols_product(joint[t], whole[...])
    downs.have_x()
    downs.have_y()
    hand(3, share_down, all_down, 1).start()
    hand(3, share_down, all_down, 2).start()
    downs.have_far()
    hand(3, share_down, all_down, 3).start()
    weights.first()
    others = spread(0, own_out, all_out, 48, 32)
    others.start()
    all_out[p, t] = own_out[...]
    hand(1, own_out, all_out, 0).start()
    summed.relay()
    weights.second()
    total = rows + summed.total()
    grad_x[...] = (grad_mid[...] + norm_back(total, normed, inverse, vecs[GAIN_1 : GAIN_1 + 1])).T
    local[:4] = sums[:4]
    local[4:5] = jnp.sum(total * normed, 0, keepdims=True)
    local[5:6] = jnp.sum(total, 0, keepdims=True)
    local[pl.ds(8 + t, 1), :] = up_sum[...]
    local[pl.ds(12 + t, 1), :WIDE] = head_q
    local[pl.ds(12 + t, 1), WIDE : 2 * WIDE] = head_v
    twin = remote(local, vec_land.at[0], v_send.at[0], v_recv.at[0], e.twin())
    twin.start()
    others.forward()
    others.have_x()
    others.have_y()
    hand(1, own_out, all_out, 1).start()
    hand(1, own_out, all_out, 2).start()
    others.have_far()
    hand(1, own_out, all_out, 3).start()
    twin.wait()
    totals[...] = local[...] + vec_land[0]
    planes = [
        remote(totals, vec_land.at[k], v_send.at[k], v_recv.at[k], e.plane(k)) for k in range(1, 4)
    ]
    for copy in planes:
        copy.start()
    weights.last(own_qkv)
    qkvs = spread(1, own_qkv, all_qkv, 144, 80)
    qkvs.start()
    hand(2, own_qkv, all_qkv, 0).start()
    all_qkv[p, t] = own_qkv[...]
    for copy in planes:
        copy.wait()
    local[...] = totals[...] + vec_land[1] + vec_land[2] + vec_land[3]
    chips = [
        remote(local, vec_land.at[3 + k], v_send.at[3 + k], v_recv.at[3 + k], e.chip(chip))
        for k, chip in ((1, e.tx), (2, e.ty), (3, e.td))
    ]
    for copy in chips:
        copy.start()

    handed(0, share, all_up)
    handed(3, share_down, all_down)
    for copy in keeps:
        copy.wait()
    for s in range(CHIPS):
        for q in range(2):
            rows = slice(q * TILE, q * TILE + 144)
            for i in range(4):
                column = D * i + HEAD_DIM * (i % 2) + 256 * s
                up_out[rows, column : column + 256] = all_up[q, s, :, 256 * i : 256 * (i + 1)]
            down_out[rows16(z % 2 * 64 + 256 * s + TILE * q, TILE)] = all_down[q, s, :TILE]
    for q in range(2):
        rows = slice(q * TILE, q * TILE + 144)
        for s in range(0, CHIPS, 2):
            pair = [all_up[q, s + i, :, 1024:].astype(F32) for i in range(2)]
            column = D * s + 1024
            up_out[rows, column : column + TILE] = jnp.concatenate(pair, 1).astype(BF16)
        down_out[rows16((1 - z % 2) * 1024 + 32 * q, 32)] = all_down[q, z, TILE:]

    handed(1, own_out, all_out)
    ahead = (CHIPS - z) % CHIPS * 16
    for s in range(CHIPS - 1):
        o_out[rows16(ahead + HEAD_DIM * s, 48)] = all_out[0, s]
        o_out[rows16(ahead + HEAD_DIM * s + 32, 32)] = all_out[1, s, :32]
    for u in range(SLOTS):
        q, first = ((0, 16 * u) if u < 3 else (1, 16 * u - 32))
        strip = all_out[q, CHIPS - 1, first : first + 16]

        @pl.when(16 * u < ahead)
        def _():
            o_out[16 * u : 16 * u + 16] = strip

        @pl.when(16 * u >= ahead)
        def _():
            o_out[192 + 16 * u : 208 + 16 * u] = strip

    qkvs.forward()
    qkvs.have_x()
    qkvs.have_y()
    hand(2, own_qkv, all_qkv, 1).start()
    hand(2, own_qkv, all_qkv, 2).start()
    qkvs.have_far()
    hand(2, own_qkv, all_qkv, 3).start()
    for copy in chips:
        copy.wait()
    totals[...] = local[...] + vec_land[4] + vec_land[5] + vec_land[6]
    wide[...] = jnp.zeros_like(wide)
    wide[:6, :D] = totals[:6]
    columns = {}
    for s, heads in enumerate(HEAD_TABLE):
        for slot, head in enumerate(heads):
            columns[head] = (s, slot * HEAD_DIM)
    lane = lax.broadcasted_iota(jnp.int32, (1, TILE), 1)
    for a in range(2):
        def span(head, side):
            s, column = columns[head]
            start = (column + a * WIDE) // TILE * TILE
            tile = totals[12 + s : 13 + s, start : start + TILE]
            return tile if column % TILE // HEAD_DIM == side else pltpu.roll(tile, HEAD_DIM, 1)

        for head in range(0, HEADS, 2):
            tile = span(head, 0)
            if head + 1 < HEADS:
                tile = jnp.where(lane < HEAD_DIM, tile, span(head + 1, 1))
            wide[6 + a : 7 + a, head * HEAD_DIM : head * HEAD_DIM + TILE] = tile
    for i in range(4):
        @pl.when(z == i)
        def _():
            row = wide[...]
            if i > 0:
                row = pltpu.roll(row, 9 * TILE - D // 4 * i, 1)
            vec_out[...] = row[:, :WIDE]
            pieces = [totals[8 + s : 9 + s, 256 * i : 256 * i + 256] for s in range(CHIPS)]
            more = totals[8 + i : 9 + i, 1024:]
            if i % 2 == 0:
                b_up_out[...] = jnp.concatenate(pieces + [more, more], 1)
            else:
                b_up_out[...] = pltpu.roll(jnp.concatenate(pieces + [more, more], 1), HEAD_DIM, 1)

    handed(2, own_qkv, all_qkv)
    source = {}
    for s, heads in enumerate(HEAD_TABLE):
        for slot, head in enumerate(heads):
            if head >= 0:
                for a in range(3):
                    source[a * HEADS + head] = (s, a * WIDE + slot * HEAD_DIM)
    for q in range(2):
        rows = slice(q * TILE, q * TILE + 144)

        def piece(g, side):
            s, column = source[g]
            tile = all_qkv[q, s, :, column // TILE * TILE : column // TILE * TILE + TILE].astype(F32)
            return tile if column % TILE // HEAD_DIM == side else pltpu.roll(tile, HEAD_DIM, 1)

        left = lax.broadcasted_iota(jnp.int32, (144, TILE), 1) < HEAD_DIM
        for g in range(0, 3 * HEADS - 1, 2):
            column = g * HEAD_DIM
            qkv_out[rows, column : column + TILE] = jnp.where(left, piece(g, 0), piece(g + 1, 1)).astype(BF16)
        column = (3 * HEADS - 1) * HEAD_DIM
        qkv_out[rows, column : column + HEAD_DIM] = piece(3 * HEADS - 1, 0)[:, :HEAD_DIM].astype(BF16)
    for user in (downs, others, qkvs, summed):
        user.sent()


def back(x, grad_mid, dq, dk, dv, hid, whole, vecs, share, others, share_down, out_own, g_out, sums, up_sum):
    heads = pltpu.VMEM((CHIPS, ROWS, WIDE), BF16)
    qkv, out = ((144, 3 * WIDE), (48, D))

    def many(count, shape):
        return pltpu.VMEM((count, *shape), BF16)

    return pl.pallas_call(
        back_kernel,
        out_shape=(
            jax.ShapeDtypeStruct((D, ROWS), BF16),
            jax.ShapeDtypeStruct((D, ROWS), F32),
            jax.ShapeDtypeStruct((D // 4, 4 * D), BF16),
            jax.ShapeDtypeStruct((D, D), BF16),
            jax.ShapeDtypeStruct((D // 4, 3 * D), BF16),
            jax.ShapeDtypeStruct((D // 4, D), BF16),
            jax.ShapeDtypeStruct((8, WIDE), F32),
            jax.ShapeDtypeStruct((1, 9 * TILE), F32),
        ),
        in_specs=vmem(17),
        out_specs=tuple(vmem(8)),
        scratch_shapes=[
            pltpu.VMEM((CHIPS, ROWS, 3 * WIDE), BF16),
            pltpu.VMEM((D, 3 * WIDE), BF16),
            many(4, qkv),
            heads, heads,
            pltpu.VMEM((CHIPS, ROWS, D), BF16),
            pltpu.VMEM((6, HALF, D), BF16),
            many(4, qkv), many(3, qkv), many(3, qkv), many(4, qkv),
            many(4, out), many(3, out), many(3, out),
            pltpu.VMEM(qkv, BF16), pltpu.VMEM(out, BF16),
            pltpu.VMEM((2, CHIPS, UP_ROWS, D), BF16),
            pltpu.VMEM((2, CHIPS, DOWN_ROWS, D), BF16),
            pltpu.VMEM((2, CHIPS, *qkv), BF16),
            pltpu.VMEM((2, CHIPS, *out), BF16),
            pltpu.VMEM((16, D), F32),
            pltpu.VMEM((7, 16, D), F32),
            pltpu.VMEM((16, D), F32),
            pltpu.VMEM((8, 9 * TILE), F32),
            dma(2, CHIPS), dma(2, CHIPS), dma(4), dma(4), dma(6), dma(6), dma(3, 6), dma(3, 6),
            dma(2, 2, 3), dma(2, 2, 3), dma(4, 4), dma(4, 4), dma(7), dma(7), dma(4),
        ],
        compiler_params=params(4, 63),
        name="back",
    )(x, grad_mid, dq, dk, dv, hid, whole, vecs, share, *others, share_down, out_own, g_out, sums, up_sum)


def plane_device(
    tokens, seq_lengths, cotangent, ln1_gain, ln1_bias, w_qkv, b_query, b_value, w_out, b_out,
    ln2_gain, ln2_bias, w_up, b_up, w_down, b_down,
):
    c = lax.axis_index("ctx")
    x, cot, lengths = (tokens[0], cotangent[0], seq_lengths[0])
    parity = (c % 2)[None].astype(jnp.int32)
    shard = D // 4

    biases = (b_query, b_value, b_out, b_down, ln1_gain, ln1_bias, ln2_gain, ln2_bias)
    q, k, v, hid, whole, out_w, vecs, halves, sent = project(
        x, cot, biases, b_up.reshape(1, D), w_qkv, w_out, w_up, w_down
    )
    halves = lax.all_gather(halves, "wsh", axis=0)

    def from_chips(*arrays):
        return [lax.ppermute(array, "ctx", list(enumerate(to))) for array, to in zip(arrays, flips)]

    flips = [[(i // 2 ^ mask) * 2 + i % 2 for i in range(2 * CHIPS)] for mask in (1, 2, 3)]
    tops = from_chips(sent, sent, sent)
    mixed, lse = attend(lengths, parity, q, k, v)
    middle = out_project(x, mixed, out_w, vecs)
    to_x, to_y, to_far, out_own, grad_mid, grad_heads, g_out, g_down, share, sums, up_sum = feed(
        middle, sent, tops, halves, vecs, out_w, mixed
    )
    others = from_chips(to_x, to_y, to_far)
    share_down = lax.psum_scatter(
        g_down.reshape(4 * DOWN_ROWS, D), "wsh", scatter_dimension=0, tiled=True
    )
    dq, dk, dv = attend_back(lengths, parity, q, k, v, mixed, grad_heads, lse)
    output, grad_x, grad_up, grad_down, grad_qkv, grad_out, vectors, grad_b_up = back(
        x, grad_mid, dq, dk, dv, hid, whole, vecs, share, others, share_down, out_own, g_out, sums, up_sum
    )
    grad_up, grad_down, grad_qkv, grad_out = (
        array.astype(F32) for array in (grad_up, grad_down, grad_qkv, grad_out)
    )

    mine = [row[:shard] for row in vectors]
    grad_b_up = grad_b_up[0, :D]
    return (
        output.T[None], grad_x.T[None],
        mine[4], mine[5], grad_qkv, mine[6], mine[7], grad_out, mine[0],
        mine[2], mine[3], grad_up, grad_b_up, grad_down, mine[1],
    )


def solution(mesh):
    in_specs = (
        P("wsh", "ctx", None),
        P("wsh", None),
        P("wsh", "ctx", None),
        P("wsh"),
        P("wsh"),
        P("wsh", None),
        P("wsh"),
        P("wsh"),
        P("wsh", None),
        P("wsh"),
        P("wsh"),
        P("wsh"),
        P("wsh", None),
        P("wsh"),
        P("wsh", None),
        P("wsh"),
    )
    out_specs = (
        P("wsh", "ctx", None),
        P("wsh", "ctx", None),
        P("wsh"),
        P("wsh"),
        P("wsh", None),
        P("wsh"),
        P("wsh"),
        P("wsh", None),
        P("wsh"),
        P("wsh"),
        P("wsh"),
        P("wsh", None),
        P("wsh"),
        P("wsh", None),
        P("wsh"),
    )
    sizes = (mesh.shape["ctx"], mesh.shape["wsh"])
    body = plane_device if sizes == (2 * CHIPS, 4) else on_device
    return jax.shard_map(
        body, mesh=mesh, in_specs=in_specs, out_specs=out_specs, check_vma=False
    )
```

```python
import functools
import math

import jax
import jax.numpy as jnp
from jax import lax
from jax.experimental import pallas as pl
from jax.experimental.pallas import tpu as pltpu
from jax.sharding import PartitionSpec as P

D = 1088
HEADS = 17
HEAD_DIM = 64


def normalize(inputs):
    center = inputs - jnp.mean(inputs, -1, keepdims=True)
    inverse = lax.rsqrt(jnp.mean(center * center, -1, keepdims=True) + 1e-05)
    return (center * inverse, inverse)


def norm_back(grad_in, normed, inverse, gain):
    scaled = grad_in * gain
    return inverse * (
        scaled
        - jnp.mean(scaled, -1, keepdims=True)
        - normed * jnp.mean(scaled * normed, -1, keepdims=True)
    )


def rows_product(left, right):
    return lax.dot_general(
        left, right, (((0,), (0,)), ((), ())), preferred_element_type=jnp.float32
    )


def cols_product(left, right):
    return lax.dot_general(
        left, right, (((1,), (1,)), ((), ())), preferred_element_type=jnp.float32
    )


def sequence_ids(lengths, positions):
    bounds = jnp.cumsum(lengths)
    return jnp.sum((positions[:, None] >= bounds[None, :]).astype(jnp.int32), axis=1)


def allowed_pairs(lengths, query_pos, key_pos):
    query_owner = sequence_ids(lengths, query_pos)
    key_owner = sequence_ids(lengths, key_pos)
    return (key_pos[None, :] <= query_pos[:, None]) & (
        (key_owner[None, :] == 0) | (key_owner[None, :] == query_owner[:, None])
    )


def over_blocks(state_in, arrays, step_fn):
    total_rows = arrays[0].shape[0]
    block_rows = math.gcd(total_rows, 512)

    def advance(block_index, state_now):
        offset = block_index * block_rows
        pieces = tuple((lax.dynamic_slice_in_dim(array, offset, block_rows, 0) for array in arrays))
        return step_fn(state_now, pieces, offset)

    return lax.fori_loop(0, total_rows // block_rows, advance, state_in)


def sectioned_sum(partials):
    shares = lax.psum_scatter(partials, "wsh", scatter_dimension=0, tiled=True)
    return lax.psum(shares, "ctx")


def on_device(
    tokens,
    seq_lengths,
    cotangent,
    ln1_gain,
    ln1_bias,
    w_qkv,
    b_query,
    b_value,
    w_out,
    b_out,
    ln2_gain,
    ln2_bias,
    w_up,
    b_up,
    w_down,
    b_down,
):
    token_rows, grad_rows = (tokens[0], cotangent[0])
    shards = (
        w_qkv,
        w_out,
        w_up,
        w_down,
        b_query,
        b_value,
        b_out,
        b_up,
        b_down,
        ln1_gain,
        ln1_bias,
        ln2_gain,
        ln2_bias,
    )
    gathered = (
        lax.all_gather(shards[0], "wsh", axis=0, tiled=True),
        lax.all_gather(shards[1], "wsh", axis=0, tiled=True),
        lax.all_gather(shards[2], "wsh", axis=0, tiled=True),
        lax.all_gather(shards[3], "wsh", axis=0, tiled=True),
        lax.all_gather(shards[4], "wsh", axis=0, tiled=True),
        lax.all_gather(shards[5], "wsh", axis=0, tiled=True),
        lax.all_gather(shards[6], "wsh", axis=0, tiled=True),
        lax.all_gather(shards[7], "wsh", axis=0, tiled=True),
        lax.all_gather(shards[8], "wsh", axis=0, tiled=True),
        lax.all_gather(shards[9], "wsh", axis=0, tiled=True),
        lax.all_gather(shards[10], "wsh", axis=0, tiled=True),
        lax.all_gather(shards[11], "wsh", axis=0, tiled=True),
        lax.all_gather(shards[12], "wsh", axis=0, tiled=True),
    )
    qkv_full, out_full, up_full, down_full = (gathered[0], gathered[1], gathered[2], gathered[3])
    query_bias, value_bias, out_bias, up_bias, down_bias = [
        piece.astype(jnp.float32) for piece in gathered[4:9]
    ]
    gain_one, shift_one, gain_two, shift_two = [
        piece.astype(jnp.float32) for piece in gathered[9:13]
    ]
    lengths = seq_lengths[0]
    tok_rows = token_rows.shape[0]
    my_pos = lax.axis_index("ctx") * tok_rows + jnp.arange(tok_rows, dtype=jnp.int32)
    scale_qk = HEAD_DIM ** (-0.5)
    inputs = token_rows.astype(jnp.float32)
    normed_one, inverse_one = normalize(inputs)
    hidden_one = (normed_one * gain_one + shift_one).astype(jnp.bfloat16)
    joint_proj = jnp.dot(hidden_one, qkv_full, preferred_element_type=jnp.float32)
    queries = (joint_proj[:, :D] + query_bias).astype(jnp.bfloat16)
    key_rows = joint_proj[:, D : 2 * D].astype(jnp.bfloat16)
    value_rows = (joint_proj[:, 2 * D :] + value_bias).astype(jnp.bfloat16)
    query_heads = queries.reshape(tok_rows, HEADS, HEAD_DIM)
    my_key_heads = key_rows.reshape(tok_rows, HEADS, HEAD_DIM)
    my_value_heads = value_rows.reshape(tok_rows, HEADS, HEAD_DIM)

    def forward_step(state_now, pieces, first_row):
        key_heads = pieces[0].reshape(-1, HEADS, HEAD_DIM)
        value_heads = pieces[1].reshape(-1, HEADS, HEAD_DIM)
        key_pos = first_row + jnp.arange(key_heads.shape[0], dtype=jnp.int32)
        allowed = allowed_pairs(lengths, my_pos, key_pos)

        def forward_compute(inner):
            peak_old, total_old, accum_old = inner
            scores = (
                jnp.einsum(
                    "qhd,khd->hqk", query_heads, key_heads, preferred_element_type=jnp.float32
                )
                * scale_qk
            )
            scores = jnp.where(allowed[None], scores, -1e30)
            peak_new = jnp.maximum(peak_old, jnp.max(scores, -1))
            factor = jnp.exp(peak_old - peak_new)
            expos = jnp.where(allowed[None], jnp.exp(scores - peak_new[:, :, None]), 0.0)
            total_new = total_old * factor + jnp.sum(expos, -1)
            accum_new = accum_old * factor.T[:, :, None] + jnp.einsum(
                "hqk,khd->qhd",
                expos.astype(jnp.bfloat16),
                value_heads,
                preferred_element_type=jnp.float32,
            )
            return (peak_new, total_new, accum_new)

        return lax.cond(jnp.any(allowed), forward_compute, lambda inner: inner, state_now)

    start_state = (
        jnp.full((HEADS, tok_rows), -1e30, jnp.float32),
        jnp.zeros((HEADS, tok_rows), jnp.float32),
        jnp.zeros((tok_rows, HEADS, HEAD_DIM), jnp.float32),
    )
    peak, total, accum = over_blocks(
        start_state,
        (
            lax.all_gather(key_rows, "ctx", axis=0, tiled=True),
            lax.all_gather(value_rows, "ctx", axis=0, tiled=True),
        ),
        forward_step,
    )
    mixed = accum / total.T[:, :, None]
    log_sum = (peak + jnp.log(total)).T
    mixed_low = mixed.reshape(tok_rows, D).astype(jnp.bfloat16)
    middle = inputs + jnp.dot(mixed_low, out_full, preferred_element_type=jnp.float32) + out_bias
    normed_two, inverse_two = normalize(middle)
    hidden_two = (normed_two * gain_two + shift_two).astype(jnp.bfloat16)
    pre_act = jnp.dot(hidden_two, up_full, preferred_element_type=jnp.float32) + up_bias
    activ_low = jax.nn.gelu(pre_act, approximate=False).astype(jnp.bfloat16)
    result = middle + jnp.dot(activ_low, down_full, preferred_element_type=jnp.float32) + down_bias
    output_rows = result.astype(jnp.bfloat16)
    grad_top_f = grad_rows.astype(jnp.float32)
    grad_down = rows_product(activ_low, grad_rows)
    grad_down_bias = jnp.sum(grad_top_f, 0)
    grad_act = cols_product(grad_rows, down_full)
    cdf_part = 0.5 * (1.0 + lax.erf(pre_act * math.sqrt(0.5)))
    pdf_part = jnp.exp(-0.5 * pre_act * pre_act) / math.sqrt(2.0 * math.pi)
    grad_pre = (grad_act * (cdf_part + pre_act * pdf_part)).astype(jnp.bfloat16)
    grad_up = rows_product(hidden_two, grad_pre)
    grad_up_bias = jnp.sum(grad_pre.astype(jnp.float32), 0)
    grad_h2 = cols_product(grad_pre, up_full)
    grad_gain_two = jnp.sum(grad_h2 * normed_two, 0)
    grad_shift_two = jnp.sum(grad_h2, 0)
    grad_mid = grad_top_f + norm_back(grad_h2, normed_two, inverse_two, gain_two)
    grad_mid_low = grad_mid.astype(jnp.bfloat16)
    grad_out_w = rows_product(mixed_low, grad_mid_low)
    grad_out_bias = jnp.sum(grad_mid_low.astype(jnp.float32), 0)
    grad_mixed = cols_product(grad_mid_low, out_full).astype(jnp.bfloat16)
    grad_heads = grad_mixed.reshape(tok_rows, HEADS, HEAD_DIM)
    delta = jnp.sum(grad_heads.astype(jnp.float32) * mixed, -1)
    lse_all, delta_all = (
        lax.all_gather(log_sum, "ctx", axis=0, tiled=True),
        lax.all_gather(delta, "ctx", axis=0, tiled=True),
    )

    def query_step(state_now, pieces, first_row):
        key_heads = pieces[0].reshape(-1, HEADS, HEAD_DIM)
        value_heads = pieces[1].reshape(-1, HEADS, HEAD_DIM)
        key_pos = first_row + jnp.arange(key_heads.shape[0], dtype=jnp.int32)
        allowed = allowed_pairs(lengths, my_pos, key_pos)

        def query_compute(accum_old):
            scores = (
                jnp.einsum(
                    "qhd,khd->hqk", query_heads, key_heads, preferred_element_type=jnp.float32
                )
                * scale_qk
            )
            probs = jnp.where(allowed[None], jnp.exp(scores - log_sum.T[:, :, None]), 0.0)
            grad_probs = jnp.einsum(
                "qhd,khd->hqk", grad_heads, value_heads, preferred_element_type=jnp.float32
            )
            grad_scores = (probs * (grad_probs - delta.T[:, :, None])).astype(jnp.bfloat16)
            return accum_old + jnp.einsum(
                "hqk,khd->qhd", grad_scores, key_heads, preferred_element_type=jnp.float32
            )

        return lax.cond(jnp.any(allowed), query_compute, lambda inner: inner, state_now)

    zero_heads = jnp.zeros((tok_rows, HEADS, HEAD_DIM), jnp.float32)
    grad_query = over_blocks(
        zero_heads,
        (
            lax.all_gather(key_rows, "ctx", axis=0, tiled=True),
            lax.all_gather(value_rows, "ctx", axis=0, tiled=True),
        ),
        query_step,
    )

    def key_step(state_now, pieces, first_row):
        other_queries = pieces[0].reshape(-1, HEADS, HEAD_DIM)
        other_grads = pieces[1].reshape(-1, HEADS, HEAD_DIM)
        other_count = other_queries.shape[0]
        other_pos = first_row + jnp.arange(other_count, dtype=jnp.int32)
        other_lse = lax.dynamic_slice_in_dim(lse_all, first_row, other_count, 0)
        other_delta = lax.dynamic_slice_in_dim(delta_all, first_row, other_count, 0)
        allowed = allowed_pairs(lengths, other_pos, my_pos)

        def key_compute(inner):
            grad_key_old, grad_value_old = inner
            scores = (
                jnp.einsum(
                    "qhd,khd->hqk", other_queries, my_key_heads, preferred_element_type=jnp.float32
                )
                * scale_qk
            )
            probs = jnp.where(allowed[None], jnp.exp(scores - other_lse.T[:, :, None]), 0.0)
            grad_value_new = grad_value_old + jnp.einsum(
                "hqk,qhd->khd",
                probs.astype(jnp.bfloat16),
                other_grads,
                preferred_element_type=jnp.float32,
            )
            grad_probs = jnp.einsum(
                "qhd,khd->hqk", other_grads, my_value_heads, preferred_element_type=jnp.float32
            )
            grad_scores = (probs * (grad_probs - other_delta.T[:, :, None])).astype(jnp.bfloat16)
            grad_key_new = grad_key_old + jnp.einsum(
                "hqk,qhd->khd", grad_scores, other_queries, preferred_element_type=jnp.float32
            )
            return (grad_key_new, grad_value_new)

        return lax.cond(jnp.any(allowed), key_compute, lambda inner: inner, state_now)

    grad_key, grad_value = over_blocks(
        (zero_heads, zero_heads),
        (
            lax.all_gather(queries, "ctx", axis=0, tiled=True),
            lax.all_gather(grad_mixed, "ctx", axis=0, tiled=True),
        ),
        key_step,
    )
    grad_joint = jnp.concatenate(
        [
            (grad_query * scale_qk).reshape(tok_rows, D),
            (grad_key * scale_qk).reshape(tok_rows, D),
            grad_value.reshape(tok_rows, D),
        ],
        axis=1,
    ).astype(jnp.bfloat16)
    grad_qkv_w = rows_product(hidden_one, grad_joint)
    grad_joint_f = grad_joint.astype(jnp.float32)
    grad_query_bias = jnp.sum(grad_joint_f[:, :D], 0)
    grad_value_bias = jnp.sum(grad_joint_f[:, 2 * D :], 0)
    grad_h1 = cols_product(grad_joint, qkv_full)
    grad_gain_one = jnp.sum(grad_h1 * normed_one, 0)
    grad_shift_one = jnp.sum(grad_h1, 0)
    grad_input = grad_mid + norm_back(grad_h1, normed_one, inverse_one, gain_one)
    matrices = (grad_qkv_w, grad_out_w, grad_up, grad_down)
    vectors = (
        grad_query_bias,
        grad_value_bias,
        grad_out_bias,
        grad_up_bias,
        grad_down_bias,
        grad_gain_one,
        grad_shift_one,
        grad_gain_two,
        grad_shift_two,
    )
    totals = sectioned_sum(matrices + vectors)
    return (
        output_rows[None],
        grad_input[None],
        totals[9],
        totals[10],
        totals[0],
        totals[4],
        totals[5],
        totals[1],
        totals[6],
        totals[11],
        totals[12],
        totals[2],
        totals[7],
        totals[3],
        totals[8],
    )


SLOTS = 5
WIDE = 384
ROWS = 256
HALF = ROWS // 2
CHIPS = 4
TILE = 128
UP_ROWS, DOWN_ROWS = (144, 160)
MESH_ID = pl.DeviceIdType.MESH
F32, BF16 = (jnp.float32, jnp.bfloat16)
NEG = -1e30
HEAD_TABLE = ((0, 5, 9, 13, -40), (1, 6, 10, 14, -40), (2, 7, 11, 15, -40), (3, 4, 8, 12, 16))
B_QUERY, B_VALUE, B_OUT, B_DOWN, GAIN_1, SHIFT_1, GAIN_2, SHIFT_2, B_UP = range(9)


def nn(left, right):
    return jnp.dot(left, right, preferred_element_type=F32)


def remote(src, dst, send, recv, where):
    return pltpu.make_async_remote_copy(
        src_ref=src, dst_ref=dst, send_sem=send, recv_sem=recv, device_id=where, device_id_type=MESH_ID
    )


def rows16(start, size):
    return pl.ds(pl.multiple_of(start, 16), size)


class Place:
    def __init__(self):
        self.c, self.z = (lax.axis_index("ctx"), lax.axis_index("wsh"))
        self.t, self.p = (self.c // 2, self.c % 2)
        self.tx, self.ty, self.td = (self.flip(1, 0), self.flip(0, 1), self.flip(1, 1))

    def flip(self, dx, dy):
        return (self.t // 2 + dy) % 2 * 2 + (self.t % 2 + dx) % 2

    def chip(self, chip):
        return (chip * 2 + self.p, self.z)

    def twin(self):
        return (self.t * 2 + 1 - self.p, self.z)

    def plane(self, step):
        return (self.c, (self.z + step) % 4)

    def greet(self, planes=True):
        barrier = pltpu.get_barrier_semaphore()
        others = [self.chip(self.tx), self.chip(self.ty), self.twin()]
        if planes:
            others += [self.plane(1), self.plane(2), self.plane(3)]
        for where in others:
            pl.semaphore_signal(barrier, inc=1, device_id=where, device_id_type=MESH_ID)
        pl.semaphore_wait(barrier, len(others))


class Gather:
    def __init__(self, e, own, view, rows, cut, send, recv):
        self.e, self.own, self.view, self.send, self.recv = (e, own, view, send, recv)
        self.parts = (pl.ds(0, cut), pl.ds(cut, rows - cut))

    def copy(self, i):
        e = self.e
        chip = (e.t, e.t, e.t, e.t, e.tx, e.ty)[i]
        part = self.parts[(0, 1, 1, 0, 0, 1)[i]]
        src = self.own if i < 4 else self.view(chip)
        where = e.chip((e.tx, e.tx, e.ty, e.ty, e.ty, e.tx)[i])
        return remote(src.at[part], self.view(chip).at[part], self.send.at[i], self.recv.at[i], where)

    def start(self):
        for i in (0, 2, 1, 3):
            self.copy(i).start()

    def forward(self):
        self.copy(0).wait_recv()
        self.copy(4).start()
        self.copy(2).wait_recv()
        self.copy(5).start()

    def have_x(self):
        self.copy(1).wait_recv()

    def have_y(self):
        self.copy(3).wait_recv()

    def have_far(self):
        self.copy(4).wait_recv()
        self.copy(5).wait_recv()

    def sent(self):
        for i in range(6):
            self.copy(i).wait_send()


class Scatter:
    def __init__(self, e, part, land, send, recv):
        self.e, self.part, self.land, self.send, self.recv = (e, part, land, send, recv)

    def copy(self, i):
        e = self.e
        chip = (e.td, e.td, e.tx, e.tx, e.ty, e.ty)[i]
        part = pl.ds((0, HALF, 0, HALF, HALF, 0)[i], HALF)
        where = e.chip((e.tx, e.ty, e.tx, e.tx, e.ty, e.ty)[i])
        return remote(
            self.part.at[chip, part], self.land.at[i], self.send.at[i], self.recv.at[i], where
        )

    def far_ready(self):
        self.copy(0).start()
        self.copy(1).start()

    def x_ready(self):
        self.copy(2).start()

    def y_ready(self):
        self.copy(4).start()

    def relay(self):
        self.copy(1).wait_recv()
        chip = self.e.tx
        self.part[chip, HALF:] = (self.part[chip, HALF:].astype(F32) + self.land[1].astype(F32)).astype(BF16)
        self.copy(3).start()
        self.copy(0).wait_recv()
        chip = self.e.ty
        self.part[chip, :HALF] = (self.part[chip, :HALF].astype(F32) + self.land[0].astype(F32)).astype(BF16)
        self.copy(5).start()

    def total(self):
        for i in (2, 4, 3, 5):
            self.copy(i).wait_recv()
        first = self.land[2].astype(F32) + self.land[5].astype(F32)
        second = self.land[4].astype(F32) + self.land[3].astype(F32)
        return jnp.concatenate([first, second], 0)

    def sent(self):
        for i in range(6):
            self.copy(i).wait_send()


class ZGather:
    def __init__(self, e, own, held, send, recv, put):
        self.e, self.own, self.held, self.send, self.recv, self.put = (e, own, held, send, recv, put)

    def copy(self, way, j):
        e = self.e
        shard = e.z - j if way == 0 else e.z + j
        src = self.own if j == 0 else self.held.at[shard]
        return remote(
            src, self.held.at[shard], self.send.at[way, j], self.recv.at[way, j], e.plane(1 if way == 0 else 3)
        )

    def sends(self, way, j):
        z = self.e.z
        return (z < 3) & (z >= j) if way == 0 else (z > 0) & (z <= 3 - j)

    def step(self, j):
        z = self.e.z
        for way in range(2):
            if j > 0:
                @pl.when(z >= j if way == 0 else z <= 3 - j)
                def _():
                    self.copy(way, j - 1).wait_recv()
            if j < 3:
                @pl.when(self.sends(way, j))
                def _():
                    self.copy(way, j).start()
            if j > 0:
                @pl.when(z >= j if way == 0 else z <= 3 - j)
                def _():
                    self.put(z - j if way == 0 else z + j)

    def sent(self):
        for way in range(2):
            for j in range(3):
                @pl.when(self.sends(way, j))
                def _():
                    self.copy(way, j).wait_send()


class ZScatter:
    def __init__(self, e, own, staged, right, left, send, recv):
        self.e, self.own, self.staged, self.land = (e, own, staged, (right, left))
        self.send, self.recv = (send, recv)

    def copy(self, way, j, src):
        return remote(
            src, self.land[way].at[j], self.send.at[way, j], self.recv.at[way, j],
            self.e.plane(1 if way == 0 else 3),
        )

    def begin(self):
        for plane, way in ((0, 0), (3, 1)):
            @pl.when(self.e.z == plane)
            def _():
                for j in range(3):
                    self.copy(way, j, self.own.at[3 - j if way == 0 else j]).start()

    def relay(self, way, j):
        dest = 3 - j if way == 0 else j
        self.copy(way, j, self.staged.at[dest]).wait_recv()
        self.staged[dest] = (self.own[dest].astype(F32) + self.land[way][j].astype(F32)).astype(BF16)
        self.copy(way, j, self.staged.at[dest]).start()

    def first(self):
        for plane, way in ((1, 0), (2, 1)):
            @pl.when(self.e.z == plane)
            def _():
                self.relay(way, 0)

    def second(self):
        for plane, way in ((1, 0), (2, 1)):
            @pl.when(self.e.z == plane)
            def _():
                self.relay(1 - way, 0)
                self.relay(way, 1)

    def last(self, out):
        right, left = self.land
        for z in range(4):
            @pl.when(self.e.z == z)
            def _():
                total = self.own[z].astype(F32)
                if z > 0:
                    self.copy(0, 3 - z, self.own.at[z]).wait_recv()
                    total = total + right[3 - z].astype(F32)
                if z < 3:
                    self.copy(1, z, self.own.at[z]).wait_recv()
                    total = total + left[z].astype(F32)
                out[...] = total.astype(BF16)
                for way in range(2):
                    for j in range((3 - z) if way == 0 else z):
                        self.copy(way, j, self.own.at[z]).wait_send()


def dma(*shape):
    return pltpu.SemaphoreType.DMA(shape)


def params(number, mib=56):
    return pltpu.CompilerParams(
        collective_id=number, has_side_effects=True, vmem_limit_bytes=mib * 2**20
    )


def vmem(count):
    return [pl.BlockSpec(memory_space=pltpu.VMEM)] * count


class Halves:
    def __init__(self, e, whole, block, keep, step, local, send, recv):
        self.e, self.whole, self.block, self.keep, self.step = (e, whole, block, keep, step)
        self.local, self.send, self.recv = (local, send, recv)

    def copies(self, src, shard):
        e = self.e
        return (
            pltpu.make_async_copy(
                src, self.whole.at[rows16(shard * self.block + e.p * self.step, self.keep)], self.local.at[shard]
            ),
            remote(
                src.at[rows16(e.p * (self.keep - self.step), self.step)],
                self.whole.at[rows16(shard * self.block + e.p * self.keep, self.step)],
                self.send.at[shard], self.recv.at[shard], e.twin(),
            ),
        )

    def put(self, src, shard):
        for copy in self.copies(src, shard):
            copy.start()

    def wait(self, src):
        for shard in range(4):
            for copy in self.copies(src, shard):
                copy.wait()


def half_tiles(source, columns):
    def piece(column, side):
        if column is None:
            return jnp.zeros((source.shape[0], TILE), F32)
        start = column // TILE * TILE
        if start + TILE > source.shape[-1]:
            part = source[:, start : start + HEAD_DIM].astype(F32)
            tile = jnp.concatenate([part, jnp.zeros_like(part)], 1)
        else:
            tile = source[:, start : start + TILE].astype(F32)
        return tile if column % TILE // HEAD_DIM == side else pltpu.roll(tile, HEAD_DIM, 1)

    tiles = []
    for i in range(0, len(columns), 2):
        first, second = (piece(columns[i], 0), piece(columns[i + 1], 1))
        lane = lax.broadcasted_iota(jnp.int32, first.shape, 1)
        tiles.append(jnp.where(lane < HEAD_DIM, first, second))
    return tiles


def head_columns(heads, first):
    return [first + head * HEAD_DIM if head >= 0 else None for head in heads] + [None]


def project_kernel(
    x, cot, bias_0, bias_1, bias_2, bias_3, bias_4, bias_5, bias_6, bias_7, b_up, w_qkv, w_out, w_up, w_down,
    q_out, k_out, v_out, h_out, whole, out_w, vecs, halves, cot_out, x_out,
    qkv_rows, half, half_o, edge, held, held_o, raw, vec_in, vec_land, bias,
    v_send, v_recv, z_send, z_recv, a_send, a_recv, w_local, w_send, w_recv, kv_send, kv_recv, r_local,
):
    e = Place()
    t, p, z = (e.t, e.p, e.z)
    rows = pltpu.make_async_copy(w_qkv.at[rows16(p * TILE, 144)], qkv_rows, r_local.at[0])
    rows.start()
    loads = []
    for i in range(4):
        column = pl.multiple_of(D * i + HEAD_DIM * (i % 2) + 256 * t, TILE)
        loads.append((w_up.at[rows16(p * TILE, 144), pl.ds(column, 256)], halves.at[pl.ds(0, 144), pl.ds(256 * i, 256)]))
    column = pl.multiple_of(1024 + 2 * D * (t // 2), TILE)
    loads.append((w_up.at[rows16(p * TILE, 144), pl.ds(column, TILE)], edge))
    loads.append((w_down.at[rows16(HEAD_DIM * (z % 2) + 256 * t + TILE * p, TILE)], halves.at[pl.ds(144, TILE)]))
    loads.append((w_down.at[rows16(1024 * (1 - z % 2) + 32 * p, 32)], halves.at[pl.ds(272, 32)]))
    loads = [pltpu.make_async_copy(src, dst, r_local.at[1 + i]) for i, (src, dst) in enumerate(loads)]
    for copy in loads:
        copy.start()
    spot = lax.broadcasted_iota(jnp.int32, (D // 4, D), 1) - D // 4 * z
    match = (spot == lax.broadcasted_iota(jnp.int32, (D // 4, D), 0)).astype(F32).astype(BF16)
    biases = (bias_0, bias_1, bias_2, bias_3, bias_4, bias_5, bias_6, bias_7)
    biases = jnp.concatenate([ref[...].astype(F32).reshape(1, D // 4) for ref in biases], 0)
    vec_in[0] = nn(biases.astype(BF16), match)
    e.greet()

    def exchange(i):
        return [
            remote(vec_in.at[i], vec_land.at[k, i], v_send.at[i, k], v_recv.at[i, k], e.plane(k))
            for k in range(1, 4)
        ]

    vectors = exchange(0)
    for copy in vectors:
        copy.start()
    into = Halves(e, whole, 272, 144, 128, w_local.at[0], w_send.at[0], w_recv.at[0])
    into_o = Halves(e, raw, 80, 48, 32, w_local.at[1], w_send.at[1], w_recv.at[1])
    chain = ZGather(
        e, half, held, z_send.at[0], z_recv.at[0], lambda shard: into.put(held.at[shard], shard)
    )
    chain_o = ZGather(
        e, half_o, held_o, z_send.at[1], z_recv.at[1], lambda shard: into_o.put(held_o.at[shard], shard)
    )
    rows.wait()
    for chip in range(CHIPS):
        @pl.when(t == chip)
        def _():
            for a in range(3):
                tiles = half_tiles(qkv_rows, head_columns(HEAD_TABLE[chip], a * D))
                for i in range(3):
                    half[:, a * WIDE + i * TILE : a * WIDE + (i + 1) * TILE] = tiles[i].astype(BF16)

    chain.step(0)
    into.put(half, z)
    inputs = x[...].astype(F32).T
    x_out[...] = inputs.astype(BF16)
    normed, _ = normalize(inputs)
    total = vec_in[0]
    for k in range(1, 4):
        vectors[k - 1].wait_recv()
        total = total + vec_land[k, 0]
    vecs[:8] = total
    h_out[t] = (normed * vecs[GAIN_1 : GAIN_1 + 1] + vecs[SHIFT_1 : SHIFT_1 + 1]).astype(BF16)
    hidden = Gather(e, h_out.at[t], lambda chip: h_out.at[chip], ROWS, HALF, a_send, a_recv)
    hidden.start()
    ahead = (CHIPS - z) % CHIPS * 16
    for m in range(3):
        unit = 16 * (2 * p + m)
        late = jnp.where(unit < ahead, unit, 192 + unit)
        first = jnp.where(t < CHIPS - 1, ahead + HEAD_DIM * t + unit, late)
        half_o[16 * m : 16 * m + 16] = w_out[rows16(first, 16)]
    for chip in range(CHIPS):
        @pl.when(t == chip)
        def _():
            tiles = half_tiles(vecs, head_columns(HEAD_TABLE[chip], 0))
            for i in range(3):
                bias[:, i * TILE : (i + 1) * TILE] = tiles[i]

    spot = lax.broadcasted_iota(jnp.int32, (D, 320), 1)
    at = jnp.where(spot < 256, HEAD_DIM * (z % 2) + 256 * t + spot, 1024 * (1 - z % 2) + spot - 256)
    match = (lax.broadcasted_iota(jnp.int32, (D, 320), 0) == at).astype(F32).astype(BF16)
    ups = nn(b_up[...].astype(F32).reshape(1, D).astype(BF16), match)
    vec_in[1] = jnp.zeros((8, D), F32)
    for i in range(4):
        @pl.when(z == i)
        def _():
            vec_in[1, 0:1, 256 * i : 256 * i + 256] = ups[0:1, :256]

    @pl.when(z == t)
    def _():
        vec_in[1, 0:1, 1024:] = ups[0:1, 256:]

    vectors = vectors + exchange(1)
    for copy in vectors[3:]:
        copy.start()
    cot_out[:ROWS] = cot[...].astype(F32).T.astype(BF16)
    cot_out[ROWS:] = jnp.zeros((8, D), BF16)
    for copy in loads:
        copy.wait()
    column = edge[...].astype(F32)
    column = jnp.where(t % 2 == 1, pltpu.roll(column, HEAD_DIM, 1), column)
    halves[:144, 1024:] = column[:, :HEAD_DIM].astype(BF16)
    chain.step(1)
    hidden.forward()
    chain.step(2)
    chain_o.step(0)
    into_o.put(half_o, z)
    total = vec_in[1]
    for k in range(1, 4):
        vectors[2 + k].wait_recv()
        total = total + vec_land[k, 1]
    vecs[8:] = total
    chain.step(3)
    into.wait(half)

    def block(k, carry):
        src = e.flip((k + 1) // 2 % 2, k // 2)

        @pl.when(k == 1)
        def _():
            hidden.have_x()

        @pl.when(k == 2)
        def _():
            hidden.have_far()

        @pl.when(k == 3)
        def _():
            hidden.have_y()

        h = h_out[src]
        bias_q, bias_v = (bias[B_QUERY : B_QUERY + 1], bias[B_VALUE : B_VALUE + 1])
        q_out[src] = ((nn(h, whole[:, :WIDE]) + bias_q).astype(BF16) * 0.125).astype(BF16)
        mine = src * 2 + p
        k_out[mine] = nn(h, whole[:, WIDE : 2 * WIDE]).astype(BF16)
        remote(k_out.at[mine], k_out.at[mine], kv_send.at[k], kv_recv.at[k], e.twin()).start()
        v_out[mine] = (nn(h, whole[:, 2 * WIDE :]) + bias_v).astype(BF16)
        remote(
            v_out.at[mine], v_out.at[mine], kv_send.at[k + CHIPS], kv_recv.at[k + CHIPS], e.twin()
        ).start()
        return carry

    lax.fori_loop(0, CHIPS, block, 0)
    chain_o.step(1)
    chain_o.step(2)
    chain_o.step(3)
    into_o.wait(half_o)

    @pl.when(t == CHIPS - 1)
    def _():
        out_w[: SLOTS * HEAD_DIM] = raw[...]

    @pl.when(t < CHIPS - 1)
    def _():
        for i in range(4):
            out_w[i * HEAD_DIM : (i + 1) * HEAD_DIM] = raw[i * 80 : i * 80 + HEAD_DIM]
        out_w[4 * HEAD_DIM : 5 * HEAD_DIM] = jnp.zeros((HEAD_DIM, D), BF16)

    out_w[SLOTS * HEAD_DIM :] = jnp.zeros((WIDE - SLOTS * HEAD_DIM, D), BF16)
    for k in range(CHIPS):
        src = e.flip((k + 1) // 2 % 2, k // 2)
        other = src * 2 + 1 - p
        mine = src * 2 + p
        for ref, j in ((k_out, k), (v_out, k + CHIPS)):
            remote(ref.at[mine], ref.at[mine], kv_send.at[j], kv_recv.at[j], e.twin()).wait_send()
            remote(ref.at[other], ref.at[other], kv_send.at[j], kv_recv.at[j], e.twin()).wait_recv()
    for user in (hidden, chain, chain_o):
        user.sent()
    for copy in vectors:
        copy.wait_send()


def project(x, cot, biases, b_up, w_qkv, w_out, w_up, w_down):
    blocks = jax.ShapeDtypeStruct((CHIPS, ROWS, WIDE), BF16)
    keys = jax.ShapeDtypeStruct((2 * CHIPS, ROWS, WIDE), BF16)
    near, far = (vmem(1), [pl.BlockSpec(memory_space=pl.ANY)])
    return pl.pallas_call(
        project_kernel,
        out_shape=(
            blocks, keys, keys,
            jax.ShapeDtypeStruct((CHIPS, ROWS, D), BF16),
            jax.ShapeDtypeStruct((D, 3 * WIDE), BF16),
            jax.ShapeDtypeStruct((WIDE, D), BF16),
            jax.ShapeDtypeStruct((16, D), F32),
            jax.ShapeDtypeStruct((UP_ROWS + DOWN_ROWS, D), BF16),
            jax.ShapeDtypeStruct((ROWS + 8, D), BF16),
            jax.ShapeDtypeStruct((ROWS, D), BF16),
        ),
        in_specs=near * 11 + far + near + far * 2,
        out_specs=tuple(near * 10),
        scratch_shapes=[
            pltpu.VMEM((144, 3 * D), BF16),
            pltpu.VMEM((144, 3 * WIDE), BF16),
            pltpu.VMEM((48, D), BF16),
            pltpu.VMEM((144, TILE), BF16),
            pltpu.VMEM((4, 144, 3 * WIDE), BF16),
            pltpu.VMEM((4, 48, D), BF16),
            pltpu.VMEM((SLOTS * HEAD_DIM, D), BF16),
            pltpu.VMEM((2, 8, D), F32),
            pltpu.VMEM((4, 2, 8, D), F32),
            pltpu.VMEM((16, WIDE), F32),
            dma(2, 4), dma(2, 4), dma(2, 2, 3), dma(2, 2, 3), dma(6), dma(6),
            dma(2, 4), dma(2, 4), dma(2, 4), dma(2 * CHIPS), dma(2 * CHIPS), dma(8),
        ],
        compiler_params=params(1),
        name="project",
    )(x, cot, *biases, b_up, w_qkv, w_out, w_up, w_down)


def tile_bounds(lengths, block):
    ends = [lengths[0]]
    for i in range(1, 4):
        ends.append(ends[-1] + lengths[i])
    first = block * ROWS
    start_first = 0 * first
    for end in ends:
        start_first = jnp.where(first >= end, end, start_first)
    free = jnp.minimum(block, ends[0] // ROWS)
    resume = jnp.maximum(free + 1, start_first // ROWS)
    masked = jnp.where(free < block, 1 + jnp.maximum(block - resume, 0), 0)
    query_pos = first + lax.broadcasted_iota(jnp.int32, (1, ROWS), 1)
    start = jnp.zeros((1, ROWS), jnp.int32)
    for end in ends:
        start = jnp.where(query_pos >= end, end, start)
    return ends[0], query_pos, start, free, resume, masked


def visible(key_block, prompt, query_pos, start):
    key_pos = key_block * ROWS + lax.broadcasted_iota(jnp.int32, (ROWS, ROWS), 0)
    return (key_pos <= query_pos) & ((key_pos < prompt) | (key_pos >= start))


def half_of(rows, h):
    lane = lax.broadcasted_iota(jnp.int32, rows.shape, 1)
    return jnp.where((lane >= h * HEAD_DIM) & (lane < (h + 1) * HEAD_DIM), rows, jnp.zeros_like(rows))


def attend_kernel(lengths, parity, q, k, v, mixed, lse, turned):
    slab = pl.program_id(0)
    for j in range(2 * CHIPS):
        turned[j] = v[j].astype(F32).T.astype(BF16)

    def run(heads):
        def one(i, carry):
            block = 2 * i + parity[0]
            prompt, query_pos, start, free, resume, masked = tile_bounds(lengths, block)
            queries = [half_of(q[i], h) for h in heads]

            def tile(j, state, mask):
                keys = k[j]
                values = turned[j]
                new = []
                for h, (peak, total, accum) in zip(heads, state):
                    scores = cols_product(keys, queries[h])
                    if mask is not None:
                        scores = jnp.where(mask, scores, NEG)
                    peak_new = jnp.maximum(peak, jnp.max(scores, 0, keepdims=True))
                    factor = jnp.exp(peak - peak_new)
                    expos = jnp.exp(scores - peak_new)
                    total_new = total * factor + jnp.sum(expos, 0, keepdims=True)
                    part = values[h * HEAD_DIM : (h + 1) * HEAD_DIM]
                    accum_new = accum * factor + nn(part, expos.astype(BF16))
                    new.append((peak_new, total_new, accum_new))
                return tuple(new)

            state = tuple(
                (
                    jnp.full((1, ROWS), NEG, F32),
                    jnp.zeros((1, ROWS), F32),
                    jnp.zeros((HEAD_DIM, ROWS), F32),
                )
                for _ in heads
            )

            def other(m, s):
                j = jnp.where(m == 0, block, jnp.where(m == 1, free, resume + m - 2))
                return tile(j, s, visible(j, prompt, query_pos, start))

            state = lax.fori_loop(0, 1 + masked, other, state)
            state = lax.fori_loop(0, free, lambda j, s: tile(j, s, None), state)
            outs = []
            for h, (peak, total, accum) in zip(heads, state):
                outs.append(accum / total)
                lse[0, pl.ds(h * CHIPS + i, 1), :] = peak + jnp.log(total)
            if len(heads) == 1:
                outs.append(jnp.zeros((HEAD_DIM, ROWS), F32))
            mixed[i] = jnp.concatenate(outs, 0).T.astype(BF16)
            return carry

        lax.fori_loop(0, CHIPS, one, 0)

    @pl.when(slab < SLOTS // 2)
    def _():
        run((0, 1))

    @pl.when(slab >= SLOTS // 2)
    def _():
        lse[...] = jnp.zeros_like(lse)
        run((0,))


def slab_spec(count):
    return pl.BlockSpec((count, ROWS, 128), lambda s, *_: (0, 0, s))


def attend(lengths, parity, q, k, v):
    return pl.pallas_call(
        attend_kernel,
        out_shape=(
            jax.ShapeDtypeStruct((CHIPS, ROWS, WIDE), BF16),
            jax.ShapeDtypeStruct((3, 2 * CHIPS, ROWS), F32),
        ),
        grid_spec=pltpu.PrefetchScalarGridSpec(
            num_scalar_prefetch=2,
            grid=(3,),
            in_specs=[slab_spec(CHIPS), slab_spec(2 * CHIPS), slab_spec(2 * CHIPS)],
            out_specs=(
                slab_spec(CHIPS),
                pl.BlockSpec((1, 2 * CHIPS, ROWS), lambda s, *_: (s, 0, 0)),
            ),
            scratch_shapes=[pltpu.VMEM((2 * CHIPS, 128, ROWS), BF16)],
        ),
        compiler_params=pltpu.CompilerParams(vmem_limit_bytes=63 * 2**20),
        cost_estimate=pl.CostEstimate(flops=4 * 10**9, bytes_accessed=5 * 10**6, transcendentals=6 * 10**6),
        name="attend",
    )(lengths, parity, q, k, v)


def attend_back_kernel(
    lengths, parity, q, k, v, mixed, grad, lse, dq, dk, dv, turned, acc_k, acc_v
):
    slab = pl.program_id(0)
    for j in range(2 * CHIPS):
        turned[j] = k[j].astype(F32).T.astype(BF16)
    acc_k[...] = jnp.zeros_like(acc_k)
    acc_v[...] = jnp.zeros_like(acc_v)

    def run(heads):
        def one(i, carry):
            block = 2 * i + parity[0]
            prompt, query_pos, start, free, resume, masked = tile_bounds(lengths, block)
            queries = [half_of(q[i], h) for h in heads]
            grads = [half_of(grad[i], h) for h in heads]
            product = (grad[i].astype(F32) * mixed[i].astype(F32)).T
            deltas = [
                jnp.sum(product[h * HEAD_DIM : (h + 1) * HEAD_DIM], 0, keepdims=True) for h in heads
            ]
            sums = [lse[0, pl.ds(h * CHIPS + i, 1), :] for h in heads]

            def tile(j, state, mask):
                keys, values, keys_t = (k[j], v[j], turned[j])
                new = []
                add_k, add_v = (None, None)
                for h, accum in zip(heads, state):
                    scores = cols_product(keys, queries[h]) - sums[h]
                    if mask is not None:
                        scores = jnp.where(mask, scores, NEG)
                    probs = jnp.exp(scores)
                    grad_probs = cols_product(values, grads[h])
                    ds = (probs * (grad_probs - deltas[h])).astype(BF16)
                    part_v = nn(probs.astype(BF16), grads[h])
                    part_k = nn(ds, queries[h])
                    add_v = part_v if add_v is None else add_v + part_v
                    add_k = part_k if add_k is None else add_k + part_k
                    new.append(accum + nn(keys_t[h * HEAD_DIM : (h + 1) * HEAD_DIM], ds))
                acc_v[j] += add_v
                acc_k[j] += add_k
                return tuple(new)

            state = tuple(jnp.zeros((HEAD_DIM, ROWS), F32) for _ in heads)

            def other(m, s):
                j = jnp.where(m == 0, block, jnp.where(m == 1, free, resume + m - 2))
                return tile(j, s, visible(j, prompt, query_pos, start))

            state = lax.fori_loop(0, 1 + masked, other, state)
            state = list(lax.fori_loop(0, free, lambda j, s: tile(j, s, None), state))
            if len(heads) == 1:
                state.append(jnp.zeros((HEAD_DIM, ROWS), F32))
            dq[i] = (jnp.concatenate(state, 0) * 0.125).T.astype(BF16)
            return carry

        lax.fori_loop(0, CHIPS, one, 0)

    @pl.when(slab < SLOTS // 2)
    def _():
        run((0, 1))

    @pl.when(slab >= SLOTS // 2)
    def _():
        run((0,))

    dk[...] = acc_k[...].astype(BF16)
    dv[...] = acc_v[...].astype(BF16)


def attend_back(lengths, parity, q, k, v, mixed, grad, lse):
    few, many = (slab_spec(CHIPS), slab_spec(2 * CHIPS))
    return pl.pallas_call(
        attend_back_kernel,
        out_shape=(
            jax.ShapeDtypeStruct((CHIPS, ROWS, WIDE), BF16),
            jax.ShapeDtypeStruct((2 * CHIPS, ROWS, WIDE), BF16),
            jax.ShapeDtypeStruct((2 * CHIPS, ROWS, WIDE), BF16),
        ),
        grid_spec=pltpu.PrefetchScalarGridSpec(
            num_scalar_prefetch=2,
            grid=(3,),
            in_specs=[
                few, many, many, few, few,
                pl.BlockSpec((1, 2 * CHIPS, ROWS), lambda s, *_: (s, 0, 0)),
            ],
            out_specs=(few, many, many),
            scratch_shapes=[
                pltpu.VMEM((2 * CHIPS, 128, ROWS), BF16),
                pltpu.VMEM((2 * CHIPS, ROWS, 128), F32),
                pltpu.VMEM((2 * CHIPS, ROWS, 128), F32),
            ],
        ),
        compiler_params=pltpu.CompilerParams(vmem_limit_bytes=63 * 2**20),
        cost_estimate=pl.CostEstimate(flops=10 * 10**9, bytes_accessed=9 * 10**6, transcendentals=6 * 10**6),
        name="attend_back",
    )(lengths, parity, q, k, v, mixed, grad, lse)


def out_kernel(x, mixed, whole, vecs, middle, part, land, send, recv):
    e = Place()
    e.greet(planes=False)
    sums = Scatter(e, part, land, send, recv)

    def block(k, carry):
        dest = e.flip(1 - k // 2, 1 - k % 2)
        part[dest] = nn(mixed[dest], whole[...]).astype(BF16)

        @pl.when(k == 0)
        def _():
            sums.far_ready()

        @pl.when(k == 1)
        def _():
            sums.x_ready()

        @pl.when(k == 2)
        def _():
            sums.y_ready()

        return carry

    lax.fori_loop(0, CHIPS - 1, block, 0)
    total = x[...].astype(F32) + vecs[B_OUT : B_OUT + 1] + nn(mixed[e.t], whole[...])
    sums.relay()
    middle[...] = total + sums.total()
    sums.sent()


def out_project(x, mixed, whole, vecs):
    return pl.pallas_call(
        out_kernel,
        out_shape=jax.ShapeDtypeStruct((ROWS, D), F32),
        in_specs=vmem(4),
        out_specs=vmem(1)[0],
        scratch_shapes=[
            pltpu.VMEM((CHIPS, ROWS, D), BF16),
            pltpu.VMEM((6, HALF, D), BF16),
            dma(6), dma(6),
        ],
        compiler_params=params(2),
        name="out_project",
    )(x, mixed, whole, vecs)


def feed_kernel(
    middle, cot, cot_x, cot_y, cot_far, halves, vecs, out_w, mixed,
    to_x, to_y, to_far, out_own, grad_mid, gh_heads, g_out, g_down, share, sums, up_sum,
    up, down, lefts, rights, part_h, gmid, sum_h_land,
    full, grad_sum, land_up, land_down, land_more, g_up, staged, z_right, z_left, raw, land_out,
    a_send, a_recv, s_send, s_recv, w_local, w_send, w_recv, d_local, d_send, d_recv, g_send, g_recv, z_send, z_recv, c_local,
):
    e = Place()
    t, p = (e.t, e.p)
    hid, act, gpre, cots = (lefts.at[0], lefts.at[1], rights.at[0], rights.at[1])
    full_up, full_down = (full.at[0], full.at[1])
    e.greet()
    into = Halves(e, up, 272, 144, 128, w_local, w_send, w_recv)
    weights = []
    for i in range(4):
        weights.extend(into.copies(halves.at[i, pl.ds(0, 144)], i))
    for i in range(5):
        src = halves.at[i, pl.ds(144, TILE)] if i < 4 else halves.at[t, pl.ds(272, 32)]
        dst = down.at[rows16(256 * i + p * TILE, TILE) if i < 4 else rows16(1024 + p * 32, 32)]
        weights.append(pltpu.make_async_copy(src, dst, d_local.at[i]))
        weights.append(remote(src, dst, d_send.at[i], d_recv.at[i], e.twin()))
    for k, (ref, chip) in enumerate(((cot, t), (cot_x, e.tx), (cot_y, e.ty), (cot_far, e.td))):
        weights.append(pltpu.make_async_copy(ref.at[pl.ds(0, ROWS)], cots.at[chip], c_local.at[k]))
    for copy in weights:
        copy.start()
    normed, inverse = normalize(middle[...])
    hid[t] = (normed * vecs[GAIN_2 : GAIN_2 + 1] + vecs[SHIFT_2 : SHIFT_2 + 1]).astype(BF16)
    hidden = Gather(e, hid.at[t], lambda chip: hid.at[chip], ROWS, HALF, a_send.at[0], a_recv.at[0])
    hidden.start()
    sum_h = Scatter(e, part_h, sum_h_land, s_send, s_recv)
    for copy in weights:
        copy.wait()
    up_sum[...] = jnp.zeros_like(up_sum)

    def block(k, carry):
        src = e.flip((k + 1) // 2 % 2, k // 2)

        @pl.when(k == 1)
        def _():
            hidden.forward()
            hidden.have_x()

        @pl.when(k == 2)
        def _():
            hidden.have_far()

        @pl.when(k == 3)
        def _():
            hidden.have_y()

        pre = nn(hid[src], up[...]) + vecs[B_UP : B_UP + 1]
        cdf = 0.5 * (1.0 + lax.erf(pre * math.sqrt(0.5)))
        slope = cdf + pre * (jnp.exp(-0.5 * pre * pre) * (1.0 / math.sqrt(2.0 * math.pi)))
        act[src] = (pre * cdf).astype(BF16)
        grad = cols_product(cots[src], down[...]) * slope
        low = grad.astype(BF16)
        gpre[src] = low
        up_sum[...] += jnp.sum(low.astype(F32), 0, keepdims=True)
        part_h[src] = cols_product(low, up[...]).astype(BF16)

        @pl.when(k == 1)
        def _():
            sum_h.x_ready()

        @pl.when(k == 2)
        def _():
            sum_h.far_ready()

        @pl.when(k == 3)
        def _():
            sum_h.y_ready()

        return carry

    lax.fori_loop(0, CHIPS, block, 0)
    sum_h.relay()

    ups = [
        remote(
            full_up.at[rows16(i * 272 + (1 - p) * TILE, UP_ROWS)], land_up.at[i],
            g_send.at[0, i], g_recv.at[0, i], e.twin(),
        )
        for i in range(4)
    ]

    def matrices(i, carry):
        full[i] = rows_product(
            lefts[i].reshape(CHIPS * ROWS, D), rights[i].reshape(CHIPS * ROWS, D)
        ).astype(BF16)

        @pl.when(i == 0)
        def _():
            for copy in ups:
                copy.start()

        return carry

    lax.fori_loop(0, 2, matrices, 0)
    swaps = [
        remote(
            full_down.at[rows16(256 * i + (1 - p) * TILE, TILE)], land_down.at[i],
            g_send.at[1, i], g_recv.at[1, i], e.twin(),
        )
        for i in range(4)
    ]
    swaps.append(
        remote(
            full_down.at[rows16(1024 + (1 - p) * 32, 32)], land_more, g_send.at[2, 0], g_recv.at[2, 0], e.twin()
        )
    )
    for copy in swaps:
        copy.start()
    for copy in ups:
        copy.wait()
    for i in range(4):
        own = full_up[rows16(i * 272 + p * TILE, UP_ROWS)].astype(F32)
        g_up[i] = (own + land_up[i].astype(F32)).astype(BF16)
    planes = ZScatter(e, g_up, staged, z_right, z_left, z_send, z_recv)
    planes.begin()
    def outs(k, carry):
        rows = nn(act[e.flip(k % 2, k // 2)], down[...])
        for i, ref in enumerate((out_own, to_x, to_y, to_far)):
            @pl.when(k == i)
            def _():
                if i == 0:
                    ref[...] = middle[...] + vecs[B_DOWN : B_DOWN + 1] + rows
                else:
                    ref[:ROWS] = rows.astype(BF16)

        return carry

    lax.fori_loop(0, CHIPS, outs, 0)

    total = part_h[t].astype(F32) + sum_h.total()
    top = cot[:ROWS].astype(F32)
    grad_middle = top + norm_back(total, normed, inverse, vecs[GAIN_2 : GAIN_2 + 1])
    grad_mid[...] = grad_middle
    low = grad_middle.astype(BF16)
    gmid[t] = low
    spread = Gather(e, gmid.at[t], lambda chip: gmid.at[chip], ROWS, HALF, a_send.at[1], a_recv.at[1])
    spread.start()
    sums[0:1] = jnp.sum(low.astype(F32), 0, keepdims=True)
    sums[1:2] = jnp.sum(top, 0, keepdims=True)
    sums[2:3] = jnp.sum(total * normed, 0, keepdims=True)
    sums[3:4] = jnp.sum(total, 0, keepdims=True)
    sums[4:8] = jnp.zeros((4, D), F32)

    planes.first()
    for copy in swaps:
        copy.wait()
    more = (full_down[rows16(1024 + p * 32, 32)].astype(F32) + land_more[...].astype(F32)).astype(BF16)
    for i in range(4):
        own = full_down[rows16(256 * i + p * TILE, TILE)].astype(F32)
        g_down[i, :TILE] = (own + land_down[i].astype(F32)).astype(BF16)
        g_down[i, TILE:] = more
    spread.forward()
    planes.second()

    def heads(k, carry):
        src = e.flip((k + 1) // 2 % 2, k // 2)

        @pl.when(k == 1)
        def _():
            spread.have_x()

        @pl.when(k == 2)
        def _():
            spread.have_far()

        @pl.when(k == 3)
        def _():
            spread.have_y()

        rows = gmid[src]
        gh_heads[src] = cols_product(rows, out_w[...]).astype(BF16)
        grad_sum[...] += rows_product(mixed[src], rows)
        return carry

    grad_sum[...] = jnp.zeros_like(grad_sum)
    lax.fori_loop(0, CHIPS, heads, 0)
    grad_out = grad_sum[...].astype(BF16)

    @pl.when(t == CHIPS - 1)
    def _():
        raw[...] = grad_out[: SLOTS * HEAD_DIM]

    @pl.when(t < CHIPS - 1)
    def _():
        for i in range(4):
            raw[i * 80 : i * 80 + HEAD_DIM] = grad_out[i * HEAD_DIM : (i + 1) * HEAD_DIM]
            raw[i * 80 + HEAD_DIM : (i + 1) * 80] = jnp.zeros((16, D), BF16)

    swaps = [
        remote(
            raw.at[rows16(i * 80 + (1 - p) * 32, 48)], land_out.at[i], g_send.at[3, i], g_recv.at[3, i], e.twin()
        )
        for i in range(4)
    ]
    for copy in swaps:
        copy.start()
    for copy in swaps:
        copy.wait()
    for i in range(4):
        own = raw[rows16(i * 80 + p * 32, 48)].astype(F32)
        g_out[i] = (own + land_out[i].astype(F32)).astype(BF16)
    planes.last(share)
    for ref in (to_x, to_y, to_far):
        ref[ROWS:] = share[...]
    for user in (hidden, spread, sum_h):
        user.sent()


def feed(middle, cot, others, halves, vecs, out_w, mixed):
    blocks = pltpu.VMEM((CHIPS, ROWS, D), BF16)
    lands = pltpu.VMEM((6, HALF, D), BF16)
    matrix = pltpu.VMEM((D, D), BF16)
    mixture = jax.ShapeDtypeStruct((ROWS + UP_ROWS, D), BF16)
    return pl.pallas_call(
        feed_kernel,
        out_shape=(
            mixture, mixture, mixture,
            jax.ShapeDtypeStruct((ROWS, D), F32),
            jax.ShapeDtypeStruct((ROWS, D), F32),
            jax.ShapeDtypeStruct((CHIPS, ROWS, WIDE), BF16),
            jax.ShapeDtypeStruct((4, 48, D), BF16),
            jax.ShapeDtypeStruct((4, DOWN_ROWS, D), BF16),
            jax.ShapeDtypeStruct((UP_ROWS, D), BF16),
            jax.ShapeDtypeStruct((8, D), F32),
            jax.ShapeDtypeStruct((1, D), F32),
        ),
        in_specs=vmem(9),
        out_specs=tuple(vmem(11)),
        scratch_shapes=[matrix, matrix]
        + [pltpu.VMEM((2, CHIPS, ROWS, D), BF16)] * 2
        + [blocks] * 2
        + [lands, pltpu.VMEM((2, D, D), BF16), pltpu.VMEM((WIDE, D), F32)]
        + [
            pltpu.VMEM((4, UP_ROWS, D), BF16),
            pltpu.VMEM((4, TILE, D), BF16),
            pltpu.VMEM((32, D), BF16),
            pltpu.VMEM((4, UP_ROWS, D), BF16),
            pltpu.VMEM((4, UP_ROWS, D), BF16),
            pltpu.VMEM((3, UP_ROWS, D), BF16),
            pltpu.VMEM((3, UP_ROWS, D), BF16),
            pltpu.VMEM((SLOTS * HEAD_DIM, D), BF16),
            pltpu.VMEM((4, 48, D), BF16),
            dma(2, 6), dma(2, 6), dma(6), dma(6), dma(4), dma(4), dma(4),
            dma(5), dma(5), dma(5), dma(4, 4), dma(4, 4), dma(2, 3), dma(2, 3), dma(4),
        ],
        compiler_params=params(3, 63),
        name="feed",
    )(middle, cot, *others, halves, vecs, out_w, mixed)


def back_kernel(
    x, grad_mid, dq, dk, dv, hid, whole, vecs, share, from_x, from_y, from_far, share_down, out_own, g_out, sums, up_sum,
    output, grad_x, up_out, down_out, qkv_out, o_out, vec_out, b_up_out,
    joint, full, land, land_k, land_v, part, rows_own, sum_land, g_qkv, z_right, z_left, s_qkv,
    s_out, zo_right, zo_left, own_qkv, own_out, all_up, all_down, all_qkv, all_out, local, vec_land, totals, wide,
    kv_send, kv_recv, g_send, g_recv, s_send, s_recv, a_send, a_recv, z_send, z_recv, t_send, t_recv, v_send, v_recv, c_local,
):
    e = Place()
    t, p, z = (e.t, e.p, e.z)
    e.greet()
    swaps = []
    for k in range(CHIPS):
        chip = e.flip(1 - k // 2, 1 - k % 2)
        for j, (ref, dst) in enumerate(((dk, land_k), (dv, land_v))):
            swaps.append(
                remote(ref.at[chip * 2 + 1 - p], dst.at[chip], kv_send.at[j, k], kv_recv.at[j, k], e.twin())
            )
    for copy in swaps:
        copy.start()

    def spread(number, own, everything, rows, cut):
        return Gather(
            e, own, lambda chip: everything.at[p, chip], rows, cut, a_send.at[number], a_recv.at[number]
        )

    def hand(number, own, everything, k):
        chip = e.flip(k % 2, k // 2)
        src = own if k == 0 else everything.at[p, chip]
        return remote(
            src, everything.at[p, chip], t_send.at[number, k], t_recv.at[number, k], e.twin()
        )

    def handed(number, own, everything):
        for k in range(CHIPS):
            chip = e.flip(k % 2, k // 2)
            copy = remote(
                own, everything.at[1 - p, chip], t_send.at[number, k], t_recv.at[number, k], e.twin()
            )
            copy.wait_recv()
            copy.wait_send()

    feeds = [share] + [ref.at[pl.ds(ROWS, UP_ROWS)] for ref in (from_x, from_y, from_far)]
    keeps = []
    for k in range(CHIPS):
        slot = all_up.at[p, e.flip(k % 2, k // 2)]
        keeps.append(pltpu.make_async_copy(feeds[k], slot, c_local.at[k]))
    downs = spread(2, share_down, all_down, DOWN_ROWS, 80)
    downs.start()
    outs = ZScatter(e, g_out, s_out, zo_right, zo_left, z_send.at[0], z_recv.at[0])
    outs.begin()
    result = out_own[...]
    for ref in (from_x, from_y, from_far):
        result = result + ref[:ROWS].astype(F32)
    output[...] = result.T.astype(BF16)
    normed, inverse = normalize(x[...].astype(F32))
    local[...] = jnp.zeros_like(local)
    for k in range(CHIPS):
        joint[k, :, :WIDE] = dq[k]

    def trades(a):
        return [
            remote(
                full.at[a, rows16(i * 272 + (1 - p) * TILE, 144)], land.at[a, i],
                g_send.at[a, i], g_recv.at[a, i], e.twin(),
            )
            for i in range(4)
        ]

    def grads(a, carry):
        @pl.when(a == 1)
        def _():
            for copy in swaps:
                copy.wait()
            head_q, head_v = (jnp.zeros((1, WIDE), F32), jnp.zeros((1, WIDE), F32))
            for k in range(CHIPS):
                mine = k * 2 + p
                low_k = (dk[mine].astype(F32) + land_k[k].astype(F32)).astype(BF16)
                low_v = (dv[mine].astype(F32) + land_v[k].astype(F32)).astype(BF16)
                joint[k, :, WIDE : 2 * WIDE] = low_k
                joint[k, :, 2 * WIDE :] = low_v
                head_q = head_q + jnp.sum(dq[k].astype(F32), 0, keepdims=True)
                head_v = head_v + jnp.sum(low_v.astype(F32), 0, keepdims=True)
            local[pl.ds(12 + t, 1), :WIDE] = head_q
            local[pl.ds(12 + t, 1), WIDE : 2 * WIDE] = head_v
            outs.first()

        right = joint[:, :, pl.ds(pl.multiple_of(a * WIDE, TILE), WIDE)]
        full[a] = rows_product(
            hid[...].reshape(CHIPS * ROWS, D), right.reshape(CHIPS * ROWS, WIDE)
        ).astype(BF16)
        for copy in trades(a):
            copy.start()
        return carry

    lax.fori_loop(0, 3, grads, 0)
    downs.forward()
    outs.second()
    summed = Scatter(e, part, sum_land, s_send, s_recv)
    weights = ZScatter(e, g_qkv, s_qkv, z_right, z_left, z_send.at[1], z_recv.at[1])

    def block(k, carry):
        dest = e.flip(1 - k // 2, 1 - k % 2)
        value = cols_product(joint[dest], whole[...])

        @pl.when(k < 3)
        def _():
            part[dest] = value.astype(BF16)

        @pl.when(k == 0)
        def _():
            summed.far_ready()
            for a in range(3):
                for copy in trades(a):
                    copy.wait()
                for i in range(4):
                    own = full[a, rows16(i * 272 + p * TILE, 144)].astype(F32)
                    g_qkv[i, :, a * WIDE : (a + 1) * WIDE] = (own + land[a, i].astype(F32)).astype(BF16)
            weights.begin()

        @pl.when(k == 1)
        def _():
            summed.x_ready()

        @pl.when(k == 2)
        def _():
            summed.y_ready()

        @pl.when(k == 3)
        def _():
            rows_own[...] = value

        return carry

    lax.fori_loop(0, CHIPS, block, 0)
    outs.last(own_out)
    for k in range(CHIPS):
        keeps[k].start()
        slot = all_up.at[p, e.flip(k % 2, k // 2)]
        remote(feeds[k], slot, t_send.at[0, k], t_recv.at[0, k], e.twin()).start()
    hand(3, share_down, all_down, 0).start()
    all_down[p, t] = share_down[...]
    downs.have_x()
    downs.have_y()
    hand(3, share_down, all_down, 1).start()
    hand(3, share_down, all_down, 2).start()
    downs.have_far()
    hand(3, share_down, all_down, 3).start()
    weights.first()
    others = spread(0, own_out, all_out, 48, 32)
    others.start()
    all_out[p, t] = own_out[...]
    hand(1, own_out, all_out, 0).start()
    summed.relay()
    weights.second()
    total = rows_own[...] + summed.total()
    grad_x[...] = (grad_mid[...] + norm_back(total, normed, inverse, vecs[GAIN_1 : GAIN_1 + 1])).T
    local[:4] = sums[:4]
    local[4:5] = jnp.sum(total * normed, 0, keepdims=True)
    local[5:6] = jnp.sum(total, 0, keepdims=True)
    local[pl.ds(8 + t, 1), :] = up_sum[...]
    twin = remote(local, vec_land.at[0], v_send.at[0], v_recv.at[0], e.twin())
    twin.start()
    others.forward()
    others.have_x()
    others.have_y()
    hand(1, own_out, all_out, 1).start()
    hand(1, own_out, all_out, 2).start()
    others.have_far()
    hand(1, own_out, all_out, 3).start()
    twin.wait()
    totals[...] = local[...] + vec_land[0]
    planes = [
        remote(totals, vec_land.at[k], v_send.at[k], v_recv.at[k], e.plane(k)) for k in range(1, 4)
    ]
    for copy in planes:
        copy.start()
    weights.last(own_qkv)
    qkvs = spread(1, own_qkv, all_qkv, 144, 80)
    qkvs.start()
    hand(2, own_qkv, all_qkv, 0).start()
    all_qkv[p, t] = own_qkv[...]
    for copy in planes:
        copy.wait()
    local[...] = totals[...] + vec_land[1] + vec_land[2] + vec_land[3]
    chips = [
        remote(local, vec_land.at[3 + k], v_send.at[3 + k], v_recv.at[3 + k], e.chip(chip))
        for k, chip in ((1, e.tx), (2, e.ty), (3, e.td))
    ]
    for copy in chips:
        copy.start()

    handed(0, share, all_up)
    handed(3, share_down, all_down)
    for copy in keeps:
        copy.wait()
    for s in range(CHIPS):
        for q in range(2):
            rows = slice(q * TILE, q * TILE + 144)
            for i in range(4):
                column = D * i + HEAD_DIM * (i % 2) + 256 * s
                up_out[rows, column : column + 256] = all_up[q, s, :, 256 * i : 256 * (i + 1)]
            down_out[rows16(z % 2 * 64 + 256 * s + TILE * q, TILE)] = all_down[q, s, :TILE]
    for q in range(2):
        rows = slice(q * TILE, q * TILE + 144)
        for s in range(0, CHIPS, 2):
            pair = [all_up[q, s + i, :, 1024:].astype(F32) for i in range(2)]
            column = D * s + 1024
            up_out[rows, column : column + TILE] = jnp.concatenate(pair, 1).astype(BF16)
        down_out[rows16((1 - z % 2) * 1024 + 32 * q, 32)] = all_down[q, z, TILE:]

    handed(1, own_out, all_out)
    ahead = (CHIPS - z) % CHIPS * 16
    for s in range(CHIPS - 1):
        o_out[rows16(ahead + HEAD_DIM * s, 48)] = all_out[0, s]
        o_out[rows16(ahead + HEAD_DIM * s + 32, 32)] = all_out[1, s, :32]
    for u in range(SLOTS):
        q, first = ((0, 16 * u) if u < 3 else (1, 16 * u - 32))
        strip = all_out[q, CHIPS - 1, first : first + 16]

        @pl.when(16 * u < ahead)
        def _():
            o_out[16 * u : 16 * u + 16] = strip

        @pl.when(16 * u >= ahead)
        def _():
            o_out[192 + 16 * u : 208 + 16 * u] = strip

    qkvs.forward()
    qkvs.have_x()
    qkvs.have_y()
    hand(2, own_qkv, all_qkv, 1).start()
    hand(2, own_qkv, all_qkv, 2).start()
    qkvs.have_far()
    hand(2, own_qkv, all_qkv, 3).start()
    for copy in chips:
        copy.wait()
    totals[...] = local[...] + vec_land[4] + vec_land[5] + vec_land[6]
    wide[...] = jnp.zeros_like(wide)
    wide[:6, :D] = totals[:6]
    columns = {}
    for s, heads in enumerate(HEAD_TABLE):
        for slot, head in enumerate(heads):
            columns[head] = (s, slot * HEAD_DIM)
    lane = lax.broadcasted_iota(jnp.int32, (1, TILE), 1)
    for a in range(2):
        def span(head, side):
            s, column = columns[head]
            start = (column + a * WIDE) // TILE * TILE
            tile = totals[12 + s : 13 + s, start : start + TILE]
            return tile if column % TILE // HEAD_DIM == side else pltpu.roll(tile, HEAD_DIM, 1)

        for head in range(0, HEADS, 2):
            tile = span(head, 0)
            if head + 1 < HEADS:
                tile = jnp.where(lane < HEAD_DIM, tile, span(head + 1, 1))
            wide[6 + a : 7 + a, head * HEAD_DIM : head * HEAD_DIM + TILE] = tile
    for i in range(4):
        @pl.when(z == i)
        def _():
            row = wide[...]
            if i > 0:
                row = pltpu.roll(row, 9 * TILE - D // 4 * i, 1)
            vec_out[...] = row[:, :WIDE]
            pieces = [totals[8 + s : 9 + s, 256 * i : 256 * i + 256] for s in range(CHIPS)]
            more = totals[8 + i : 9 + i, 1024:]
            if i % 2 == 0:
                b_up_out[...] = jnp.concatenate(pieces + [more, more], 1)
            else:
                b_up_out[...] = pltpu.roll(jnp.concatenate(pieces + [more, more], 1), HEAD_DIM, 1)

    handed(2, own_qkv, all_qkv)
    source = {}
    for s, heads in enumerate(HEAD_TABLE):
        for slot, head in enumerate(heads):
            if head >= 0:
                for a in range(3):
                    source[a * HEADS + head] = (s, a * WIDE + slot * HEAD_DIM)
    for q in range(2):
        rows = slice(q * TILE, q * TILE + 144)

        def piece(g, side):
            s, column = source[g]
            tile = all_qkv[q, s, :, column // TILE * TILE : column // TILE * TILE + TILE].astype(F32)
            return tile if column % TILE // HEAD_DIM == side else pltpu.roll(tile, HEAD_DIM, 1)

        left = lax.broadcasted_iota(jnp.int32, (144, TILE), 1) < HEAD_DIM
        for g in range(0, 3 * HEADS - 1, 2):
            column = g * HEAD_DIM
            qkv_out[rows, column : column + TILE] = jnp.where(left, piece(g, 0), piece(g + 1, 1)).astype(BF16)
        column = (3 * HEADS - 1) * HEAD_DIM
        qkv_out[rows, column : column + HEAD_DIM] = piece(3 * HEADS - 1, 0)[:, :HEAD_DIM].astype(BF16)
    for user in (downs, others, qkvs, summed):
        user.sent()


def back(x, grad_mid, dq, dk, dv, hid, whole, vecs, share, others, share_down, out_own, g_out, sums, up_sum):
    heads = pltpu.VMEM((CHIPS, ROWS, WIDE), BF16)
    qkv, out = ((144, 3 * WIDE), (48, D))

    def many(count, shape):
        return pltpu.VMEM((count, *shape), BF16)

    return pl.pallas_call(
        back_kernel,
        out_shape=(
            jax.ShapeDtypeStruct((D, ROWS), BF16),
            jax.ShapeDtypeStruct((D, ROWS), F32),
            jax.ShapeDtypeStruct((D // 4, 4 * D), BF16),
            jax.ShapeDtypeStruct((D, D), BF16),
            jax.ShapeDtypeStruct((D // 4, 3 * D), BF16),
            jax.ShapeDtypeStruct((D // 4, D), BF16),
            jax.ShapeDtypeStruct((8, WIDE), F32),
            jax.ShapeDtypeStruct((1, 9 * TILE), F32),
        ),
        in_specs=vmem(17),
        out_specs=tuple(vmem(8)),
        scratch_shapes=[
            pltpu.VMEM((CHIPS, ROWS, 3 * WIDE), BF16),
            pltpu.VMEM((3, D, WIDE), BF16),
            pltpu.VMEM((3, 4, 144, WIDE), BF16),
            heads, heads,
            pltpu.VMEM((CHIPS, ROWS, D), BF16),
            pltpu.VMEM((ROWS, D), F32),
            pltpu.VMEM((6, HALF, D), BF16),
            many(4, qkv), many(3, qkv), many(3, qkv), many(4, qkv),
            many(4, out), many(3, out), many(3, out),
            pltpu.VMEM(qkv, BF16), pltpu.VMEM(out, BF16),
            pltpu.VMEM((2, CHIPS, UP_ROWS, D), BF16),
            pltpu.VMEM((2, CHIPS, DOWN_ROWS, D), BF16),
            pltpu.VMEM((2, CHIPS, *qkv), BF16),
            pltpu.VMEM((2, CHIPS, *out), BF16),
            pltpu.VMEM((16, D), F32),
            pltpu.VMEM((7, 16, D), F32),
            pltpu.VMEM((16, D), F32),
            pltpu.VMEM((8, 9 * TILE), F32),
            dma(2, CHIPS), dma(2, CHIPS), dma(3, 4), dma(3, 4), dma(6), dma(6), dma(3, 6), dma(3, 6),
            dma(2, 2, 3), dma(2, 2, 3), dma(4, 4), dma(4, 4), dma(7), dma(7), dma(4),
        ],
        compiler_params=params(4, 63),
        name="back",
    )(x, grad_mid, dq, dk, dv, hid, whole, vecs, share, *others, share_down, out_own, g_out, sums, up_sum)


def plane_device(
    tokens, seq_lengths, cotangent, ln1_gain, ln1_bias, w_qkv, b_query, b_value, w_out, b_out,
    ln2_gain, ln2_bias, w_up, b_up, w_down, b_down,
):
    c = lax.axis_index("ctx")
    lengths = seq_lengths[0]
    parity = (c % 2)[None].astype(jnp.int32)
    shard = D // 4

    biases = (b_query, b_value, b_out, b_down, ln1_gain, ln1_bias, ln2_gain, ln2_bias)
    q, k, v, hid, whole, out_w, vecs, halves, sent, x = project(
        tokens[0].T, cotangent[0].T, biases, b_up, w_qkv, w_out, w_up, w_down
    )
    halves = lax.all_gather(halves, "wsh", axis=0)

    def from_chips(*arrays):
        return [lax.ppermute(array, "ctx", list(enumerate(to))) for array, to in zip(arrays, flips)]

    flips = [[(i // 2 ^ mask) * 2 + i % 2 for i in range(2 * CHIPS)] for mask in (1, 2, 3)]
    tops = from_chips(sent, sent, sent)
    mixed, lse = attend(lengths, parity, q, k, v)
    middle = out_project(x, mixed, out_w, vecs)
    to_x, to_y, to_far, out_own, grad_mid, grad_heads, g_out, g_down, share, sums, up_sum = feed(
        middle, sent, tops, halves, vecs, out_w, mixed
    )
    others = from_chips(to_x, to_y, to_far)
    share_down = lax.psum_scatter(
        g_down.reshape(4 * DOWN_ROWS, D), "wsh", scatter_dimension=0, tiled=True
    )
    dq, dk, dv = attend_back(lengths, parity, q, k, v, mixed, grad_heads, lse)
    output, grad_x, grad_up, grad_down, grad_qkv, grad_out, vectors, grad_b_up = back(
        x, grad_mid, dq, dk, dv, hid, whole, vecs, share, others, share_down, out_own, g_out, sums, up_sum
    )
    grad_up, grad_down, grad_qkv, grad_out = (
        array.astype(F32) for array in (grad_up, grad_down, grad_qkv, grad_out)
    )

    mine = [row[:shard] for row in vectors]
    grad_b_up = grad_b_up[0, :D]
    return (
        output.T[None], grad_x.T[None],
        mine[4], mine[5], grad_qkv, mine[6], mine[7], grad_out, mine[0],
        mine[2], mine[3], grad_up, grad_b_up, grad_down, mine[1],
    )


def solution(mesh):
    in_specs = (
        P("wsh", "ctx", None),
        P("wsh", None),
        P("wsh", "ctx", None),
        P("wsh"),
        P("wsh"),
        P("wsh", None),
        P("wsh"),
        P("wsh"),
        P("wsh", None),
        P("wsh"),
        P("wsh"),
        P("wsh"),
        P("wsh", None),
        P("wsh"),
        P("wsh", None),
        P("wsh"),
    )
    out_specs = (
        P("wsh", "ctx", None),
        P("wsh", "ctx", None),
        P("wsh"),
        P("wsh"),
        P("wsh", None),
        P("wsh"),
        P("wsh"),
        P("wsh", None),
        P("wsh"),
        P("wsh"),
        P("wsh"),
        P("wsh", None),
        P("wsh"),
        P("wsh", None),
        P("wsh"),
    )
    sizes = (mesh.shape["ctx"], mesh.shape["wsh"])
    body = plane_device if sizes == (2 * CHIPS, 4) else on_device
    return jax.shard_map(
        body, mesh=mesh, in_specs=in_specs, out_specs=out_specs, check_vma=False
    )
```

```python
import functools
import math

import jax
import jax.numpy as jnp
from jax import lax
from jax.experimental import pallas as pl
from jax.experimental.pallas import tpu as pltpu
from jax.sharding import PartitionSpec as P

D = 1088
HEADS = 17
HEAD_DIM = 64


def normalize(inputs):
    center = inputs - jnp.mean(inputs, -1, keepdims=True)
    inverse = lax.rsqrt(jnp.mean(center * center, -1, keepdims=True) + 1e-05)
    return (center * inverse, inverse)


def norm_back(grad_in, normed, inverse, gain):
    scaled = grad_in * gain
    return inverse * (
        scaled
        - jnp.mean(scaled, -1, keepdims=True)
        - normed * jnp.mean(scaled * normed, -1, keepdims=True)
    )


def rows_product(left, right):
    return lax.dot_general(
        left, right, (((0,), (0,)), ((), ())), preferred_element_type=jnp.float32
    )


def cols_product(left, right):
    return lax.dot_general(
        left, right, (((1,), (1,)), ((), ())), preferred_element_type=jnp.float32
    )


def sequence_ids(lengths, positions):
    bounds = jnp.cumsum(lengths)
    return jnp.sum((positions[:, None] >= bounds[None, :]).astype(jnp.int32), axis=1)


def allowed_pairs(lengths, query_pos, key_pos):
    query_owner = sequence_ids(lengths, query_pos)
    key_owner = sequence_ids(lengths, key_pos)
    return (key_pos[None, :] <= query_pos[:, None]) & (
        (key_owner[None, :] == 0) | (key_owner[None, :] == query_owner[:, None])
    )


def over_blocks(state_in, arrays, step_fn):
    total_rows = arrays[0].shape[0]
    block_rows = math.gcd(total_rows, 512)

    def advance(block_index, state_now):
        offset = block_index * block_rows
        pieces = tuple((lax.dynamic_slice_in_dim(array, offset, block_rows, 0) for array in arrays))
        return step_fn(state_now, pieces, offset)

    return lax.fori_loop(0, total_rows // block_rows, advance, state_in)


def sectioned_sum(partials):
    shares = lax.psum_scatter(partials, "wsh", scatter_dimension=0, tiled=True)
    return lax.psum(shares, "ctx")


def on_device(
    tokens,
    seq_lengths,
    cotangent,
    ln1_gain,
    ln1_bias,
    w_qkv,
    b_query,
    b_value,
    w_out,
    b_out,
    ln2_gain,
    ln2_bias,
    w_up,
    b_up,
    w_down,
    b_down,
):
    token_rows, grad_rows = (tokens[0], cotangent[0])
    shards = (
        w_qkv,
        w_out,
        w_up,
        w_down,
        b_query,
        b_value,
        b_out,
        b_up,
        b_down,
        ln1_gain,
        ln1_bias,
        ln2_gain,
        ln2_bias,
    )
    gathered = (
        lax.all_gather(shards[0], "wsh", axis=0, tiled=True),
        lax.all_gather(shards[1], "wsh", axis=0, tiled=True),
        lax.all_gather(shards[2], "wsh", axis=0, tiled=True),
        lax.all_gather(shards[3], "wsh", axis=0, tiled=True),
        lax.all_gather(shards[4], "wsh", axis=0, tiled=True),
        lax.all_gather(shards[5], "wsh", axis=0, tiled=True),
        lax.all_gather(shards[6], "wsh", axis=0, tiled=True),
        lax.all_gather(shards[7], "wsh", axis=0, tiled=True),
        lax.all_gather(shards[8], "wsh", axis=0, tiled=True),
        lax.all_gather(shards[9], "wsh", axis=0, tiled=True),
        lax.all_gather(shards[10], "wsh", axis=0, tiled=True),
        lax.all_gather(shards[11], "wsh", axis=0, tiled=True),
        lax.all_gather(shards[12], "wsh", axis=0, tiled=True),
    )
    qkv_full, out_full, up_full, down_full = (gathered[0], gathered[1], gathered[2], gathered[3])
    query_bias, value_bias, out_bias, up_bias, down_bias = [
        piece.astype(jnp.float32) for piece in gathered[4:9]
    ]
    gain_one, shift_one, gain_two, shift_two = [
        piece.astype(jnp.float32) for piece in gathered[9:13]
    ]
    lengths = seq_lengths[0]
    tok_rows = token_rows.shape[0]
    my_pos = lax.axis_index("ctx") * tok_rows + jnp.arange(tok_rows, dtype=jnp.int32)
    scale_qk = HEAD_DIM ** (-0.5)
    inputs = token_rows.astype(jnp.float32)
    normed_one, inverse_one = normalize(inputs)
    hidden_one = (normed_one * gain_one + shift_one).astype(jnp.bfloat16)
    joint_proj = jnp.dot(hidden_one, qkv_full, preferred_element_type=jnp.float32)
    queries = (joint_proj[:, :D] + query_bias).astype(jnp.bfloat16)
    key_rows = joint_proj[:, D : 2 * D].astype(jnp.bfloat16)
    value_rows = (joint_proj[:, 2 * D :] + value_bias).astype(jnp.bfloat16)
    query_heads = queries.reshape(tok_rows, HEADS, HEAD_DIM)
    my_key_heads = key_rows.reshape(tok_rows, HEADS, HEAD_DIM)
    my_value_heads = value_rows.reshape(tok_rows, HEADS, HEAD_DIM)

    def forward_step(state_now, pieces, first_row):
        key_heads = pieces[0].reshape(-1, HEADS, HEAD_DIM)
        value_heads = pieces[1].reshape(-1, HEADS, HEAD_DIM)
        key_pos = first_row + jnp.arange(key_heads.shape[0], dtype=jnp.int32)
        allowed = allowed_pairs(lengths, my_pos, key_pos)

        def forward_compute(inner):
            peak_old, total_old, accum_old = inner
            scores = (
                jnp.einsum(
                    "qhd,khd->hqk", query_heads, key_heads, preferred_element_type=jnp.float32
                )
                * scale_qk
            )
            scores = jnp.where(allowed[None], scores, -1e30)
            peak_new = jnp.maximum(peak_old, jnp.max(scores, -1))
            factor = jnp.exp(peak_old - peak_new)
            expos = jnp.where(allowed[None], jnp.exp(scores - peak_new[:, :, None]), 0.0)
            total_new = total_old * factor + jnp.sum(expos, -1)
            accum_new = accum_old * factor.T[:, :, None] + jnp.einsum(
                "hqk,khd->qhd",
                expos.astype(jnp.bfloat16),
                value_heads,
                preferred_element_type=jnp.float32,
            )
            return (peak_new, total_new, accum_new)

        return lax.cond(jnp.any(allowed), forward_compute, lambda inner: inner, state_now)

    start_state = (
        jnp.full((HEADS, tok_rows), -1e30, jnp.float32),
        jnp.zeros((HEADS, tok_rows), jnp.float32),
        jnp.zeros((tok_rows, HEADS, HEAD_DIM), jnp.float32),
    )
    peak, total, accum = over_blocks(
        start_state,
        (
            lax.all_gather(key_rows, "ctx", axis=0, tiled=True),
            lax.all_gather(value_rows, "ctx", axis=0, tiled=True),
        ),
        forward_step,
    )
    mixed = accum / total.T[:, :, None]
    log_sum = (peak + jnp.log(total)).T
    mixed_low = mixed.reshape(tok_rows, D).astype(jnp.bfloat16)
    middle = inputs + jnp.dot(mixed_low, out_full, preferred_element_type=jnp.float32) + out_bias
    normed_two, inverse_two = normalize(middle)
    hidden_two = (normed_two * gain_two + shift_two).astype(jnp.bfloat16)
    pre_act = jnp.dot(hidden_two, up_full, preferred_element_type=jnp.float32) + up_bias
    activ_low = jax.nn.gelu(pre_act, approximate=False).astype(jnp.bfloat16)
    result = middle + jnp.dot(activ_low, down_full, preferred_element_type=jnp.float32) + down_bias
    output_rows = result.astype(jnp.bfloat16)
    grad_top_f = grad_rows.astype(jnp.float32)
    grad_down = rows_product(activ_low, grad_rows)
    grad_down_bias = jnp.sum(grad_top_f, 0)
    grad_act = cols_product(grad_rows, down_full)
    cdf_part = 0.5 * (1.0 + lax.erf(pre_act * math.sqrt(0.5)))
    pdf_part = jnp.exp(-0.5 * pre_act * pre_act) / math.sqrt(2.0 * math.pi)
    grad_pre = (grad_act * (cdf_part + pre_act * pdf_part)).astype(jnp.bfloat16)
    grad_up = rows_product(hidden_two, grad_pre)
    grad_up_bias = jnp.sum(grad_pre.astype(jnp.float32), 0)
    grad_h2 = cols_product(grad_pre, up_full)
    grad_gain_two = jnp.sum(grad_h2 * normed_two, 0)
    grad_shift_two = jnp.sum(grad_h2, 0)
    grad_mid = grad_top_f + norm_back(grad_h2, normed_two, inverse_two, gain_two)
    grad_mid_low = grad_mid.astype(jnp.bfloat16)
    grad_out_w = rows_product(mixed_low, grad_mid_low)
    grad_out_bias = jnp.sum(grad_mid_low.astype(jnp.float32), 0)
    grad_mixed = cols_product(grad_mid_low, out_full).astype(jnp.bfloat16)
    grad_heads = grad_mixed.reshape(tok_rows, HEADS, HEAD_DIM)
    delta = jnp.sum(grad_heads.astype(jnp.float32) * mixed, -1)
    lse_all, delta_all = (
        lax.all_gather(log_sum, "ctx", axis=0, tiled=True),
        lax.all_gather(delta, "ctx", axis=0, tiled=True),
    )

    def query_step(state_now, pieces, first_row):
        key_heads = pieces[0].reshape(-1, HEADS, HEAD_DIM)
        value_heads = pieces[1].reshape(-1, HEADS, HEAD_DIM)
        key_pos = first_row + jnp.arange(key_heads.shape[0], dtype=jnp.int32)
        allowed = allowed_pairs(lengths, my_pos, key_pos)

        def query_compute(accum_old):
            scores = (
                jnp.einsum(
                    "qhd,khd->hqk", query_heads, key_heads, preferred_element_type=jnp.float32
                )
                * scale_qk
            )
            probs = jnp.where(allowed[None], jnp.exp(scores - log_sum.T[:, :, None]), 0.0)
            grad_probs = jnp.einsum(
                "qhd,khd->hqk", grad_heads, value_heads, preferred_element_type=jnp.float32
            )
            grad_scores = (probs * (grad_probs - delta.T[:, :, None])).astype(jnp.bfloat16)
            return accum_old + jnp.einsum(
                "hqk,khd->qhd", grad_scores, key_heads, preferred_element_type=jnp.float32
            )

        return lax.cond(jnp.any(allowed), query_compute, lambda inner: inner, state_now)

    zero_heads = jnp.zeros((tok_rows, HEADS, HEAD_DIM), jnp.float32)
    grad_query = over_blocks(
        zero_heads,
        (
            lax.all_gather(key_rows, "ctx", axis=0, tiled=True),
            lax.all_gather(value_rows, "ctx", axis=0, tiled=True),
        ),
        query_step,
    )

    def key_step(state_now, pieces, first_row):
        other_queries = pieces[0].reshape(-1, HEADS, HEAD_DIM)
        other_grads = pieces[1].reshape(-1, HEADS, HEAD_DIM)
        other_count = other_queries.shape[0]
        other_pos = first_row + jnp.arange(other_count, dtype=jnp.int32)
        other_lse = lax.dynamic_slice_in_dim(lse_all, first_row, other_count, 0)
        other_delta = lax.dynamic_slice_in_dim(delta_all, first_row, other_count, 0)
        allowed = allowed_pairs(lengths, other_pos, my_pos)

        def key_compute(inner):
            grad_key_old, grad_value_old = inner
            scores = (
                jnp.einsum(
                    "qhd,khd->hqk", other_queries, my_key_heads, preferred_element_type=jnp.float32
                )
                * scale_qk
            )
            probs = jnp.where(allowed[None], jnp.exp(scores - other_lse.T[:, :, None]), 0.0)
            grad_value_new = grad_value_old + jnp.einsum(
                "hqk,qhd->khd",
                probs.astype(jnp.bfloat16),
                other_grads,
                preferred_element_type=jnp.float32,
            )
            grad_probs = jnp.einsum(
                "qhd,khd->hqk", other_grads, my_value_heads, preferred_element_type=jnp.float32
            )
            grad_scores = (probs * (grad_probs - other_delta.T[:, :, None])).astype(jnp.bfloat16)
            grad_key_new = grad_key_old + jnp.einsum(
                "hqk,qhd->khd", grad_scores, other_queries, preferred_element_type=jnp.float32
            )
            return (grad_key_new, grad_value_new)

        return lax.cond(jnp.any(allowed), key_compute, lambda inner: inner, state_now)

    grad_key, grad_value = over_blocks(
        (zero_heads, zero_heads),
        (
            lax.all_gather(queries, "ctx", axis=0, tiled=True),
            lax.all_gather(grad_mixed, "ctx", axis=0, tiled=True),
        ),
        key_step,
    )
    grad_joint = jnp.concatenate(
        [
            (grad_query * scale_qk).reshape(tok_rows, D),
            (grad_key * scale_qk).reshape(tok_rows, D),
            grad_value.reshape(tok_rows, D),
        ],
        axis=1,
    ).astype(jnp.bfloat16)
    grad_qkv_w = rows_product(hidden_one, grad_joint)
    grad_joint_f = grad_joint.astype(jnp.float32)
    grad_query_bias = jnp.sum(grad_joint_f[:, :D], 0)
    grad_value_bias = jnp.sum(grad_joint_f[:, 2 * D :], 0)
    grad_h1 = cols_product(grad_joint, qkv_full)
    grad_gain_one = jnp.sum(grad_h1 * normed_one, 0)
    grad_shift_one = jnp.sum(grad_h1, 0)
    grad_input = grad_mid + norm_back(grad_h1, normed_one, inverse_one, gain_one)
    matrices = (grad_qkv_w, grad_out_w, grad_up, grad_down)
    vectors = (
        grad_query_bias,
        grad_value_bias,
        grad_out_bias,
        grad_up_bias,
        grad_down_bias,
        grad_gain_one,
        grad_shift_one,
        grad_gain_two,
        grad_shift_two,
    )
    totals = sectioned_sum(matrices + vectors)
    return (
        output_rows[None],
        grad_input[None],
        totals[9],
        totals[10],
        totals[0],
        totals[4],
        totals[5],
        totals[1],
        totals[6],
        totals[11],
        totals[12],
        totals[2],
        totals[7],
        totals[3],
        totals[8],
    )


SLOTS = 5
WIDE = 384
ROWS = 256
HALF = ROWS // 2
CHIPS = 4
TILE = 128
UP_ROWS, DOWN_ROWS = (144, 160)
MESH_ID = pl.DeviceIdType.MESH
F32, BF16 = (jnp.float32, jnp.bfloat16)
NEG = -1e30
HEAD_TABLE = ((0, 5, 9, 13, -40), (1, 6, 10, 14, -40), (2, 7, 11, 15, -40), (3, 4, 8, 12, 16))
B_QUERY, B_VALUE, B_OUT, B_DOWN, GAIN_1, SHIFT_1, GAIN_2, SHIFT_2, B_UP = range(9)


def nn(left, right):
    return jnp.dot(left, right, preferred_element_type=F32)


def remote(src, dst, send, recv, where):
    return pltpu.make_async_remote_copy(
        src_ref=src, dst_ref=dst, send_sem=send, recv_sem=recv, device_id=where, device_id_type=MESH_ID
    )


def rows16(start, size):
    return pl.ds(pl.multiple_of(start, 16), size)


class Place:
    def __init__(self):
        self.c, self.z = (lax.axis_index("ctx"), lax.axis_index("wsh"))
        self.t, self.p = (self.c // 2, self.c % 2)
        self.tx, self.ty, self.td = (self.flip(1, 0), self.flip(0, 1), self.flip(1, 1))

    def flip(self, dx, dy):
        return (self.t // 2 + dy) % 2 * 2 + (self.t % 2 + dx) % 2

    def chip(self, chip):
        return (chip * 2 + self.p, self.z)

    def twin(self):
        return (self.t * 2 + 1 - self.p, self.z)

    def plane(self, step):
        return (self.c, (self.z + step) % 4)

    def greet(self, planes=True):
        barrier = pltpu.get_barrier_semaphore()
        others = [self.chip(self.tx), self.chip(self.ty), self.twin()]
        if planes:
            others += [self.plane(1), self.plane(2), self.plane(3)]
        for where in others:
            pl.semaphore_signal(barrier, inc=1, device_id=where, device_id_type=MESH_ID)
        pl.semaphore_wait(barrier, len(others))


class Gather:
    def __init__(self, e, own, view, rows, cut, send, recv):
        self.e, self.own, self.view, self.send, self.recv = (e, own, view, send, recv)
        self.parts = (pl.ds(0, cut), pl.ds(cut, rows - cut))

    def copy(self, i):
        e = self.e
        chip = (e.t, e.t, e.t, e.t, e.tx, e.ty)[i]
        part = self.parts[(0, 1, 1, 0, 0, 1)[i]]
        src = self.own if i < 4 else self.view(chip)
        where = e.chip((e.tx, e.tx, e.ty, e.ty, e.ty, e.tx)[i])
        return remote(src.at[part], self.view(chip).at[part], self.send.at[i], self.recv.at[i], where)

    def start(self):
        for i in (0, 2, 1, 3):
            self.copy(i).start()

    def forward(self):
        self.copy(0).wait_recv()
        self.copy(4).start()
        self.copy(2).wait_recv()
        self.copy(5).start()

    def have_x(self):
        self.copy(1).wait_recv()

    def have_y(self):
        self.copy(3).wait_recv()

    def have_far(self):
        self.copy(4).wait_recv()
        self.copy(5).wait_recv()

    def sent(self):
        for i in range(6):
            self.copy(i).wait_send()


class Scatter:
    def __init__(self, e, part, land, send, recv):
        self.e, self.part, self.land, self.send, self.recv = (e, part, land, send, recv)

    def copy(self, i):
        e = self.e
        chip = (e.td, e.td, e.tx, e.tx, e.ty, e.ty)[i]
        part = pl.ds((0, HALF, 0, HALF, HALF, 0)[i], HALF)
        where = e.chip((e.tx, e.ty, e.tx, e.tx, e.ty, e.ty)[i])
        return remote(
            self.part.at[chip, part], self.land.at[i], self.send.at[i], self.recv.at[i], where
        )

    def far_ready(self):
        self.copy(0).start()
        self.copy(1).start()

    def x_ready(self):
        self.copy(2).start()

    def y_ready(self):
        self.copy(4).start()

    def relay(self):
        self.copy(1).wait_recv()
        chip = self.e.tx
        self.part[chip, HALF:] = (self.part[chip, HALF:].astype(F32) + self.land[1].astype(F32)).astype(BF16)
        self.copy(3).start()
        self.copy(0).wait_recv()
        chip = self.e.ty
        self.part[chip, :HALF] = (self.part[chip, :HALF].astype(F32) + self.land[0].astype(F32)).astype(BF16)
        self.copy(5).start()

    def total(self):
        for i in (2, 4, 3, 5):
            self.copy(i).wait_recv()
        first = self.land[2].astype(F32) + self.land[5].astype(F32)
        second = self.land[4].astype(F32) + self.land[3].astype(F32)
        return jnp.concatenate([first, second], 0)

    def sent(self):
        for i in range(6):
            self.copy(i).wait_send()


class ZGather:
    def __init__(self, e, own, held, send, recv, put):
        self.e, self.own, self.held, self.send, self.recv, self.put = (e, own, held, send, recv, put)

    def copy(self, way, j):
        e = self.e
        shard = e.z - j if way == 0 else e.z + j
        src = self.own if j == 0 else self.held.at[shard]
        return remote(
            src, self.held.at[shard], self.send.at[way, j], self.recv.at[way, j], e.plane(1 if way == 0 else 3)
        )

    def sends(self, way, j):
        z = self.e.z
        return (z < 3) & (z >= j) if way == 0 else (z > 0) & (z <= 3 - j)

    def step(self, j):
        z = self.e.z
        for way in range(2):
            if j > 0:
                @pl.when(z >= j if way == 0 else z <= 3 - j)
                def _():
                    self.copy(way, j - 1).wait_recv()
            if j < 3:
                @pl.when(self.sends(way, j))
                def _():
                    self.copy(way, j).start()
            if j > 0:
                @pl.when(z >= j if way == 0 else z <= 3 - j)
                def _():
                    self.put(z - j if way == 0 else z + j)

    def sent(self):
        for way in range(2):
            for j in range(3):
                @pl.when(self.sends(way, j))
                def _():
                    self.copy(way, j).wait_send()


class ZScatter:
    def __init__(self, e, own, staged, right, left, send, recv):
        self.e, self.own, self.staged, self.land = (e, own, staged, (right, left))
        self.send, self.recv = (send, recv)

    def copy(self, way, j, src):
        return remote(
            src, self.land[way].at[j], self.send.at[way, j], self.recv.at[way, j],
            self.e.plane(1 if way == 0 else 3),
        )

    def begin(self):
        for plane, way in ((0, 0), (3, 1)):
            @pl.when(self.e.z == plane)
            def _():
                for j in range(3):
                    self.copy(way, j, self.own.at[3 - j if way == 0 else j]).start()

    def relay(self, way, j):
        dest = 3 - j if way == 0 else j
        self.copy(way, j, self.staged.at[dest]).wait_recv()
        self.staged[dest] = (self.own[dest].astype(F32) + self.land[way][j].astype(F32)).astype(BF16)
        self.copy(way, j, self.staged.at[dest]).start()

    def first(self):
        for plane, way in ((1, 0), (2, 1)):
            @pl.when(self.e.z == plane)
            def _():
                self.relay(way, 0)

    def second(self):
        for plane, way in ((1, 0), (2, 1)):
            @pl.when(self.e.z == plane)
            def _():
                self.relay(1 - way, 0)
                self.relay(way, 1)

    def last(self, out):
        right, left = self.land
        for z in range(4):
            @pl.when(self.e.z == z)
            def _():
                total = self.own[z].astype(F32)
                if z > 0:
                    self.copy(0, 3 - z, self.own.at[z]).wait_recv()
                    total = total + right[3 - z].astype(F32)
                if z < 3:
                    self.copy(1, z, self.own.at[z]).wait_recv()
                    total = total + left[z].astype(F32)
                out[...] = total.astype(BF16)
                for way in range(2):
                    for j in range((3 - z) if way == 0 else z):
                        self.copy(way, j, self.own.at[z]).wait_send()


def dma(*shape):
    return pltpu.SemaphoreType.DMA(shape)


def params(number, mib=56):
    return pltpu.CompilerParams(
        collective_id=number, has_side_effects=True, vmem_limit_bytes=mib * 2**20
    )


def vmem(count):
    return [pl.BlockSpec(memory_space=pltpu.VMEM)] * count


class Halves:
    def __init__(self, e, whole, block, keep, step, local, send, recv):
        self.e, self.whole, self.block, self.keep, self.step = (e, whole, block, keep, step)
        self.local, self.send, self.recv = (local, send, recv)

    def copies(self, src, shard):
        e = self.e
        return (
            pltpu.make_async_copy(
                src, self.whole.at[rows16(shard * self.block + e.p * self.step, self.keep)], self.local.at[shard]
            ),
            remote(
                src.at[rows16(e.p * (self.keep - self.step), self.step)],
                self.whole.at[rows16(shard * self.block + e.p * self.keep, self.step)],
                self.send.at[shard], self.recv.at[shard], e.twin(),
            ),
        )

    def put(self, src, shard):
        for copy in self.copies(src, shard):
            copy.start()

    def wait(self, src):
        for shard in range(4):
            for copy in self.copies(src, shard):
                copy.wait()


def half_tiles(source, columns):
    def piece(column, side):
        if column is None:
            return jnp.zeros((source.shape[0], TILE), F32)
        start = column // TILE * TILE
        if start + TILE > source.shape[-1]:
            part = source[:, start : start + HEAD_DIM].astype(F32)
            tile = jnp.concatenate([part, jnp.zeros_like(part)], 1)
        else:
            tile = source[:, start : start + TILE].astype(F32)
        return tile if column % TILE // HEAD_DIM == side else pltpu.roll(tile, HEAD_DIM, 1)

    tiles = []
    for i in range(0, len(columns), 2):
        first, second = (piece(columns[i], 0), piece(columns[i + 1], 1))
        lane = lax.broadcasted_iota(jnp.int32, first.shape, 1)
        tiles.append(jnp.where(lane < HEAD_DIM, first, second))
    return tiles


def head_columns(heads, first):
    return [first + head * HEAD_DIM if head >= 0 else None for head in heads] + [None]


def project_kernel(
    x, cot, bias_0, bias_1, bias_2, bias_3, bias_4, bias_5, bias_6, bias_7, b_up, w_qkv, w_out, w_up, w_down,
    q_out, k_out, v_out, h_out, whole, out_w, vecs, halves, cot_out, x_out,
    qkv_rows, half, half_o, edge, held, held_o, raw, vec_in, vec_land, bias,
    v_send, v_recv, z_send, z_recv, a_send, a_recv, w_local, w_send, w_recv, kv_send, kv_recv, r_local,
):
    e = Place()
    t, p, z = (e.t, e.p, e.z)
    rows = pltpu.make_async_copy(w_qkv.at[rows16(p * TILE, 144)], qkv_rows, r_local.at[0])
    rows.start()
    loads = []
    for i in range(4):
        column = pl.multiple_of(D * i + HEAD_DIM * (i % 2) + 256 * t, TILE)
        loads.append((w_up.at[rows16(p * TILE, 144), pl.ds(column, 256)], halves.at[pl.ds(0, 144), pl.ds(256 * i, 256)]))
    column = pl.multiple_of(1024 + 2 * D * (t // 2), TILE)
    loads.append((w_up.at[rows16(p * TILE, 144), pl.ds(column, TILE)], edge))
    loads.append((w_down.at[rows16(HEAD_DIM * (z % 2) + 256 * t + TILE * p, TILE)], halves.at[pl.ds(144, TILE)]))
    loads.append((w_down.at[rows16(1024 * (1 - z % 2) + 32 * p, 32)], halves.at[pl.ds(272, 32)]))
    loads = [pltpu.make_async_copy(src, dst, r_local.at[1 + i]) for i, (src, dst) in enumerate(loads)]
    for copy in loads:
        copy.start()
    spot = lax.broadcasted_iota(jnp.int32, (D // 4, D), 1) - D // 4 * z
    match = (spot == lax.broadcasted_iota(jnp.int32, (D // 4, D), 0)).astype(F32).astype(BF16)
    biases = (bias_0, bias_1, bias_2, bias_3, bias_4, bias_5, bias_6, bias_7)
    biases = jnp.concatenate([ref[...].astype(F32).reshape(1, D // 4) for ref in biases], 0)
    vec_in[0] = nn(biases.astype(BF16), match)
    e.greet()

    def exchange(i):
        return [
            remote(vec_in.at[i], vec_land.at[k, i], v_send.at[i, k], v_recv.at[i, k], e.plane(k))
            for k in range(1, 4)
        ]

    vectors = exchange(0)
    for copy in vectors:
        copy.start()
    into = Halves(e, whole, 272, 144, 128, w_local.at[0], w_send.at[0], w_recv.at[0])
    into_o = Halves(e, raw, 80, 48, 32, w_local.at[1], w_send.at[1], w_recv.at[1])
    chain = ZGather(
        e, half, held, z_send.at[0], z_recv.at[0], lambda shard: into.put(held.at[shard], shard)
    )
    chain_o = ZGather(
        e, half_o, held_o, z_send.at[1], z_recv.at[1], lambda shard: into_o.put(held_o.at[shard], shard)
    )
    rows.wait()
    for chip in range(CHIPS):
        @pl.when(t == chip)
        def _():
            for a in range(3):
                tiles = half_tiles(qkv_rows, head_columns(HEAD_TABLE[chip], a * D))
                for i in range(3):
                    half[:, a * WIDE + i * TILE : a * WIDE + (i + 1) * TILE] = tiles[i].astype(BF16)

    chain.step(0)
    into.put(half, z)
    inputs = x[...].astype(F32).T
    x_out[...] = inputs.astype(BF16)
    normed, _ = normalize(inputs)
    total = vec_in[0]
    for k in range(1, 4):
        vectors[k - 1].wait_recv()
        total = total + vec_land[k, 0]
    vecs[:8] = total
    h_out[t] = (normed * vecs[GAIN_1 : GAIN_1 + 1] + vecs[SHIFT_1 : SHIFT_1 + 1]).astype(BF16)
    hidden = Gather(e, h_out.at[t], lambda chip: h_out.at[chip], ROWS, HALF, a_send, a_recv)
    hidden.start()
    ahead = (CHIPS - z) % CHIPS * 16
    for m in range(3):
        unit = 16 * (2 * p + m)
        late = jnp.where(unit < ahead, unit, 192 + unit)
        first = jnp.where(t < CHIPS - 1, ahead + HEAD_DIM * t + unit, late)
        half_o[16 * m : 16 * m + 16] = w_out[rows16(first, 16)]
    for chip in range(CHIPS):
        @pl.when(t == chip)
        def _():
            tiles = half_tiles(vecs, head_columns(HEAD_TABLE[chip], 0))
            for i in range(3):
                bias[:, i * TILE : (i + 1) * TILE] = tiles[i]

    spot = lax.broadcasted_iota(jnp.int32, (D, 320), 1)
    at = jnp.where(spot < 256, HEAD_DIM * (z % 2) + 256 * t + spot, 1024 * (1 - z % 2) + spot - 256)
    match = (lax.broadcasted_iota(jnp.int32, (D, 320), 0) == at).astype(F32).astype(BF16)
    ups = nn(b_up[...].astype(F32).reshape(1, D).astype(BF16), match)
    vec_in[1] = jnp.zeros((8, D), F32)
    for i in range(4):
        @pl.when(z == i)
        def _():
            vec_in[1, 0:1, 256 * i : 256 * i + 256] = ups[0:1, :256]

    @pl.when(z == t)
    def _():
        vec_in[1, 0:1, 1024:] = ups[0:1, 256:]

    vectors = vectors + exchange(1)
    for copy in vectors[3:]:
        copy.start()
    cot_out[:ROWS] = cot[...].astype(F32).T.astype(BF16)
    cot_out[ROWS:] = jnp.zeros((8, D), BF16)
    for copy in loads:
        copy.wait()
    column = edge[...].astype(F32)
    column = jnp.where(t % 2 == 1, pltpu.roll(column, HEAD_DIM, 1), column)
    halves[:144, 1024:] = column[:, :HEAD_DIM].astype(BF16)
    chain.step(1)
    hidden.forward()
    chain.step(2)
    chain_o.step(0)
    into_o.put(half_o, z)
    total = vec_in[1]
    for k in range(1, 4):
        vectors[2 + k].wait_recv()
        total = total + vec_land[k, 1]
    vecs[8:] = total
    chain.step(3)
    into.wait(half)

    def block(k, carry):
        src = e.flip((k + 1) // 2 % 2, k // 2)

        @pl.when(k == 1)
        def _():
            hidden.have_x()

        @pl.when(k == 2)
        def _():
            hidden.have_far()

        @pl.when(k == 3)
        def _():
            hidden.have_y()

        h = h_out[src]
        bias_q, bias_v = (bias[B_QUERY : B_QUERY + 1], bias[B_VALUE : B_VALUE + 1])
        q_out[src] = ((nn(h, whole[:, :WIDE]) + bias_q).astype(BF16) * 0.125).astype(BF16)
        mine = src * 2 + p
        k_out[mine] = nn(h, whole[:, WIDE : 2 * WIDE]).astype(BF16)
        remote(k_out.at[mine], k_out.at[mine], kv_send.at[k], kv_recv.at[k], e.twin()).start()
        v_out[mine] = (nn(h, whole[:, 2 * WIDE :]) + bias_v).astype(BF16)
        remote(
            v_out.at[mine], v_out.at[mine], kv_send.at[k + CHIPS], kv_recv.at[k + CHIPS], e.twin()
        ).start()
        return carry

    lax.fori_loop(0, CHIPS, block, 0)
    chain_o.step(1)
    chain_o.step(2)
    chain_o.step(3)
    into_o.wait(half_o)

    @pl.when(t == CHIPS - 1)
    def _():
        out_w[: SLOTS * HEAD_DIM] = raw[...]

    @pl.when(t < CHIPS - 1)
    def _():
        for i in range(4):
            out_w[i * HEAD_DIM : (i + 1) * HEAD_DIM] = raw[i * 80 : i * 80 + HEAD_DIM]
        out_w[4 * HEAD_DIM : 5 * HEAD_DIM] = jnp.zeros((HEAD_DIM, D), BF16)

    out_w[SLOTS * HEAD_DIM :] = jnp.zeros((WIDE - SLOTS * HEAD_DIM, D), BF16)
    for k in range(CHIPS):
        src = e.flip((k + 1) // 2 % 2, k // 2)
        other = src * 2 + 1 - p
        mine = src * 2 + p
        for ref, j in ((k_out, k), (v_out, k + CHIPS)):
            remote(ref.at[mine], ref.at[mine], kv_send.at[j], kv_recv.at[j], e.twin()).wait_send()
            remote(ref.at[other], ref.at[other], kv_send.at[j], kv_recv.at[j], e.twin()).wait_recv()
    for user in (hidden, chain, chain_o):
        user.sent()
    for copy in vectors:
        copy.wait_send()


def project(x, cot, biases, b_up, w_qkv, w_out, w_up, w_down):
    blocks = jax.ShapeDtypeStruct((CHIPS, ROWS, WIDE), BF16)
    keys = jax.ShapeDtypeStruct((2 * CHIPS, ROWS, WIDE), BF16)
    near, far = (vmem(1), [pl.BlockSpec(memory_space=pl.ANY)])
    return pl.pallas_call(
        project_kernel,
        out_shape=(
            blocks, keys, keys,
            jax.ShapeDtypeStruct((CHIPS, ROWS, D), BF16),
            jax.ShapeDtypeStruct((D, 3 * WIDE), BF16),
            jax.ShapeDtypeStruct((WIDE, D), BF16),
            jax.ShapeDtypeStruct((16, D), F32),
            jax.ShapeDtypeStruct((UP_ROWS + DOWN_ROWS, D), BF16),
            jax.ShapeDtypeStruct((ROWS + 8, D), BF16),
            jax.ShapeDtypeStruct((ROWS, D), BF16),
        ),
        in_specs=near * 11 + far + near + far * 2,
        out_specs=tuple(near * 10),
        scratch_shapes=[
            pltpu.VMEM((144, 3 * D), BF16),
            pltpu.VMEM((144, 3 * WIDE), BF16),
            pltpu.VMEM((48, D), BF16),
            pltpu.VMEM((144, TILE), BF16),
            pltpu.VMEM((4, 144, 3 * WIDE), BF16),
            pltpu.VMEM((4, 48, D), BF16),
            pltpu.VMEM((SLOTS * HEAD_DIM, D), BF16),
            pltpu.VMEM((2, 8, D), F32),
            pltpu.VMEM((4, 2, 8, D), F32),
            pltpu.VMEM((16, WIDE), F32),
            dma(2, 4), dma(2, 4), dma(2, 2, 3), dma(2, 2, 3), dma(6), dma(6),
            dma(2, 4), dma(2, 4), dma(2, 4), dma(2 * CHIPS), dma(2 * CHIPS), dma(8),
        ],
        compiler_params=params(1),
        name="project",
    )(x, cot, *biases, b_up, w_qkv, w_out, w_up, w_down)


def tile_bounds(lengths, block):
    ends = [lengths[0]]
    for i in range(1, 4):
        ends.append(ends[-1] + lengths[i])
    first = block * ROWS
    start_first = 0 * first
    for end in ends:
        start_first = jnp.where(first >= end, end, start_first)
    free = jnp.minimum(block, ends[0] // ROWS)
    resume = jnp.maximum(free + 1, start_first // ROWS)
    masked = jnp.where(free < block, 1 + jnp.maximum(block - resume, 0), 0)
    query_pos = first + lax.broadcasted_iota(jnp.int32, (1, ROWS), 1)
    start = jnp.zeros((1, ROWS), jnp.int32)
    for end in ends:
        start = jnp.where(query_pos >= end, end, start)
    return ends[0], query_pos, start, free, resume, masked


def visible(key_block, prompt, query_pos, start):
    key_pos = key_block * ROWS + lax.broadcasted_iota(jnp.int32, (ROWS, ROWS), 0)
    return (key_pos <= query_pos) & ((key_pos < prompt) | (key_pos >= start))


def half_of(rows, h):
    lane = lax.broadcasted_iota(jnp.int32, rows.shape, 1)
    return jnp.where((lane >= h * HEAD_DIM) & (lane < (h + 1) * HEAD_DIM), rows, jnp.zeros_like(rows))


def attend_kernel(lengths, parity, q, k, v, mixed, lse, turned):
    slab = pl.program_id(0)
    for j in range(2 * CHIPS):
        turned[j] = v[j].astype(F32).T.astype(BF16)

    def run(heads):
        def one(i, carry):
            block = 2 * i + parity[0]
            prompt, query_pos, start, free, resume, masked = tile_bounds(lengths, block)
            queries = [half_of(q[i], h) for h in heads]

            def tile(j, state, mask):
                keys = k[j]
                values = turned[j]
                new = []
                for h, (peak, total, accum) in zip(heads, state):
                    scores = cols_product(keys, queries[h])
                    if mask is not None:
                        scores = jnp.where(mask, scores, NEG)
                    peak_new = jnp.maximum(peak, jnp.max(scores, 0, keepdims=True))
                    factor = jnp.exp(peak - peak_new)
                    expos = jnp.exp(scores - peak_new)
                    total_new = total * factor + jnp.sum(expos, 0, keepdims=True)
                    part = values[h * HEAD_DIM : (h + 1) * HEAD_DIM]
                    accum_new = accum * factor + nn(part, expos.astype(BF16))
                    new.append((peak_new, total_new, accum_new))
                return tuple(new)

            state = tuple(
                (
                    jnp.full((1, ROWS), NEG, F32),
                    jnp.zeros((1, ROWS), F32),
                    jnp.zeros((HEAD_DIM, ROWS), F32),
                )
                for _ in heads
            )

            def other(m, s):
                j = jnp.where(m == 0, block, jnp.where(m == 1, free, resume + m - 2))
                return tile(j, s, visible(j, prompt, query_pos, start))

            state = lax.fori_loop(0, 1 + masked, other, state)
            state = lax.fori_loop(0, free, lambda j, s: tile(j, s, None), state)
            outs = []
            for h, (peak, total, accum) in zip(heads, state):
                outs.append(accum / total)
                lse[0, pl.ds(h * CHIPS + i, 1), :] = peak + jnp.log(total)
            if len(heads) == 1:
                outs.append(jnp.zeros((HEAD_DIM, ROWS), F32))
            mixed[i] = jnp.concatenate(outs, 0).T.astype(BF16)
            return carry

        lax.fori_loop(0, CHIPS, one, 0)

    @pl.when(slab < SLOTS // 2)
    def _():
        run((0, 1))

    @pl.when(slab >= SLOTS // 2)
    def _():
        lse[...] = jnp.zeros_like(lse)
        run((0,))


def slab_spec(count):
    return pl.BlockSpec((count, ROWS, 128), lambda s, *_: (0, 0, s))


def attend(lengths, parity, q, k, v):
    return pl.pallas_call(
        attend_kernel,
        out_shape=(
            jax.ShapeDtypeStruct((CHIPS, ROWS, WIDE), BF16),
            jax.ShapeDtypeStruct((3, 2 * CHIPS, ROWS), F32),
        ),
        grid_spec=pltpu.PrefetchScalarGridSpec(
            num_scalar_prefetch=2,
            grid=(3,),
            in_specs=[slab_spec(CHIPS), slab_spec(2 * CHIPS), slab_spec(2 * CHIPS)],
            out_specs=(
                slab_spec(CHIPS),
                pl.BlockSpec((1, 2 * CHIPS, ROWS), lambda s, *_: (s, 0, 0)),
            ),
            scratch_shapes=[pltpu.VMEM((2 * CHIPS, 128, ROWS), BF16)],
        ),
        compiler_params=pltpu.CompilerParams(vmem_limit_bytes=63 * 2**20),
        cost_estimate=pl.CostEstimate(flops=4 * 10**9, bytes_accessed=5 * 10**6, transcendentals=6 * 10**6),
        name="attend",
    )(lengths, parity, q, k, v)


def attend_back_kernel(
    lengths, parity, q, k, v, mixed, grad, lse, dq, dk, dv, turned, acc_k, acc_v
):
    slab = pl.program_id(0)
    for j in range(2 * CHIPS):
        turned[j] = k[j].astype(F32).T.astype(BF16)
    acc_k[...] = jnp.zeros_like(acc_k)
    acc_v[...] = jnp.zeros_like(acc_v)

    def run(heads):
        def one(i, carry):
            block = 2 * i + parity[0]
            prompt, query_pos, start, free, resume, masked = tile_bounds(lengths, block)
            queries = [half_of(q[i], h) for h in heads]
            grads = [half_of(grad[i], h) for h in heads]
            product = (grad[i].astype(F32) * mixed[i].astype(F32)).T
            deltas = [
                jnp.sum(product[h * HEAD_DIM : (h + 1) * HEAD_DIM], 0, keepdims=True) for h in heads
            ]
            sums = [lse[0, pl.ds(h * CHIPS + i, 1), :] for h in heads]

            def tile(j, state, mask):
                keys, values, keys_t = (k[j], v[j], turned[j])
                new = []
                add_k, add_v = (None, None)
                for h, accum in zip(heads, state):
                    scores = cols_product(keys, queries[h]) - sums[h]
                    if mask is not None:
                        scores = jnp.where(mask, scores, NEG)
                    probs = jnp.exp(scores)
                    grad_probs = cols_product(values, grads[h])
                    ds = (probs * (grad_probs - deltas[h])).astype(BF16)
                    part_v = nn(probs.astype(BF16), grads[h])
                    part_k = nn(ds, queries[h])
                    add_v = part_v if add_v is None else add_v + part_v
                    add_k = part_k if add_k is None else add_k + part_k
                    new.append(accum + nn(keys_t[h * HEAD_DIM : (h + 1) * HEAD_DIM], ds))
                acc_v[j] += add_v
                acc_k[j] += add_k
                return tuple(new)

            state = tuple(jnp.zeros((HEAD_DIM, ROWS), F32) for _ in heads)

            def other(m, s):
                j = jnp.where(m == 0, block, jnp.where(m == 1, free, resume + m - 2))
                return tile(j, s, visible(j, prompt, query_pos, start))

            state = lax.fori_loop(0, 1 + masked, other, state)
            state = list(lax.fori_loop(0, free, lambda j, s: tile(j, s, None), state))
            if len(heads) == 1:
                state.append(jnp.zeros((HEAD_DIM, ROWS), F32))
            dq[i] = (jnp.concatenate(state, 0) * 0.125).T.astype(BF16)
            return carry

        lax.fori_loop(0, CHIPS, one, 0)

    @pl.when(slab < SLOTS // 2)
    def _():
        run((0, 1))

    @pl.when(slab >= SLOTS // 2)
    def _():
        run((0,))

    dk[...] = acc_k[...].astype(BF16)
    dv[...] = acc_v[...].astype(BF16)


def attend_back(lengths, parity, q, k, v, mixed, grad, lse):
    few, many = (slab_spec(CHIPS), slab_spec(2 * CHIPS))
    return pl.pallas_call(
        attend_back_kernel,
        out_shape=(
            jax.ShapeDtypeStruct((CHIPS, ROWS, WIDE), BF16),
            jax.ShapeDtypeStruct((2 * CHIPS, ROWS, WIDE), BF16),
            jax.ShapeDtypeStruct((2 * CHIPS, ROWS, WIDE), BF16),
        ),
        grid_spec=pltpu.PrefetchScalarGridSpec(
            num_scalar_prefetch=2,
            grid=(3,),
            in_specs=[
                few, many, many, few, few,
                pl.BlockSpec((1, 2 * CHIPS, ROWS), lambda s, *_: (s, 0, 0)),
            ],
            out_specs=(few, many, many),
            scratch_shapes=[
                pltpu.VMEM((2 * CHIPS, 128, ROWS), BF16),
                pltpu.VMEM((2 * CHIPS, ROWS, 128), F32),
                pltpu.VMEM((2 * CHIPS, ROWS, 128), F32),
            ],
        ),
        compiler_params=pltpu.CompilerParams(vmem_limit_bytes=63 * 2**20),
        cost_estimate=pl.CostEstimate(flops=10 * 10**9, bytes_accessed=9 * 10**6, transcendentals=6 * 10**6),
        name="attend_back",
    )(lengths, parity, q, k, v, mixed, grad, lse)


def out_kernel(x, mixed, whole, vecs, middle, part, land, send, recv):
    e = Place()
    e.greet(planes=False)
    sums = Scatter(e, part, land, send, recv)

    def block(k, carry):
        dest = e.flip(1 - k // 2, 1 - k % 2)
        part[dest] = nn(mixed[dest], whole[...]).astype(BF16)

        @pl.when(k == 0)
        def _():
            sums.far_ready()

        @pl.when(k == 1)
        def _():
            sums.x_ready()

        @pl.when(k == 2)
        def _():
            sums.y_ready()

        return carry

    lax.fori_loop(0, CHIPS - 1, block, 0)
    total = x[...].astype(F32) + vecs[B_OUT : B_OUT + 1] + nn(mixed[e.t], whole[...])
    sums.relay()
    middle[...] = total + sums.total()
    sums.sent()


def out_project(x, mixed, whole, vecs):
    return pl.pallas_call(
        out_kernel,
        out_shape=jax.ShapeDtypeStruct((ROWS, D), F32),
        in_specs=vmem(4),
        out_specs=vmem(1)[0],
        scratch_shapes=[
            pltpu.VMEM((CHIPS, ROWS, D), BF16),
            pltpu.VMEM((6, HALF, D), BF16),
            dma(6), dma(6),
        ],
        compiler_params=params(2),
        name="out_project",
    )(x, mixed, whole, vecs)


def feed_kernel(
    middle, cot, cot_x, cot_y, cot_far, halves, vecs, out_w, mixed,
    to_x, to_y, to_far, out_own, grad_mid, gh_heads, g_out, g_down, share, sums, up_sum,
    up, down, lefts, rights, part_h, gmid, sum_h_land,
    full, grad_sum, land_up, land_down, land_more, g_up, staged, z_right, z_left, raw, land_out,
    a_send, a_recv, s_send, s_recv, w_local, w_send, w_recv, d_local, d_send, d_recv, g_send, g_recv, z_send, z_recv, c_local,
):
    e = Place()
    t, p = (e.t, e.p)
    hid, act, gpre, cots = (lefts.at[0], lefts.at[1], rights.at[0], rights.at[1])
    full_up, full_down = (full.at[0], full.at[1])
    e.greet()
    into = Halves(e, up, 272, 144, 128, w_local, w_send, w_recv)
    weights = []
    for i in range(4):
        weights.extend(into.copies(halves.at[i, pl.ds(0, 144)], i))
    for i in range(5):
        src = halves.at[i, pl.ds(144, TILE)] if i < 4 else halves.at[t, pl.ds(272, 32)]
        dst = down.at[rows16(256 * i + p * TILE, TILE) if i < 4 else rows16(1024 + p * 32, 32)]
        weights.append(pltpu.make_async_copy(src, dst, d_local.at[i]))
        weights.append(remote(src, dst, d_send.at[i], d_recv.at[i], e.twin()))
    for k, (ref, chip) in enumerate(((cot, t), (cot_x, e.tx), (cot_y, e.ty), (cot_far, e.td))):
        weights.append(pltpu.make_async_copy(ref.at[pl.ds(0, ROWS)], cots.at[chip], c_local.at[k]))
    for copy in weights:
        copy.start()
    normed, inverse = normalize(middle[...])
    hid[t] = (normed * vecs[GAIN_2 : GAIN_2 + 1] + vecs[SHIFT_2 : SHIFT_2 + 1]).astype(BF16)
    hidden = Gather(e, hid.at[t], lambda chip: hid.at[chip], ROWS, HALF, a_send.at[0], a_recv.at[0])
    hidden.start()
    sum_h = Scatter(e, part_h, sum_h_land, s_send, s_recv)
    for copy in weights:
        copy.wait()
    up_sum[...] = jnp.zeros_like(up_sum)

    def block(k, carry):
        src = e.flip((k + 1) // 2 % 2, k // 2)

        @pl.when(k == 1)
        def _():
            hidden.forward()
            hidden.have_x()

        @pl.when(k == 2)
        def _():
            hidden.have_far()

        @pl.when(k == 3)
        def _():
            hidden.have_y()

        pre = nn(hid[src], up[...]) + vecs[B_UP : B_UP + 1]
        cdf = 0.5 * (1.0 + lax.erf(pre * math.sqrt(0.5)))
        slope = cdf + pre * (jnp.exp(-0.5 * pre * pre) * (1.0 / math.sqrt(2.0 * math.pi)))
        act[src] = (pre * cdf).astype(BF16)
        grad = cols_product(cots[src], down[...]) * slope
        low = grad.astype(BF16)
        gpre[src] = low
        up_sum[...] += jnp.sum(low.astype(F32), 0, keepdims=True)
        part_h[src] = cols_product(low, up[...]).astype(BF16)

        @pl.when(k == 1)
        def _():
            sum_h.x_ready()

        @pl.when(k == 2)
        def _():
            sum_h.far_ready()

        @pl.when(k == 3)
        def _():
            sum_h.y_ready()

        return carry

    lax.fori_loop(0, CHIPS, block, 0)
    sum_h.relay()

    ups = [
        remote(
            full_up.at[rows16(i * 272 + (1 - p) * TILE, UP_ROWS)], land_up.at[i],
            g_send.at[0, i], g_recv.at[0, i], e.twin(),
        )
        for i in range(4)
    ]

    def matrices(i, carry):
        full[i] = rows_product(
            lefts[i].reshape(CHIPS * ROWS, D), rights[i].reshape(CHIPS * ROWS, D)
        ).astype(BF16)

        @pl.when(i == 0)
        def _():
            for copy in ups:
                copy.start()

        return carry

    lax.fori_loop(0, 2, matrices, 0)
    swaps = [
        remote(
            full_down.at[rows16(256 * i + (1 - p) * TILE, TILE)], land_down.at[i],
            g_send.at[1, i], g_recv.at[1, i], e.twin(),
        )
        for i in range(4)
    ]
    swaps.append(
        remote(
            full_down.at[rows16(1024 + (1 - p) * 32, 32)], land_more, g_send.at[2, 0], g_recv.at[2, 0], e.twin()
        )
    )
    for copy in swaps:
        copy.start()
    for copy in ups:
        copy.wait()
    for i in range(4):
        own = full_up[rows16(i * 272 + p * TILE, UP_ROWS)].astype(F32)
        g_up[i] = (own + land_up[i].astype(F32)).astype(BF16)
    planes = ZScatter(e, g_up, staged, z_right, z_left, z_send, z_recv)
    planes.begin()
    def outs(k, carry):
        rows = nn(act[e.flip(k % 2, k // 2)], down[...])
        for i, ref in enumerate((out_own, to_x, to_y, to_far)):
            @pl.when(k == i)
            def _():
                if i == 0:
                    ref[...] = middle[...] + vecs[B_DOWN : B_DOWN + 1] + rows
                else:
                    ref[:ROWS] = rows.astype(BF16)

        return carry

    lax.fori_loop(0, CHIPS, outs, 0)

    total = part_h[t].astype(F32) + sum_h.total()
    top = cot[:ROWS].astype(F32)
    grad_middle = top + norm_back(total, normed, inverse, vecs[GAIN_2 : GAIN_2 + 1])
    grad_mid[...] = grad_middle
    low = grad_middle.astype(BF16)
    gmid[t] = low
    spread = Gather(e, gmid.at[t], lambda chip: gmid.at[chip], ROWS, HALF, a_send.at[1], a_recv.at[1])
    spread.start()
    sums[0:1] = jnp.sum(low.astype(F32), 0, keepdims=True)
    sums[1:2] = jnp.sum(top, 0, keepdims=True)
    sums[2:3] = jnp.sum(total * normed, 0, keepdims=True)
    sums[3:4] = jnp.sum(total, 0, keepdims=True)
    sums[4:8] = jnp.zeros((4, D), F32)

    planes.first()
    for copy in swaps:
        copy.wait()
    more = (full_down[rows16(1024 + p * 32, 32)].astype(F32) + land_more[...].astype(F32)).astype(BF16)
    for i in range(4):
        own = full_down[rows16(256 * i + p * TILE, TILE)].astype(F32)
        g_down[i, :TILE] = (own + land_down[i].astype(F32)).astype(BF16)
        g_down[i, TILE:] = more
    spread.forward()
    planes.second()

    def heads(k, carry):
        src = e.flip((k + 1) // 2 % 2, k // 2)

        @pl.when(k == 1)
        def _():
            spread.have_x()

        @pl.when(k == 2)
        def _():
            spread.have_far()

        @pl.when(k == 3)
        def _():
            spread.have_y()

        rows = gmid[src]
        gh_heads[src] = cols_product(rows, out_w[...]).astype(BF16)
        grad_sum[...] += rows_product(mixed[src], rows)
        return carry

    grad_sum[...] = jnp.zeros_like(grad_sum)
    lax.fori_loop(0, CHIPS, heads, 0)
    grad_out = grad_sum[...].astype(BF16)

    @pl.when(t == CHIPS - 1)
    def _():
        raw[...] = grad_out[: SLOTS * HEAD_DIM]

    @pl.when(t < CHIPS - 1)
    def _():
        for i in range(4):
            raw[i * 80 : i * 80 + HEAD_DIM] = grad_out[i * HEAD_DIM : (i + 1) * HEAD_DIM]
            raw[i * 80 + HEAD_DIM : (i + 1) * 80] = jnp.zeros((16, D), BF16)

    swaps = [
        remote(
            raw.at[rows16(i * 80 + (1 - p) * 32, 48)], land_out.at[i], g_send.at[3, i], g_recv.at[3, i], e.twin()
        )
        for i in range(4)
    ]
    for copy in swaps:
        copy.start()
    for copy in swaps:
        copy.wait()
    for i in range(4):
        own = raw[rows16(i * 80 + p * 32, 48)].astype(F32)
        g_out[i] = (own + land_out[i].astype(F32)).astype(BF16)
    planes.last(share)
    for ref in (to_x, to_y, to_far):
        ref[ROWS:] = share[...]
    for user in (hidden, spread, sum_h):
        user.sent()


def feed(middle, cot, others, halves, vecs, out_w, mixed):
    blocks = pltpu.VMEM((CHIPS, ROWS, D), BF16)
    lands = pltpu.VMEM((6, HALF, D), BF16)
    matrix = pltpu.VMEM((D, D), BF16)
    mixture = jax.ShapeDtypeStruct((ROWS + UP_ROWS, D), BF16)
    return pl.pallas_call(
        feed_kernel,
        out_shape=(
            mixture, mixture, mixture,
            jax.ShapeDtypeStruct((ROWS, D), F32),
            jax.ShapeDtypeStruct((ROWS, D), F32),
            jax.ShapeDtypeStruct((CHIPS, ROWS, WIDE), BF16),
            jax.ShapeDtypeStruct((4, 48, D), BF16),
            jax.ShapeDtypeStruct((4, DOWN_ROWS, D), BF16),
            jax.ShapeDtypeStruct((UP_ROWS, D), BF16),
            jax.ShapeDtypeStruct((8, D), F32),
            jax.ShapeDtypeStruct((1, D), F32),
        ),
        in_specs=vmem(9),
        out_specs=tuple(vmem(11)),
        scratch_shapes=[matrix, matrix]
        + [pltpu.VMEM((2, CHIPS, ROWS, D), BF16)] * 2
        + [blocks] * 2
        + [lands, pltpu.VMEM((2, D, D), BF16), pltpu.VMEM((WIDE, D), F32)]
        + [
            pltpu.VMEM((4, UP_ROWS, D), BF16),
            pltpu.VMEM((4, TILE, D), BF16),
            pltpu.VMEM((32, D), BF16),
            pltpu.VMEM((4, UP_ROWS, D), BF16),
            pltpu.VMEM((4, UP_ROWS, D), BF16),
            pltpu.VMEM((3, UP_ROWS, D), BF16),
            pltpu.VMEM((3, UP_ROWS, D), BF16),
            pltpu.VMEM((SLOTS * HEAD_DIM, D), BF16),
            pltpu.VMEM((4, 48, D), BF16),
            dma(2, 6), dma(2, 6), dma(6), dma(6), dma(4), dma(4), dma(4),
            dma(5), dma(5), dma(5), dma(4, 4), dma(4, 4), dma(2, 3), dma(2, 3), dma(4),
        ],
        compiler_params=params(3, 63),
        name="feed",
    )(middle, cot, *others, halves, vecs, out_w, mixed)


def back_kernel(
    x, grad_mid, dq, dk, dv, hid, whole, vecs, share, from_x, from_y, from_far, share_down, out_own, g_out, sums, up_sum,
    output, grad_x, up_out, down_out, qkv_out, o_out, vec_out, b_up_out,
    joint, full, land, land_k, land_v, part, rows_own, sum_land, g_qkv, z_right, z_left, s_qkv,
    s_out, zo_right, zo_left, own_qkv, own_out, all_up, all_down, all_qkv, all_out, local, vec_land, totals, wide,
    kv_send, kv_recv, g_send, g_recv, s_send, s_recv, a_send, a_recv, z_send, z_recv, t_send, t_recv, v_send, v_recv, c_local,
):
    e = Place()
    t, p, z = (e.t, e.p, e.z)
    e.greet()
    swaps = []
    for k in range(CHIPS):
        chip = e.flip(1 - k // 2, 1 - k % 2)
        for j, (ref, dst) in enumerate(((dk, land_k), (dv, land_v))):
            swaps.append(
                remote(ref.at[chip * 2 + 1 - p], dst.at[chip], kv_send.at[j, k], kv_recv.at[j, k], e.twin())
            )
    for copy in swaps:
        copy.start()

    def spread(number, own, everything, rows, cut):
        return Gather(
            e, own, lambda chip: everything.at[p, chip], rows, cut, a_send.at[number], a_recv.at[number]
        )

    def hand(number, own, everything, k):
        chip = e.flip(k % 2, k // 2)
        src = own if k == 0 else everything.at[p, chip]
        return remote(
            src, everything.at[p, chip], t_send.at[number, k], t_recv.at[number, k], e.twin()
        )

    def handed(number, own, everything):
        for k in range(CHIPS):
            chip = e.flip(k % 2, k // 2)
            copy = remote(
                own, everything.at[1 - p, chip], t_send.at[number, k], t_recv.at[number, k], e.twin()
            )
            copy.wait_recv()
            copy.wait_send()

    feeds = [share] + [ref.at[pl.ds(ROWS, UP_ROWS)] for ref in (from_x, from_y, from_far)]
    keeps = []
    for k in range(CHIPS):
        slot = all_up.at[p, e.flip(k % 2, k // 2)]
        keeps.append(pltpu.make_async_copy(feeds[k], slot, c_local.at[k]))
    downs = spread(2, share_down, all_down, DOWN_ROWS, 80)
    downs.start()
    outs = ZScatter(e, g_out, s_out, zo_right, zo_left, z_send.at[0], z_recv.at[0])
    outs.begin()
    local[...] = jnp.zeros_like(local)
    for k in range(CHIPS):
        joint[k, :, :WIDE] = dq[k]

    def trades(a):
        return [
            remote(
                full.at[a, rows16(i * 272 + (1 - p) * TILE, 144)], land.at[a, i],
                g_send.at[a, i], g_recv.at[a, i], e.twin(),
            )
            for i in range(4)
        ]

    def grads(a, carry):
        @pl.when(a == 1)
        def _():
            for copy in swaps:
                copy.wait()
            head_q, head_v = (jnp.zeros((1, WIDE), F32), jnp.zeros((1, WIDE), F32))
            for k in range(CHIPS):
                mine = k * 2 + p
                low_k = (dk[mine].astype(F32) + land_k[k].astype(F32)).astype(BF16)
                low_v = (dv[mine].astype(F32) + land_v[k].astype(F32)).astype(BF16)
                joint[k, :, WIDE : 2 * WIDE] = low_k
                joint[k, :, 2 * WIDE :] = low_v
                head_q = head_q + jnp.sum(dq[k].astype(F32), 0, keepdims=True)
                head_v = head_v + jnp.sum(low_v.astype(F32), 0, keepdims=True)
            local[pl.ds(12 + t, 1), :WIDE] = head_q
            local[pl.ds(12 + t, 1), WIDE : 2 * WIDE] = head_v
            outs.first()

        right = joint[:, :, pl.ds(pl.multiple_of(a * WIDE, TILE), WIDE)]
        full[a] = rows_product(
            hid[...].reshape(CHIPS * ROWS, D), right.reshape(CHIPS * ROWS, WIDE)
        ).astype(BF16)
        for copy in trades(a):
            copy.start()
        return carry

    lax.fori_loop(0, 3, grads, 0)
    downs.forward()
    outs.second()
    summed = Scatter(e, part, sum_land, s_send, s_recv)
    weights = ZScatter(e, g_qkv, s_qkv, z_right, z_left, z_send.at[1], z_recv.at[1])

    def block(k, carry):
        dest = e.flip(1 - k // 2, 1 - k % 2)
        value = cols_product(joint[dest], whole[...])

        @pl.when(k < 3)
        def _():
            part[dest] = value.astype(BF16)

        @pl.when(k == 0)
        def _():
            summed.far_ready()
            for a in range(3):
                for copy in trades(a):
                    copy.wait()
                for i in range(4):
                    own = full[a, rows16(i * 272 + p * TILE, 144)].astype(F32)
                    g_qkv[i, :, a * WIDE : (a + 1) * WIDE] = (own + land[a, i].astype(F32)).astype(BF16)
            weights.begin()

        @pl.when(k == 1)
        def _():
            summed.x_ready()

        @pl.when(k == 2)
        def _():
            summed.y_ready()

        @pl.when(k == 3)
        def _():
            rows_own[...] = value

        return carry

    lax.fori_loop(0, CHIPS, block, 0)
    outs.last(own_out)
    for k in range(CHIPS):
        keeps[k].start()
        slot = all_up.at[p, e.flip(k % 2, k // 2)]
        remote(feeds[k], slot, t_send.at[0, k], t_recv.at[0, k], e.twin()).start()
    hand(3, share_down, all_down, 0).start()
    all_down[p, t] = share_down[...]
    downs.have_x()
    downs.have_y()
    hand(3, share_down, all_down, 1).start()
    hand(3, share_down, all_down, 2).start()
    downs.have_far()
    hand(3, share_down, all_down, 3).start()
    weights.first()
    others = spread(0, own_out, all_out, 48, 32)
    others.start()
    all_out[p, t] = own_out[...]
    hand(1, own_out, all_out, 0).start()
    summed.relay()
    weights.second()
    others.forward()
    weights.last(own_qkv)
    qkvs = spread(1, own_qkv, all_qkv, 144, 80)
    qkvs.start()
    hand(2, own_qkv, all_qkv, 0).start()
    all_qkv[p, t] = own_qkv[...]
    normed, inverse = normalize(x[...].astype(F32))
    total = rows_own[...] + summed.total()
    local[:4] = sums[:4]
    local[4:5] = jnp.sum(total * normed, 0, keepdims=True)
    local[5:6] = jnp.sum(total, 0, keepdims=True)
    local[pl.ds(8 + t, 1), :] = up_sum[...]
    twin = remote(local, vec_land.at[0], v_send.at[0], v_recv.at[0], e.twin())
    twin.start()
    grad_x[...] = (grad_mid[...] + norm_back(total, normed, inverse, vecs[GAIN_1 : GAIN_1 + 1])).T
    twin.wait()
    totals[...] = local[...] + vec_land[0]
    planes = [
        remote(totals, vec_land.at[k], v_send.at[k], v_recv.at[k], e.plane(k)) for k in range(1, 4)
    ]
    for copy in planes:
        copy.start()
    qkvs.forward()
    others.have_x()
    others.have_y()
    hand(1, own_out, all_out, 1).start()
    hand(1, own_out, all_out, 2).start()
    others.have_far()
    hand(1, own_out, all_out, 3).start()
    handed(0, share, all_up)
    for copy in keeps:
        copy.wait()

    def lay_up(q, carry):
        rows = rows16(q * TILE, 144)
        for s in range(CHIPS):
            for i in range(4):
                column = D * i + HEAD_DIM * (i % 2) + 256 * s
                up_out[rows, column : column + 256] = all_up[q, s, :, 256 * i : 256 * (i + 1)]
        for s in range(0, CHIPS, 2):
            pair = [all_up[q, s + i, :, 1024:].astype(F32) for i in range(2)]
            column = D * s + 1024
            up_out[rows, column : column + TILE] = jnp.concatenate(pair, 1).astype(BF16)
        return carry

    lax.fori_loop(0, 2, lay_up, 0)
    qkvs.have_x()
    hand(2, own_qkv, all_qkv, 1).start()
    qkvs.have_y()
    hand(2, own_qkv, all_qkv, 2).start()
    for copy in planes:
        copy.wait()
    local[...] = totals[...] + vec_land[1] + vec_land[2] + vec_land[3]
    chips = [
        remote(local, vec_land.at[3 + k], v_send.at[3 + k], v_recv.at[3 + k], e.chip(chip))
        for k, chip in ((1, e.tx), (2, e.ty), (3, e.td))
    ]
    for copy in chips:
        copy.start()
    qkvs.have_far()
    hand(2, own_qkv, all_qkv, 3).start()

    result = out_own[...]
    for ref in (from_x, from_y, from_far):
        result = result + ref[:ROWS].astype(F32)
    output[...] = result.T.astype(BF16)
    handed(3, share_down, all_down)
    for q in range(2):
        for s in range(CHIPS):
            down_out[rows16(z % 2 * 64 + 256 * s + TILE * q, TILE)] = all_down[q, s, :TILE]
        down_out[rows16((1 - z % 2) * 1024 + 32 * q, 32)] = all_down[q, z, TILE:]
    handed(1, own_out, all_out)
    ahead = (CHIPS - z) % CHIPS * 16
    for s in range(CHIPS - 1):
        o_out[rows16(ahead + HEAD_DIM * s, 48)] = all_out[0, s]
        o_out[rows16(ahead + HEAD_DIM * s + 32, 32)] = all_out[1, s, :32]
    for u in range(SLOTS):
        q, first = ((0, 16 * u) if u < 3 else (1, 16 * u - 32))
        strip = all_out[q, CHIPS - 1, first : first + 16]

        @pl.when(16 * u < ahead)
        def _():
            o_out[16 * u : 16 * u + 16] = strip

        @pl.when(16 * u >= ahead)
        def _():
            o_out[192 + 16 * u : 208 + 16 * u] = strip

    for copy in chips:
        copy.wait()
    totals[...] = local[...] + vec_land[4] + vec_land[5] + vec_land[6]
    wide[...] = jnp.zeros_like(wide)
    wide[:6, :D] = totals[:6]
    columns = {}
    for s, heads in enumerate(HEAD_TABLE):
        for slot, head in enumerate(heads):
            columns[head] = (s, slot * HEAD_DIM)
    lane = lax.broadcasted_iota(jnp.int32, (1, TILE), 1)
    for a in range(2):
        def span(head, side):
            s, column = columns[head]
            start = (column + a * WIDE) // TILE * TILE
            tile = totals[12 + s : 13 + s, start : start + TILE]
            return tile if column % TILE // HEAD_DIM == side else pltpu.roll(tile, HEAD_DIM, 1)

        for head in range(0, HEADS, 2):
            tile = span(head, 0)
            if head + 1 < HEADS:
                tile = jnp.where(lane < HEAD_DIM, tile, span(head + 1, 1))
            wide[6 + a : 7 + a, head * HEAD_DIM : head * HEAD_DIM + TILE] = tile
    for i in range(4):
        @pl.when(z == i)
        def _():
            row = wide[...]
            if i > 0:
                row = pltpu.roll(row, 9 * TILE - D // 4 * i, 1)
            vec_out[...] = row[:, :WIDE]
            pieces = [totals[8 + s : 9 + s, 256 * i : 256 * i + 256] for s in range(CHIPS)]
            more = totals[8 + i : 9 + i, 1024:]
            if i % 2 == 0:
                b_up_out[...] = jnp.concatenate(pieces + [more, more], 1)
            else:
                b_up_out[...] = pltpu.roll(jnp.concatenate(pieces + [more, more], 1), HEAD_DIM, 1)

    handed(2, own_qkv, all_qkv)
    source = {}
    for s, heads in enumerate(HEAD_TABLE):
        for slot, head in enumerate(heads):
            if head >= 0:
                for a in range(3):
                    source[a * HEADS + head] = (s, a * WIDE + slot * HEAD_DIM)

    def lay_qkv(q, carry):
        rows = rows16(q * TILE, 144)

        def piece(g, side):
            s, column = source[g]
            tile = all_qkv[q, s, :, column // TILE * TILE : column // TILE * TILE + TILE].astype(F32)
            return tile if column % TILE // HEAD_DIM == side else pltpu.roll(tile, HEAD_DIM, 1)

        left = lax.broadcasted_iota(jnp.int32, (144, TILE), 1) < HEAD_DIM
        for g in range(0, 3 * HEADS - 1, 2):
            column = g * HEAD_DIM
            qkv_out[rows, column : column + TILE] = jnp.where(left, piece(g, 0), piece(g + 1, 1)).astype(BF16)
        column = (3 * HEADS - 1) * HEAD_DIM
        qkv_out[rows, column : column + HEAD_DIM] = piece(3 * HEADS - 1, 0)[:, :HEAD_DIM].astype(BF16)
        return carry

    lax.fori_loop(0, 2, lay_qkv, 0)
    for user in (downs, others, qkvs, summed):
        user.sent()


def back(x, grad_mid, dq, dk, dv, hid, whole, vecs, share, others, share_down, out_own, g_out, sums, up_sum):
    heads = pltpu.VMEM((CHIPS, ROWS, WIDE), BF16)
    qkv, out = ((144, 3 * WIDE), (48, D))

    def many(count, shape):
        return pltpu.VMEM((count, *shape), BF16)

    return pl.pallas_call(
        back_kernel,
        out_shape=(
            jax.ShapeDtypeStruct((D, ROWS), BF16),
            jax.ShapeDtypeStruct((D, ROWS), F32),
            jax.ShapeDtypeStruct((D // 4, 4 * D), BF16),
            jax.ShapeDtypeStruct((D, D), BF16),
            jax.ShapeDtypeStruct((D // 4, 3 * D), BF16),
            jax.ShapeDtypeStruct((D // 4, D), BF16),
            jax.ShapeDtypeStruct((8, WIDE), F32),
            jax.ShapeDtypeStruct((1, 9 * TILE), F32),
        ),
        in_specs=vmem(17),
        out_specs=tuple(vmem(8)),
        scratch_shapes=[
            pltpu.VMEM((CHIPS, ROWS, 3 * WIDE), BF16),
            pltpu.VMEM((3, D, WIDE), BF16),
            pltpu.VMEM((3, 4, 144, WIDE), BF16),
            heads, heads,
            pltpu.VMEM((CHIPS, ROWS, D), BF16),
            pltpu.VMEM((ROWS, D), F32),
            pltpu.VMEM((6, HALF, D), BF16),
            many(4, qkv), many(3, qkv), many(3, qkv), many(4, qkv),
            many(4, out), many(3, out), many(3, out),
            pltpu.VMEM(qkv, BF16), pltpu.VMEM(out, BF16),
            pltpu.VMEM((2, CHIPS, UP_ROWS, D), BF16),
            pltpu.VMEM((2, CHIPS, DOWN_ROWS, D), BF16),
            pltpu.VMEM((2, CHIPS, *qkv), BF16),
            pltpu.VMEM((2, CHIPS, *out), BF16),
            pltpu.VMEM((16, D), F32),
            pltpu.VMEM((7, 16, D), F32),
            pltpu.VMEM((16, D), F32),
            pltpu.VMEM((8, 9 * TILE), F32),
            dma(2, CHIPS), dma(2, CHIPS), dma(3, 4), dma(3, 4), dma(6), dma(6), dma(3, 6), dma(3, 6),
            dma(2, 2, 3), dma(2, 2, 3), dma(4, 4), dma(4, 4), dma(7), dma(7), dma(4),
        ],
        compiler_params=params(4, 63),
        name="back",
    )(x, grad_mid, dq, dk, dv, hid, whole, vecs, share, *others, share_down, out_own, g_out, sums, up_sum)


def plane_device(
    tokens, seq_lengths, cotangent, ln1_gain, ln1_bias, w_qkv, b_query, b_value, w_out, b_out,
    ln2_gain, ln2_bias, w_up, b_up, w_down, b_down,
):
    c = lax.axis_index("ctx")
    lengths = seq_lengths[0]
    parity = (c % 2)[None].astype(jnp.int32)
    shard = D // 4

    biases = (b_query, b_value, b_out, b_down, ln1_gain, ln1_bias, ln2_gain, ln2_bias)
    q, k, v, hid, whole, out_w, vecs, halves, sent, x = project(
        tokens[0].T, cotangent[0].T, biases, b_up, w_qkv, w_out, w_up, w_down
    )
    halves = lax.all_gather(halves, "wsh", axis=0)

    def from_chips(*arrays):
        return [lax.ppermute(array, "ctx", list(enumerate(to))) for array, to in zip(arrays, flips)]

    flips = [[(i // 2 ^ mask) * 2 + i % 2 for i in range(2 * CHIPS)] for mask in (1, 2, 3)]
    tops = from_chips(sent, sent, sent)
    mixed, lse = attend(lengths, parity, q, k, v)
    middle = out_project(x, mixed, out_w, vecs)
    to_x, to_y, to_far, out_own, grad_mid, grad_heads, g_out, g_down, share, sums, up_sum = feed(
        middle, sent, tops, halves, vecs, out_w, mixed
    )
    others = from_chips(to_x, to_y, to_far)
    share_down = lax.psum_scatter(
        g_down.reshape(4 * DOWN_ROWS, D), "wsh", scatter_dimension=0, tiled=True
    )
    dq, dk, dv = attend_back(lengths, parity, q, k, v, mixed, grad_heads, lse)
    output, grad_x, grad_up, grad_down, grad_qkv, grad_out, vectors, grad_b_up = back(
        x, grad_mid, dq, dk, dv, hid, whole, vecs, share, others, share_down, out_own, g_out, sums, up_sum
    )
    grad_up, grad_down, grad_qkv, grad_out = (
        array.astype(F32) for array in (grad_up, grad_down, grad_qkv, grad_out)
    )

    mine = [row[:shard] for row in vectors]
    grad_b_up = grad_b_up[0, :D]
    return (
        output.T[None], grad_x.T[None],
        mine[4], mine[5], grad_qkv, mine[6], mine[7], grad_out, mine[0],
        mine[2], mine[3], grad_up, grad_b_up, grad_down, mine[1],
    )


def solution(mesh):
    in_specs = (
        P("wsh", "ctx", None),
        P("wsh", None),
        P("wsh", "ctx", None),
        P("wsh"),
        P("wsh"),
        P("wsh", None),
        P("wsh"),
        P("wsh"),
        P("wsh", None),
        P("wsh"),
        P("wsh"),
        P("wsh"),
        P("wsh", None),
        P("wsh"),
        P("wsh", None),
        P("wsh"),
    )
    out_specs = (
        P("wsh", "ctx", None),
        P("wsh", "ctx", None),
        P("wsh"),
        P("wsh"),
        P("wsh", None),
        P("wsh"),
        P("wsh"),
        P("wsh", None),
        P("wsh"),
        P("wsh"),
        P("wsh"),
        P("wsh", None),
        P("wsh"),
        P("wsh", None),
        P("wsh"),
    )
    sizes = (mesh.shape["ctx"], mesh.shape["wsh"])
    body = plane_device if sizes == (2 * CHIPS, 4) else on_device
    return jax.shard_map(
        body, mesh=mesh, in_specs=in_specs, out_specs=out_specs, check_vma=False
    )
```

```python
import functools
import math

import jax
import jax.numpy as jnp
from jax import lax
from jax.experimental import pallas as pl
from jax.experimental.pallas import tpu as pltpu
from jax.sharding import PartitionSpec as P

D = 1088
HEADS = 17
HEAD_DIM = 64


def normalize(inputs):
    center = inputs - jnp.mean(inputs, -1, keepdims=True)
    inverse = lax.rsqrt(jnp.mean(center * center, -1, keepdims=True) + 1e-05)
    return (center * inverse, inverse)


def norm_back(grad_in, normed, inverse, gain):
    scaled = grad_in * gain
    return inverse * (
        scaled
        - jnp.mean(scaled, -1, keepdims=True)
        - normed * jnp.mean(scaled * normed, -1, keepdims=True)
    )


def rows_product(left, right):
    return lax.dot_general(
        left, right, (((0,), (0,)), ((), ())), preferred_element_type=jnp.float32
    )


def cols_product(left, right):
    return lax.dot_general(
        left, right, (((1,), (1,)), ((), ())), preferred_element_type=jnp.float32
    )


def sequence_ids(lengths, positions):
    bounds = jnp.cumsum(lengths)
    return jnp.sum((positions[:, None] >= bounds[None, :]).astype(jnp.int32), axis=1)


def allowed_pairs(lengths, query_pos, key_pos):
    query_owner = sequence_ids(lengths, query_pos)
    key_owner = sequence_ids(lengths, key_pos)
    return (key_pos[None, :] <= query_pos[:, None]) & (
        (key_owner[None, :] == 0) | (key_owner[None, :] == query_owner[:, None])
    )


def over_blocks(state_in, arrays, step_fn):
    total_rows = arrays[0].shape[0]
    block_rows = math.gcd(total_rows, 512)

    def advance(block_index, state_now):
        offset = block_index * block_rows
        pieces = tuple((lax.dynamic_slice_in_dim(array, offset, block_rows, 0) for array in arrays))
        return step_fn(state_now, pieces, offset)

    return lax.fori_loop(0, total_rows // block_rows, advance, state_in)


def sectioned_sum(partials):
    shares = lax.psum_scatter(partials, "wsh", scatter_dimension=0, tiled=True)
    return lax.psum(shares, "ctx")


def on_device(
    tokens,
    seq_lengths,
    cotangent,
    ln1_gain,
    ln1_bias,
    w_qkv,
    b_query,
    b_value,
    w_out,
    b_out,
    ln2_gain,
    ln2_bias,
    w_up,
    b_up,
    w_down,
    b_down,
):
    token_rows, grad_rows = (tokens[0], cotangent[0])
    shards = (
        w_qkv,
        w_out,
        w_up,
        w_down,
        b_query,
        b_value,
        b_out,
        b_up,
        b_down,
        ln1_gain,
        ln1_bias,
        ln2_gain,
        ln2_bias,
    )
    gathered = (
        lax.all_gather(shards[0], "wsh", axis=0, tiled=True),
        lax.all_gather(shards[1], "wsh", axis=0, tiled=True),
        lax.all_gather(shards[2], "wsh", axis=0, tiled=True),
        lax.all_gather(shards[3], "wsh", axis=0, tiled=True),
        lax.all_gather(shards[4], "wsh", axis=0, tiled=True),
        lax.all_gather(shards[5], "wsh", axis=0, tiled=True),
        lax.all_gather(shards[6], "wsh", axis=0, tiled=True),
        lax.all_gather(shards[7], "wsh", axis=0, tiled=True),
        lax.all_gather(shards[8], "wsh", axis=0, tiled=True),
        lax.all_gather(shards[9], "wsh", axis=0, tiled=True),
        lax.all_gather(shards[10], "wsh", axis=0, tiled=True),
        lax.all_gather(shards[11], "wsh", axis=0, tiled=True),
        lax.all_gather(shards[12], "wsh", axis=0, tiled=True),
    )
    qkv_full, out_full, up_full, down_full = (gathered[0], gathered[1], gathered[2], gathered[3])
    query_bias, value_bias, out_bias, up_bias, down_bias = [
        piece.astype(jnp.float32) for piece in gathered[4:9]
    ]
    gain_one, shift_one, gain_two, shift_two = [
        piece.astype(jnp.float32) for piece in gathered[9:13]
    ]
    lengths = seq_lengths[0]
    tok_rows = token_rows.shape[0]
    my_pos = lax.axis_index("ctx") * tok_rows + jnp.arange(tok_rows, dtype=jnp.int32)
    scale_qk = HEAD_DIM ** (-0.5)
    inputs = token_rows.astype(jnp.float32)
    normed_one, inverse_one = normalize(inputs)
    hidden_one = (normed_one * gain_one + shift_one).astype(jnp.bfloat16)
    joint_proj = jnp.dot(hidden_one, qkv_full, preferred_element_type=jnp.float32)
    queries = (joint_proj[:, :D] + query_bias).astype(jnp.bfloat16)
    key_rows = joint_proj[:, D : 2 * D].astype(jnp.bfloat16)
    value_rows = (joint_proj[:, 2 * D :] + value_bias).astype(jnp.bfloat16)
    query_heads = queries.reshape(tok_rows, HEADS, HEAD_DIM)
    my_key_heads = key_rows.reshape(tok_rows, HEADS, HEAD_DIM)
    my_value_heads = value_rows.reshape(tok_rows, HEADS, HEAD_DIM)

    def forward_step(state_now, pieces, first_row):
        key_heads = pieces[0].reshape(-1, HEADS, HEAD_DIM)
        value_heads = pieces[1].reshape(-1, HEADS, HEAD_DIM)
        key_pos = first_row + jnp.arange(key_heads.shape[0], dtype=jnp.int32)
        allowed = allowed_pairs(lengths, my_pos, key_pos)

        def forward_compute(inner):
            peak_old, total_old, accum_old = inner
            scores = (
                jnp.einsum(
                    "qhd,khd->hqk", query_heads, key_heads, preferred_element_type=jnp.float32
                )
                * scale_qk
            )
            scores = jnp.where(allowed[None], scores, -1e30)
            peak_new = jnp.maximum(peak_old, jnp.max(scores, -1))
            factor = jnp.exp(peak_old - peak_new)
            expos = jnp.where(allowed[None], jnp.exp(scores - peak_new[:, :, None]), 0.0)
            total_new = total_old * factor + jnp.sum(expos, -1)
            accum_new = accum_old * factor.T[:, :, None] + jnp.einsum(
                "hqk,khd->qhd",
                expos.astype(jnp.bfloat16),
                value_heads,
                preferred_element_type=jnp.float32,
            )
            return (peak_new, total_new, accum_new)

        return lax.cond(jnp.any(allowed), forward_compute, lambda inner: inner, state_now)

    start_state = (
        jnp.full((HEADS, tok_rows), -1e30, jnp.float32),
        jnp.zeros((HEADS, tok_rows), jnp.float32),
        jnp.zeros((tok_rows, HEADS, HEAD_DIM), jnp.float32),
    )
    peak, total, accum = over_blocks(
        start_state,
        (
            lax.all_gather(key_rows, "ctx", axis=0, tiled=True),
            lax.all_gather(value_rows, "ctx", axis=0, tiled=True),
        ),
        forward_step,
    )
    mixed = accum / total.T[:, :, None]
    log_sum = (peak + jnp.log(total)).T
    mixed_low = mixed.reshape(tok_rows, D).astype(jnp.bfloat16)
    middle = inputs + jnp.dot(mixed_low, out_full, preferred_element_type=jnp.float32) + out_bias
    normed_two, inverse_two = normalize(middle)
    hidden_two = (normed_two * gain_two + shift_two).astype(jnp.bfloat16)
    pre_act = jnp.dot(hidden_two, up_full, preferred_element_type=jnp.float32) + up_bias
    activ_low = jax.nn.gelu(pre_act, approximate=False).astype(jnp.bfloat16)
    result = middle + jnp.dot(activ_low, down_full, preferred_element_type=jnp.float32) + down_bias
    output_rows = result.astype(jnp.bfloat16)
    grad_top_f = grad_rows.astype(jnp.float32)
    grad_down = rows_product(activ_low, grad_rows)
    grad_down_bias = jnp.sum(grad_top_f, 0)
    grad_act = cols_product(grad_rows, down_full)
    cdf_part = 0.5 * (1.0 + lax.erf(pre_act * math.sqrt(0.5)))
    pdf_part = jnp.exp(-0.5 * pre_act * pre_act) / math.sqrt(2.0 * math.pi)
    grad_pre = (grad_act * (cdf_part + pre_act * pdf_part)).astype(jnp.bfloat16)
    grad_up = rows_product(hidden_two, grad_pre)
    grad_up_bias = jnp.sum(grad_pre.astype(jnp.float32), 0)
    grad_h2 = cols_product(grad_pre, up_full)
    grad_gain_two = jnp.sum(grad_h2 * normed_two, 0)
    grad_shift_two = jnp.sum(grad_h2, 0)
    grad_mid = grad_top_f + norm_back(grad_h2, normed_two, inverse_two, gain_two)
    grad_mid_low = grad_mid.astype(jnp.bfloat16)
    grad_out_w = rows_product(mixed_low, grad_mid_low)
    grad_out_bias = jnp.sum(grad_mid_low.astype(jnp.float32), 0)
    grad_mixed = cols_product(grad_mid_low, out_full).astype(jnp.bfloat16)
    grad_heads = grad_mixed.reshape(tok_rows, HEADS, HEAD_DIM)
    delta = jnp.sum(grad_heads.astype(jnp.float32) * mixed, -1)
    lse_all, delta_all = (
        lax.all_gather(log_sum, "ctx", axis=0, tiled=True),
        lax.all_gather(delta, "ctx", axis=0, tiled=True),
    )

    def query_step(state_now, pieces, first_row):
        key_heads = pieces[0].reshape(-1, HEADS, HEAD_DIM)
        value_heads = pieces[1].reshape(-1, HEADS, HEAD_DIM)
        key_pos = first_row + jnp.arange(key_heads.shape[0], dtype=jnp.int32)
        allowed = allowed_pairs(lengths, my_pos, key_pos)

        def query_compute(accum_old):
            scores = (
                jnp.einsum(
                    "qhd,khd->hqk", query_heads, key_heads, preferred_element_type=jnp.float32
                )
                * scale_qk
            )
            probs = jnp.where(allowed[None], jnp.exp(scores - log_sum.T[:, :, None]), 0.0)
            grad_probs = jnp.einsum(
                "qhd,khd->hqk", grad_heads, value_heads, preferred_element_type=jnp.float32
            )
            grad_scores = (probs * (grad_probs - delta.T[:, :, None])).astype(jnp.bfloat16)
            return accum_old + jnp.einsum(
                "hqk,khd->qhd", grad_scores, key_heads, preferred_element_type=jnp.float32
            )

        return lax.cond(jnp.any(allowed), query_compute, lambda inner: inner, state_now)

    zero_heads = jnp.zeros((tok_rows, HEADS, HEAD_DIM), jnp.float32)
    grad_query = over_blocks(
        zero_heads,
        (
            lax.all_gather(key_rows, "ctx", axis=0, tiled=True),
            lax.all_gather(value_rows, "ctx", axis=0, tiled=True),
        ),
        query_step,
    )

    def key_step(state_now, pieces, first_row):
        other_queries = pieces[0].reshape(-1, HEADS, HEAD_DIM)
        other_grads = pieces[1].reshape(-1, HEADS, HEAD_DIM)
        other_count = other_queries.shape[0]
        other_pos = first_row + jnp.arange(other_count, dtype=jnp.int32)
        other_lse = lax.dynamic_slice_in_dim(lse_all, first_row, other_count, 0)
        other_delta = lax.dynamic_slice_in_dim(delta_all, first_row, other_count, 0)
        allowed = allowed_pairs(lengths, other_pos, my_pos)

        def key_compute(inner):
            grad_key_old, grad_value_old = inner
            scores = (
                jnp.einsum(
                    "qhd,khd->hqk", other_queries, my_key_heads, preferred_element_type=jnp.float32
                )
                * scale_qk
            )
            probs = jnp.where(allowed[None], jnp.exp(scores - other_lse.T[:, :, None]), 0.0)
            grad_value_new = grad_value_old + jnp.einsum(
                "hqk,qhd->khd",
                probs.astype(jnp.bfloat16),
                other_grads,
                preferred_element_type=jnp.float32,
            )
            grad_probs = jnp.einsum(
                "qhd,khd->hqk", other_grads, my_value_heads, preferred_element_type=jnp.float32
            )
            grad_scores = (probs * (grad_probs - other_delta.T[:, :, None])).astype(jnp.bfloat16)
            grad_key_new = grad_key_old + jnp.einsum(
                "hqk,qhd->khd", grad_scores, other_queries, preferred_element_type=jnp.float32
            )
            return (grad_key_new, grad_value_new)

        return lax.cond(jnp.any(allowed), key_compute, lambda inner: inner, state_now)

    grad_key, grad_value = over_blocks(
        (zero_heads, zero_heads),
        (
            lax.all_gather(queries, "ctx", axis=0, tiled=True),
            lax.all_gather(grad_mixed, "ctx", axis=0, tiled=True),
        ),
        key_step,
    )
    grad_joint = jnp.concatenate(
        [
            (grad_query * scale_qk).reshape(tok_rows, D),
            (grad_key * scale_qk).reshape(tok_rows, D),
            grad_value.reshape(tok_rows, D),
        ],
        axis=1,
    ).astype(jnp.bfloat16)
    grad_qkv_w = rows_product(hidden_one, grad_joint)
    grad_joint_f = grad_joint.astype(jnp.float32)
    grad_query_bias = jnp.sum(grad_joint_f[:, :D], 0)
    grad_value_bias = jnp.sum(grad_joint_f[:, 2 * D :], 0)
    grad_h1 = cols_product(grad_joint, qkv_full)
    grad_gain_one = jnp.sum(grad_h1 * normed_one, 0)
    grad_shift_one = jnp.sum(grad_h1, 0)
    grad_input = grad_mid + norm_back(grad_h1, normed_one, inverse_one, gain_one)
    matrices = (grad_qkv_w, grad_out_w, grad_up, grad_down)
    vectors = (
        grad_query_bias,
        grad_value_bias,
        grad_out_bias,
        grad_up_bias,
        grad_down_bias,
        grad_gain_one,
        grad_shift_one,
        grad_gain_two,
        grad_shift_two,
    )
    totals = sectioned_sum(matrices + vectors)
    return (
        output_rows[None],
        grad_input[None],
        totals[9],
        totals[10],
        totals[0],
        totals[4],
        totals[5],
        totals[1],
        totals[6],
        totals[11],
        totals[12],
        totals[2],
        totals[7],
        totals[3],
        totals[8],
    )


SLOTS = 5
WIDE = 384
ROWS = 256
HALF = ROWS // 2
CHIPS = 4
TILE = 128
UP_ROWS, DOWN_ROWS = (144, 160)
MESH_ID = pl.DeviceIdType.MESH
F32, BF16 = (jnp.float32, jnp.bfloat16)
NEG = -1e30
HEAD_TABLE = ((0, 5, 9, 13, -40), (1, 6, 10, 14, -40), (2, 7, 11, 15, -40), (3, 4, 8, 12, 16))
B_QUERY, B_VALUE, B_OUT, B_DOWN, GAIN_1, SHIFT_1, GAIN_2, SHIFT_2, B_UP = range(9)


def nn(left, right):
    return jnp.dot(left, right, preferred_element_type=F32)


def remote(src, dst, send, recv, where):
    return pltpu.make_async_remote_copy(
        src_ref=src, dst_ref=dst, send_sem=send, recv_sem=recv, device_id=where, device_id_type=MESH_ID
    )


def rows16(start, size):
    return pl.ds(pl.multiple_of(start, 16), size)


class Place:
    def __init__(self):
        self.c, self.z = (lax.axis_index("ctx"), lax.axis_index("wsh"))
        self.t, self.p = (self.c // 2, self.c % 2)
        self.tx, self.ty, self.td = (self.flip(1, 0), self.flip(0, 1), self.flip(1, 1))

    def flip(self, dx, dy):
        return (self.t // 2 + dy) % 2 * 2 + (self.t % 2 + dx) % 2

    def chip(self, chip):
        return (chip * 2 + self.p, self.z)

    def twin(self):
        return (self.t * 2 + 1 - self.p, self.z)

    def plane(self, step):
        return (self.c, (self.z + step) % 4)

    def greet(self, planes=True):
        barrier = pltpu.get_barrier_semaphore()
        others = [self.chip(self.tx), self.chip(self.ty), self.twin()]
        if planes:
            others += [self.plane(1), self.plane(2), self.plane(3)]
        for where in others:
            pl.semaphore_signal(barrier, inc=1, device_id=where, device_id_type=MESH_ID)
        pl.semaphore_wait(barrier, len(others))


class Gather:
    def __init__(self, e, own, view, rows, cut, send, recv):
        self.e, self.own, self.view, self.send, self.recv = (e, own, view, send, recv)
        self.parts = (pl.ds(0, cut), pl.ds(cut, rows - cut))

    def copy(self, i):
        e = self.e
        chip = (e.t, e.t, e.t, e.t, e.tx, e.ty)[i]
        part = self.parts[(0, 1, 1, 0, 0, 1)[i]]
        src = self.own if i < 4 else self.view(chip)
        where = e.chip((e.tx, e.tx, e.ty, e.ty, e.ty, e.tx)[i])
        return remote(src.at[part], self.view(chip).at[part], self.send.at[i], self.recv.at[i], where)

    def start(self):
        for i in (0, 2, 1, 3):
            self.copy(i).start()

    def forward(self):
        self.copy(0).wait_recv()
        self.copy(4).start()
        self.copy(2).wait_recv()
        self.copy(5).start()

    def have_x(self):
        self.copy(1).wait_recv()

    def have_y(self):
        self.copy(3).wait_recv()

    def have_far(self):
        self.copy(4).wait_recv()
        self.copy(5).wait_recv()

    def sent(self):
        for i in range(6):
            self.copy(i).wait_send()


class Scatter:
    def __init__(self, e, part, land, send, recv):
        self.e, self.part, self.land, self.send, self.recv = (e, part, land, send, recv)

    def copy(self, i):
        e = self.e
        chip = (e.td, e.td, e.tx, e.tx, e.ty, e.ty)[i]
        part = pl.ds((0, HALF, 0, HALF, HALF, 0)[i], HALF)
        where = e.chip((e.tx, e.ty, e.tx, e.tx, e.ty, e.ty)[i])
        return remote(
            self.part.at[chip, part], self.land.at[i], self.send.at[i], self.recv.at[i], where
        )

    def far_ready(self):
        self.copy(0).start()
        self.copy(1).start()

    def x_ready(self):
        self.copy(2).start()

    def y_ready(self):
        self.copy(4).start()

    def relay(self):
        self.copy(1).wait_recv()
        chip = self.e.tx
        self.part[chip, HALF:] = (self.part[chip, HALF:].astype(F32) + self.land[1].astype(F32)).astype(BF16)
        self.copy(3).start()
        self.copy(0).wait_recv()
        chip = self.e.ty
        self.part[chip, :HALF] = (self.part[chip, :HALF].astype(F32) + self.land[0].astype(F32)).astype(BF16)
        self.copy(5).start()

    def total(self):
        for i in (2, 4, 3, 5):
            self.copy(i).wait_recv()
        first = self.land[2].astype(F32) + self.land[5].astype(F32)
        second = self.land[4].astype(F32) + self.land[3].astype(F32)
        return jnp.concatenate([first, second], 0)

    def sent(self):
        for i in range(6):
            self.copy(i).wait_send()


class ZGather:
    def __init__(self, e, own, held, send, recv, put):
        self.e, self.own, self.held, self.send, self.recv, self.put = (e, own, held, send, recv, put)

    def copy(self, way, j):
        e = self.e
        shard = e.z - j if way == 0 else e.z + j
        src = self.own if j == 0 else self.held.at[shard]
        return remote(
            src, self.held.at[shard], self.send.at[way, j], self.recv.at[way, j], e.plane(1 if way == 0 else 3)
        )

    def sends(self, way, j):
        z = self.e.z
        return (z < 3) & (z >= j) if way == 0 else (z > 0) & (z <= 3 - j)

    def step(self, j):
        z = self.e.z
        for way in range(2):
            if j > 0:
                @pl.when(z >= j if way == 0 else z <= 3 - j)
                def _():
                    self.copy(way, j - 1).wait_recv()
            if j < 3:
                @pl.when(self.sends(way, j))
                def _():
                    self.copy(way, j).start()
            if j > 0:
                @pl.when(z >= j if way == 0 else z <= 3 - j)
                def _():
                    self.put(z - j if way == 0 else z + j)

    def sent(self):
        for way in range(2):
            for j in range(3):
                @pl.when(self.sends(way, j))
                def _():
                    self.copy(way, j).wait_send()


class ZScatter:
    def __init__(self, e, own, staged, right, left, send, recv):
        self.e, self.own, self.staged, self.land = (e, own, staged, (right, left))
        self.send, self.recv = (send, recv)

    def copy(self, way, j, src):
        return remote(
            src, self.land[way].at[j], self.send.at[way, j], self.recv.at[way, j],
            self.e.plane(1 if way == 0 else 3),
        )

    def begin(self):
        for plane, way in ((0, 0), (3, 1)):
            @pl.when(self.e.z == plane)
            def _():
                for j in range(3):
                    self.copy(way, j, self.own.at[3 - j if way == 0 else j]).start()

    def relay(self, way, j):
        dest = 3 - j if way == 0 else j
        self.copy(way, j, self.staged.at[dest]).wait_recv()
        self.staged[dest] = (self.own[dest].astype(F32) + self.land[way][j].astype(F32)).astype(BF16)
        self.copy(way, j, self.staged.at[dest]).start()

    def first(self):
        for plane, way in ((1, 0), (2, 1)):
            @pl.when(self.e.z == plane)
            def _():
                self.relay(way, 0)

    def second(self):
        for plane, way in ((1, 0), (2, 1)):
            @pl.when(self.e.z == plane)
            def _():
                self.relay(1 - way, 0)
                self.relay(way, 1)

    def last(self, out):
        right, left = self.land
        for z in range(4):
            @pl.when(self.e.z == z)
            def _():
                total = self.own[z].astype(F32)
                if z > 0:
                    self.copy(0, 3 - z, self.own.at[z]).wait_recv()
                    total = total + right[3 - z].astype(F32)
                if z < 3:
                    self.copy(1, z, self.own.at[z]).wait_recv()
                    total = total + left[z].astype(F32)
                out[...] = total.astype(BF16)
                for way in range(2):
                    for j in range((3 - z) if way == 0 else z):
                        self.copy(way, j, self.own.at[z]).wait_send()


def dma(*shape):
    return pltpu.SemaphoreType.DMA(shape)


def params(number, mib=56):
    return pltpu.CompilerParams(
        collective_id=number, has_side_effects=True, vmem_limit_bytes=mib * 2**20
    )


def vmem(count):
    return [pl.BlockSpec(memory_space=pltpu.VMEM)] * count


class Halves:
    def __init__(self, e, whole, block, keep, step, local, send, recv):
        self.e, self.whole, self.block, self.keep, self.step = (e, whole, block, keep, step)
        self.local, self.send, self.recv = (local, send, recv)

    def copies(self, src, shard):
        e = self.e
        return (
            pltpu.make_async_copy(
                src, self.whole.at[rows16(shard * self.block + e.p * self.step, self.keep)], self.local.at[shard]
            ),
            remote(
                src.at[rows16(e.p * (self.keep - self.step), self.step)],
                self.whole.at[rows16(shard * self.block + e.p * self.keep, self.step)],
                self.send.at[shard], self.recv.at[shard], e.twin(),
            ),
        )

    def put(self, src, shard):
        for copy in self.copies(src, shard):
            copy.start()

    def wait(self, src):
        for shard in range(4):
            for copy in self.copies(src, shard):
                copy.wait()


def half_tiles(source, columns):
    def piece(column, side):
        if column is None:
            return jnp.zeros((source.shape[0], TILE), F32)
        start = column // TILE * TILE
        if start + TILE > source.shape[-1]:
            part = source[:, start : start + HEAD_DIM].astype(F32)
            tile = jnp.concatenate([part, jnp.zeros_like(part)], 1)
        else:
            tile = source[:, start : start + TILE].astype(F32)
        return tile if column % TILE // HEAD_DIM == side else pltpu.roll(tile, HEAD_DIM, 1)

    tiles = []
    for i in range(0, len(columns), 2):
        first, second = (piece(columns[i], 0), piece(columns[i + 1], 1))
        lane = lax.broadcasted_iota(jnp.int32, first.shape, 1)
        tiles.append(jnp.where(lane < HEAD_DIM, first, second))
    return tiles


def head_columns(heads, first):
    return [first + head * HEAD_DIM if head >= 0 else None for head in heads] + [None]


def project_kernel(
    x, cot, bias_0, bias_1, bias_2, bias_3, bias_4, bias_5, bias_6, bias_7, b_up, w_qkv, w_out, w_up, w_down,
    q_out, k_out, v_out, h_out, whole, out_w, vecs, halves, cot_out, x_out,
    qkv_rows, half, half_o, edge, held, held_o, raw, vec_in, vec_land, bias,
    v_send, v_recv, z_send, z_recv, a_send, a_recv, w_local, w_send, w_recv, kv_send, kv_recv, r_local,
):
    e = Place()
    t, p, z = (e.t, e.p, e.z)
    rows = pltpu.make_async_copy(w_qkv.at[rows16(p * TILE, 144)], qkv_rows, r_local.at[0])
    rows.start()
    loads = []
    for i in range(4):
        column = pl.multiple_of(D * i + HEAD_DIM * (i % 2) + 256 * t, TILE)
        loads.append((w_up.at[rows16(p * TILE, 144), pl.ds(column, 256)], halves.at[pl.ds(0, 144), pl.ds(256 * i, 256)]))
    column = pl.multiple_of(1024 + 2 * D * (t // 2), TILE)
    loads.append((w_up.at[rows16(p * TILE, 144), pl.ds(column, TILE)], edge))
    loads.append((w_down.at[rows16(HEAD_DIM * (z % 2) + 256 * t + TILE * p, TILE)], halves.at[pl.ds(144, TILE)]))
    loads.append((w_down.at[rows16(1024 * (1 - z % 2) + 32 * p, 32)], halves.at[pl.ds(272, 32)]))
    loads = [pltpu.make_async_copy(src, dst, r_local.at[1 + i]) for i, (src, dst) in enumerate(loads)]
    for copy in loads:
        copy.start()
    spot = lax.broadcasted_iota(jnp.int32, (D // 4, D), 1) - D // 4 * z
    match = (spot == lax.broadcasted_iota(jnp.int32, (D // 4, D), 0)).astype(F32).astype(BF16)
    biases = (bias_0, bias_1, bias_2, bias_3, bias_4, bias_5, bias_6, bias_7)
    biases = jnp.concatenate([ref[...].astype(F32).reshape(1, D // 4) for ref in biases], 0)
    vec_in[0] = nn(biases.astype(BF16), match)
    e.greet()

    def exchange(i):
        return [
            remote(vec_in.at[i], vec_land.at[k, i], v_send.at[i, k], v_recv.at[i, k], e.plane(k))
            for k in range(1, 4)
        ]

    vectors = exchange(0)
    for copy in vectors:
        copy.start()
    into = Halves(e, whole, 272, 144, 128, w_local.at[0], w_send.at[0], w_recv.at[0])
    into_o = Halves(e, raw, 80, 48, 32, w_local.at[1], w_send.at[1], w_recv.at[1])
    chain = ZGather(
        e, half, held, z_send.at[0], z_recv.at[0], lambda shard: into.put(held.at[shard], shard)
    )
    chain_o = ZGather(
        e, half_o, held_o, z_send.at[1], z_recv.at[1], lambda shard: into_o.put(held_o.at[shard], shard)
    )
    rows.wait()
    for chip in range(CHIPS):
        @pl.when(t == chip)
        def _():
            for a in range(3):
                tiles = half_tiles(qkv_rows, head_columns(HEAD_TABLE[chip], a * D))
                for i in range(3):
                    half[:, a * WIDE + i * TILE : a * WIDE + (i + 1) * TILE] = tiles[i].astype(BF16)

    chain.step(0)
    into.put(half, z)
    inputs = x[...].astype(F32).T
    x_out[...] = inputs.astype(BF16)
    normed, _ = normalize(inputs)
    total = vec_in[0]
    for k in range(1, 4):
        vectors[k - 1].wait_recv()
        total = total + vec_land[k, 0]
    vecs[:8] = total
    h_out[t] = (normed * vecs[GAIN_1 : GAIN_1 + 1] + vecs[SHIFT_1 : SHIFT_1 + 1]).astype(BF16)
    hidden = Gather(e, h_out.at[t], lambda chip: h_out.at[chip], ROWS, HALF, a_send, a_recv)
    hidden.start()
    ahead = (CHIPS - z) % CHIPS * 16
    for m in range(3):
        unit = 16 * (2 * p + m)
        late = jnp.where(unit < ahead, unit, 192 + unit)
        first = jnp.where(t < CHIPS - 1, ahead + HEAD_DIM * t + unit, late)
        half_o[16 * m : 16 * m + 16] = w_out[rows16(first, 16)]
    for chip in range(CHIPS):
        @pl.when(t == chip)
        def _():
            tiles = half_tiles(vecs, head_columns(HEAD_TABLE[chip], 0))
            for i in range(3):
                bias[:, i * TILE : (i + 1) * TILE] = tiles[i]

    spot = lax.broadcasted_iota(jnp.int32, (D, 320), 1)
    at = jnp.where(spot < 256, HEAD_DIM * (z % 2) + 256 * t + spot, 1024 * (1 - z % 2) + spot - 256)
    match = (lax.broadcasted_iota(jnp.int32, (D, 320), 0) == at).astype(F32).astype(BF16)
    ups = nn(b_up[...].astype(F32).reshape(1, D).astype(BF16), match)
    vec_in[1] = jnp.zeros((8, D), F32)
    for i in range(4):
        @pl.when(z == i)
        def _():
            vec_in[1, 0:1, 256 * i : 256 * i + 256] = ups[0:1, :256]

    @pl.when(z == t)
    def _():
        vec_in[1, 0:1, 1024:] = ups[0:1, 256:]

    vectors = vectors + exchange(1)
    for copy in vectors[3:]:
        copy.start()
    cot_out[:ROWS] = cot[...].astype(F32).T.astype(BF16)
    cot_out[ROWS:] = jnp.zeros((8, D), BF16)
    for copy in loads:
        copy.wait()
    column = edge[...].astype(F32)
    column = jnp.where(t % 2 == 1, pltpu.roll(column, HEAD_DIM, 1), column)
    halves[:144, 1024:] = column[:, :HEAD_DIM].astype(BF16)
    chain.step(1)
    hidden.forward()
    chain.step(2)
    chain_o.step(0)
    into_o.put(half_o, z)
    total = vec_in[1]
    for k in range(1, 4):
        vectors[2 + k].wait_recv()
        total = total + vec_land[k, 1]
    vecs[8:] = total
    chain.step(3)
    into.wait(half)
    chain_o.step(1)

    def block(k, carry):
        src = e.flip((k + 1) // 2 % 2, k // 2)

        @pl.when(k == 1)
        def _():
            hidden.have_x()

        @pl.when(k == 2)
        def _():
            hidden.have_far()

        @pl.when(k == 3)
        def _():
            hidden.have_y()

        h = h_out[src]
        bias_q, bias_v = (bias[B_QUERY : B_QUERY + 1], bias[B_VALUE : B_VALUE + 1])
        q_out[src] = ((nn(h, whole[:, :WIDE]) + bias_q).astype(BF16) * 0.125).astype(BF16)
        mine = src * 2 + p
        k_out[mine] = nn(h, whole[:, WIDE : 2 * WIDE]).astype(BF16)
        remote(k_out.at[mine], k_out.at[mine], kv_send.at[k], kv_recv.at[k], e.twin()).start()
        v_out[mine] = (nn(h, whole[:, 2 * WIDE :]) + bias_v).astype(BF16)
        remote(
            v_out.at[mine], v_out.at[mine], kv_send.at[k + CHIPS], kv_recv.at[k + CHIPS], e.twin()
        ).start()

        @pl.when(k == 1)
        def _():
            chain_o.step(2)

        @pl.when(k == 3)
        def _():
            chain_o.step(3)

        return carry

    lax.fori_loop(0, CHIPS, block, 0)
    into_o.wait(half_o)

    @pl.when(t == CHIPS - 1)
    def _():
        out_w[: SLOTS * HEAD_DIM] = raw[...]

    @pl.when(t < CHIPS - 1)
    def _():
        for i in range(4):
            out_w[i * HEAD_DIM : (i + 1) * HEAD_DIM] = raw[i * 80 : i * 80 + HEAD_DIM]
        out_w[4 * HEAD_DIM : 5 * HEAD_DIM] = jnp.zeros((HEAD_DIM, D), BF16)

    out_w[SLOTS * HEAD_DIM :] = jnp.zeros((WIDE - SLOTS * HEAD_DIM, D), BF16)
    for k in range(CHIPS):
        src = e.flip((k + 1) // 2 % 2, k // 2)
        other = src * 2 + 1 - p
        mine = src * 2 + p
        for ref, j in ((k_out, k), (v_out, k + CHIPS)):
            remote(ref.at[mine], ref.at[mine], kv_send.at[j], kv_recv.at[j], e.twin()).wait_send()
            remote(ref.at[other], ref.at[other], kv_send.at[j], kv_recv.at[j], e.twin()).wait_recv()
    for user in (hidden, chain, chain_o):
        user.sent()
    for copy in vectors:
        copy.wait_send()


def project(x, cot, biases, b_up, w_qkv, w_out, w_up, w_down):
    blocks = jax.ShapeDtypeStruct((CHIPS, ROWS, WIDE), BF16)
    keys = jax.ShapeDtypeStruct((2 * CHIPS, ROWS, WIDE), BF16)
    near, far = (vmem(1), [pl.BlockSpec(memory_space=pl.ANY)])
    return pl.pallas_call(
        project_kernel,
        out_shape=(
            blocks, keys, keys,
            jax.ShapeDtypeStruct((CHIPS, ROWS, D), BF16),
            jax.ShapeDtypeStruct((D, 3 * WIDE), BF16),
            jax.ShapeDtypeStruct((WIDE, D), BF16),
            jax.ShapeDtypeStruct((16, D), F32),
            jax.ShapeDtypeStruct((UP_ROWS + DOWN_ROWS, D), BF16),
            jax.ShapeDtypeStruct((ROWS + 8, D), BF16),
            jax.ShapeDtypeStruct((ROWS, D), BF16),
        ),
        in_specs=near * 11 + far + near + far * 2,
        out_specs=tuple(near * 10),
        scratch_shapes=[
            pltpu.VMEM((144, 3 * D), BF16),
            pltpu.VMEM((144, 3 * WIDE), BF16),
            pltpu.VMEM((48, D), BF16),
            pltpu.VMEM((144, TILE), BF16),
            pltpu.VMEM((4, 144, 3 * WIDE), BF16),
            pltpu.VMEM((4, 48, D), BF16),
            pltpu.VMEM((SLOTS * HEAD_DIM, D), BF16),
            pltpu.VMEM((2, 8, D), F32),
            pltpu.VMEM((4, 2, 8, D), F32),
            pltpu.VMEM((16, WIDE), F32),
            dma(2, 4), dma(2, 4), dma(2, 2, 3), dma(2, 2, 3), dma(6), dma(6),
            dma(2, 4), dma(2, 4), dma(2, 4), dma(2 * CHIPS), dma(2 * CHIPS), dma(8),
        ],
        compiler_params=params(1),
        name="project",
    )(x, cot, *biases, b_up, w_qkv, w_out, w_up, w_down)


def tile_bounds(lengths, block):
    ends = [lengths[0]]
    for i in range(1, 4):
        ends.append(ends[-1] + lengths[i])
    first = block * ROWS
    start_first = 0 * first
    for end in ends:
        start_first = jnp.where(first >= end, end, start_first)
    free = jnp.minimum(block, ends[0] // ROWS)
    resume = jnp.maximum(free + 1, start_first // ROWS)
    masked = jnp.where(free < block, 1 + jnp.maximum(block - resume, 0), 0)
    query_pos = first + lax.broadcasted_iota(jnp.int32, (1, ROWS), 1)
    start = jnp.zeros((1, ROWS), jnp.int32)
    for end in ends:
        start = jnp.where(query_pos >= end, end, start)
    return ends[0], query_pos, start, free, resume, masked


def visible(key_block, prompt, query_pos, start):
    key_pos = key_block * ROWS + lax.broadcasted_iota(jnp.int32, (ROWS, ROWS), 0)
    return (key_pos <= query_pos) & ((key_pos < prompt) | (key_pos >= start))


def half_of(rows, h):
    lane = lax.broadcasted_iota(jnp.int32, rows.shape, 1)
    return jnp.where((lane >= h * HEAD_DIM) & (lane < (h + 1) * HEAD_DIM), rows, jnp.zeros_like(rows))


def attend_kernel(lengths, parity, q, k, v, mixed, lse, turned):
    slab = pl.program_id(0)
    for j in range(2 * CHIPS):
        turned[j] = v[j].astype(F32).T.astype(BF16)

    def run(heads):
        def one(i, carry):
            block = 2 * i + parity[0]
            prompt, query_pos, start, free, resume, masked = tile_bounds(lengths, block)
            queries = [half_of(q[i], h) for h in heads]

            def tile(j, state, mask):
                keys = k[j]
                values = turned[j]
                new = []
                for h, (peak, total, accum) in zip(heads, state):
                    scores = cols_product(keys, queries[h])
                    if mask is not None:
                        scores = jnp.where(mask, scores, NEG)
                    peak_new = jnp.maximum(peak, jnp.max(scores, 0, keepdims=True))
                    factor = jnp.exp(peak - peak_new)
                    expos = jnp.exp(scores - peak_new)
                    total_new = total * factor + jnp.sum(expos, 0, keepdims=True)
                    part = values[h * HEAD_DIM : (h + 1) * HEAD_DIM]
                    accum_new = accum * factor + nn(part, expos.astype(BF16))
                    new.append((peak_new, total_new, accum_new))
                return tuple(new)

            state = tuple(
                (
                    jnp.full((1, ROWS), NEG, F32),
                    jnp.zeros((1, ROWS), F32),
                    jnp.zeros((HEAD_DIM, ROWS), F32),
                )
                for _ in heads
            )

            def other(m, s):
                j = jnp.where(m == 0, block, jnp.where(m == 1, free, resume + m - 2))
                return tile(j, s, visible(j, prompt, query_pos, start))

            state = lax.fori_loop(0, 1 + masked, other, state)
            state = lax.fori_loop(0, free, lambda j, s: tile(j, s, None), state)
            outs = []
            for h, (peak, total, accum) in zip(heads, state):
                outs.append(accum / total)
                lse[0, pl.ds(h * CHIPS + i, 1), :] = peak + jnp.log(total)
            if len(heads) == 1:
                outs.append(jnp.zeros((HEAD_DIM, ROWS), F32))
            mixed[i] = jnp.concatenate(outs, 0).T.astype(BF16)
            return carry

        lax.fori_loop(0, CHIPS, one, 0)

    @pl.when(slab < SLOTS // 2)
    def _():
        run((0, 1))

    @pl.when(slab >= SLOTS // 2)
    def _():
        lse[...] = jnp.zeros_like(lse)
        run((0,))


def slab_spec(count):
    return pl.BlockSpec((count, ROWS, 128), lambda s, *_: (0, 0, s))


def attend(lengths, parity, q, k, v):
    return pl.pallas_call(
        attend_kernel,
        out_shape=(
            jax.ShapeDtypeStruct((CHIPS, ROWS, WIDE), BF16),
            jax.ShapeDtypeStruct((3, 2 * CHIPS, ROWS), F32),
        ),
        grid_spec=pltpu.PrefetchScalarGridSpec(
            num_scalar_prefetch=2,
            grid=(3,),
            in_specs=[slab_spec(CHIPS), slab_spec(2 * CHIPS), slab_spec(2 * CHIPS)],
            out_specs=(
                slab_spec(CHIPS),
                pl.BlockSpec((1, 2 * CHIPS, ROWS), lambda s, *_: (s, 0, 0)),
            ),
            scratch_shapes=[pltpu.VMEM((2 * CHIPS, 128, ROWS), BF16)],
        ),
        compiler_params=pltpu.CompilerParams(vmem_limit_bytes=63 * 2**20),
        cost_estimate=pl.CostEstimate(flops=4 * 10**9, bytes_accessed=5 * 10**6, transcendentals=6 * 10**6),
        name="attend",
    )(lengths, parity, q, k, v)


def attend_back_kernel(
    lengths, parity, q, k, v, mixed, grad, lse, dq, dk, dv, turned, acc_k, acc_v
):
    slab = pl.program_id(0)
    for j in range(2 * CHIPS):
        turned[j] = k[j].astype(F32).T.astype(BF16)
    acc_k[...] = jnp.zeros_like(acc_k)
    acc_v[...] = jnp.zeros_like(acc_v)

    def run(heads):
        def one(i, carry):
            block = 2 * i + parity[0]
            prompt, query_pos, start, free, resume, masked = tile_bounds(lengths, block)
            queries = [half_of(q[i], h) for h in heads]
            grads = [half_of(grad[i], h) for h in heads]
            product = (grad[i].astype(F32) * mixed[i].astype(F32)).T
            deltas = [
                jnp.sum(product[h * HEAD_DIM : (h + 1) * HEAD_DIM], 0, keepdims=True) for h in heads
            ]
            sums = [lse[0, pl.ds(h * CHIPS + i, 1), :] for h in heads]

            def tile(j, state, mask):
                keys, values, keys_t = (k[j], v[j], turned[j])
                new = []
                add_k, add_v = (None, None)
                for h, accum in zip(heads, state):
                    scores = cols_product(keys, queries[h]) - sums[h]
                    if mask is not None:
                        scores = jnp.where(mask, scores, NEG)
                    probs = jnp.exp(scores)
                    grad_probs = cols_product(values, grads[h])
                    ds = (probs * (grad_probs - deltas[h])).astype(BF16)
                    part_v = nn(probs.astype(BF16), grads[h])
                    part_k = nn(ds, queries[h])
                    add_v = part_v if add_v is None else add_v + part_v
                    add_k = part_k if add_k is None else add_k + part_k
                    new.append(accum + nn(keys_t[h * HEAD_DIM : (h + 1) * HEAD_DIM], ds))
                acc_v[j] += add_v
                acc_k[j] += add_k
                return tuple(new)

            state = tuple(jnp.zeros((HEAD_DIM, ROWS), F32) for _ in heads)

            def other(m, s):
                j = jnp.where(m == 0, block, jnp.where(m == 1, free, resume + m - 2))
                return tile(j, s, visible(j, prompt, query_pos, start))

            state = lax.fori_loop(0, 1 + masked, other, state)
            state = list(lax.fori_loop(0, free, lambda j, s: tile(j, s, None), state))
            if len(heads) == 1:
                state.append(jnp.zeros((HEAD_DIM, ROWS), F32))
            dq[i] = (jnp.concatenate(state, 0) * 0.125).T.astype(BF16)
            return carry

        lax.fori_loop(0, CHIPS, one, 0)

    @pl.when(slab < SLOTS // 2)
    def _():
        run((0, 1))

    @pl.when(slab >= SLOTS // 2)
    def _():
        run((0,))

    dk[...] = acc_k[...].astype(BF16)
    dv[...] = acc_v[...].astype(BF16)


def attend_back(lengths, parity, q, k, v, mixed, grad, lse):
    few, many = (slab_spec(CHIPS), slab_spec(2 * CHIPS))
    return pl.pallas_call(
        attend_back_kernel,
        out_shape=(
            jax.ShapeDtypeStruct((CHIPS, ROWS, WIDE), BF16),
            jax.ShapeDtypeStruct((2 * CHIPS, ROWS, WIDE), BF16),
            jax.ShapeDtypeStruct((2 * CHIPS, ROWS, WIDE), BF16),
        ),
        grid_spec=pltpu.PrefetchScalarGridSpec(
            num_scalar_prefetch=2,
            grid=(3,),
            in_specs=[
                few, many, many, few, few,
                pl.BlockSpec((1, 2 * CHIPS, ROWS), lambda s, *_: (s, 0, 0)),
            ],
            out_specs=(few, many, many),
            scratch_shapes=[
                pltpu.VMEM((2 * CHIPS, 128, ROWS), BF16),
                pltpu.VMEM((2 * CHIPS, ROWS, 128), F32),
                pltpu.VMEM((2 * CHIPS, ROWS, 128), F32),
            ],
        ),
        compiler_params=pltpu.CompilerParams(vmem_limit_bytes=63 * 2**20),
        cost_estimate=pl.CostEstimate(flops=10 * 10**9, bytes_accessed=9 * 10**6, transcendentals=6 * 10**6),
        name="attend_back",
    )(lengths, parity, q, k, v, mixed, grad, lse)


def out_kernel(x, mixed, whole, vecs, middle, part, land, send, recv):
    e = Place()
    e.greet(planes=False)
    sums = Scatter(e, part, land, send, recv)

    def block(k, carry):
        dest = e.flip(1 - k // 2, 1 - k % 2)
        part[dest] = nn(mixed[dest], whole[...]).astype(BF16)

        @pl.when(k == 0)
        def _():
            sums.far_ready()

        @pl.when(k == 1)
        def _():
            sums.x_ready()

        @pl.when(k == 2)
        def _():
            sums.y_ready()

        return carry

    lax.fori_loop(0, CHIPS - 1, block, 0)
    total = x[...].astype(F32) + vecs[B_OUT : B_OUT + 1] + nn(mixed[e.t], whole[...])
    sums.relay()
    middle[...] = total + sums.total()
    sums.sent()


def out_project(x, mixed, whole, vecs):
    return pl.pallas_call(
        out_kernel,
        out_shape=jax.ShapeDtypeStruct((ROWS, D), F32),
        in_specs=vmem(4),
        out_specs=vmem(1)[0],
        scratch_shapes=[
            pltpu.VMEM((CHIPS, ROWS, D), BF16),
            pltpu.VMEM((6, HALF, D), BF16),
            dma(6), dma(6),
        ],
        compiler_params=params(2),
        name="out_project",
    )(x, mixed, whole, vecs)


def feed_kernel(
    middle, cot, cot_x, cot_y, cot_far, halves, vecs, out_w, mixed,
    to_x, to_y, to_far, out_own, grad_mid, gh_heads, g_out, g_down, share, sums, up_sum,
    up, down, lefts, rights, part_h, gmid, sum_h_land,
    full, grad_sum, land_up, land_down, land_more, g_up, staged, z_right, z_left, raw, land_out,
    a_send, a_recv, s_send, s_recv, w_local, w_send, w_recv, d_local, d_send, d_recv, g_send, g_recv, z_send, z_recv, c_local,
):
    e = Place()
    t, p = (e.t, e.p)
    hid, act, gpre, cots = (lefts.at[0], lefts.at[1], rights.at[0], rights.at[1])
    full_up, full_down = (full.at[0], full.at[1])
    e.greet()
    into = Halves(e, up, 272, 144, 128, w_local, w_send, w_recv)
    weights = []
    for i in range(4):
        weights.extend(into.copies(halves.at[i, pl.ds(0, 144)], i))
    for i in range(5):
        src = halves.at[i, pl.ds(144, TILE)] if i < 4 else halves.at[t, pl.ds(272, 32)]
        dst = down.at[rows16(256 * i + p * TILE, TILE) if i < 4 else rows16(1024 + p * 32, 32)]
        weights.append(pltpu.make_async_copy(src, dst, d_local.at[i]))
        weights.append(remote(src, dst, d_send.at[i], d_recv.at[i], e.twin()))
    for k, (ref, chip) in enumerate(((cot, t), (cot_x, e.tx), (cot_y, e.ty), (cot_far, e.td))):
        weights.append(pltpu.make_async_copy(ref.at[pl.ds(0, ROWS)], cots.at[chip], c_local.at[k]))
    for copy in weights:
        copy.start()
    normed, inverse = normalize(middle[...])
    hid[t] = (normed * vecs[GAIN_2 : GAIN_2 + 1] + vecs[SHIFT_2 : SHIFT_2 + 1]).astype(BF16)
    hidden = Gather(e, hid.at[t], lambda chip: hid.at[chip], ROWS, HALF, a_send.at[0], a_recv.at[0])
    hidden.start()
    sum_h = Scatter(e, part_h, sum_h_land, s_send, s_recv)
    for copy in weights:
        copy.wait()
    up_sum[...] = jnp.zeros_like(up_sum)

    def block(k, carry):
        src = e.flip((k + 1) // 2 % 2, k // 2)

        @pl.when(k == 1)
        def _():
            hidden.forward()
            hidden.have_x()

        @pl.when(k == 2)
        def _():
            hidden.have_far()

        @pl.when(k == 3)
        def _():
            hidden.have_y()

        pre = nn(hid[src], up[...]) + vecs[B_UP : B_UP + 1]
        cdf = 0.5 * (1.0 + lax.erf(pre * math.sqrt(0.5)))
        slope = cdf + pre * (jnp.exp(-0.5 * pre * pre) * (1.0 / math.sqrt(2.0 * math.pi)))
        act[src] = (pre * cdf).astype(BF16)
        grad = cols_product(cots[src], down[...]) * slope
        low = grad.astype(BF16)
        gpre[src] = low
        up_sum[...] += jnp.sum(low.astype(F32), 0, keepdims=True)
        part_h[src] = cols_product(low, up[...]).astype(BF16)

        @pl.when(k == 1)
        def _():
            sum_h.x_ready()

        @pl.when(k == 2)
        def _():
            sum_h.far_ready()

        @pl.when(k == 3)
        def _():
            sum_h.y_ready()

        return carry

    lax.fori_loop(0, CHIPS, block, 0)
    sum_h.relay()

    ups = [
        remote(
            full_up.at[rows16(i * 272 + (1 - p) * TILE, UP_ROWS)], land_up.at[i],
            g_send.at[0, i], g_recv.at[0, i], e.twin(),
        )
        for i in range(4)
    ]

    def matrices(i, carry):
        full[i] = rows_product(
            lefts[i].reshape(CHIPS * ROWS, D), rights[i].reshape(CHIPS * ROWS, D)
        ).astype(BF16)

        @pl.when(i == 0)
        def _():
            for copy in ups:
                copy.start()

        return carry

    lax.fori_loop(0, 2, matrices, 0)
    swaps = [
        remote(
            full_down.at[rows16(256 * i + (1 - p) * TILE, TILE)], land_down.at[i],
            g_send.at[1, i], g_recv.at[1, i], e.twin(),
        )
        for i in range(4)
    ]
    swaps.append(
        remote(
            full_down.at[rows16(1024 + (1 - p) * 32, 32)], land_more, g_send.at[2, 0], g_recv.at[2, 0], e.twin()
        )
    )
    for copy in swaps:
        copy.start()
    for copy in ups:
        copy.wait()
    for i in range(4):
        own = full_up[rows16(i * 272 + p * TILE, UP_ROWS)].astype(F32)
        g_up[i] = (own + land_up[i].astype(F32)).astype(BF16)
    planes = ZScatter(e, g_up, staged, z_right, z_left, z_send, z_recv)
    planes.begin()
    def outs(k, carry):
        rows = nn(act[e.flip(k % 2, k // 2)], down[...])
        for i, ref in enumerate((out_own, to_x, to_y, to_far)):
            @pl.when(k == i)
            def _():
                if i == 0:
                    ref[...] = middle[...] + vecs[B_DOWN : B_DOWN + 1] + rows
                else:
                    ref[:ROWS] = rows.astype(BF16)

        return carry

    lax.fori_loop(0, CHIPS, outs, 0)

    total = part_h[t].astype(F32) + sum_h.total()
    top = cot[:ROWS].astype(F32)
    grad_middle = top + norm_back(total, normed, inverse, vecs[GAIN_2 : GAIN_2 + 1])
    grad_mid[...] = grad_middle
    low = grad_middle.astype(BF16)
    gmid[t] = low
    spread = Gather(e, gmid.at[t], lambda chip: gmid.at[chip], ROWS, HALF, a_send.at[1], a_recv.at[1])
    spread.start()
    sums[0:1] = jnp.sum(low.astype(F32), 0, keepdims=True)
    sums[1:2] = jnp.sum(top, 0, keepdims=True)
    sums[2:3] = jnp.sum(total * normed, 0, keepdims=True)
    sums[3:4] = jnp.sum(total, 0, keepdims=True)
    sums[4:8] = jnp.zeros((4, D), F32)

    planes.first()
    for copy in swaps:
        copy.wait()
    more = (full_down[rows16(1024 + p * 32, 32)].astype(F32) + land_more[...].astype(F32)).astype(BF16)
    for i in range(4):
        own = full_down[rows16(256 * i + p * TILE, TILE)].astype(F32)
        g_down[i, :TILE] = (own + land_down[i].astype(F32)).astype(BF16)
        g_down[i, TILE:] = more
    spread.forward()
    planes.second()

    def heads(k, carry):
        src = e.flip((k + 1) // 2 % 2, k // 2)

        @pl.when(k == 1)
        def _():
            spread.have_x()

        @pl.when(k == 2)
        def _():
            spread.have_far()

        @pl.when(k == 3)
        def _():
            spread.have_y()

        rows = gmid[src]
        gh_heads[src] = cols_product(rows, out_w[...]).astype(BF16)
        grad_sum[...] += rows_product(mixed[src], rows)
        return carry

    grad_sum[...] = jnp.zeros_like(grad_sum)
    lax.fori_loop(0, CHIPS, heads, 0)
    grad_out = grad_sum[...].astype(BF16)

    @pl.when(t == CHIPS - 1)
    def _():
        raw[...] = grad_out[: SLOTS * HEAD_DIM]

    @pl.when(t < CHIPS - 1)
    def _():
        for i in range(4):
            raw[i * 80 : i * 80 + HEAD_DIM] = grad_out[i * HEAD_DIM : (i + 1) * HEAD_DIM]
            raw[i * 80 + HEAD_DIM : (i + 1) * 80] = jnp.zeros((16, D), BF16)

    swaps = [
        remote(
            raw.at[rows16(i * 80 + (1 - p) * 32, 48)], land_out.at[i], g_send.at[3, i], g_recv.at[3, i], e.twin()
        )
        for i in range(4)
    ]
    for copy in swaps:
        copy.start()
    for copy in swaps:
        copy.wait()
    for i in range(4):
        own = raw[rows16(i * 80 + p * 32, 48)].astype(F32)
        g_out[i] = (own + land_out[i].astype(F32)).astype(BF16)
    planes.last(share)
    for ref in (to_x, to_y, to_far):
        ref[ROWS:] = share[...]
    for user in (hidden, spread, sum_h):
        user.sent()


def feed(middle, cot, others, halves, vecs, out_w, mixed):
    blocks = pltpu.VMEM((CHIPS, ROWS, D), BF16)
    lands = pltpu.VMEM((6, HALF, D), BF16)
    matrix = pltpu.VMEM((D, D), BF16)
    mixture = jax.ShapeDtypeStruct((ROWS + UP_ROWS, D), BF16)
    return pl.pallas_call(
        feed_kernel,
        out_shape=(
            mixture, mixture, mixture,
            jax.ShapeDtypeStruct((ROWS, D), F32),
            jax.ShapeDtypeStruct((ROWS, D), F32),
            jax.ShapeDtypeStruct((CHIPS, ROWS, WIDE), BF16),
            jax.ShapeDtypeStruct((4, 48, D), BF16),
            jax.ShapeDtypeStruct((4, DOWN_ROWS, D), BF16),
            jax.ShapeDtypeStruct((UP_ROWS, D), BF16),
            jax.ShapeDtypeStruct((8, D), F32),
            jax.ShapeDtypeStruct((1, D), F32),
        ),
        in_specs=vmem(9),
        out_specs=tuple(vmem(11)),
        scratch_shapes=[matrix, matrix]
        + [pltpu.VMEM((2, CHIPS, ROWS, D), BF16)] * 2
        + [blocks] * 2
        + [lands, pltpu.VMEM((2, D, D), BF16), pltpu.VMEM((WIDE, D), F32)]
        + [
            pltpu.VMEM((4, UP_ROWS, D), BF16),
            pltpu.VMEM((4, TILE, D), BF16),
            pltpu.VMEM((32, D), BF16),
            pltpu.VMEM((4, UP_ROWS, D), BF16),
            pltpu.VMEM((4, UP_ROWS, D), BF16),
            pltpu.VMEM((3, UP_ROWS, D), BF16),
            pltpu.VMEM((3, UP_ROWS, D), BF16),
            pltpu.VMEM((SLOTS * HEAD_DIM, D), BF16),
            pltpu.VMEM((4, 48, D), BF16),
            dma(2, 6), dma(2, 6), dma(6), dma(6), dma(4), dma(4), dma(4),
            dma(5), dma(5), dma(5), dma(4, 4), dma(4, 4), dma(2, 3), dma(2, 3), dma(4),
        ],
        compiler_params=params(3, 63),
        name="feed",
    )(middle, cot, *others, halves, vecs, out_w, mixed)


def back_kernel(
    x, grad_mid, dq, dk, dv, hid, whole, vecs, share, from_x, from_y, from_far, share_down, out_own, g_out, sums, up_sum,
    output, grad_x, up_out, down_out, qkv_out, o_out, vec_out, b_up_out,
    joint, full, land, land_k, land_v, part, rows_own, sum_land, g_qkv, z_right, z_left, s_qkv,
    s_out, zo_right, zo_left, own_qkv, own_out, all_up, all_down, all_qkv, all_out, local, vec_land, totals, wide,
    kv_send, kv_recv, g_send, g_recv, s_send, s_recv, a_send, a_recv, z_send, z_recv, t_send, t_recv, v_send, v_recv, c_local,
):
    e = Place()
    t, p, z = (e.t, e.p, e.z)
    e.greet()
    swaps = []
    for k in range(CHIPS):
        chip = e.flip(1 - k // 2, 1 - k % 2)
        for j, (ref, dst) in enumerate(((dk, land_k), (dv, land_v))):
            swaps.append(
                remote(ref.at[chip * 2 + 1 - p], dst.at[chip], kv_send.at[j, k], kv_recv.at[j, k], e.twin())
            )
    for copy in swaps:
        copy.start()

    def spread(number, own, everything, rows, cut):
        return Gather(
            e, own, lambda chip: everything.at[p, chip], rows, cut, a_send.at[number], a_recv.at[number]
        )

    def hand(number, own, everything, k):
        chip = e.flip(k % 2, k // 2)
        src = own if k == 0 else everything.at[p, chip]
        return remote(
            src, everything.at[p, chip], t_send.at[number, k], t_recv.at[number, k], e.twin()
        )

    def handed(number, own, everything):
        for k in range(CHIPS):
            chip = e.flip(k % 2, k // 2)
            copy = remote(
                own, everything.at[1 - p, chip], t_send.at[number, k], t_recv.at[number, k], e.twin()
            )
            copy.wait_recv()
            copy.wait_send()

    feeds = [share] + [ref.at[pl.ds(ROWS, UP_ROWS)] for ref in (from_x, from_y, from_far)]
    keeps = []
    for k in range(CHIPS):
        slot = all_up.at[p, e.flip(k % 2, k // 2)]
        keeps.append(pltpu.make_async_copy(feeds[k], slot, c_local.at[k]))
    downs = spread(2, share_down, all_down, DOWN_ROWS, 80)
    downs.start()
    outs = ZScatter(e, g_out, s_out, zo_right, zo_left, z_send.at[0], z_recv.at[0])
    outs.begin()
    local[...] = jnp.zeros_like(local)
    for k in range(CHIPS):
        joint[k, :, :WIDE] = dq[k]

    def trades(a):
        return [
            remote(
                full.at[a, rows16(i * 272 + (1 - p) * TILE, 144)], land.at[a, i],
                g_send.at[a, i], g_recv.at[a, i], e.twin(),
            )
            for i in range(4)
        ]

    def grads(a, carry):
        @pl.when(a == 1)
        def _():
            for copy in swaps:
                copy.wait()
            head_q, head_v = (jnp.zeros((1, WIDE), F32), jnp.zeros((1, WIDE), F32))
            for k in range(CHIPS):
                mine = k * 2 + p
                low_k = (dk[mine].astype(F32) + land_k[k].astype(F32)).astype(BF16)
                low_v = (dv[mine].astype(F32) + land_v[k].astype(F32)).astype(BF16)
                joint[k, :, WIDE : 2 * WIDE] = low_k
                joint[k, :, 2 * WIDE :] = low_v
                head_q = head_q + jnp.sum(dq[k].astype(F32), 0, keepdims=True)
                head_v = head_v + jnp.sum(low_v.astype(F32), 0, keepdims=True)
            local[pl.ds(12 + t, 1), :WIDE] = head_q
            local[pl.ds(12 + t, 1), WIDE : 2 * WIDE] = head_v
            outs.first()

        right = joint[:, :, pl.ds(pl.multiple_of(a * WIDE, TILE), WIDE)]
        full[a] = rows_product(
            hid[...].reshape(CHIPS * ROWS, D), right.reshape(CHIPS * ROWS, WIDE)
        ).astype(BF16)
        for copy in trades(a):
            copy.start()
        return carry

    lax.fori_loop(0, 3, grads, 0)
    downs.forward()
    outs.second()
    summed = Scatter(e, part, sum_land, s_send, s_recv)
    weights = ZScatter(e, g_qkv, s_qkv, z_right, z_left, z_send.at[1], z_recv.at[1])

    def block(k, carry):
        dest = e.flip(1 - k // 2, 1 - k % 2)
        value = cols_product(joint[dest], whole[...])

        @pl.when(k < 3)
        def _():
            part[dest] = value.astype(BF16)

        @pl.when(k == 0)
        def _():
            summed.far_ready()
            for a in range(3):
                for copy in trades(a):
                    copy.wait()
                for i in range(4):
                    own = full[a, rows16(i * 272 + p * TILE, 144)].astype(F32)
                    g_qkv[i, :, a * WIDE : (a + 1) * WIDE] = (own + land[a, i].astype(F32)).astype(BF16)
            weights.begin()

        @pl.when(k == 1)
        def _():
            summed.x_ready()

        @pl.when(k == 2)
        def _():
            summed.y_ready()

        @pl.when(k == 3)
        def _():
            rows_own[...] = value

        return carry

    lax.fori_loop(0, CHIPS, block, 0)
    outs.last(own_out)
    for k in range(CHIPS):
        keeps[k].start()
        slot = all_up.at[p, e.flip(k % 2, k // 2)]
        remote(feeds[k], slot, t_send.at[0, k], t_recv.at[0, k], e.twin()).start()
    hand(3, share_down, all_down, 0).start()
    all_down[p, t] = share_down[...]
    downs.have_x()
    downs.have_y()
    hand(3, share_down, all_down, 1).start()
    hand(3, share_down, all_down, 2).start()
    downs.have_far()
    hand(3, share_down, all_down, 3).start()
    weights.first()
    others = spread(0, own_out, all_out, 48, 32)
    others.start()
    all_out[p, t] = own_out[...]
    hand(1, own_out, all_out, 0).start()
    summed.relay()
    weights.second()
    others.forward()
    weights.last(own_qkv)
    qkvs = spread(1, own_qkv, all_qkv, 144, 80)
    qkvs.start()
    hand(2, own_qkv, all_qkv, 0).start()
    all_qkv[p, t] = own_qkv[...]
    normed, inverse = normalize(x[...].astype(F32))
    total = rows_own[...] + summed.total()
    local[:4] = sums[:4]
    local[4:5] = jnp.sum(total * normed, 0, keepdims=True)
    local[5:6] = jnp.sum(total, 0, keepdims=True)
    local[pl.ds(8 + t, 1), :] = up_sum[...]
    twin = remote(local, vec_land.at[0], v_send.at[0], v_recv.at[0], e.twin())
    twin.start()
    grad_x[...] = (grad_mid[...] + norm_back(total, normed, inverse, vecs[GAIN_1 : GAIN_1 + 1])).T
    twin.wait()
    totals[...] = local[...] + vec_land[0]
    planes = [
        remote(totals, vec_land.at[k], v_send.at[k], v_recv.at[k], e.plane(k)) for k in range(1, 4)
    ]
    for copy in planes:
        copy.start()
    qkvs.forward()
    others.have_x()
    others.have_y()
    hand(1, own_out, all_out, 1).start()
    hand(1, own_out, all_out, 2).start()
    others.have_far()
    hand(1, own_out, all_out, 3).start()
    handed(0, share, all_up)
    for copy in keeps:
        copy.wait()

    def lay_up(q, carry):
        rows = rows16(q * TILE, 144)
        for s in range(CHIPS):
            for i in range(4):
                column = D * i + HEAD_DIM * (i % 2) + 256 * s
                up_out[rows, column : column + 256] = all_up[q, s, :, 256 * i : 256 * (i + 1)]
        for s in range(0, CHIPS, 2):
            pair = [all_up[q, s + i, :, 1024:].astype(F32) for i in range(2)]
            column = D * s + 1024
            up_out[rows, column : column + TILE] = jnp.concatenate(pair, 1).astype(BF16)
        return carry

    lax.fori_loop(0, 2, lay_up, 0)
    qkvs.have_x()
    hand(2, own_qkv, all_qkv, 1).start()
    qkvs.have_y()
    hand(2, own_qkv, all_qkv, 2).start()
    for copy in planes:
        copy.wait()
    local[...] = totals[...] + vec_land[1] + vec_land[2] + vec_land[3]
    chips = [
        remote(local, vec_land.at[3 + k], v_send.at[3 + k], v_recv.at[3 + k], e.chip(chip))
        for k, chip in ((1, e.tx), (2, e.ty), (3, e.td))
    ]
    for copy in chips:
        copy.start()
    qkvs.have_far()
    hand(2, own_qkv, all_qkv, 3).start()

    result = out_own[...]
    for ref in (from_x, from_y, from_far):
        result = result + ref[:ROWS].astype(F32)
    output[...] = result.T.astype(BF16)
    handed(3, share_down, all_down)
    for q in range(2):
        for s in range(CHIPS):
            down_out[rows16(z % 2 * 64 + 256 * s + TILE * q, TILE)] = all_down[q, s, :TILE]
        down_out[rows16((1 - z % 2) * 1024 + 32 * q, 32)] = all_down[q, z, TILE:]
    handed(1, own_out, all_out)
    ahead = (CHIPS - z) % CHIPS * 16
    for s in range(CHIPS - 1):
        o_out[rows16(ahead + HEAD_DIM * s, 48)] = all_out[0, s]
        o_out[rows16(ahead + HEAD_DIM * s + 32, 32)] = all_out[1, s, :32]
    for u in range(SLOTS):
        q, first = ((0, 16 * u) if u < 3 else (1, 16 * u - 32))
        strip = all_out[q, CHIPS - 1, first : first + 16]

        @pl.when(16 * u < ahead)
        def _():
            o_out[16 * u : 16 * u + 16] = strip

        @pl.when(16 * u >= ahead)
        def _():
            o_out[192 + 16 * u : 208 + 16 * u] = strip

    for copy in chips:
        copy.wait()
    totals[...] = local[...] + vec_land[4] + vec_land[5] + vec_land[6]
    wide[...] = jnp.zeros_like(wide)
    wide[:6, :D] = totals[:6]
    columns = {}
    for s, heads in enumerate(HEAD_TABLE):
        for slot, head in enumerate(heads):
            columns[head] = (s, slot * HEAD_DIM)
    lane = lax.broadcasted_iota(jnp.int32, (1, TILE), 1)
    for a in range(2):
        def span(head, side):
            s, column = columns[head]
            start = (column + a * WIDE) // TILE * TILE
            tile = totals[12 + s : 13 + s, start : start + TILE]
            return tile if column % TILE // HEAD_DIM == side else pltpu.roll(tile, HEAD_DIM, 1)

        for head in range(0, HEADS, 2):
            tile = span(head, 0)
            if head + 1 < HEADS:
                tile = jnp.where(lane < HEAD_DIM, tile, span(head + 1, 1))
            wide[6 + a : 7 + a, head * HEAD_DIM : head * HEAD_DIM + TILE] = tile
    for i in range(4):
        @pl.when(z == i)
        def _():
            row = wide[...]
            if i > 0:
                row = pltpu.roll(row, 9 * TILE - D // 4 * i, 1)
            vec_out[...] = row[:, :WIDE]
            pieces = [totals[8 + s : 9 + s, 256 * i : 256 * i + 256] for s in range(CHIPS)]
            more = totals[8 + i : 9 + i, 1024:]
            if i % 2 == 0:
                b_up_out[...] = jnp.concatenate(pieces + [more, more], 1)
            else:
                b_up_out[...] = pltpu.roll(jnp.concatenate(pieces + [more, more], 1), HEAD_DIM, 1)

    handed(2, own_qkv, all_qkv)
    source = {}
    for s, heads in enumerate(HEAD_TABLE):
        for slot, head in enumerate(heads):
            if head >= 0:
                for a in range(3):
                    source[a * HEADS + head] = (s, a * WIDE + slot * HEAD_DIM)

    def lay_qkv(q, carry):
        rows = rows16(q * TILE, 144)

        def piece(g, side):
            s, column = source[g]
            tile = all_qkv[q, s, :, column // TILE * TILE : column // TILE * TILE + TILE].astype(F32)
            return tile if column % TILE // HEAD_DIM == side else pltpu.roll(tile, HEAD_DIM, 1)

        left = lax.broadcasted_iota(jnp.int32, (144, TILE), 1) < HEAD_DIM
        for g in range(0, 3 * HEADS - 1, 2):
            column = g * HEAD_DIM
            qkv_out[rows, column : column + TILE] = jnp.where(left, piece(g, 0), piece(g + 1, 1)).astype(BF16)
        column = (3 * HEADS - 1) * HEAD_DIM
        qkv_out[rows, column : column + HEAD_DIM] = piece(3 * HEADS - 1, 0)[:, :HEAD_DIM].astype(BF16)
        return carry

    lax.fori_loop(0, 2, lay_qkv, 0)
    for user in (downs, others, qkvs, summed):
        user.sent()


def back(x, grad_mid, dq, dk, dv, hid, whole, vecs, share, others, share_down, out_own, g_out, sums, up_sum):
    heads = pltpu.VMEM((CHIPS, ROWS, WIDE), BF16)
    qkv, out = ((144, 3 * WIDE), (48, D))

    def many(count, shape):
        return pltpu.VMEM((count, *shape), BF16)

    return pl.pallas_call(
        back_kernel,
        out_shape=(
            jax.ShapeDtypeStruct((D, ROWS), BF16),
            jax.ShapeDtypeStruct((D, ROWS), F32),
            jax.ShapeDtypeStruct((D // 4, 4 * D), BF16),
            jax.ShapeDtypeStruct((D, D), BF16),
            jax.ShapeDtypeStruct((D // 4, 3 * D), BF16),
            jax.ShapeDtypeStruct((D // 4, D), BF16),
            jax.ShapeDtypeStruct((8, WIDE), F32),
            jax.ShapeDtypeStruct((1, 9 * TILE), F32),
        ),
        in_specs=vmem(17),
        out_specs=tuple(vmem(8)),
        scratch_shapes=[
            pltpu.VMEM((CHIPS, ROWS, 3 * WIDE), BF16),
            pltpu.VMEM((3, D, WIDE), BF16),
            pltpu.VMEM((3, 4, 144, WIDE), BF16),
            heads, heads,
            pltpu.VMEM((CHIPS, ROWS, D), BF16),
            pltpu.VMEM((ROWS, D), F32),
            pltpu.VMEM((6, HALF, D), BF16),
            many(4, qkv), many(3, qkv), many(3, qkv), many(4, qkv),
            many(4, out), many(3, out), many(3, out),
            pltpu.VMEM(qkv, BF16), pltpu.VMEM(out, BF16),
            pltpu.VMEM((2, CHIPS, UP_ROWS, D), BF16),
            pltpu.VMEM((2, CHIPS, DOWN_ROWS, D), BF16),
            pltpu.VMEM((2, CHIPS, *qkv), BF16),
            pltpu.VMEM((2, CHIPS, *out), BF16),
            pltpu.VMEM((16, D), F32),
            pltpu.VMEM((7, 16, D), F32),
            pltpu.VMEM((16, D), F32),
            pltpu.VMEM((8, 9 * TILE), F32),
            dma(2, CHIPS), dma(2, CHIPS), dma(3, 4), dma(3, 4), dma(6), dma(6), dma(3, 6), dma(3, 6),
            dma(2, 2, 3), dma(2, 2, 3), dma(4, 4), dma(4, 4), dma(7), dma(7), dma(4),
        ],
        compiler_params=params(4, 63),
        name="back",
    )(x, grad_mid, dq, dk, dv, hid, whole, vecs, share, *others, share_down, out_own, g_out, sums, up_sum)


def plane_device(
    tokens, seq_lengths, cotangent, ln1_gain, ln1_bias, w_qkv, b_query, b_value, w_out, b_out,
    ln2_gain, ln2_bias, w_up, b_up, w_down, b_down,
):
    c = lax.axis_index("ctx")
    lengths = seq_lengths[0]
    parity = (c % 2)[None].astype(jnp.int32)
    shard = D // 4

    biases = (b_query, b_value, b_out, b_down, ln1_gain, ln1_bias, ln2_gain, ln2_bias)
    q, k, v, hid, whole, out_w, vecs, halves, sent, x = project(
        tokens[0].T, cotangent[0].T, biases, b_up, w_qkv, w_out, w_up, w_down
    )
    halves = lax.all_gather(halves, "wsh", axis=0)

    def from_chips(*arrays):
        return [lax.ppermute(array, "ctx", list(enumerate(to))) for array, to in zip(arrays, flips)]

    flips = [[(i // 2 ^ mask) * 2 + i % 2 for i in range(2 * CHIPS)] for mask in (1, 2, 3)]
    tops = from_chips(sent, sent, sent)
    mixed, lse = attend(lengths, parity, q, k, v)
    middle = out_project(x, mixed, out_w, vecs)
    to_x, to_y, to_far, out_own, grad_mid, grad_heads, g_out, g_down, share, sums, up_sum = feed(
        middle, sent, tops, halves, vecs, out_w, mixed
    )
    others = from_chips(to_x, to_y, to_far)
    share_down = lax.psum_scatter(
        g_down.reshape(4 * DOWN_ROWS, D), "wsh", scatter_dimension=0, tiled=True
    )
    dq, dk, dv = attend_back(lengths, parity, q, k, v, mixed, grad_heads, lse)
    output, grad_x, grad_up, grad_down, grad_qkv, grad_out, vectors, grad_b_up = back(
        x, grad_mid, dq, dk, dv, hid, whole, vecs, share, others, share_down, out_own, g_out, sums, up_sum
    )
    grad_up, grad_down, grad_qkv, grad_out = (
        array.astype(F32) for array in (grad_up, grad_down, grad_qkv, grad_out)
    )

    mine = [row[:shard] for row in vectors]
    grad_b_up = grad_b_up[0, :D]
    return (
        output.T[None], grad_x.T[None],
        mine[4], mine[5], grad_qkv, mine[6], mine[7], grad_out, mine[0],
        mine[2], mine[3], grad_up, grad_b_up, grad_down, mine[1],
    )


def solution(mesh):
    in_specs = (
        P("wsh", "ctx", None),
        P("wsh", None),
        P("wsh", "ctx", None),
        P("wsh"),
        P("wsh"),
        P("wsh", None),
        P("wsh"),
        P("wsh"),
        P("wsh", None),
        P("wsh"),
        P("wsh"),
        P("wsh"),
        P("wsh", None),
        P("wsh"),
        P("wsh", None),
        P("wsh"),
    )
    out_specs = (
        P("wsh", "ctx", None),
        P("wsh", "ctx", None),
        P("wsh"),
        P("wsh"),
        P("wsh", None),
        P("wsh"),
        P("wsh"),
        P("wsh", None),
        P("wsh"),
        P("wsh"),
        P("wsh"),
        P("wsh", None),
        P("wsh"),
        P("wsh", None),
        P("wsh"),
    )
    sizes = (mesh.shape["ctx"], mesh.shape["wsh"])
    body = plane_device if sizes == (2 * CHIPS, 4) else on_device
    return jax.shard_map(
        body, mesh=mesh, in_specs=in_specs, out_specs=out_specs, check_vma=False
    )
```
